32 devices in a mesh: dp: 8 (over z, y), tensor: 4 (over x, core).
Axes of the slice: x: 2, y: 2, z: 4, core: 2. Of those that a mesh axis runs over, the one named last changes fastest.
Arguments:
- audio_codes: int32 [24, 768, 4], P('dp'), may hold values from 0 to 2047
- delay_mask: int32 [24, 768, 4], P('dp'), may hold values from 0 to 1, as said below
- frame_mask: int32 [24, 768], P('dp'), may hold values from 0 to 1, as said below
- text_states: bfloat16 [24, 256, 768], P('dp'), may hold values from -6 to 6
- text_mask: int32 [24, 256], P('dp'), may hold values from 0 to 1, as said below
- attention: float32 [8, 1024, 1024], P(None, 'dp', 'tensor')
- feedforward: float32 [2, 1024, 4096], P(None, 'dp', 'tensor')
- tables: float32 [8, 1024, 2048], P(None, 'dp', 'tensor')
- text_proj: float32 [1024, 768], P('tensor', 'dp'), may hold values from -0.21875 to 0.21875
- norm_params: float32 [9, 1024], P(None, 'dp')
- attention_first: float32 [8, 1024, 1024], P(None, 'dp', 'tensor'), may hold values from -3.8146973e-06 to 3.8146973e-06
- attention_second: float32 [8, 1024, 1024], P(None, 'dp', 'tensor'), may hold values from 4.6591724e-13 to 1.863669e-12
- feedforward_first: float32 [2, 1024, 4096], P(None, 'dp', 'tensor'), may hold values from -3.8146973e-06 to 3.8146973e-06
- feedforward_second: float32 [2, 1024, 4096], P(None, 'dp', 'tensor'), may hold values from 4.6591724e-13 to 1.863669e-12
- tables_first: float32 [8, 1024, 2048], P(None, 'dp', 'tensor'), may hold values from -3.8146973e-06 to 3.8146973e-06
- tables_second: float32 [8, 1024, 2048], P(None, 'dp', 'tensor'), may hold values from 4.6591724e-13 to 1.863669e-12
- text_first: float32 [1024, 768], P('tensor', 'dp'), may hold values from -3.8146973e-06 to 3.8146973e-06
- text_second: float32 [1024, 768], P('tensor', 'dp'), may hold values from 4.6591724e-13 to 1.863669e-12
- norm_first: float32 [9, 1024], P(None, 'dp'), may hold values from -3.8146973e-05 to 3.8146973e-05
- norm_second: float32 [9, 1024], P(None, 'dp'), may hold values from 4.6591724e-11 to 1.863669e-10
Outputs:
- mean_loss: float32 [], replicated
- valid_count: float32 [], replicated
- grad_norm: float32 [], replicated
- new_attention: float32 [8, 1024, 1024], P(None, 'dp', 'tensor')
- low_attention: bfloat16 [8, 1024, 1024], P(None, 'dp', 'tensor')
- new_attention_first: float32 [8, 1024, 1024], P(None, 'dp', 'tensor')
- new_attention_second: float32 [8, 1024, 1024], P(None, 'dp', 'tensor')
- new_feedforward: float32 [2, 1024, 4096], P(None, 'dp', 'tensor')
- low_feedforward: bfloat16 [2, 1024, 4096], P(None, 'dp', 'tensor')
- new_feedforward_first: float32 [2, 1024, 4096], P(None, 'dp', 'tensor')
- new_feedforward_second: float32 [2, 1024, 4096], P(None, 'dp', 'tensor')
- new_tables: float32 [8, 1024, 2048], P(None, 'dp', 'tensor')
- low_tables: bfloat16 [8, 1024, 2048], P(None, 'dp', 'tensor')
- new_tables_first: float32 [8, 1024, 2048], P(None, 'dp', 'tensor')
- new_tables_second: float32 [8, 1024, 2048], P(None, 'dp', 'tensor')
- new_text_proj: float32 [1024, 768], P('tensor', 'dp')
- low_text_proj: bfloat16 [1024, 768], P('tensor', 'dp')
- new_text_first: float32 [1024, 768], P('tensor', 'dp')
- new_text_second: float32 [1024, 768], P('tensor', 'dp')
- new_norm_params: float32 [9, 1024], P(None, 'dp')
- new_norm_first: float32 [9, 1024], P(None, 'dp')
- new_norm_second: float32 [9, 1024], P(None, 'dp')
The draws below stay inside these ranges and needn't reach their ends.
Inputs may be any that keep to these rules, and one draw needn't show every extreme that they name: Each clip's frame_mask is 1 on a prefix of at least 384 frames and 0 after it; some clip is full. delay_mask[c, s, k] is 1 exactly where k <= s < n_c + k, with n_c the length of clip c's prefix in frame_mask. Each clip's text_mask is 1 on a prefix of at least 64 positions and 0 after it; some clip is full.
All inputs are finite; a program needn't handle non-finite values.
Results may differ from the reference program's by a relative error of at most 0.017.
Values may be sent and summed in bfloat16 or wider, within the bound.
No kernel may reach another device: no remote copies, remote signals or barrier semaphores. Data moves between devices by JAX's collectives and lax.ppermute only.
A program may use at most 320 MiB of HBM per device.

```python
import math
import jax
import jax.numpy as jnp
import numpy as np
from jax import lax

D = 1024
HEADS = 16
HEAD_DIM = 64
FF = 4096
CODEBOOK_COUNT = 4
CODES = 2048
TDIM = 768
FRAMES = 768
TEXT = 256
QBLOCK = 768
STEP = 5
CLIPS = 24


def clip_lengths(key, longest, shortest):
    drawn = jax.random.randint(key, (CLIPS,), shortest, longest + 1)
    return drawn.at[0].set(longest)


def draw_frame_mask(key, part):
    lengths = clip_lengths(jax.random.fold_in(key, 11), FRAMES, FRAMES // 2)
    return (jnp.arange(FRAMES, dtype=jnp.int32)[None, :] < lengths[:, None]).astype(jnp.int32)


def draw_delay_mask(key, part):
    lengths = clip_lengths(jax.random.fold_in(key, 11), FRAMES, FRAMES // 2)
    frame_index = jnp.arange(FRAMES, dtype=jnp.int32)[None, :, None]
    book_index = jnp.arange(CODEBOOK_COUNT, dtype=jnp.int32)[None, None, :]
    inside = (frame_index >= book_index) & (frame_index < lengths[:, None, None] + book_index)
    return inside.astype(jnp.int32)


def draw_text_mask(key, part):
    lengths = clip_lengths(jax.random.fold_in(key, 23), TEXT, TEXT // 4)
    return (jnp.arange(TEXT, dtype=jnp.int32)[None, :] < lengths[:, None]).astype(jnp.int32)


def draw_attention(key, part):
    normal = jax.random.normal(key, (8, D, D), jnp.float32)
    scales = jnp.concatenate([jnp.full((6, 1, 1), D ** (-0.5), jnp.float32), jnp.full((2, 1, 1), (D // 16) ** (-0.5), jnp.float32)], 0)
    return normal * scales


def draw_feedforward(key, part):
    normal = jax.random.normal(key, (2, D, FF), jnp.float32)
    scales = jnp.concatenate([jnp.full((1, 1, 1), D ** (-0.5), jnp.float32), jnp.full((1, 1, 1), FF ** (-0.5), jnp.float32)], 0)
    return normal * scales


def draw_tables(key, part):
    first_key, second_lookup_key = jax.random.split(key)
    embed = jax.random.normal(first_key, (CODEBOOK_COUNT, D, CODES), jnp.float32) * 0.25
    heads = jax.random.normal(second_lookup_key, (CODEBOOK_COUNT, D, CODES), jnp.float32) * (2.0 / D ** 0.5)
    return jnp.concatenate([embed, heads], 0)


def draw_norm_params(key, part):
    first_key, second_lookup_key = jax.random.split(key)
    gains = 1.0 + 0.15 * jax.random.normal(first_key, (4, D), jnp.float32)
    shifts = 0.3 * jax.random.normal(second_lookup_key, (5, D), jnp.float32)
    return jnp.concatenate([gains, shifts], 0)


def place_ends(values, key, low, top_value):
    spot = [jax.random.randint(jax.random.fold_in(key, axis), (), 0, length) for axis, length in enumerate(values.shape)]
    widest = values.shape.index(max(values.shape))
    next_to = spot[:widest] + [(spot[widest] + 1) % values.shape[widest]] + spot[widest + 1:]
    return values.at[tuple(spot)].set(low).at[tuple(next_to)].set(top_value)


def levels(stream_key, dims, pieces, least, top_value):
    def one(axis_at, shards_of):
        draws = jax.random.uniform(jax.random.fold_in(jax.random.fold_in(stream_key, 6), axis_at), (shards_of,), jnp.float32, least / len(pieces), top_value / len(pieces))
        return jnp.repeat(jnp.exp(draws), dims[axis_at] // shards_of).reshape((-1,) + (1,) * (len(dims) - axis_at - 1))

    gain = one(*pieces[0])
    for cut in pieces[1:]:
        gain = gain * one(*cut)
    return gain


def rank_table(number_of, lean):
    portions = [(1 << 20) // math.isqrt(grade ** lean) + 1 for grade in range(1, number_of + 1)]
    deviation = 1 + sum(portions) // (1 << 30)
    return np.cumsum(np.array([max(1, weight // deviation) for weight in portions]))


def ranked_ids(own_key, shape, count, lean):
    grid = rank_table(count, lean)
    pick = jax.random.randint(jax.random.fold_in(own_key, 1), shape, 0, int(grid[count - 1]))
    rank = jnp.searchsorted(jnp.asarray(grid, jnp.int32), pick, side="right")
    return jax.random.permutation(jax.random.fold_in(own_key, 2), count)[rank].astype(jnp.int32)


def gaussian(stream_key, shape, width, most, cuts=(), kind=jnp.bfloat16):
    gain = levels(stream_key, shape, cuts, -0.22, 0.18) if cuts else 1.0
    result = jax.random.normal(stream_key, shape, jnp.float32) * width * gain
    return jnp.minimum(jnp.maximum(result, -most), most).astype(kind)


def setup_inputs(seed: int = 0) -> dict:
    keys = jax.random.split(jax.random.key(seed), 21)
    audio_codes = place_ends(ranked_ids(keys[0], (CLIPS, FRAMES, CODEBOOK_COUNT), CODES, 2), jax.random.fold_in(keys[0], 3), 0, CODES - 1).astype(jnp.int32)
    delay_mask = draw_delay_mask(jax.random.fold_in(keys[20], 71), 0)
    frame_mask = draw_frame_mask(jax.random.fold_in(keys[20], 71), 0)
    text_states = gaussian(keys[3], (CLIPS, TEXT, TDIM), 1.0, 6.0, ((0, 8),))
    text_mask = draw_text_mask(jax.random.fold_in(keys[20], 71), 0)
    attention = draw_attention(jax.random.fold_in(keys[20], 71), 0)
    feedforward = draw_feedforward(jax.random.fold_in(keys[20], 71), 0)
    tables = draw_tables(jax.random.fold_in(keys[20], 71), 0)
    text_proj = gaussian(keys[8], (D, TDIM), TDIM ** -0.5, 0.21875, ((0, 4), (1, 8)), jnp.float32)
    norm_params = draw_norm_params(jax.random.fold_in(keys[20], 71), 0)
    attention_first = gaussian(keys[10], (8, D, D), (0.004 / (8 * D * D + 2 * D * FF + 2 * CODEBOOK_COUNT * D * CODES + D * TDIM) ** 0.5), 3.814697265625e-06, ((1, 8), (2, 4)), jnp.float32)
    attention_second = jnp.clip(jnp.exp(math.log(1.863668941393115e-12) - 1.3862944 * jax.random.uniform(keys[11], (8, D, D), jnp.float32) ** levels(keys[11], (8, D, D), ((1, 8), (2, 4)), -0.2, 0.2)), 4.659172353482788e-13, 1.863668941393115e-12)
    feedforward_first = gaussian(keys[12], (2, D, FF), (0.004 / (8 * D * D + 2 * D * FF + 2 * CODEBOOK_COUNT * D * CODES + D * TDIM) ** 0.5), 3.814697265625e-06, ((1, 8), (2, 4)), jnp.float32)
    feedforward_second = jnp.clip(jnp.exp(math.log(1.863668941393115e-12) - 1.3862944 * jax.random.uniform(keys[13], (2, D, FF), jnp.float32) ** levels(keys[13], (2, D, FF), ((1, 8), (2, 4)), -0.2, 0.2)), 4.659172353482788e-13, 1.863668941393115e-12)
    tables_first = gaussian(keys[14], (2 * CODEBOOK_COUNT, D, CODES), (0.004 / (8 * D * D + 2 * D * FF + 2 * CODEBOOK_COUNT * D * CODES + D * TDIM) ** 0.5), 3.814697265625e-06, ((1, 8), (2, 4)), jnp.float32)
    tables_second = jnp.clip(jnp.exp(math.log(1.863668941393115e-12) - 1.3862944 * jax.random.uniform(keys[15], (2 * CODEBOOK_COUNT, D, CODES), jnp.float32) ** levels(keys[15], (2 * CODEBOOK_COUNT, D, CODES), ((1, 8), (2, 4)), -0.2, 0.2)), 4.659172353482788e-13, 1.863668941393115e-12)
    text_first = gaussian(keys[16], (D, TDIM), (0.004 / (8 * D * D + 2 * D * FF + 2 * CODEBOOK_COUNT * D * CODES + D * TDIM) ** 0.5), 3.814697265625e-06, ((0, 4), (1, 8)), jnp.float32)
    text_second = jnp.clip(jnp.exp(math.log(1.863668941393115e-12) - 1.3862944 * jax.random.uniform(keys[17], (D, TDIM), jnp.float32) ** levels(keys[17], (D, TDIM), ((0, 4), (1, 8)), -0.2, 0.2)), 4.659172353482788e-13, 1.863668941393115e-12)
    norm_first = gaussian(keys[18], (9, D), (0.04 / (8 * D * D + 2 * D * FF + 2 * CODEBOOK_COUNT * D * CODES + D * TDIM) ** 0.5), 3.814697265625e-05, ((1, 8),), jnp.float32)
    norm_second = jnp.clip(jnp.exp(math.log(1.863668941393115e-10) - 1.3862944 * jax.random.uniform(keys[19], (9, D), jnp.float32) ** levels(keys[19], (9, D), ((1, 8),), -0.2, 0.2)), 4.659172353482788e-11, 1.863668941393115e-10)
    return {"audio_codes": audio_codes, "delay_mask": delay_mask, "frame_mask": frame_mask, "text_states": text_states, "text_mask": text_mask, "attention": attention, "feedforward": feedforward, "tables": tables, "text_proj": text_proj, "norm_params": norm_params, "attention_first": attention_first, "attention_second": attention_second, "feedforward_first": feedforward_first, "feedforward_second": feedforward_second, "tables_first": tables_first, "tables_second": tables_second, "text_first": text_first, "text_second": text_second, "norm_first": norm_first, "norm_second": norm_second}


@jax.custom_vjp
def low(v):
    return lax.optimization_barrier(v.astype(jnp.bfloat16)).astype(jnp.float32)

@jax.custom_vjp
def reduced_backward(v):
    return v

def low_keep(v):
    return (low(v), None)

def low_pass(kept, grad):
    return (grad,)

def back_keep(v):
    return (v, None)

def back_low(kept, grad):
    return (low(grad),)
low.defvjp(low_keep, low_pass)
reduced_backward.defvjp(back_keep, back_low)
peak_value = lax.Precision.HIGHEST
clip_limit = 0.004
stability_offset = 1e-08
weight_decay = 0.01
moment_decay = 0.5
rate_matrix = 0.03
rate_table = 0.05
rate_norm = 0.2

def layer_norm(values, gain_row, shift_row):
    center = values - lax.optimization_barrier(jnp.mean(values, axis=-1, keepdims=True))
    spread = lax.optimization_barrier(jnp.mean(center * center, axis=-1, keepdims=True))
    return center * lax.rsqrt(spread + 1e-05) * gain_row + shift_row

def positions_table(position_count, feature_count):
    half_width = feature_count // 2
    frequency = jnp.exp(jnp.arange(half_width, dtype=jnp.float32) * (-math.log(10000.0) / (half_width - 1)))
    angles = jnp.arange(position_count, dtype=jnp.float32)[:, None] * frequency[None, :]
    return jnp.concatenate([jnp.cos(angles), jnp.sin(angles)], axis=1)

def allowed_mask(block_start, key_valid, causal):
    key_count = key_valid.shape[0]
    allowed = jnp.broadcast_to(key_valid[None, :] > 0, (QBLOCK, key_count))
    if causal:
        row_index = block_start + jnp.arange(QBLOCK, dtype=jnp.int32)
        allowed = allowed & (row_index[:, None] >= jnp.arange(key_count, dtype=jnp.int32)[None, :])
    return allowed

def attend(queries, key_rows, value_rows, key_valid, causal):
    frames = queries.shape[0]
    blocks = frames // QBLOCK
    query_blocks = queries.reshape(blocks, QBLOCK, HEADS, HEAD_DIM)
    starts = jnp.arange(blocks, dtype=jnp.int32) * QBLOCK

    def one_block(inputs):
        query_rows, block_start = inputs
        products = jnp.einsum('qhe,khe->hqk', query_rows, key_rows, precision=peak_value)
        scores = reduced_backward(products * HEAD_DIM ** (-0.5))
        scores = jnp.where(allowed_mask(block_start, key_valid, causal)[None], scores, -1e+30)
        highest_score = lax.optimization_barrier(jnp.max(scores, axis=-1, keepdims=True))
        exponent = jnp.exp(scores - highest_score)
        weights = exponent / lax.optimization_barrier(jnp.sum(exponent, axis=-1, keepdims=True))
        return jnp.einsum('hqk,khe->qhe', low(weights), value_rows, precision=peak_value)
    outputs = lax.map(jax.checkpoint(one_block), (query_blocks, starts))
    return outputs.reshape(frames, HEADS * HEAD_DIM)

def forward(params, clip_codes, clip_targets, clip_weight, clip_text, clip_valid):
    attention, feedforward, tables, text_proj, norm_params = [low(weight) for weight in params]
    frames = clip_codes.shape[0]
    embedded = jnp.zeros((frames, D), jnp.float32)
    for codebook in range(CODEBOOK_COUNT):
        embedded = embedded + jnp.take(tables[codebook], clip_codes[:, codebook], axis=1).T
    hidden = reduced_backward(embedded) + positions_table(frames, D)
    head_shape = (frames, HEADS, HEAD_DIM)
    normalized_rows = low(layer_norm(hidden, norm_params[0], norm_params[4]))
    projected = [low(reduced_backward(jnp.dot(normalized_rows, attention[member], precision=peak_value))) for member in range(3)]
    mixed = attend(projected[0].reshape(head_shape), projected[1].reshape(head_shape), projected[2].reshape(head_shape), jnp.ones((frames,), jnp.int32), True)
    mixed = low(reduced_backward(mixed))
    hidden = hidden + reduced_backward(jnp.dot(mixed, attention[6].T, precision=peak_value))
    normalized_rows = low(layer_norm(hidden, norm_params[1], norm_params[5]))
    cross_query = low(reduced_backward(jnp.dot(normalized_rows, attention[3], precision=peak_value)))
    text_hidden = low(reduced_backward(jnp.dot(clip_text, text_proj.T, precision=peak_value) + norm_params[8]))
    text_shape = (clip_text.shape[0], HEADS, HEAD_DIM)
    cross_key = low(reduced_backward(jnp.dot(text_hidden, attention[4], precision=peak_value)))
    cross_value = low(reduced_backward(jnp.dot(text_hidden, attention[5], precision=peak_value)))
    mixed = attend(cross_query.reshape(head_shape), cross_key.reshape(text_shape), cross_value.reshape(text_shape), clip_valid, False)
    mixed = low(reduced_backward(mixed))
    hidden = hidden + reduced_backward(jnp.dot(mixed, attention[7].T, precision=peak_value))
    normalized_rows = low(layer_norm(hidden, norm_params[2], norm_params[6]))
    inner_values = reduced_backward(jnp.dot(normalized_rows, feedforward[0], precision=peak_value))
    activated = low(jax.nn.gelu(inner_values, approximate=False))
    hidden = hidden + reduced_backward(jnp.dot(activated, feedforward[1].T, precision=peak_value))
    normalized_rows = low(layer_norm(hidden, norm_params[3], norm_params[7]))
    output_logits = reduced_backward(jnp.einsum('nj,cja->nca', normalized_rows, tables[CODEBOOK_COUNT:], precision=peak_value))
    highest_logit = lax.optimization_barrier(jnp.max(output_logits, axis=-1, keepdims=True))
    log_total = highest_logit[..., 0] + jnp.log(lax.optimization_barrier(jnp.sum(jnp.exp(output_logits - highest_logit), axis=-1)))
    picked = jnp.take_along_axis(output_logits, clip_targets[..., None], axis=-1)[..., 0]
    return jnp.sum((log_total - picked) * clip_weight)

def adam_update(weight, gradient, first_moment, second_moment, step_rate, factor):
    clipped = gradient * factor
    new_first = moment_decay * first_moment + (1.0 - moment_decay) * clipped
    new_second = moment_decay * second_moment + (1.0 - moment_decay) * clipped * clipped
    first_hat = new_first / (1.0 - moment_decay ** STEP)
    second_hat = new_second / (1.0 - moment_decay ** STEP)
    new_weight = weight * (1.0 - step_rate * weight_decay) - step_rate * first_hat / (jnp.sqrt(second_hat) + stability_offset)
    return (new_weight, new_first, new_second)

def reference(audio_codes, delay_mask, frame_mask, text_states, text_mask, attention, feedforward, tables, text_proj, norm_params, attention_first, attention_second, feedforward_first, feedforward_second, tables_first, tables_second, text_first, text_second, norm_first, norm_second):
    frame_live = (jnp.arange(FRAMES, dtype=jnp.int32) < FRAMES - 1).astype(jnp.int32)
    loss_weight = (delay_mask * frame_mask[:, :, None] * frame_live[None, :, None]).astype(jnp.float32)
    targets = jnp.roll(audio_codes, -1, axis=1)
    valid_count = jnp.sum(loss_weight)
    params = (attention, feedforward, tables, text_proj, norm_params)
    zero_grads = tuple((jnp.zeros_like(weight) for weight in params))

    def one_clip(carried, inputs):
        gradients, loss_total = carried
        clip_codes, clip_targets, clip_weight, clip_text, clip_valid = inputs

        def clip_forward(weights):
            return forward(weights, clip_codes, clip_targets, clip_weight, clip_text, clip_valid)
        clip_value, pullback = jax.vjp(clip_forward, params)
        clip_grads, = pullback(jnp.ones_like(clip_value) / valid_count)
        return ((jax.tree.map(jnp.add, gradients, clip_grads), loss_total + clip_value), None)
    (gradients, loss_total), unused = lax.scan(one_clip, (zero_grads, jnp.zeros((), jnp.float32)), (audio_codes, targets, loss_weight, text_states.astype(jnp.float32), text_mask))
    squares = sum((jnp.sum(gradient * gradient) for gradient in gradients))
    grad_norm = jnp.sqrt(squares)
    factor = clip_limit / jnp.maximum(grad_norm, clip_limit)
    attn_new, attn_first_new, attn_second_new = adam_update(attention, gradients[0], attention_first, attention_second, rate_matrix, factor)
    ffn_new, updated_feedforward_first, ffn_second_new = adam_update(feedforward, gradients[1], feedforward_first, feedforward_second, rate_matrix, factor)
    table_new, table_first_new, table_second_new = adam_update(tables, gradients[2], tables_first, tables_second, rate_table, factor)
    text_new, text_first_new, text_second_new = adam_update(text_proj, gradients[3], text_first, text_second, rate_matrix, factor)
    norm_new, norm_first_new, norm_second_new = adam_update(norm_params, gradients[4], norm_first, norm_second, rate_norm, factor)
    return (loss_total / valid_count, valid_count, grad_norm, attn_new, attn_new.astype(jnp.bfloat16), attn_first_new, attn_second_new, ffn_new, ffn_new.astype(jnp.bfloat16), updated_feedforward_first, ffn_second_new, table_new, table_new.astype(jnp.bfloat16), table_first_new, table_second_new, text_new, text_new.astype(jnp.bfloat16), text_first_new, text_second_new, norm_new, norm_first_new, norm_second_new)
```

```python
from functools import partial
import math

import jax
import jax.numpy as jnp
from jax import lax
from jax.experimental import pallas as pl
from jax.experimental.pallas import tpu as pltpu
from jax.sharding import PartitionSpec as P

HEAD_DIM = 64
STEP = 5
BLOCK = 256
NEG = -1e30
LOW = jnp.bfloat16
F32 = jnp.float32

clip_limit = 0.004
stability_offset = 1e-08
weight_decay = 0.01
moment_decay = 0.5
rate_matrix = 0.03
rate_table = 0.05
rate_norm = 0.2


def nn(a, b):
    return lax.dot_general(a, b, (((1,), (0,)), ((), ())), preferred_element_type=F32)


def nt(a, b):
    return lax.dot_general(a, b, (((1,), (1,)), ((), ())), preferred_element_type=F32)


def tn(a, b):
    return lax.dot_general(a, b, (((0,), (0,)), ((), ())), preferred_element_type=F32)


def sds(shape, kind):
    return jax.ShapeDtypeStruct(shape, kind)


def scalars():
    return pl.BlockSpec(memory_space=pltpu.SMEM)


def whole(a):
    rank = len(a.shape)
    return pl.BlockSpec(a.shape, lambda i: (0,) * rank)


def member(a, axis, size, index):
    block = a.shape[:axis] + (size,) + a.shape[axis + 1 :]
    place = tuple(index if d == axis else 0 for d in range(len(a.shape)))
    return pl.BlockSpec(block, lambda i: place)


def later(body, count, at):
    def ordered(*refs):
        return body(*refs[:at], *refs[at + count :])

    return ordered


def anywhere():
    return pl.BlockSpec(memory_space=pl.ANY)


def kernel(body, outs, operands, specs, flops=0, scratch=(), name=None, exps=0, after=(), limit=40):
    outs = tuple(outs)
    nbytes = sum(math.prod(o.shape) * jnp.dtype(o.dtype).itemsize for o in outs)
    for a, s in zip(operands, specs):
        shape = a.shape if s.block_shape is None else s.block_shape
        nbytes += math.prod(shape) * jnp.dtype(a.dtype).itemsize
    return pl.pallas_call(
        later(body, len(after), len(operands)),
        out_shape=outs,
        grid=(1,),
        in_specs=list(specs) + [anywhere()] * len(after),
        out_specs=tuple(whole(o) for o in outs),
        scratch_shapes=scratch,
        compiler_params=pltpu.CompilerParams(vmem_limit_bytes=limit << 20),
        cost_estimate=pl.CostEstimate(
            flops=int(flops), bytes_accessed=int(nbytes), transcendentals=int(exps)
        ),
        name=name,
    )(*operands, *after)


def flat(ref):
    w = ref[...]
    return w.reshape(-1, w.shape[-1])


def half_rows(core, height):
    return (
        pl.ds(pl.multiple_of(core * height, height), height),
        pl.ds(pl.multiple_of((1 - core) * height, height), height),
    )


def attend_block(query, keys, values, head_masks, diagonal, bias):
    rows, width = query.shape
    lane = lax.broadcasted_iota(jnp.int32, (rows, 128), 1)
    column = lax.broadcasted_iota(jnp.int32, (rows, width), 1) // HEAD_DIM
    mixed = jnp.zeros((rows, width), F32)
    totals = jnp.zeros((rows, 128), F32)
    count = keys.shape[0]
    for h, mask in enumerate(head_masks):
        s = nt(query * mask, keys)
        if diagonal is not None:
            last = jnp.where(diagonal, s[:, count - rows :], NEG)
            s = last if count == rows else jnp.concatenate([s[:, : count - rows], last], axis=1)
        if bias is not None:
            s = s + bias
        top = jnp.max(s, axis=1, keepdims=True)
        e = jnp.exp(s - top)
        total = jnp.sum(e, axis=1, keepdims=True)
        p = (e * (1.0 / total)).astype(LOW)
        mixed = jnp.where(column == h, nn(p, values), mixed)
        totals = jnp.where(lane == h, top + jnp.log(total), totals)
    return mixed, totals


def masks_of(width):
    head = lax.broadcasted_iota(jnp.int32, (1, width), 1) // HEAD_DIM
    return [(head == h).astype(F32).astype(LOW) for h in range(width // HEAD_DIM)]


def triangle(size):
    row = lax.broadcasted_iota(jnp.int32, (size, size), 0)
    col = lax.broadcasted_iota(jnp.int32, (size, size), 1)
    return row >= col


def self_forward_body(
    core_ref, own_ref, got_ref, wq_ref, wk_ref, wv_ref, wo_ref,
    q_ref, k_ref, v_ref, o_ref, lse_ref, keep_ref, send_ref, tot_ref,
):
    height = own_ref.shape[0]
    frames, width = q_ref.shape
    mine, other = half_rows(core_ref[0], height)
    for w_ref, to_ref in ((wq_ref, q_ref), (wk_ref, k_ref), (wv_ref, v_ref)):
        w = flat(w_ref)
        to_ref[mine, :] = nn(own_ref[...], w).astype(LOW)
        to_ref[other, :] = nn(got_ref[...], w).astype(LOW)
    scale = jnp.asarray(HEAD_DIM**-0.5, LOW)
    head_masks = masks_of(width)
    diagonal = triangle(BLOCK)
    for i in range(frames // BLOCK):
        rows = slice(i * BLOCK, (i + 1) * BLOCK)
        mixed, totals = attend_block(
            q_ref[rows, :] * scale,
            k_ref[: (i + 1) * BLOCK, :],
            v_ref[: (i + 1) * BLOCK, :],
            head_masks,
            diagonal,
            None,
        )
        o_ref[rows, :] = mixed.astype(LOW)
        tot_ref[rows, :] = totals
    lse_ref[...] = jnp.transpose(tot_ref[...])[:8, :]
    wo = flat(wo_ref)
    send_ref[...] = nt(o_ref[other, :], wo).astype(LOW)
    keep_ref[...] = nt(o_ref[mine, :], wo)


def cross_forward_body(
    core_ref, own_ref, got_ref, bias_ref, k_ref, v_ref, wq_ref, wo_ref,
    q_ref, o_ref, lse_ref, keep_ref, send_ref, tot_ref,
):
    height = own_ref.shape[0]
    frames, width = q_ref.shape
    mine, other = half_rows(core_ref[0], height)
    w = flat(wq_ref)
    q_ref[mine, :] = nn(own_ref[...], w).astype(LOW)
    q_ref[other, :] = nn(got_ref[...], w).astype(LOW)
    scale = jnp.asarray(HEAD_DIM**-0.5, LOW)
    head_masks = masks_of(width)
    for i in range(frames // BLOCK):
        rows = slice(i * BLOCK, (i + 1) * BLOCK)
        mixed, totals = attend_block(
            q_ref[rows, :] * scale, k_ref[...], v_ref[...], head_masks, None, bias_ref[...]
        )
        o_ref[rows, :] = mixed.astype(LOW)
        tot_ref[rows, :] = totals
    lse_ref[...] = jnp.transpose(tot_ref[...])[:8, :]
    wo = flat(wo_ref)
    send_ref[...] = nt(o_ref[other, :], wo).astype(LOW)
    keep_ref[...] = nt(o_ref[mine, :], wo)


def erf(x):
    return lax.erf(x)


def ffn_forward_body(
    core_ref, own_ref, got_ref, w1_ref, w2_ref, act_ref, slope_ref, keep_ref, send_ref
):
    height = own_ref.shape[0]
    mine, other = half_rows(core_ref[0], height)
    w1 = flat(w1_ref)
    w2 = flat(w2_ref)
    for source, rows, to_ref in ((got_ref, other, send_ref), (own_ref, mine, keep_ref)):
        u = nn(source[...], w1)
        phi = 0.5 * (1.0 + erf(u * (2.0**-0.5)))
        act = (u * phi).astype(LOW)
        density = jnp.exp(-0.5 * u * u) * ((2.0 * math.pi) ** -0.5)
        act_ref[rows, :] = act
        slope_ref[rows, :] = (phi + u * density).astype(LOW)
        to_ref[...] = nt(act, w2).astype(to_ref.dtype)


def head_forward_body(
    core_ref, own_ref, got_ref, target_ref, w_ref, logits_ref, stats_ref, tot_ref
):
    height = own_ref.shape[0]
    books, vocab = w_ref.shape[1], w_ref.shape[3]
    halves = half_rows(core_ref[0], height)
    lane = lax.broadcasted_iota(jnp.int32, (height, 128), 1)
    code = lax.broadcasted_iota(jnp.int32, (height, vocab), 1)
    for source, rows in zip((own_ref, got_ref), halves):
        target = target_ref[rows, :]
        y = source[...]
        totals = jnp.zeros((height, 128), F32)
        for k in range(books):
            w = w_ref[:, k].reshape(-1, vocab)
            s = nn(y, w)
            logits_ref[rows, k * vocab : (k + 1) * vocab] = s
            top = jnp.max(s, axis=1, keepdims=True)
            total = jnp.sum(jnp.exp(s - top), axis=1, keepdims=True)
            pick = jnp.sum(jnp.where(code == target[:, k : k + 1], s, 0.0), axis=1, keepdims=True)
            totals = jnp.where(lane == k, top + jnp.log(total), totals)
            totals = jnp.where(lane == books + k, pick, totals)
        tot_ref[rows, :] = totals
    stats_ref[...] = jnp.transpose(tot_ref[...])[: 2 * books, :]


def head_backward_body(
    core_ref, logits_ref, total_ref, weight_ref, target_ref, w_ref,
    grad_ref, keep_ref, send_ref, col_ref,
):
    height = keep_ref.shape[0]
    books, vocab = w_ref.shape[1], w_ref.shape[3]
    mine, other = half_rows(core_ref[0], height)
    frames = logits_ref.shape[0]
    wide = jnp.concatenate(
        [total_ref[...], jnp.zeros((128 - total_ref.shape[0], frames), F32)], axis=0
    )
    col_ref[...] = jnp.transpose(wide)
    code = lax.broadcasted_iota(jnp.int32, (height, vocab), 1)
    for rows, to_ref in ((other, send_ref), (mine, keep_ref)):
        target = target_ref[rows, :]
        weight = weight_ref[rows, :]
        total = col_ref[rows, :]
        acc = None
        for k in range(books):
            s = logits_ref[rows, k * vocab : (k + 1) * vocab]
            p = jnp.exp(s - total[:, k : k + 1])
            hit = jnp.where(code == target[:, k : k + 1], 1.0, 0.0)
            g = ((p - hit) * weight[:, k : k + 1]).astype(LOW)
            grad_ref[rows, k * vocab : (k + 1) * vocab] = g
            part = nt(g, w_ref[:, k].reshape(-1, vocab))
            acc = part if acc is None else acc + part
        to_ref[...] = acc.astype(to_ref.dtype)


def ffn_backward_body(
    core_ref, own_ref, got_ref, slope_ref, w1_ref, w2_ref, grad_ref, keep_ref, send_ref
):
    height = own_ref.shape[0]
    mine, other = half_rows(core_ref[0], height)
    w1 = flat(w1_ref)
    w2 = flat(w2_ref)
    for source, rows, to_ref in ((got_ref, other, send_ref), (own_ref, mine, keep_ref)):
        g = (nn(source[...], w2) * slope_ref[rows, :].astype(F32)).astype(LOW)
        grad_ref[rows, :] = g
        to_ref[...] = nt(g, w1).astype(to_ref.dtype)


def attend_back(
    q, k, v, g, lse, head_masks, scale, diagonal, bias, dq_ref, rows, dk_ref, dv_ref, first
):
    count, width = k.shape
    step = q.shape[0]
    dq = jnp.zeros((step, width), F32)
    dk = jnp.zeros((count, width), F32)
    dv = jnp.zeros((count, width), F32)
    for h, mask in enumerate(head_masks):
        qm = q * mask
        gm = g * mask
        s = nt(k, qm)
        if diagonal is not None:
            last = jnp.where(diagonal, s[count - step :, :], NEG)
            s = last if count == step else jnp.concatenate([s[: count - step, :], last], axis=0)
        if bias is not None:
            s = s + bias
        p = jnp.exp(s - lse[h : h + 1, :])
        dp = nt(v, gm)
        inner = jnp.sum(p * dp, axis=0, keepdims=True)
        ds = (p * (dp - inner)).astype(LOW)
        dq = dq + tn(ds, k * mask)
        dk = dk + nn(ds, qm)
        dv = dv + nn(p.astype(LOW), gm)
    dq_ref[rows, :] = (dq * scale).astype(LOW)
    dk_ref[:count, :] = dk if first else dk_ref[:count, :] + dk
    dv_ref[:count, :] = dv if first else dv_ref[:count, :] + dv


def self_backward_body(
    core_ref, own_ref, got_ref, q_ref, k_ref, v_ref, lse_ref, wq_ref, wk_ref, wv_ref, wo_ref,
    grad_ref, keep_ref, send_ref, g_ref, dq_ref, dk_acc, dv_acc,
):
    height = own_ref.shape[0]
    frames, width = q_ref.shape
    mine, other = half_rows(core_ref[0], height)
    wo = flat(wo_ref)
    g_ref[mine, :] = nn(own_ref[...], wo).astype(LOW)
    g_ref[other, :] = nn(got_ref[...], wo).astype(LOW)
    scale = HEAD_DIM**-0.5
    head_masks = masks_of(width)
    row = lax.broadcasted_iota(jnp.int32, (BLOCK, BLOCK), 0)
    col = lax.broadcasted_iota(jnp.int32, (BLOCK, BLOCK), 1)
    diagonal = col >= row
    blocks = frames // BLOCK
    for i in reversed(range(blocks)):
        rows = slice(i * BLOCK, (i + 1) * BLOCK)
        count = (i + 1) * BLOCK
        attend_back(
            q_ref[rows, :] * jnp.asarray(scale, LOW),
            k_ref[:count, :],
            v_ref[:count, :],
            g_ref[rows, :],
            lse_ref[:, rows],
            head_masks,
            scale,
            diagonal,
            None,
            dq_ref,
            rows,
            dk_acc,
            dv_acc,
            i == blocks - 1,
        )
    grad_ref[:, :width] = dq_ref[...]
    grad_ref[:, width : 2 * width] = dk_acc[...].astype(LOW)
    grad_ref[:, 2 * width :] = dv_acc[...].astype(LOW)
    for rows, to_ref in ((other, send_ref), (mine, keep_ref)):
        part = None
        for n, w_ref in enumerate((wq_ref, wk_ref, wv_ref)):
            term = nt(grad_ref[rows, n * width : (n + 1) * width], flat(w_ref))
            part = term if part is None else part + term
        to_ref[...] = part.astype(to_ref.dtype)


def cross_backward_body(
    core_ref, own_ref, got_ref, bias_ref, q_ref, k_ref, v_ref, lse_ref, wq_ref, wo_ref,
    dq_ref, dk_ref, dv_ref, keep_ref, send_ref, g_ref, dk_acc, dv_acc,
):
    height = own_ref.shape[0]
    frames, width = q_ref.shape
    mine, other = half_rows(core_ref[0], height)
    wo = flat(wo_ref)
    g_ref[mine, :] = nn(own_ref[...], wo).astype(LOW)
    g_ref[other, :] = nn(got_ref[...], wo).astype(LOW)
    scale = HEAD_DIM**-0.5
    head_masks = masks_of(width)
    for i in range(frames // BLOCK):
        rows = slice(i * BLOCK, (i + 1) * BLOCK)
        attend_back(
            q_ref[rows, :] * jnp.asarray(scale, LOW),
            k_ref[...],
            v_ref[...],
            g_ref[rows, :],
            lse_ref[:, rows],
            head_masks,
            scale,
            None,
            bias_ref[...],
            dq_ref,
            rows,
            dk_acc,
            dv_acc,
            i == 0,
        )
    dk_ref[...] = dk_acc[...].astype(LOW)
    dv_ref[...] = dv_acc[...].astype(LOW)
    wq = flat(wq_ref)
    for rows, to_ref in ((other, send_ref), (mine, keep_ref)):
        to_ref[...] = nt(dq_ref[rows, :], wq).astype(to_ref.dtype)


def normalize(values, gain, shift):
    center = values - jnp.mean(values, axis=1, keepdims=True)
    spread = jnp.mean(center * center, axis=1, keepdims=True)
    return center * lax.rsqrt(spread + 1e-05) * gain + shift


def norm_body(which, hidden_ref, part_ref, far_ref, norm_ref, new_ref, out_ref):
    new = hidden_ref[...] + (part_ref[...].astype(F32) + far_ref[...].astype(F32))
    new_ref[...] = new
    out_ref[...] = normalize(
        new, norm_ref[which : which + 1, :], norm_ref[which + 4 : which + 5, :]
    ).astype(LOW)


def embed_norm_body(side_ref, place_ref, norm_ref, *refs):
    *part_refs, new_ref, out_ref = refs
    side = side_ref[0]
    rows = part_refs[0].shape[0]
    for s, part in enumerate(part_refs):
        at = pl.ds(pl.multiple_of((side ^ s) * rows, rows), rows)
        new_ref[at, :] = part[...].astype(F32) + place_ref[at, :]
    out_ref[...] = normalize(new_ref[...], norm_ref[0:1, :], norm_ref[4:5, :]).astype(LOW)


def norm_back_body(which, hidden_ref, part_ref, far_ref, *refs):
    *before, norm_ref, new_ref, low_ref, sums_ref = refs
    values = hidden_ref[...]
    grad = part_ref[...].astype(F32) + far_ref[...].astype(F32)
    gain = norm_ref[which : which + 1, :]
    center = values - jnp.mean(values, axis=1, keepdims=True)
    spread = jnp.mean(center * center, axis=1, keepdims=True)
    inverse = lax.rsqrt(spread + 1e-05)
    unit = center * inverse
    scaled = grad * gain
    first = jnp.mean(scaled, axis=1, keepdims=True)
    second = jnp.mean(scaled * unit, axis=1, keepdims=True)
    new = inverse * (scaled - first - unit * second)
    if before:
        new = before[0][...] + new
    new_ref[...] = new
    low_ref[...] = new.astype(LOW)

    @pl.when(pl.program_id(0) == 0)
    def _():
        sums_ref[...] = jnp.zeros(sums_ref.shape, F32)

    sums_ref[0:1, :] += jnp.sum(grad * unit, axis=0, keepdims=True)
    sums_ref[1:2, :] += jnp.sum(grad, axis=0, keepdims=True)


def norm_rows_kernel(body, outs, operands, norm_rows, after, steps=4):
    height, width = operands[0].shape
    rows = height // steps

    def spec(a):
        if a.shape[0] == height:
            return pl.BlockSpec((rows, width), lambda i: (i, 0))
        return pl.BlockSpec(a.shape, lambda i: (0, 0))

    operands = list(operands) + [norm_rows]
    nbytes = sum(
        math.prod(a.shape) * jnp.dtype(a.dtype).itemsize for a in operands + list(outs)
    )
    return pl.pallas_call(
        later(body, len(after), len(operands)),
        out_shape=tuple(outs),
        grid=(steps,),
        in_specs=[spec(a) for a in operands] + [anywhere()] * len(after),
        out_specs=tuple(spec(o) for o in outs),
        compiler_params=pltpu.CompilerParams(vmem_limit_bytes=24 << 20),
        cost_estimate=pl.CostEstimate(
            flops=20 * height * width, bytes_accessed=nbytes, transcendentals=0
        ),
        name="norm",
    )(*operands, *after)


def weight_grad_body(clips, core_ref, *refs):
    pairs = refs[: 2 * clips]
    rights = refs[2 * clips : 3 * clips]
    out_ref, turned = refs[3 * clips :]
    height = pairs[0].shape[0]
    frames = rights[0].shape[0]

    @pl.when(pl.program_id(0) == 0)
    def _():
        core = core_ref[0]
        for c in range(clips):
            for j, at in ((0, core), (1, 1 - core)):
                place = pl.ds(pl.multiple_of(c * frames + at * height, 128), height)
                turned[:, place] = jnp.transpose(pairs[2 * c + j][...])

    total = None
    for c in range(clips):
        part = nn(turned[:, c * frames : (c + 1) * frames], rights[c][...])
        total = part if total is None else total + part
    out_ref[...] = total.astype(LOW).reshape(out_ref.shape)


def weight_grad(core, pairs, rights, dp, group, name, after):
    clips = len(pairs)
    width = pairs[0][0].shape[1]
    frames, columns = rights[0].shape
    lefts = [half for pair in pairs for half in pair]
    members = columns // group
    nbytes = 2 * (2 * clips * frames * (width + columns) // 2 + width * columns)
    return pl.pallas_call(
        later(partial(weight_grad_body, clips), 1, 1 + 3 * clips),
        out_shape=sds((dp, members, width // dp, group), LOW),
        grid=(members,),
        in_specs=[scalars()]
        + [pl.BlockSpec(a.shape, lambda i: (0, 0)) for a in lefts]
        + [pl.BlockSpec((frames, group), lambda i: (0, i)) for _ in rights]
        + [anywhere()],
        out_specs=pl.BlockSpec((dp, 1, width // dp, group), lambda i: (0, i, 0, 0)),
        scratch_shapes=[pltpu.VMEM((width, clips * frames), LOW)],
        compiler_params=pltpu.CompilerParams(vmem_limit_bytes=56 << 20),
        cost_estimate=pl.CostEstimate(
            flops=2 * clips * frames * width * columns, bytes_accessed=nbytes, transcendentals=0
        ),
        name=name,
    )(core, *lefts, *rights, after)


def embed_body(base_ref, codes_ref, *refs):
    *table_refs, out_ref = refs
    books, features, vocab = table_refs[0].shape
    rows = codes_ref.shape[1]
    chunk = min(256, vocab)
    code = lax.broadcasted_iota(jnp.int32, (rows, chunk), 1)
    acc = jnp.zeros((rows, features), F32)
    for k in range(books):
        column = codes_ref[0, :, k : k + 1]
        for b, table in enumerate(table_refs):
            local = column - base_ref[b]
            for v in range(0, vocab, chunk):
                hit = jnp.where(code == local - v, 1.0, 0.0).astype(LOW)
                acc = acc + nt(hit, table[k, :, v : v + chunk])
    out_ref[0] = acc.astype(LOW)


def embed(base, codes, tables, after):
    blocks, rows, books = codes.shape
    features = tables[0].shape[1]
    vocab = tables[0].shape[2] * len(tables)
    return pl.pallas_call(
        later(embed_body, len(after), 2 + len(tables)),
        out_shape=sds((blocks, rows, features), LOW),
        grid=(blocks,),
        in_specs=[scalars(), pl.BlockSpec((1, rows, books), lambda i: (i, 0, 0))]
        + [whole(t) for t in tables]
        + [anywhere()] * len(after),
        out_specs=pl.BlockSpec((1, rows, features), lambda i: (i, 0, 0)),
        compiler_params=pltpu.CompilerParams(vmem_limit_bytes=56 << 20),
        cost_estimate=pl.CostEstimate(
            flops=4 * blocks * rows * books * vocab * features,
            bytes_accessed=2 * books * vocab * features + blocks * rows * (features + 512),
            transcendentals=0,
        ),
        name="embed",
    )(base, codes, *tables, *after)


def embed_back_body(base_ref, codes_ref, *refs):
    *grad_refs, out_ref, all_ref = refs
    rows, features = grad_refs[0].shape
    vocab = out_ref.shape[3]
    book = pl.program_id(1)
    chunk = min(256, vocab)

    @pl.when((pl.program_id(0) == 0) & (book == 0))
    def _():
        for j, g in enumerate(grad_refs):
            all_ref[j * rows : (j + 1) * rows, :] = g[...]

    base = base_ref[pl.program_id(0)]
    line = codes_ref[0]
    line = line[0:1, :]
    code = lax.broadcasted_iota(jnp.int32, (chunk, line.shape[1]), 0)
    for v in range(0, vocab, chunk):
        hit = jnp.where(code == line - (base + v), 1.0, 0.0).astype(LOW)
        out_ref[0, 0, :, v : v + chunk] = jnp.transpose(nn(hit, all_ref[...])).astype(LOW)


def embed_back(base, lines, grads, vocab):
    parts = base.shape[0]
    books, _, total = lines.shape
    features = grads[0].shape[1]
    return pl.pallas_call(
        embed_back_body,
        out_shape=sds((parts, books, features, vocab), LOW),
        grid=(parts, books),
        in_specs=[scalars(), pl.BlockSpec((1, 8, total), lambda i, k: (k, 0, 0))]
        + [pl.BlockSpec(g.shape, lambda i, k: (0, 0)) for g in grads],
        out_specs=pl.BlockSpec((1, 1, features, vocab), lambda i, k: (i, k, 0, 0)),
        scratch_shapes=[pltpu.VMEM((total, features), LOW)],
        compiler_params=pltpu.CompilerParams(vmem_limit_bytes=56 << 20),
        cost_estimate=pl.CostEstimate(
            flops=4 * parts * books * vocab * features * total,
            bytes_accessed=2 * parts * books * features * vocab + 2 * total * features,
            transcendentals=0,
        ),
        name="embed_back",
    )(base, lines, *grads)


def gather_features_body(where_ref, *refs):
    *part_refs, out_ref = refs
    features = part_refs[0].shape[1]
    for m, part in enumerate(part_refs):
        at = pl.ds(pl.multiple_of(where_ref[m] * features, features), features)
        out_ref[:, at] = part[...]


def split_features_body(where_ref, side_ref, *refs):
    clips = side_ref.shape[0] - 1
    grads, outs = refs[:clips], refs[clips:]
    features = outs[0].shape[1]
    rows = outs[0].shape[0] // clips
    at_rows = pl.ds(pl.multiple_of(side_ref[0] * rows, rows), rows)
    for m, out_ref in enumerate(outs):
        at = pl.ds(pl.multiple_of(where_ref[m] * features, features), features)
        for c in range(clips):
            out_ref[c * rows : (c + 1) * rows, :] = grads[c][at_rows, at]


def text_body(where_ref, *refs):
    *part_refs, wk_ref, wv_ref, tp_ref, k_ref, v_ref = refs
    columns = part_refs[0].shape[1]
    for m, part in enumerate(part_refs):
        at = pl.ds(pl.multiple_of(where_ref[m] * columns, columns), columns)
        tp_ref[:, at] = part[...]
    tp = tp_ref[...]
    k_ref[...] = nn(tp, flat(wk_ref)).astype(LOW)
    v_ref[...] = nn(tp, flat(wv_ref)).astype(LOW)


def text_back_body(dk_ref, dv_ref, wk_ref, wv_ref, tp_ref, part_ref, gk_ref, gv_ref):
    dk, dv = dk_ref[...], dv_ref[...]
    part_ref[...] = (nt(dk, flat(wk_ref)) + nt(dv, flat(wv_ref))).astype(LOW)
    turned = jnp.transpose(tp_ref[...])
    gk_ref[...] = nn(turned, dk).astype(LOW).reshape(gk_ref.shape)
    gv_ref[...] = nn(turned, dv).astype(LOW).reshape(gv_ref.shape)


def positions_rows(start, count, feature_count):
    half_width = feature_count // 2
    frequency = jnp.exp(
        jnp.arange(half_width, dtype=F32) * (-math.log(10000.0) / (half_width - 1))
    )
    angles = (start + jnp.arange(count, dtype=jnp.int32)).astype(F32)[:, None] * frequency[None, :]
    return jnp.concatenate([jnp.cos(angles), jnp.sin(angles)], axis=1)


def adam_update(weight, gradient, first_moment, second_moment, step_rate, factor):
    clipped = gradient * factor
    new_first = moment_decay * first_moment + (1.0 - moment_decay) * clipped
    new_second = moment_decay * second_moment + (1.0 - moment_decay) * clipped * clipped
    first_hat = new_first / (1.0 - moment_decay**STEP)
    second_hat = new_second / (1.0 - moment_decay**STEP)
    new_weight = weight * (1.0 - step_rate * weight_decay) - step_rate * first_hat / (
        jnp.sqrt(second_hat) + stability_offset
    )
    return (new_weight, new_first, new_second)


def swap(values, axis, mask):
    size = lax.axis_size(axis)
    return lax.ppermute(values, axis, [(i, i ^ mask) for i in range(size)])


def on_device(
    audio_codes,
    delay_mask,
    frame_mask,
    text_states,
    text_mask,
    attention,
    feedforward,
    tables,
    text_proj,
    norm_params,
    attention_first,
    attention_second,
    feedforward_first,
    feedforward_second,
    tables_first,
    tables_second,
    text_first,
    text_second,
    norm_first,
    norm_second,
):
    clips, frames, books = audio_codes.shape
    text_len, text_width = text_states.shape[1:]
    dp = lax.axis_size("dp")
    tensor = lax.axis_size("tensor")
    group = lax.axis_index("dp")
    place = lax.axis_index("tensor")
    core = place & 1
    side = place >> 1
    sides = tensor // 2
    height = frames // 2
    strip = height // sides
    share = attention.shape[1]
    columns = attention.shape[2]
    width = share * dp
    vocab = tables.shape[2]
    text_share = text_proj.shape[1]
    core_arg = core.astype(jnp.int32).reshape(1)
    side_arg = side.astype(jnp.int32).reshape(1)
    swap_core = partial(swap, axis="tensor", mask=1)

    def spread_tensor(values):
        held = [values]
        mask = tensor // 2
        order = [0]
        while mask:
            held = held + [swap(v, "tensor", mask) for v in held]
            order = order + [o | mask for o in order]
            mask //= 2
        return [v for _, v in sorted(zip(order, held), key=lambda t: t[0])]

    def collect_tensor(parts):
        mask = 1
        live = {m: p for m, p in enumerate(parts)}
        while mask < tensor:
            fresh = {}
            for m in live:
                if not m & mask:
                    got = swap(live[m | mask].astype(LOW), "tensor", mask)
                    fresh[m] = live[m].astype(F32) + got.astype(F32)
            live = fresh
            mask *= 2
        return live[0]

    def across(values):
        own = values
        mask = 2
        rest = None
        while mask < tensor:
            got = swap(own, "tensor", mask)
            mask *= 2
            if mask < tensor:
                own = (own.astype(F32) + got.astype(F32)).astype(LOW)
            rest = got
        if rest is None:
            rest = jnp.zeros_like(own)
        return own, rest

    def total_over(values, axes):
        for axis in axes:
            mask = 1
            while mask < lax.axis_size(axis):
                values = values + swap(values, axis, mask)
                mask *= 2
        return values

    last = []

    def run(body, outs, operands, specs, after=(), **rest):
        results = kernel(body, outs, operands, specs, after=last + list(after), **rest)
        last[:] = [results[-1]]
        return results

    norm_pad = jnp.pad(norm_params.astype(LOW), ((0, 16 - norm_params.shape[0]), (0, columns - share)))
    attn_flat = jnp.concatenate(
        [attention.astype(LOW).reshape(-1, columns), text_proj.astype(LOW).T, norm_pad], axis=0
    )
    attn_all = lax.all_gather(attn_flat, "dp", axis=0)
    ffn_all = lax.all_gather(feedforward.astype(LOW), "dp", axis=0)
    head_all = lax.all_gather(tables[books:].astype(LOW), "dp", axis=0)

    frame_live = (jnp.arange(frames, dtype=jnp.int32) < frames - 1).astype(jnp.int32)
    weight_int = delay_mask * frame_mask[:, :, None] * frame_live[None, :, None]
    start = core * height + side * strip
    strip_codes = lax.dynamic_slice_in_dim(audio_codes, start, strip, 1)
    lines = jnp.transpose(strip_codes, (2, 0, 1)).reshape(books, clips * strip)
    count_line = jnp.broadcast_to(jnp.sum(weight_int), (1, clips * strip))
    packet = jnp.concatenate([lines, count_line], axis=0)[None]
    mask = 1
    while mask < dp:
        packet = jnp.concatenate([packet, swap(packet, "dp", mask)], axis=0)
        mask *= 2
    valid_count = jnp.sum(packet[:, books, 0]).astype(F32)
    all_lines = packet[:, :books]
    all_codes = jnp.transpose(all_lines, (0, 2, 1))
    back_lines = jnp.broadcast_to(
        jnp.transpose(all_lines, (1, 0, 2)).reshape(books, 1, dp * clips * strip),
        (books, 8, dp * clips * strip),
    )
    vocab_base = (place ^ jnp.arange(tensor, dtype=jnp.int32)) * vocab
    group_order = group ^ jnp.arange(dp, dtype=jnp.int32)
    place_order = place ^ jnp.arange(tensor, dtype=jnp.int32)

    table_parts = spread_tensor(tables[:books].astype(LOW))
    step = max(1, dp // 4)
    arrived = [None] * dp
    for low_end in reversed(range(0, dp, step)):
        embedded = embed(
            vocab_base, all_codes[low_end : low_end + step], table_parts, list(last)
        )
        last[:] = [embedded]
        for m in range(low_end, low_end + step):
            piece = embedded[m - low_end]
            arrived[m] = swap(piece, "dp", m) if m else piece
    aligned = share % 128 == 0
    if aligned:
        (strips,) = run(
            gather_features_body,
            [sds((clips * strip, width), LOW)],
            [group_order] + arrived,
            [scalars()] + [whole(a) for a in arrived],
            name="gather_features",
        )
    else:
        strips = jnp.take(jnp.stack(arrived), group_order, axis=0)
        strips = jnp.transpose(strips, (1, 0, 2)).reshape(clips * strip, width)
    placed = positions_rows(core * height, height, width)

    norm_rows = attn_all[:, 8 * share + text_share :, :share]
    norm_rows = jnp.transpose(norm_rows, (1, 0, 2)).reshape(16, width).astype(F32)

    def w_attn(n):
        return member(attn_all, 1, share, n)

    def w_ffn(n):
        return member(ffn_all, 1, 1, n)

    half_sds = sds((height, width), F32)
    half_low = sds((height, width), LOW)

    def norm_step(which, hidden, parts):
        new, out = norm_rows_kernel(
            partial(norm_body, which), [half_sds, half_low], [hidden, *parts], norm_rows, last
        )
        last[:] = [out]
        return new, (out, swap_core(out))

    def norm_back(which, hidden, parts, before):
        operands = [hidden, *parts] + ([before] if before is not None else [])
        new, out, sums = norm_rows_kernel(
            partial(norm_back_body, which),
            [half_sds, half_low, sds((8, width), F32)],
            operands,
            norm_rows,
            last,
        )
        last[:] = [out]
        return new, (out, swap_core(out)), sums

    def reduce_rows(keep, send):
        got = swap_core(send)
        return across((keep + got.astype(F32)).astype(LOW))

    text_rows = text_states.reshape(clips * text_len, text_width)
    text_weight = attn_all[:, 8 * share : 8 * share + text_share, :].reshape(text_width, columns)
    text_bias = lax.dynamic_slice_in_dim(norm_rows[8], place * columns, columns, 0)
    text_local = (nn(text_rows, text_weight) + text_bias).astype(LOW)
    text_parts = spread_tensor(text_local)
    text_bias_row = jnp.where(text_mask > 0, 0.0, NEG).astype(F32)
    bias_columns = jnp.transpose(text_bias_row)

    full = sds((frames, columns), LOW)
    lse_sds = sds((8, frames), F32)
    tot = [pltpu.VMEM((frames, 128), F32)]
    heads = columns // HEAD_DIM
    score_flops = 2 * heads * frames * HEAD_DIM
    units = feedforward.shape[2]
    inner = sds((frames, units), LOW)
    every = range(clips)

    def embed_step(c):
        mine = strips[c * strip : (c + 1) * strip]
        parts = [mine] + [swap(mine, "tensor", 2 * s) for s in range(1, sides)]
        operands = [side_arg, placed, norm_rows] + parts
        new, out = run(
            embed_norm_body,
            [half_sds, half_low],
            operands,
            [scalars()] + [whole(a) for a in operands[1:]],
            flops=10 * height * width,
            name="embed_norm",
        )
        return new, (out, swap_core(out))

    def self_step(pair):
        operands = [core_arg, *pair, attn_all, attn_all, attn_all, attn_all]
        *kept, keep, send = run(
            self_forward_body,
            [full, full, full, full, lse_sds, half_sds, half_low],
            operands,
            [scalars()] + [whole(a) for a in pair] + [w_attn(0), w_attn(1), w_attn(2), w_attn(6)],
            flops=8 * frames * width * columns + 4 * score_flops * frames,
            scratch=tot,
            name="self_forward",
        )
        return kept, reduce_rows(keep, send)

    def text_step():
        operands = [place_order] + text_parts + [attn_all, attn_all]
        return run(
            text_body,
            [
                sds((clips * text_len, width), LOW),
                sds((clips * text_len, columns), LOW),
                sds((clips * text_len, columns), LOW),
            ],
            operands,
            [scalars()] + [whole(a) for a in text_parts] + [w_attn(4), w_attn(5)],
            flops=4 * clips * text_len * width * columns,
            name="text",
        )

    def cross_step(c, pair):
        k = text_key[c * text_len : (c + 1) * text_len]
        v = text_value[c * text_len : (c + 1) * text_len]
        operands = [core_arg, *pair, text_bias_row[c : c + 1], k, v, attn_all, attn_all]
        q, o, lse, keep, send = run(
            cross_forward_body,
            [full, full, lse_sds, half_sds, half_low],
            operands,
            [scalars()] + [whole(a) for a in operands[1:6]] + [w_attn(3), w_attn(7)],
            flops=4 * frames * width * columns + 4 * score_flops * text_len,
            scratch=tot,
            name="cross_forward",
        )
        return (q, k, v, o, lse), reduce_rows(keep, send)

    def ffn_step(pair):
        *kept, keep, send = run(
            ffn_forward_body,
            [inner, inner, half_sds, half_low],
            [core_arg, *pair, ffn_all, ffn_all],
            [scalars()] + [whole(a) for a in pair] + [w_ffn(0), w_ffn(1)],
            flops=4 * frames * width * units,
            name="ffn_forward",
        )
        return kept, reduce_rows(keep, send)

    hidden = [[None] * clips for _ in range(4)]
    pairs = [[None] * clips for _ in range(4)]
    kept = [[None] * clips for _ in range(3)]
    moving = [None] * clips
    for c in every:
        hidden[0][c], pairs[0][c] = embed_step(c)
        kept[0][c], moving[c] = self_step(pairs[0][c])
    text_hidden, text_key, text_value = text_step()
    for c in every:
        hidden[1][c], pairs[1][c] = norm_step(1, hidden[0][c], moving[c])
        kept[1][c], moving[c] = cross_step(c, pairs[1][c])
    for c in every:
        hidden[2][c], pairs[2][c] = norm_step(2, hidden[1][c], moving[c])
        kept[2][c], moving[c] = ffn_step(pairs[2][c])

    targets = (jnp.roll(audio_codes, -1, axis=1) - place * vocab).astype(jnp.int32)
    loss_weight = weight_int.astype(F32)
    grad_weight = loss_weight / valid_count
    loss_part = [None] * clips
    sums = [[], [], [], []]

    def head_step(c, pair):
        operands = [core_arg, *pair, targets[c], head_all]
        logits, stats = run(
            head_forward_body,
            [sds((frames, books * vocab), F32), sds((2 * books, frames), F32)],
            operands,
            [scalars()] + [whole(a) for a in operands[1:]],
            flops=2 * frames * width * books * vocab,
            scratch=tot,
            name="head_forward",
        )
        total, pick = stats[:books], stats[books:]
        mask = 1
        while mask < tensor:
            far = swap(jnp.concatenate([total, pick], axis=0), "tensor", mask)
            high = jnp.maximum(total, far[:books])
            total = high + jnp.log(jnp.exp(total - high) + jnp.exp(far[:books] - high))
            pick = pick + far[books:]
            mask *= 2
        loss_part[c] = jnp.sum((total - pick) * jnp.transpose(loss_weight[c]))
        return logits, jnp.concatenate([total, total], axis=0)

    def head_back_step(c, logits, total):
        operands = [core_arg, logits, total, grad_weight[c], targets[c], head_all]
        grad, keep, send = run(
            head_backward_body,
            [sds((frames, books * vocab), LOW), half_sds, half_low],
            operands,
            [scalars()] + [whole(a) for a in operands[1:]],
            flops=2 * frames * width * books * vocab,
            scratch=tot,
            name="head_backward",
        )
        return grad, reduce_rows(keep, send)

    def weights(lefts, rights, group_columns, name):
        result = weight_grad(core_arg, lefts, rights, dp, group_columns, name, last[0])
        last[:] = [result]
        return result

    logit_grads = [None] * clips
    ready = [None] * clips
    for c in every:
        hidden[3][c], pairs[3][c] = norm_step(3, hidden[2][c], moving[c])
        ready[c] = head_step(c, pairs[3][c])
        if c:
            logit_grads[c - 1], moving[c - 1] = head_back_step(c - 1, *ready[c - 1])
    logit_grads[-1], moving[-1] = head_back_step(clips - 1, *ready[-1])
    head_grads = weights(pairs[3], logit_grads, vocab, "head_weights")
    head_sum = lax.psum_scatter(head_grads, "dp", scatter_dimension=0, tiled=False)

    def ffn_back_step(c, pair):
        slope = kept[2][c][1]
        grad, keep, send = run(
            ffn_backward_body,
            [inner, half_sds, half_low],
            [core_arg, *pair, slope, ffn_all, ffn_all],
            [scalars()] + [whole(a) for a in pair] + [whole(slope), w_ffn(0), w_ffn(1)],
            flops=4 * frames * width * units,
            name="ffn_backward",
        )
        return grad, reduce_rows(keep, send)

    grads = [None] * clips
    back_pairs = [[None] * clips for _ in range(4)]
    inner_grads = [None] * clips
    for c in every:
        grads[c], back_pairs[3][c], s = norm_back(3, hidden[3][c], moving[c], None)
        sums[3].append(s)
        inner_grads[c], moving[c] = ffn_back_step(c, back_pairs[3][c])
    ffn_two = weights(back_pairs[3], [k[0] for k in kept[2]], units, "ffn_two_weights")
    ffn_one = weights(pairs[2], inner_grads, units, "ffn_one_weights")
    ffn_sum = lax.psum_scatter(
        jnp.concatenate([ffn_one, ffn_two], axis=1), "dp", scatter_dimension=0, tiled=False
    )

    acc_text = [pltpu.VMEM((text_len, columns), F32)] * 2
    small = sds((text_len, columns), LOW)

    def cross_back_step(c, pair):
        q, k, v, o, lse = kept[1][c]
        bias = bias_columns[:, c : c + 1]
        operands = [core_arg, *pair, bias, q, k, v, lse, attn_all, attn_all]
        dq, dk, dv, keep, send = run(
            cross_backward_body,
            [full, small, small, half_sds, half_low],
            operands,
            [scalars()] + [whole(a) for a in operands[1:8]] + [w_attn(3), w_attn(7)],
            flops=4 * frames * width * columns + 10 * score_flops * text_len,
            scratch=[pltpu.VMEM((frames, columns), LOW)] + acc_text,
            name="cross_backward",
        )
        return (dq, dk, dv), reduce_rows(keep, send)

    cross_grads = [None] * clips
    for c in every:
        grads[c], back_pairs[2][c], s = norm_back(2, hidden[2][c], moving[c], grads[c])
        sums[2].append(s)
        cross_grads[c], moving[c] = cross_back_step(c, back_pairs[2][c])
    text_dk = jnp.concatenate([g[1] for g in cross_grads], axis=0)
    text_dv = jnp.concatenate([g[2] for g in cross_grads], axis=0)
    text_part, text_gk, text_gv = run(
        text_back_body,
        [
            sds((clips * text_len, width), LOW),
            sds((dp, 1, share, columns), LOW),
            sds((dp, 1, share, columns), LOW),
        ],
        [text_dk, text_dv, attn_all, attn_all, text_hidden],
        [whole(text_dk), whole(text_dv), w_attn(4), w_attn(5), whole(text_hidden)],
        flops=8 * clips * text_len * width * columns,
        name="text_back",
    )
    text_grad = collect_tensor(
        [
            lax.dynamic_slice_in_dim(text_part, place_order[m] * columns, columns, 1)
            for m in range(tensor)
        ]
    ).astype(LOW)
    text_proj_grad = tn(text_rows, text_grad).astype(LOW)
    bias_grad = jnp.sum(text_grad.astype(F32), axis=0)
    cross_out = weights(back_pairs[2], [k[3] for k in kept[1]], columns, "cross_out_weights")
    cross_query = weights(pairs[1], [g[0] for g in cross_grads], columns, "cross_query_weights")

    acc_self = [pltpu.VMEM((frames, columns), F32)] * 2

    def self_back_step(c, pair):
        q, k, v, o, lse = kept[0][c]
        operands = [core_arg, *pair, q, k, v, lse, attn_all, attn_all, attn_all, attn_all]
        grad, keep, send = run(
            self_backward_body,
            [sds((frames, 3 * columns), LOW), half_sds, half_low],
            operands,
            [scalars()]
            + [whole(a) for a in operands[1:7]]
            + [w_attn(0), w_attn(1), w_attn(2), w_attn(6)],
            flops=8 * frames * width * columns + 10 * score_flops * frames,
            scratch=[pltpu.VMEM((frames, columns), LOW)] * 2 + acc_self,
            name="self_backward",
        )
        return grad, reduce_rows(keep, send)

    self_grads = [None] * clips
    for c in every:
        grads[c], back_pairs[1][c], s = norm_back(1, hidden[1][c], moving[c], grads[c])
        sums[1].append(s)
        self_grads[c], moving[c] = self_back_step(c, back_pairs[1][c])
    self_out = weights(back_pairs[1], [k[3] for k in kept[0]], columns, "self_out_weights")
    self_in = weights(pairs[0], self_grads, columns, "self_in_weights")
    attn_grads = jnp.concatenate(
        [
            a.reshape(dp, -1, columns)
            for a in (
                self_in,
                cross_query,
                text_gk,
                text_gv,
                self_out,
                cross_out,
                text_proj_grad.reshape(dp, text_share, columns),
            )
        ],
        axis=1,
    )
    attn_sum = lax.psum_scatter(attn_grads, "dp", scatter_dimension=0, tiled=False)

    zero_lows = [None] * clips
    for c in every:
        _, (zero_lows[c], _), s = norm_back(0, hidden[0][c], moving[c], grads[c])
        sums[0].append(s)
    if aligned:
        pieces = run(
            split_features_body,
            [sds((clips * strip, share), LOW)] * dp,
            [group_order, jnp.broadcast_to(side_arg, (clips + 1,))] + zero_lows,
            [scalars(), scalars()] + [whole(a) for a in zero_lows],
            name="split_features",
        )
    else:
        rows = jnp.concatenate(
            [lax.dynamic_slice_in_dim(a, side * strip, strip, 0) for a in zero_lows], axis=0
        )
        rows = jnp.transpose(rows.reshape(clips * strip, dp, share), (1, 0, 2))
        pieces = list(jnp.take(rows, group_order, axis=0))
    rows_all = [pieces[0]] + [swap(pieces[m], "dp", m) for m in range(1, dp)]
    embed_parts = embed_back(vocab_base, back_lines, rows_all, vocab)
    grad_embed = collect_tensor([embed_parts[m] for m in range(tensor)])

    norm_part = jnp.concatenate(
        [sum(s)[0:1] for s in sums] + [sum(s)[1:2] for s in sums], axis=0
    ) * (1.0 / sides)
    bias_row = lax.dynamic_update_slice_in_dim(
        jnp.zeros((width,), F32), bias_grad, place * columns, 0
    )
    norm_total = total_over(
        jnp.concatenate([norm_part, bias_row[None]], axis=0), ("tensor", "dp")
    )
    grad_norm_rows = lax.dynamic_slice_in_dim(norm_total, group * share, share, 1)

    grad_attention = attn_sum[: 8 * share].reshape(attention.shape).astype(F32)
    grad_text_proj = jnp.transpose(attn_sum[8 * share :]).astype(F32)
    grad_feedforward = ffn_sum.astype(F32)
    grad_heads = head_sum.astype(F32)
    local_square = (
        jnp.sum(grad_attention * grad_attention)
        + jnp.sum(grad_feedforward * grad_feedforward)
        + jnp.sum(grad_heads * grad_heads)
        + jnp.sum(grad_embed * grad_embed)
        + jnp.sum(grad_text_proj * grad_text_proj)
        + jnp.sum(grad_norm_rows * grad_norm_rows) / tensor
    )
    both = total_over(
        jnp.stack([local_square, sum(loss_part) / tensor]).reshape(1, 2), ("tensor", "dp")
    )[0]
    grad_norm = jnp.sqrt(both[0])
    mean_loss = both[1] / valid_count
    factor = clip_limit / jnp.maximum(grad_norm, clip_limit)
    grad_tables = jnp.concatenate([grad_embed, grad_heads], 0)
    attn_new, attn_first_new, attn_second_new = adam_update(
        attention, grad_attention, attention_first, attention_second, rate_matrix, factor
    )
    ffn_new, ffn_first_new, ffn_second_new = adam_update(
        feedforward, grad_feedforward, feedforward_first, feedforward_second, rate_matrix, factor
    )
    table_new, table_first_new, table_second_new = adam_update(
        tables, grad_tables, tables_first, tables_second, rate_table, factor
    )
    text_new, text_first_new, text_second_new = adam_update(
        text_proj, grad_text_proj, text_first, text_second, rate_matrix, factor
    )
    norm_new, norm_first_new, norm_second_new = adam_update(
        norm_params, grad_norm_rows, norm_first, norm_second, rate_norm, factor
    )
    return (
        mean_loss,
        valid_count,
        grad_norm,
        attn_new,
        attn_new.astype(LOW),
        attn_first_new,
        attn_second_new,
        ffn_new,
        ffn_new.astype(LOW),
        ffn_first_new,
        ffn_second_new,
        table_new,
        table_new.astype(LOW),
        table_first_new,
        table_second_new,
        text_new,
        text_new.astype(LOW),
        text_first_new,
        text_second_new,
        norm_new,
        norm_first_new,
        norm_second_new,
    )


def solution(mesh):
    clip3 = P("dp", None, None)
    clip2 = P("dp", None)
    matrix = P(None, "dp", "tensor")
    text = P("tensor", "dp")
    norm = P(None, "dp")
    placed = (
        (clip3, clip3, clip2, clip3, clip2)
        + (matrix, matrix, matrix, text, norm)
        + (matrix,) * 6
        + (text, text, norm, norm)
    )
    return jax.shard_map(
        on_device,
        mesh=mesh,
        in_specs=placed,
        out_specs=(P(), P(), P()) + (matrix,) * 12 + (text,) * 4 + (norm,) * 3,
        check_vma=False,
    )
```

```python
from functools import partial
import math

import jax
import jax.numpy as jnp
from jax import lax
from jax.experimental import pallas as pl
from jax.experimental.pallas import tpu as pltpu
from jax.sharding import PartitionSpec as P

HEAD_DIM = 64
STEP = 5
BLOCK = 256
NEG = -1e30
LOW = jnp.bfloat16
F32 = jnp.float32

clip_limit = 0.004
stability_offset = 1e-08
weight_decay = 0.01
moment_decay = 0.5
rate_matrix = 0.03
rate_table = 0.05
rate_norm = 0.2


def nn(a, b):
    return lax.dot_general(a, b, (((1,), (0,)), ((), ())), preferred_element_type=F32)


def nt(a, b):
    return lax.dot_general(a, b, (((1,), (1,)), ((), ())), preferred_element_type=F32)


def tn(a, b):
    return lax.dot_general(a, b, (((0,), (0,)), ((), ())), preferred_element_type=F32)


def sds(shape, kind):
    return jax.ShapeDtypeStruct(shape, kind)


def scalars():
    return pl.BlockSpec(memory_space=pltpu.SMEM)


def anywhere():
    return pl.BlockSpec(memory_space=pl.ANY)


def in_hbm():
    return pl.BlockSpec(memory_space=pltpu.HBM)


def in_vmem():
    return pl.BlockSpec(memory_space=pltpu.VMEM)


def whole(a):
    rank = len(a.shape)
    return pl.BlockSpec(a.shape, lambda i: (0,) * rank)


def later(body, count, at):
    def ordered(*refs):
        return body(*refs[:at], *refs[at + count :])

    return ordered


class Scalar:
    def __init__(self, array):
        self.array = array


class Window:
    def __init__(self, array, shape, pick):
        self.array, self.shape, self.pick = array, tuple(shape), pick


class Flow:
    def __init__(self, shape):
        self.shape = shape


class Copy:
    def __init__(self, i):
        self.i = i


class Shared:
    def __init__(self, shape, kind):
        self.full, self.array = sds(shape, kind), None


class Into:
    def __init__(self, shared, shape, pick):
        self.shared, self.shape, self.pick = shared, tuple(shape), pick


def everything(ref):
    return ref


def nbytes_of(shape, kind):
    return math.prod(shape) * jnp.dtype(kind).itemsize


def kernel(body, outs, operands, flops=0, scratch=(), name=None, exps=0, after=(), limit=32):
    arrays, specs, windows = [], [], []
    for a in operands:
        if isinstance(a, Scalar):
            arrays.append(a.array)
            specs.append(scalars())
            windows.append(None)
        elif isinstance(a, Window):
            arrays.append(a.array)
            specs.append(in_hbm())
            windows.append(a)
        else:
            arrays.append(a)
            specs.append(in_vmem())
            windows.append(None)
    aliases, out_shapes, out_specs, out_parts, owners = {}, [], [], [], []
    extra = []
    for o in outs:
        if isinstance(o, Into):
            if o.shared not in owners:
                if o.shared.array is not None:
                    aliases[len(arrays) + len(extra)] = len(out_shapes)
                    extra.append(o.shared.array)
                out_shapes.append(o.shared.full)
                out_specs.append(in_hbm())
                owners.append(o.shared)
            out_parts.append(("put", o.shape, o.shared.full.dtype, o.pick, owners.index(o.shared)))
            continue
        if isinstance(o, Flow):
            out_parts.append(("flow", None, None, None, len(out_shapes)))
            out_shapes.append(o.shape)
            out_specs.append(in_vmem())
        elif isinstance(o, Copy):
            a = operands[o.i]
            out_parts.append(("copy", o.i, None, None, len(out_shapes)))
            out_shapes.append(sds(a.shape, a.dtype))
            out_specs.append(in_hbm())
        else:
            out_parts.append(("put", o.shape, o.dtype, everything, len(out_shapes)))
            out_shapes.append(o)
            out_specs.append(in_hbm())
        owners.append(None)
    moved = [w for w in windows if w is not None]
    made = [p for p in out_parts if p[0] == "put"]
    count_in, count_extra, count_after = len(arrays), len(extra), len(after)
    count_out, count_moved, count_arrays = len(outs), len(moved), len(out_shapes)

    def run_body(*refs):
        refs = list(refs)
        ins = refs[:count_in]
        at = count_in + count_extra + count_after
        out_refs = refs[at : at + count_arrays]
        at += count_arrays
        in_buffers = refs[at : at + count_moved]
        at += count_moved
        made_buffers = refs[at : at + len(made)]
        at += len(made)
        in_sems, out_sems = refs[at], refs[at + 1]
        rest = refs[at + 2 :]
        views, copies, waited = [], {}, set()
        n = 0
        for i, (ref, w) in enumerate(zip(ins, windows)):
            if w is None:
                views.append(ref)
            else:
                copies[i] = pltpu.make_async_copy(w.pick(ref), in_buffers[n], in_sems.at[n])
                copies[i].start()
                views.append(in_buffers[n])
                n += 1
        sent, sources = {}, {}

        def need(*which):
            for i in which:
                if i in copies and i not in waited:
                    waited.add(i)
                    copies[i].wait()

        def put(*which):
            for j in which:
                if j in sources:
                    source, target = sources[j]
                    sent[j] = pltpu.make_async_copy(source, target, out_sems.at[j])
                    sent[j].start()

        body_outs = []
        n = 0
        for j, (kind, what, _, pick, owner) in enumerate(out_parts):
            if kind == "put":
                sources[j] = (made_buffers[n], pick(out_refs[owner]))
                body_outs.append(made_buffers[n])
                n += 1
            elif kind == "copy":
                sources[j] = (ins[what], out_refs[owner])
                put(j)
            else:
                body_outs.append(out_refs[owner])
        body(need, put, *views, *body_outs, *rest)
        need(*copies)
        put(*(j for j in sources if j not in sent))
        for copy in sent.values():
            copy.wait()

    nbytes = sum(nbytes_of(w.shape, w.array.dtype) for w in moved)
    nbytes += sum(nbytes_of(p[1], p[2]) for p in made)
    results = pl.pallas_call(
        run_body,
        out_shape=tuple(out_shapes),
        in_specs=specs + [anywhere()] * (count_extra + count_after),
        out_specs=tuple(out_specs),
        input_output_aliases=aliases,
        scratch_shapes=[pltpu.VMEM(w.shape, w.array.dtype) for w in moved]
        + [pltpu.VMEM(p[1], p[2]) for p in made]
        + [
            pltpu.SemaphoreType.DMA((max(1, count_moved),)),
            pltpu.SemaphoreType.DMA((max(1, count_out),)),
        ]
        + list(scratch),
        compiler_params=pltpu.CompilerParams(vmem_limit_bytes=limit << 20),
        cost_estimate=pl.CostEstimate(
            flops=int(flops), bytes_accessed=int(nbytes), transcendentals=int(exps)
        ),
        name=name,
    )(*arrays, *extra, *after)
    for owner, result in zip(owners, results):
        if owner is not None:
            owner.array = result
    return [r for owner, r in zip(owners, results) if owner is None] or [results[-1]]


def flat(ref):
    w = ref[...]
    return w.reshape(-1, w.shape[-1])


def half_rows(core, height):
    return (
        pl.ds(pl.multiple_of(core * height, height), height),
        pl.ds(pl.multiple_of((1 - core) * height, height), height),
    )


def attend_block(query, keys, values, head_masks, diagonal, bias):
    rows, width = query.shape
    lane = lax.broadcasted_iota(jnp.int32, (rows, 128), 1)
    column = lax.broadcasted_iota(jnp.int32, (rows, width), 1) // HEAD_DIM
    mixed = jnp.zeros((rows, width), F32)
    totals = jnp.zeros((rows, 128), F32)
    count = keys.shape[0]
    for h, mask in enumerate(head_masks):
        s = nt(query * mask, keys)
        if diagonal is not None:
            last = jnp.where(diagonal, s[:, count - rows :], NEG)
            s = last if count == rows else jnp.concatenate([s[:, : count - rows], last], axis=1)
        if bias is not None:
            s = s + bias
        top = jnp.max(s, axis=1, keepdims=True)
        e = jnp.exp(s - top)
        total = jnp.sum(e, axis=1, keepdims=True)
        p = (e * (1.0 / total)).astype(LOW)
        mixed = jnp.where(column == h, nn(p, values), mixed)
        totals = jnp.where(lane == h, top + jnp.log(total), totals)
    return mixed, totals


def masks_of(width):
    head = lax.broadcasted_iota(jnp.int32, (1, width), 1) // HEAD_DIM
    return [(head == h).astype(F32).astype(LOW) for h in range(width // HEAD_DIM)]


def triangle(size):
    row = lax.broadcasted_iota(jnp.int32, (size, size), 0)
    col = lax.broadcasted_iota(jnp.int32, (size, size), 1)
    return row >= col


def self_forward_body(
    need, put, core_ref, own_ref, wq_ref, got_ref, wk_ref, wv_ref, wo_ref,
    q_ref, k_ref, v_ref, o_ref, lse_ref, keep_ref, send_ref, tot_ref,
):
    height = own_ref.shape[0]
    frames, width = q_ref.shape
    mine, other = half_rows(core_ref[0], height)
    need(1)
    for i, w_ref, to_ref in ((2, wq_ref, q_ref), (4, wk_ref, k_ref), (5, wv_ref, v_ref)):
        need(i)
        w = flat(w_ref)
        to_ref[mine, :] = nn(own_ref[...], w).astype(LOW)
        need(3)
        to_ref[other, :] = nn(got_ref[...], w).astype(LOW)
    put(0, 1, 2)
    scale = jnp.asarray(HEAD_DIM**-0.5, LOW)
    head_masks = masks_of(width)
    diagonal = triangle(BLOCK)
    for i in range(frames // BLOCK):
        rows = slice(i * BLOCK, (i + 1) * BLOCK)
        mixed, totals = attend_block(
            q_ref[rows, :] * scale,
            k_ref[: (i + 1) * BLOCK, :],
            v_ref[: (i + 1) * BLOCK, :],
            head_masks,
            diagonal,
            None,
        )
        o_ref[rows, :] = mixed.astype(LOW)
        tot_ref[rows, :] = totals
    put(3)
    need(6)
    wo = flat(wo_ref)
    send_ref[...] = nt(o_ref[other, :], wo).astype(LOW)
    put(6)
    keep_ref[...] = nt(o_ref[mine, :], wo).astype(LOW)
    put(5)
    lse_ref[...] = jnp.transpose(tot_ref[...])[:8, :]


def cross_forward_body(
    need, put, core_ref, own_ref, wq_ref, got_ref, bias_ref, k_ref, v_ref, wo_ref,
    q_ref, o_ref, lse_ref, keep_ref, send_ref, tot_ref,
):
    height = own_ref.shape[0]
    frames, width = q_ref.shape
    mine, other = half_rows(core_ref[0], height)
    need(1, 2)
    w = flat(wq_ref)
    q_ref[mine, :] = nn(own_ref[...], w).astype(LOW)
    need(3)
    q_ref[other, :] = nn(got_ref[...], w).astype(LOW)
    put(0)
    scale = jnp.asarray(HEAD_DIM**-0.5, LOW)
    head_masks = masks_of(width)
    need(4, 5, 6)
    for i in range(frames // BLOCK):
        rows = slice(i * BLOCK, (i + 1) * BLOCK)
        mixed, totals = attend_block(
            q_ref[rows, :] * scale, k_ref[...], v_ref[...], head_masks, None, bias_ref[...]
        )
        o_ref[rows, :] = mixed.astype(LOW)
        tot_ref[rows, :] = totals
    put(1)
    need(7)
    wo = flat(wo_ref)
    send_ref[...] = nt(o_ref[other, :], wo).astype(LOW)
    put(4)
    keep_ref[...] = nt(o_ref[mine, :], wo).astype(LOW)
    put(3)
    lse_ref[...] = jnp.transpose(tot_ref[...])[:8, :]


def ffn_forward_body(
    need, put, core_ref, own_ref, got_ref, w1_ref, w2_ref,
    act_ref, slope_ref, keep_ref, send_ref,
):
    height = own_ref.shape[0]
    mine, other = half_rows(core_ref[0], height)
    need(1, 2, 3)
    w1 = flat(w1_ref)
    for j, source, rows, to_ref in (
        (3, got_ref, other, send_ref),
        (2, own_ref, mine, keep_ref),
    ):
        u = nn(source[...], w1)
        phi = 0.5 * (1.0 + lax.erf(u * (2.0**-0.5)))
        act = (u * phi).astype(LOW)
        density = jnp.exp(-0.5 * u * u) * ((2.0 * math.pi) ** -0.5)
        act_ref[rows, :] = act
        slope_ref[rows, :] = (phi + u * density).astype(LOW)
        need(4)
        to_ref[...] = nt(act, flat(w2_ref)).astype(to_ref.dtype)
        put(j)


def head_forward_body(
    need, put, core_ref, own_ref, target_ref, got_ref, *refs
):
    *w_refs, logits_ref, stats_ref, tot_ref = refs
    height = own_ref.shape[0]
    books = len(w_refs)
    vocab = w_refs[0].shape[2]
    halves = half_rows(core_ref[0], height)
    lane = lax.broadcasted_iota(jnp.int32, (height, 128), 1)
    code = lax.broadcasted_iota(jnp.int32, (height, vocab), 1)
    need(1, 2)
    totals = [jnp.zeros((height, 128), F32)] * 2
    for k, w_ref in enumerate(w_refs):
        need(4 + k)
        w = flat(w_ref)
        for j, (source, rows) in enumerate(zip((own_ref, got_ref), halves)):
            need(1 + 2 * j)
            s = nn(source[...], w)
            logits_ref[rows, k * vocab : (k + 1) * vocab] = s
            top = jnp.max(s, axis=1, keepdims=True)
            total = jnp.sum(jnp.exp(s - top), axis=1, keepdims=True)
            hit = code == target_ref[rows, k : k + 1]
            pick = jnp.sum(jnp.where(hit, s, 0.0), axis=1, keepdims=True)
            totals[j] = jnp.where(lane == k, top + jnp.log(total), totals[j])
            totals[j] = jnp.where(lane == books + k, pick, totals[j])
    put(0)
    for rows, t in zip(halves, totals):
        tot_ref[rows, :] = t
    stats_ref[...] = jnp.transpose(tot_ref[...])[: 2 * books, :]


def head_backward_body(
    need, put, core_ref, total_ref, weight_ref, target_ref, logits_ref, *refs
):
    *w_refs, grad_ref, keep_ref, send_ref, col_ref = refs
    height = keep_ref.shape[0]
    books = len(w_refs)
    vocab = w_refs[0].shape[2]
    mine, other = half_rows(core_ref[0], height)
    frames = logits_ref.shape[0]
    need(1, 2, 3)
    wide = jnp.concatenate(
        [total_ref[...], jnp.zeros((128 - total_ref.shape[0], frames), F32)], axis=0
    )
    col_ref[...] = jnp.transpose(wide)
    code = lax.broadcasted_iota(jnp.int32, (height, vocab), 1)
    need(4)
    for j, rows, to_ref in ((2, other, send_ref), (1, mine, keep_ref)):
        weight = weight_ref[rows, :]
        total = col_ref[rows, :]
        acc = None
        for k, w_ref in enumerate(w_refs):
            s = logits_ref[rows, k * vocab : (k + 1) * vocab]
            p = jnp.exp(s - total[:, k : k + 1])
            hit = jnp.where(code == target_ref[rows, k : k + 1], 1.0, 0.0)
            g = ((p - hit) * weight[:, k : k + 1]).astype(LOW)
            grad_ref[rows, k * vocab : (k + 1) * vocab] = g
            need(5 + k)
            part = nt(g, flat(w_ref))
            acc = part if acc is None else acc + part
        to_ref[...] = acc.astype(to_ref.dtype)
        put(j)


def ffn_backward_body(
    need, put, core_ref, own_ref, got_ref, w2_ref, slope_ref, w1_ref,
    grad_ref, keep_ref, send_ref,
):
    height = own_ref.shape[0]
    mine, other = half_rows(core_ref[0], height)
    need(1, 2, 3, 4)
    w2 = flat(w2_ref)
    for j, source, rows, to_ref in (
        (2, got_ref, other, send_ref),
        (1, own_ref, mine, keep_ref),
    ):
        g = (nn(source[...], w2) * slope_ref[rows, :].astype(F32)).astype(LOW)
        grad_ref[rows, :] = g
        need(5)
        to_ref[...] = nt(g, flat(w1_ref)).astype(to_ref.dtype)
        put(j)


def attend_back(
    q, k, v, g, lse, head_masks, scale, diagonal, bias, dq_ref, rows, dk_ref, dv_ref, first
):
    count, width = k.shape
    step = q.shape[0]
    dq = jnp.zeros((step, width), F32)
    dk = jnp.zeros((count, width), F32)
    dv = jnp.zeros((count, width), F32)
    for h, mask in enumerate(head_masks):
        qm = q * mask
        gm = g * mask
        s = nt(k, qm)
        if diagonal is not None:
            last = jnp.where(diagonal, s[count - step :, :], NEG)
            s = last if count == step else jnp.concatenate([s[: count - step, :], last], axis=0)
        if bias is not None:
            s = s + bias
        p = jnp.exp(s - lse[h : h + 1, :])
        dp = nt(v, gm)
        inner = jnp.sum(p * dp, axis=0, keepdims=True)
        ds = (p * (dp - inner)).astype(LOW)
        dq = dq + tn(ds, k * mask)
        dk = dk + nn(ds, qm)
        dv = dv + nn(p.astype(LOW), gm)
    dq_ref[rows, :width] = (dq * scale).astype(LOW)
    dk_ref[:count, :] = dk if first else dk_ref[:count, :] + dk
    dv_ref[:count, :] = dv if first else dv_ref[:count, :] + dv


def self_backward_body(
    need, put, core_ref, own_ref, wo_ref, got_ref, q_ref, k_ref, v_ref, lse_ref,
    wq_ref, wk_ref, wv_ref, grad_ref, keep_ref, send_ref, g_ref, dk_acc, dv_acc,
):
    height = own_ref.shape[0]
    frames, width = q_ref.shape
    mine, other = half_rows(core_ref[0], height)
    need(1, 2)
    wo = flat(wo_ref)
    g_ref[mine, :] = nn(own_ref[...], wo).astype(LOW)
    need(3)
    g_ref[other, :] = nn(got_ref[...], wo).astype(LOW)
    scale = HEAD_DIM**-0.5
    head_masks = masks_of(width)
    row = lax.broadcasted_iota(jnp.int32, (BLOCK, BLOCK), 0)
    col = lax.broadcasted_iota(jnp.int32, (BLOCK, BLOCK), 1)
    diagonal = col >= row
    blocks = frames // BLOCK
    need(4, 5, 6, 7)
    for i in reversed(range(blocks)):
        rows = slice(i * BLOCK, (i + 1) * BLOCK)
        count = (i + 1) * BLOCK
        attend_back(
            q_ref[rows, :] * jnp.asarray(scale, LOW),
            k_ref[:count, :],
            v_ref[:count, :],
            g_ref[rows, :],
            lse_ref[:, rows],
            head_masks,
            scale,
            diagonal,
            None,
            grad_ref,
            rows,
            dk_acc,
            dv_acc,
            i == blocks - 1,
        )
    grad_ref[:, width : 2 * width] = dk_acc[...].astype(LOW)
    grad_ref[:, 2 * width :] = dv_acc[...].astype(LOW)
    put(0)
    need(8, 9, 10)
    for j, rows, to_ref in ((2, other, send_ref), (1, mine, keep_ref)):
        part = None
        for n, w_ref in enumerate((wq_ref, wk_ref, wv_ref)):
            term = nt(grad_ref[rows, n * width : (n + 1) * width], flat(w_ref))
            part = term if part is None else part + term
        to_ref[...] = part.astype(to_ref.dtype)
        put(j)


def cross_backward_body(
    need, put, core_ref, own_ref, wo_ref, got_ref, bias_ref, q_ref, k_ref, v_ref, lse_ref, wq_ref,
    dq_ref, dk_ref, dv_ref, keep_ref, send_ref, g_ref, dk_acc, dv_acc,
):
    height = own_ref.shape[0]
    frames, width = q_ref.shape
    mine, other = half_rows(core_ref[0], height)
    need(1, 2)
    wo = flat(wo_ref)
    g_ref[mine, :] = nn(own_ref[...], wo).astype(LOW)
    need(3)
    g_ref[other, :] = nn(got_ref[...], wo).astype(LOW)
    scale = HEAD_DIM**-0.5
    head_masks = masks_of(width)
    need(4, 5, 6, 7, 8)
    for i in range(frames // BLOCK):
        rows = slice(i * BLOCK, (i + 1) * BLOCK)
        attend_back(
            q_ref[rows, :] * jnp.asarray(scale, LOW),
            k_ref[...],
            v_ref[...],
            g_ref[rows, :],
            lse_ref[:, rows],
            head_masks,
            scale,
            None,
            bias_ref[...],
            dq_ref,
            rows,
            dk_acc,
            dv_acc,
            i == 0,
        )
    put(0)
    need(9)
    wq = flat(wq_ref)
    for j, rows, to_ref in ((4, other, send_ref), (3, mine, keep_ref)):
        to_ref[...] = nt(dq_ref[rows, :], wq).astype(to_ref.dtype)
        put(j)
    dk_ref[...] = dk_acc[...].astype(LOW)
    dv_ref[...] = dv_acc[...].astype(LOW)


def normalize(values, gain, shift):
    center = values - jnp.mean(values, axis=1, keepdims=True)
    spread = jnp.mean(center * center, axis=1, keepdims=True)
    return center * lax.rsqrt(spread + 1e-05) * gain + shift


def add_body(keep_ref, got_ref, out_ref):
    out_ref[...] = (keep_ref[...].astype(F32) + got_ref[...].astype(F32)).astype(LOW)


def norm_body(which, hidden_ref, part_ref, far_ref, norm_ref, new_ref, out_ref):
    new = hidden_ref[...] + (part_ref[...].astype(F32) + far_ref[...].astype(F32))
    new_ref[...] = new
    out_ref[...] = normalize(
        new, norm_ref[which : which + 1, :], norm_ref[which + 4 : which + 5, :]
    ).astype(LOW)


def embed_norm_body(need, put, side_ref, place_ref, norm_ref, *refs):
    *part_refs, new_ref, out_ref = refs
    side = side_ref[0]
    rows = part_refs[0].shape[0]
    need(1, 2)
    for s, part in enumerate(part_refs):
        need(3 + s)
        at = pl.ds(pl.multiple_of((side ^ s) * rows, rows), rows)
        new = part[...].astype(F32) + place_ref[at, :]
        new_ref[at, :] = new
        out_ref[at, :] = normalize(new, norm_ref[0:1, :], norm_ref[4:5, :]).astype(LOW)
    put(1, 0)


def norm_back_body(which, hidden_ref, part_ref, far_ref, *refs):
    *before, norm_ref, new_ref, low_ref, sums_ref = refs
    values = hidden_ref[...]
    grad = part_ref[...].astype(F32) + far_ref[...].astype(F32)
    gain = norm_ref[which : which + 1, :]
    center = values - jnp.mean(values, axis=1, keepdims=True)
    spread = jnp.mean(center * center, axis=1, keepdims=True)
    inverse = lax.rsqrt(spread + 1e-05)
    unit = center * inverse
    scaled = grad * gain
    first = jnp.mean(scaled, axis=1, keepdims=True)
    second = jnp.mean(scaled * unit, axis=1, keepdims=True)
    new = inverse * (scaled - first - unit * second)
    if before:
        new = before[0][...] + new
    new_ref[...] = new
    low_ref[...] = new.astype(LOW)
    sums_ref[...] = jnp.concatenate(
        [
            jnp.sum(grad * unit, axis=0, keepdims=True),
            jnp.sum(grad, axis=0, keepdims=True),
            jnp.zeros((6, values.shape[1]), F32),
        ],
        axis=0,
    )


def weight_grad_body(clips, turn_left, need, put, core_ref, *refs):
    lefts = refs[: 2 * clips]
    rights = refs[2 * clips : 3 * clips]
    outs = refs[3 * clips : -1]
    turned = refs[-1]
    height, width = lefts[0].shape
    frames = rights[0].shape[0]
    group = outs[0].shape[2]
    core = core_ref[0]

    def place(c, at):
        return pl.ds(pl.multiple_of(c * frames + at * height, 128), height)

    if turn_left:
        for m, out_ref in enumerate(outs):
            total = None
            for c in range(clips):
                if m == 0:
                    for j, at in ((0, core), (1, 1 - core)):
                        need(1 + 2 * c + j)
                        turned[:, place(c, at)] = jnp.transpose(lefts[2 * c + j][...])
                    need(1 + 2 * clips + c)
                part = nn(
                    turned[:, c * frames : (c + 1) * frames],
                    rights[c][:, m * group : (m + 1) * group],
                )
                total = part if total is None else total + part
            out_ref[...] = total.astype(LOW).reshape(out_ref.shape)
            put(m)
    else:
        total = None
        for c in range(clips):
            need(1 + 2 * clips + c)
            turned[:, c * frames : (c + 1) * frames] = jnp.transpose(rights[c][...])
            for j, at in ((0, core), (1, 1 - core)):
                need(1 + 2 * c + j)
                part = nn(turned[:, place(c, at)], lefts[2 * c + j][...])
                total = part if total is None else total + part
        for m, out_ref in enumerate(outs):
            member = total[m * group : (m + 1) * group, :]
            out_ref[...] = jnp.transpose(member).astype(LOW).reshape(out_ref.shape)
            put(m)


def norm_rows_kernel(body, outs, operands, norm_rows, after, name="norm"):
    height, width = operands[0].shape
    operands = list(operands) + ([] if norm_rows is None else [norm_rows])
    nbytes = sum(nbytes_of(a.shape, a.dtype) for a in operands + list(outs))
    return pl.pallas_call(
        later(body, len(after), len(operands)),
        out_shape=tuple(outs),
        in_specs=[in_vmem()] * len(operands) + [anywhere()] * len(after),
        out_specs=tuple(in_vmem() for _ in outs),
        compiler_params=pltpu.CompilerParams(vmem_limit_bytes=16 << 20),
        cost_estimate=pl.CostEstimate(
            flops=20 * height * width, bytes_accessed=nbytes // 4, transcendentals=0
        ),
        name=name,
    )(*operands, *after)


def embed_body(base_ref, codes_ref, *refs):
    *table_refs, out_ref = refs
    books, features, vocab = table_refs[0].shape
    rows = codes_ref.shape[1]
    chunk = min(256, vocab)
    code = lax.broadcasted_iota(jnp.int32, (rows, chunk), 1)
    acc = jnp.zeros((rows, features), F32)
    for k in range(books):
        column = codes_ref[0, :, k : k + 1]
        for b, table in enumerate(table_refs):
            local = column - base_ref[b]
            for v in range(0, vocab, chunk):
                hit = jnp.where(code == local - v, 1.0, 0.0).astype(LOW)
                acc = acc + nt(hit, table[k, :, v : v + chunk])
    out_ref[0] = acc.astype(LOW)


def embed(base, codes, tables, after):
    blocks, rows, books = codes.shape
    features = tables[0].shape[1]
    vocab = tables[0].shape[2] * len(tables)
    return pl.pallas_call(
        later(embed_body, len(after), 2 + len(tables)),
        out_shape=sds((blocks, rows, features), LOW),
        grid=(blocks,),
        in_specs=[scalars(), pl.BlockSpec((1, rows, books), lambda i: (i, 0, 0))]
        + [in_vmem() for t in tables]
        + [anywhere()] * len(after),
        out_specs=pl.BlockSpec((1, rows, features), lambda i: (i, 0, 0)),
        compiler_params=pltpu.CompilerParams(vmem_limit_bytes=32 << 20),
        cost_estimate=pl.CostEstimate(
            flops=4 * blocks * rows * books * vocab * features,
            bytes_accessed=2 * books * vocab * features + blocks * rows * (features + 512),
            transcendentals=0,
        ),
        name="embed",
    )(base, codes, *tables, *after)


def embed_back_body(base_ref, codes_ref, *refs):
    *grad_refs, out_ref, all_ref = refs
    rows, features = grad_refs[0].shape
    vocab = out_ref.shape[3]
    book = pl.program_id(1)
    chunk = min(256, vocab)

    @pl.when((pl.program_id(0) == 0) & (book == 0))
    def _():
        for j, g in enumerate(grad_refs):
            all_ref[j * rows : (j + 1) * rows, :] = g[...]

    base = base_ref[pl.program_id(0)]
    line = codes_ref[0]
    line = line[0:1, :]
    code = lax.broadcasted_iota(jnp.int32, (chunk, line.shape[1]), 0)
    for v in range(0, vocab, chunk):
        hit = jnp.where(code == line - (base + v), 1.0, 0.0).astype(LOW)
        out_ref[0, 0, :, v : v + chunk] = jnp.transpose(nn(hit, all_ref[...])).astype(LOW)


def embed_back(base, lines, grads, vocab):
    parts = base.shape[0]
    books, _, total = lines.shape
    features = grads[0].shape[1]
    return pl.pallas_call(
        embed_back_body,
        out_shape=sds((parts, books, features, vocab), LOW),
        grid=(parts, books),
        in_specs=[scalars(), pl.BlockSpec((1, 8, total), lambda i, k: (k, 0, 0))]
        + [pl.BlockSpec(g.shape, lambda i, k: (0, 0)) for g in grads],
        out_specs=pl.BlockSpec((1, 1, features, vocab), lambda i, k: (i, k, 0, 0)),
        scratch_shapes=[pltpu.VMEM((total, features), LOW)],
        compiler_params=pltpu.CompilerParams(vmem_limit_bytes=32 << 20),
        cost_estimate=pl.CostEstimate(
            flops=4 * parts * books * vocab * features * total,
            bytes_accessed=2 * parts * books * features * vocab + 2 * total * features,
            transcendentals=0,
        ),
        name="embed_back",
    )(base, lines, *grads)


def gather_features_body(need, put, where_ref, *refs):
    *part_refs, out_ref = refs
    features = part_refs[0].shape[1]
    for m, part in enumerate(part_refs):
        need(1 + m)
        at = pl.ds(pl.multiple_of(where_ref[m] * features, features), features)
        out_ref[:, at] = part[...]


def split_features_body(need, put, where_ref, side_ref, *refs):
    clips = side_ref.shape[0] - 1
    grads, outs = refs[:clips], refs[clips:]
    features = outs[0].shape[1]
    rows = outs[0].shape[0] // clips
    at_rows = pl.ds(pl.multiple_of(side_ref[0] * rows, rows), rows)
    need(*range(2, 2 + clips))
    for m, out_ref in reversed(list(enumerate(outs))):
        at = pl.ds(pl.multiple_of(where_ref[m] * features, features), features)
        for c in range(clips):
            out_ref[c * rows : (c + 1) * rows, :] = grads[c][at_rows, at]
        put(m)


def text_body(need, put, where_ref, *refs):
    *part_refs, wk_ref, wv_ref, tp_ref, k_ref, v_ref = refs
    columns = part_refs[0].shape[1]
    for m, part in enumerate(part_refs):
        need(1 + m)
        at = pl.ds(pl.multiple_of(where_ref[m] * columns, columns), columns)
        tp_ref[:, at] = part[...]
    put(0)
    for j, w_ref, to_ref in ((1, wk_ref, k_ref), (2, wv_ref, v_ref)):
        need(len(part_refs) + j)
        to_ref[...] = nn(tp_ref[...], flat(w_ref)).astype(LOW)
        put(j)


def text_back_body(clips, need, put, where_ref, *refs):
    dks, dvs = refs[:clips], refs[clips : 2 * clips]
    wk_ref, wv_ref, tp_ref = refs[2 * clips : 2 * clips + 3]
    *part_refs, gk_ref, gv_ref, full_ref = refs[2 * clips + 3 :]
    columns = part_refs[0].shape[1]
    length = dks[0].shape[0]
    need(*range(1, 1 + 2 * clips + 2))
    wk, wv = flat(wk_ref), flat(wv_ref)
    for c in range(clips):
        tp_rows = slice(c * length, (c + 1) * length)
        full_ref[tp_rows, :] = (nt(dks[c][...], wk) + nt(dvs[c][...], wv)).astype(LOW)
    for m, part_ref in enumerate(part_refs):
        at = pl.ds(pl.multiple_of(where_ref[m] * columns, columns), columns)
        part_ref[...] = full_ref[:, at]
    put(*range(len(part_refs)))
    need(3 + 2 * clips)
    turned = jnp.transpose(tp_ref[...])
    for j, grads, to_ref in ((0, dks, gk_ref), (1, dvs, gv_ref)):
        total = None
        for c in range(clips):
            part = nn(turned[:, c * length : (c + 1) * length], grads[c][...])
            total = part if total is None else total + part
        to_ref[...] = total.astype(LOW).reshape(to_ref.shape)
        put(len(part_refs) + j)


def text_weight_body(need, put, rows_ref, grad_ref, out_ref):
    need(0, 1)
    out_ref[...] = tn(rows_ref[...], grad_ref[...]).astype(LOW).reshape(out_ref.shape)


def positions_rows(start, count, feature_count):
    half_width = feature_count // 2
    frequency = jnp.exp(
        jnp.arange(half_width, dtype=F32) * (-math.log(10000.0) / (half_width - 1))
    )
    angles = (start + jnp.arange(count, dtype=jnp.int32)).astype(F32)[:, None] * frequency[None, :]
    return jnp.concatenate([jnp.cos(angles), jnp.sin(angles)], axis=1)


def adam_update(weight, gradient, first_moment, second_moment, step_rate, factor):
    clipped = gradient * factor
    new_first = moment_decay * first_moment + (1.0 - moment_decay) * clipped
    new_second = moment_decay * second_moment + (1.0 - moment_decay) * clipped * clipped
    first_hat = new_first / (1.0 - moment_decay**STEP)
    second_hat = new_second / (1.0 - moment_decay**STEP)
    new_weight = weight * (1.0 - step_rate * weight_decay) - step_rate * first_hat / (
        jnp.sqrt(second_hat) + stability_offset
    )
    return (new_weight, new_first, new_second)


def swap(values, axis, mask):
    size = lax.axis_size(axis)
    return lax.ppermute(values, axis, [(i, i ^ mask) for i in range(size)])


def on_device(
    audio_codes,
    delay_mask,
    frame_mask,
    text_states,
    text_mask,
    attention,
    feedforward,
    tables,
    text_proj,
    norm_params,
    attention_first,
    attention_second,
    feedforward_first,
    feedforward_second,
    tables_first,
    tables_second,
    text_first,
    text_second,
    norm_first,
    norm_second,
):
    clips, frames, books = audio_codes.shape
    text_len, text_width = text_states.shape[1:]
    dp = lax.axis_size("dp")
    tensor = lax.axis_size("tensor")
    group = lax.axis_index("dp")
    place = lax.axis_index("tensor")
    core = place & 1
    side = place >> 1
    sides = tensor // 2
    height = frames // 2
    strip = height // sides
    share = attention.shape[1]
    columns = attention.shape[2]
    width = share * dp
    vocab = tables.shape[2]
    text_share = text_proj.shape[1]
    core_arg = Scalar(core.astype(jnp.int32).reshape(1))
    side_arg = Scalar(side.astype(jnp.int32).reshape(1))
    swap_core = partial(swap, axis="tensor", mask=1)

    def spread_tensor(values):
        held = [values]
        mask = tensor // 2
        order = [0]
        while mask:
            held = held + [swap(v, "tensor", mask) for v in held]
            order = order + [o | mask for o in order]
            mask //= 2
        return [v for _, v in sorted(zip(order, held), key=lambda t: t[0])]

    def collect_tensor(parts):
        mask = 1
        live = {m: p for m, p in enumerate(parts)}
        while mask < tensor:
            fresh = {}
            for m in live:
                if not m & mask:
                    got = swap(live[m | mask].astype(LOW), "tensor", mask)
                    fresh[m] = live[m].astype(F32) + got.astype(F32)
            live = fresh
            mask *= 2
        return live[0]

    def across(values):
        own = values
        mask = 2
        rest = None
        while mask < tensor:
            got = swap(own, "tensor", mask)
            mask *= 2
            if mask < tensor:
                own = (own.astype(F32) + got.astype(F32)).astype(LOW)
            rest = got
        if rest is None:
            rest = jnp.zeros_like(own)
        return own, rest

    def total_over(values, axes):
        for axis in axes:
            mask = 1
            while mask < lax.axis_size(axis):
                values = values + swap(values, axis, mask)
                mask *= 2
        return values

    last = []

    def run(body, outs, operands, **rest):
        shared = [o.shared.array for o in outs if isinstance(o, Into)]
        wait_for = [a for a in last if not any(a is b for b in shared)]
        results = kernel(body, outs, operands, after=wait_for, **rest)
        last[:] = [results[-1]]
        return results

    norm_pad = jnp.pad(norm_params.astype(LOW), ((0, 16 - norm_params.shape[0]), (0, columns - share)))
    attn_flat = jnp.concatenate(
        [attention.astype(LOW).reshape(-1, columns), text_proj.astype(LOW).T, norm_pad], axis=0
    )
    attn_all = lax.all_gather(attn_flat, "dp", axis=0)
    ffn_all = lax.all_gather(feedforward.astype(LOW), "dp", axis=0)
    head_all = lax.all_gather(tables[books:].astype(LOW), "dp", axis=0)

    frame_live = (jnp.arange(frames, dtype=jnp.int32) < frames - 1).astype(jnp.int32)
    weight_int = delay_mask * frame_mask[:, :, None] * frame_live[None, :, None]
    start = core * height + side * strip
    strip_codes = lax.dynamic_slice_in_dim(audio_codes, start, strip, 1)
    lines = jnp.transpose(strip_codes, (2, 0, 1)).reshape(books, clips * strip)
    count_line = jnp.broadcast_to(jnp.sum(weight_int), (1, clips * strip))
    packet = jnp.concatenate([lines, count_line], axis=0)[None]
    mask = 1
    while mask < dp:
        packet = jnp.concatenate([packet, swap(packet, "dp", mask)], axis=0)
        mask *= 2
    valid_count = jnp.sum(packet[:, books, 0]).astype(F32)
    all_lines = packet[:, :books]
    all_codes = jnp.transpose(all_lines, (0, 2, 1))
    back_lines = jnp.broadcast_to(
        jnp.transpose(all_lines, (1, 0, 2)).reshape(books, 1, dp * clips * strip),
        (books, 8, dp * clips * strip),
    )
    vocab_base = (place ^ jnp.arange(tensor, dtype=jnp.int32)) * vocab
    group_order = group ^ jnp.arange(dp, dtype=jnp.int32)
    place_order = place ^ jnp.arange(tensor, dtype=jnp.int32)

    table_parts = spread_tensor(tables[:books].astype(LOW))
    step = max(1, dp // 4)
    arrived = [None] * dp
    for low_end in reversed(range(0, dp, step)):
        embedded = embed(
            vocab_base, all_codes[low_end : low_end + step], table_parts, list(last)
        )
        last[:] = [embedded]
        for m in range(low_end, low_end + step):
            piece = embedded[m - low_end]
            arrived[m] = swap(piece, "dp", m) if m else piece
    aligned = share % 128 == 0
    if aligned:
        (strips,) = run(
            gather_features_body,
            [Flow(sds((clips * strip, width), LOW))],
            [Scalar(group_order)] + arrived,
            name="gather_features",
        )
    else:
        strips = jnp.take(jnp.stack(arrived), group_order, axis=0)
        strips = jnp.transpose(strips, (1, 0, 2)).reshape(clips * strip, width)
    placed = positions_rows(core * height, height, width)

    norm_rows = attn_all[:, 8 * share + text_share :, :share]
    norm_rows = jnp.transpose(norm_rows, (1, 0, 2)).reshape(16, width).astype(F32)

    def w_attn(n):
        return Window(
            attn_all, (dp, share, columns), lambda ref: ref.at[:, pl.ds(n * share, share), :]
        )

    def w_member(array, n):
        return Window(array, (dp,) + array.shape[2:], lambda ref: ref.at[:, n])

    half_sds = sds((height, width), F32)
    half_low = sds((height, width), LOW)
    flow = Flow(half_low)

    def fetch(a):
        return Window(a, a.shape, everything)


    def norm_step(which, hidden, parts):
        new, out = norm_rows_kernel(
            partial(norm_body, which), [half_sds, half_low], [hidden, *parts], norm_rows, last
        )
        last[:] = [out]
        return new, (out, swap_core(out))

    def norm_back(which, hidden, parts, before):
        operands = [hidden, *parts] + ([before] if before is not None else [])
        new, out, sums = norm_rows_kernel(
            partial(norm_back_body, which),
            [half_sds, half_low, sds((8, width), F32)],
            operands,
            norm_rows,
            last,
        )
        last[:] = [out]
        return new, (out, swap_core(out)), sums

    waiting = []
    moving = [None] * clips

    def flush():
        if waiting:
            c, keep, got = waiting.pop()
            (part,) = norm_rows_kernel(add_body, [half_low], [keep, got], None, last, name="add")
            last[:] = [part]
            moving[c] = across(part)

    def reduce_rows(c, keep, send):
        waiting.append((c, keep, swap_core(send)))

    text_rows = text_states.reshape(clips * text_len, text_width)
    text_weight = attn_all[:, 8 * share : 8 * share + text_share, :].reshape(text_width, columns)
    text_bias = lax.dynamic_slice_in_dim(norm_rows[8], place * columns, columns, 0)
    text_local = (nn(text_rows, text_weight) + text_bias).astype(LOW)
    text_parts = spread_tensor(text_local)
    text_bias_row = jnp.where(text_mask > 0, 0.0, NEG).astype(F32)
    bias_columns = jnp.transpose(text_bias_row)

    full = sds((frames, columns), LOW)
    lse_sds = sds((8, frames), F32)
    tot = [pltpu.VMEM((frames, 128), F32)]
    heads = columns // HEAD_DIM
    score_flops = 2 * heads * frames * HEAD_DIM
    units = feedforward.shape[2]
    inner = sds((frames, units), LOW)
    every = range(clips)

    def embed_step(c):
        mine = strips[c * strip : (c + 1) * strip]
        parts = [mine] + [swap(mine, "tensor", 2 * s) for s in range(1, sides)]
        new, out = run(
            embed_norm_body,
            [Flow(half_sds), Flow(half_low)],
            [side_arg, placed, norm_rows] + parts,
            flops=10 * height * width,
            name="embed_norm",
        )
        return new, (out, swap_core(out))

    def self_step(c, pair):
        own, got = pair
        *saved, keep, send, left, right = run(
            self_forward_body,
            [full, full, full, full, lse_sds, flow, flow, Copy(1), Copy(3)],
            [core_arg, own, w_attn(0), got, w_attn(1), w_attn(2), w_attn(6)],
            flops=8 * frames * width * columns + 4 * score_flops * frames,
            scratch=tot,
            name="self_forward",
        )
        pairs[0][c] = (left, right)
        reduce_rows(c, keep, send)
        return saved

    text_full = sds((clips * text_len, width), LOW)
    text_cols = sds((clips * text_len, columns), LOW)

    def text_step():
        return run(
            text_body,
            [text_full, text_cols, text_cols],
            [Scalar(place_order)] + text_parts + [w_attn(4), w_attn(5)],
            flops=4 * clips * text_len * width * columns,
            name="text",
        )

    def text_rows_of(array, c):
        return Window(
            array, (text_len, columns), lambda ref: ref.at[pl.ds(c * text_len, text_len), :]
        )

    def cross_step(c, pair):
        own, got = pair
        k, v = text_rows_of(text_key, c), text_rows_of(text_value, c)
        q, o, lse, keep, send, left, right = run(
            cross_forward_body,
            [full, full, lse_sds, flow, flow, Copy(1), Copy(3)],
            [core_arg, own, w_attn(3), got, text_bias_row[c : c + 1], k, v, w_attn(7)],
            flops=4 * frames * width * columns + 4 * score_flops * text_len,
            scratch=tot,
            name="cross_forward",
        )
        pairs[1][c] = (left, right)
        reduce_rows(c, keep, send)
        return (q, k, v, o, lse)

    def ffn_step(c, pair):
        *saved, keep, send, left, right = run(
            ffn_forward_body,
            [inner, inner, flow, flow, Copy(1), Copy(2)],
            [core_arg, *pair, w_member(ffn_all, 0), w_member(ffn_all, 1)],
            flops=4 * frames * width * units,
            name="ffn_forward",
        )
        pairs[2][c] = (left, right)
        reduce_rows(c, keep, send)
        return saved

    hidden = [[None] * clips for _ in range(4)]
    pairs = [[None] * clips for _ in range(4)]
    kept = [[None] * clips for _ in range(3)]
    for c in every:
        hidden[0][c], pairs[0][c] = embed_step(c)
        flush()
        kept[0][c] = self_step(c, pairs[0][c])
    text_hidden, text_key, text_value = text_step()
    for c in every:
        hidden[1][c], pairs[1][c] = norm_step(1, hidden[0][c], moving[c])
        flush()
        kept[1][c] = cross_step(c, pairs[1][c])
    for c in every:
        hidden[2][c], pairs[2][c] = norm_step(2, hidden[1][c], moving[c])
        flush()
        kept[2][c] = ffn_step(c, pairs[2][c])

    targets = (jnp.roll(audio_codes, -1, axis=1) - place * vocab).astype(jnp.int32)
    loss_weight = weight_int.astype(F32)
    grad_weight = loss_weight / valid_count
    loss_part = [None] * clips
    sums = [[], [], [], []]

    def head_step(c, pair):
        own, got = pair
        logits, stats, left, right = run(
            head_forward_body,
            [
                sds((frames, books * vocab), F32),
                Flow(sds((2 * books, frames), F32)),
                Copy(1),
                Copy(3),
            ],
            [core_arg, own, targets[c], got] + [w_member(head_all, k) for k in range(books)],
            flops=2 * frames * width * books * vocab,
            scratch=tot,
            name="head_forward",
        )
        pairs[3][c] = (left, right)
        total, pick = stats[:books], stats[books:]
        mask = 1
        while mask < tensor:
            far = swap(jnp.concatenate([total, pick], axis=0), "tensor", mask)
            high = jnp.maximum(total, far[:books])
            total = high + jnp.log(jnp.exp(total - high) + jnp.exp(far[:books] - high))
            pick = pick + far[books:]
            mask *= 2
        loss_part[c] = jnp.sum((total - pick) * jnp.transpose(loss_weight[c]))
        return logits, jnp.concatenate([total, total], axis=0)

    def head_back_step(c, logits, total):
        grad, keep, send = run(
            head_backward_body,
            [sds((frames, books * vocab), LOW), flow, flow],
            [core_arg, total, grad_weight[c], targets[c], fetch(logits)]
            + [w_member(head_all, k) for k in range(books)],
            flops=2 * frames * width * books * vocab,
            scratch=tot,
            name="head_backward",
        )
        reduce_rows(c, keep, send)
        return grad

    attn_shared = Shared((dp, 8 * share + text_share, columns), LOW)
    ffn_shared = Shared((dp,) + feedforward.shape, LOW)
    head_shared = Shared((dp, books, share, vocab), LOW)

    def attn_into(n):
        return Into(
            attn_shared,
            (dp, share, columns),
            lambda ref: ref.at[:, pl.ds(n * share, share), :],
        )

    def member_into(shared, n):
        return Into(shared, (dp,) + shared.full.shape[2:], lambda ref: ref.at[:, n])

    def weights(lefts, rights, outs, name):
        total = rights[0].shape[1]
        turn_left = 2 * total > width
        run(
            partial(weight_grad_body, clips, turn_left),
            outs,
            [core_arg] + [fetch(half) for pair in lefts for half in pair] + [fetch(a) for a in rights],
            flops=2 * clips * frames * width * total,
            scratch=[pltpu.VMEM((width if turn_left else total, clips * frames), LOW)],
            name=name,
            limit=48,
        )

    logit_grads = [None] * clips
    ready = [None] * clips
    for c in every:
        hidden[3][c], pairs[3][c] = norm_step(3, hidden[2][c], moving[c])
        flush()
        ready[c] = head_step(c, pairs[3][c])
        if c:
            flush()
            logit_grads[c - 1] = head_back_step(c - 1, *ready[c - 1])
    flush()
    logit_grads[-1] = head_back_step(clips - 1, *ready[-1])

    def ffn_back_step(c, pair):
        own, got = pair
        grad, keep, send, left, right = run(
            ffn_backward_body,
            [inner, flow, flow, Copy(1), Copy(2)],
            [core_arg, own, got, w_member(ffn_all, 1), fetch(kept[2][c][1]), w_member(ffn_all, 0)],
            flops=4 * frames * width * units,
            name="ffn_backward",
        )
        back_pairs[3][c] = (left, right)
        reduce_rows(c, keep, send)
        return grad

    grads = [None] * clips
    back_pairs = [[None] * clips for _ in range(4)]
    inner_grads = [None] * clips
    for c in every:
        grads[c], back_pairs[3][c], s = norm_back(3, hidden[3][c], moving[c], None)
        sums[3].append(s)
        flush()
        inner_grads[c] = ffn_back_step(c, back_pairs[3][c])
        if c == 0:
            head_into = [member_into(head_shared, k) for k in range(books)]
            weights(pairs[3], logit_grads, head_into, "head_weights")
    head_sum = lax.psum_scatter(head_shared.array, "dp", scatter_dimension=0, tiled=False)

    acc_text = [pltpu.VMEM((text_len, columns), F32)] * 2
    small = sds((text_len, columns), LOW)

    def cross_back_step(c, pair):
        own, got = pair
        q, k, v, o, lse = kept[1][c]
        bias = bias_columns[:, c : c + 1]
        dq, dk, dv, keep, send, left, right = run(
            cross_backward_body,
            [full, small, small, flow, flow, Copy(1), Copy(3)],
            [core_arg, own, w_attn(7), got, bias, fetch(q), k, v, fetch(lse), w_attn(3)],
            flops=4 * frames * width * columns + 10 * score_flops * text_len,
            scratch=[pltpu.VMEM((frames, columns), LOW)] + acc_text,
            name="cross_backward",
        )
        back_pairs[2][c] = (left, right)
        reduce_rows(c, keep, send)
        return (dq, dk, dv)

    cross_grads = [None] * clips
    for c in every:
        grads[c], back_pairs[2][c], s = norm_back(2, hidden[2][c], moving[c], grads[c])
        sums[2].append(s)
        flush()
        cross_grads[c] = cross_back_step(c, back_pairs[2][c])
        if c == 0:
            weights(
                back_pairs[3], [k[0] for k in kept[2]], [member_into(ffn_shared, 1)], "ffn_two"
            )
        if c == min(1, clips - 1):
            weights(pairs[2], inner_grads, [member_into(ffn_shared, 0)], "ffn_one")
    ffn_sum = lax.psum_scatter(ffn_shared.array, "dp", scatter_dimension=0, tiled=False)

    def text_back_step():
        results = run(
            partial(text_back_body, clips),
            [Flow(text_cols)] * tensor + [attn_into(4), attn_into(5)],
            [Scalar(place_order)]
            + [fetch(g[1]) for g in cross_grads]
            + [fetch(g[2]) for g in cross_grads]
            + [w_attn(4), w_attn(5), fetch(text_hidden)],
            flops=8 * clips * text_len * width * columns,
            scratch=[pltpu.VMEM((clips * text_len, width), LOW)],
            name="text_back",
        )
        return collect_tensor(results).astype(LOW)

    acc_self = [pltpu.VMEM((frames, columns), F32)] * 2

    def self_back_step(c, pair):
        own, got = pair
        q, k, v, o, lse = kept[0][c]
        grad, keep, send, left, right = run(
            self_backward_body,
            [sds((frames, 3 * columns), LOW), flow, flow, Copy(1), Copy(3)],
            [core_arg, own, w_attn(6), got]
            + [fetch(a) for a in (q, k, v, lse)]
            + [w_attn(0), w_attn(1), w_attn(2)],
            flops=8 * frames * width * columns + 10 * score_flops * frames,
            scratch=[pltpu.VMEM((frames, columns), LOW)] + acc_self,
            name="self_backward",
        )
        back_pairs[1][c] = (left, right)
        reduce_rows(c, keep, send)
        return grad

    self_grads = [None] * clips
    for c in every:
        grads[c], back_pairs[1][c], s = norm_back(1, hidden[1][c], moving[c], grads[c])
        sums[1].append(s)
        flush()
        self_grads[c] = self_back_step(c, back_pairs[1][c])
        if c == 0:
            text_grad = text_back_step()
            weights(back_pairs[2], [k[3] for k in kept[1]], [attn_into(7)], "cross_out")
        if c == min(1, clips - 1):
            weights(pairs[1], [g[0] for g in cross_grads], [attn_into(3)], "cross_query")
    bias_grad = jnp.sum(text_grad.astype(F32), axis=0)

    zero_lows = [None] * clips

    def zero_step(c):
        _, (zero_lows[c], _), s = norm_back(0, hidden[0][c], moving[c], grads[c])
        sums[0].append(s)

    zero_step(0)
    flush()
    text_into = Into(
        attn_shared,
        (dp, text_share, columns),
        lambda ref: ref.at[:, pl.ds(8 * share, text_share), :],
    )
    run(
        text_weight_body,
        [text_into],
        [text_rows, text_grad],
        flops=2 * clips * text_len * text_width * columns,
        name="text_weight",
    )
    weights(back_pairs[1], [k[3] for k in kept[0]], [attn_into(6)], "self_out")
    weights(pairs[0], self_grads, [attn_into(n) for n in range(3)], "self_in")
    attn_sum = lax.psum_scatter(attn_shared.array, "dp", scatter_dimension=0, tiled=False)
    for c in range(1, clips):
        zero_step(c)

    if aligned:
        pieces = run(
            split_features_body,
            [Flow(sds((clips * strip, share), LOW))] * dp,
            [
                Scalar(group_order),
                Scalar(jnp.broadcast_to(side.astype(jnp.int32), (clips + 1,))),
            ]
            + zero_lows,
            name="split_features",
        )
    else:
        rows = jnp.concatenate(
            [lax.dynamic_slice_in_dim(a, side * strip, strip, 0) for a in zero_lows], axis=0
        )
        rows = jnp.transpose(rows.reshape(clips * strip, dp, share), (1, 0, 2))
        pieces = list(jnp.take(rows, group_order, axis=0))
    rows_all = [pieces[0]] + [swap(pieces[m], "dp", m) for m in range(1, dp)]
    embed_parts = embed_back(vocab_base, back_lines, rows_all, vocab)
    grad_embed = collect_tensor([embed_parts[m] for m in range(tensor)])

    norm_part = jnp.concatenate(
        [sum(s)[0:1] for s in sums] + [sum(s)[1:2] for s in sums], axis=0
    ) * (1.0 / sides)
    bias_row = lax.dynamic_update_slice_in_dim(
        jnp.zeros((width,), F32), bias_grad, place * columns, 0
    )
    norm_total = total_over(
        jnp.concatenate([norm_part, bias_row[None]], axis=0), ("tensor", "dp")
    )
    grad_norm_rows = lax.dynamic_slice_in_dim(norm_total, group * share, share, 1)

    grad_attention = attn_sum[: 8 * share].reshape(attention.shape).astype(F32)
    grad_text_proj = jnp.transpose(attn_sum[8 * share :]).astype(F32)
    grad_feedforward = ffn_sum.astype(F32)
    grad_heads = head_sum.astype(F32)
    local_square = (
        jnp.sum(grad_attention * grad_attention)
        + jnp.sum(grad_feedforward * grad_feedforward)
        + jnp.sum(grad_heads * grad_heads)
        + jnp.sum(grad_embed * grad_embed)
        + jnp.sum(grad_text_proj * grad_text_proj)
        + jnp.sum(grad_norm_rows * grad_norm_rows) / tensor
    )
    both = total_over(
        jnp.stack([local_square, sum(loss_part) / tensor]).reshape(1, 2), ("tensor", "dp")
    )[0]
    grad_norm = jnp.sqrt(both[0])
    mean_loss = both[1] / valid_count
    factor = clip_limit / jnp.maximum(grad_norm, clip_limit)
    grad_tables = jnp.concatenate([grad_embed, grad_heads], 0)
    attn_new, attn_first_new, attn_second_new = adam_update(
        attention, grad_attention, attention_first, attention_second, rate_matrix, factor
    )
    ffn_new, ffn_first_new, ffn_second_new = adam_update(
        feedforward, grad_feedforward, feedforward_first, feedforward_second, rate_matrix, factor
    )
    table_new, table_first_new, table_second_new = adam_update(
        tables, grad_tables, tables_first, tables_second, rate_table, factor
    )
    text_new, text_first_new, text_second_new = adam_update(
        text_proj, grad_text_proj, text_first, text_second, rate_matrix, factor
    )
    norm_new, norm_first_new, norm_second_new = adam_update(
        norm_params, grad_norm_rows, norm_first, norm_second, rate_norm, factor
    )
    return (
        mean_loss,
        valid_count,
        grad_norm,
        attn_new,
        attn_new.astype(LOW),
        attn_first_new,
        attn_second_new,
        ffn_new,
        ffn_new.astype(LOW),
        ffn_first_new,
        ffn_second_new,
        table_new,
        table_new.astype(LOW),
        table_first_new,
        table_second_new,
        text_new,
        text_new.astype(LOW),
        text_first_new,
        text_second_new,
        norm_new,
        norm_first_new,
        norm_second_new,
    )


def solution(mesh):
    clip3 = P("dp", None, None)
    clip2 = P("dp", None)
    matrix = P(None, "dp", "tensor")
    text = P("tensor", "dp")
    norm = P(None, "dp")
    placed = (
        (clip3, clip3, clip2, clip3, clip2)
        + (matrix, matrix, matrix, text, norm)
        + (matrix,) * 6
        + (text, text, norm, norm)
    )
    return jax.shard_map(
        on_device,
        mesh=mesh,
        in_specs=placed,
        out_specs=(P(), P(), P()) + (matrix,) * 12 + (text,) * 4 + (norm,) * 3,
        check_vma=False,
    )
```

```python
from functools import partial
import math

import jax
import jax.numpy as jnp
from jax import lax
from jax.experimental import pallas as pl
from jax.experimental.pallas import tpu as pltpu
from jax.sharding import PartitionSpec as P

HEAD_DIM = 64
STEP = 5
BLOCK = 256
NEG = -1e30
LOW = jnp.bfloat16
F32 = jnp.float32

clip_limit = 0.004
stability_offset = 1e-08
weight_decay = 0.01
moment_decay = 0.5
rate_matrix = 0.03
rate_table = 0.05
rate_norm = 0.2


def nn(a, b):
    return lax.dot_general(a, b, (((1,), (0,)), ((), ())), preferred_element_type=F32)


def nt(a, b):
    return lax.dot_general(a, b, (((1,), (1,)), ((), ())), preferred_element_type=F32)


def tn(a, b):
    return lax.dot_general(a, b, (((0,), (0,)), ((), ())), preferred_element_type=F32)


def sds(shape, kind):
    return jax.ShapeDtypeStruct(shape, kind)


def scalars():
    return pl.BlockSpec(memory_space=pltpu.SMEM)


def anywhere():
    return pl.BlockSpec(memory_space=pl.ANY)


def in_hbm():
    return pl.BlockSpec(memory_space=pltpu.HBM)


def in_vmem():
    return pl.BlockSpec(memory_space=pltpu.VMEM)


def whole(a):
    rank = len(a.shape)
    return pl.BlockSpec(a.shape, lambda i: (0,) * rank)


def later(body, count, at):
    def ordered(*refs):
        return body(*refs[:at], *refs[at + count :])

    return ordered


class Scalar:
    def __init__(self, array):
        self.array = array


class Window:
    def __init__(self, array, shape, pick):
        self.array, self.shape, self.pick = array, tuple(shape), pick


def hold(array, space):
    return pltpu.with_memory_space_constraint(array, space)


def free(array):
    return pltpu.with_memory_space_constraint(array, pl.ANY)


class Flow:
    def __init__(self, shape):
        self.shape = shape


class Copy:
    def __init__(self, i):
        self.i = i


class Carry:
    def __init__(self, array):
        self.array = array


class Shared:
    def __init__(self, shape, kind):
        self.full, self.array = sds(shape, kind), None


class Into:
    def __init__(self, shared, shape, pick):
        self.shared, self.shape, self.pick = shared, tuple(shape), pick


def everything(ref):
    return ref


def nbytes_of(shape, kind):
    return math.prod(shape) * jnp.dtype(kind).itemsize


def kernel(body, outs, operands, flops=0, scratch=(), name=None, exps=0, after=(), margin=12):
    arrays, specs, windows, shown = [], [], [], []
    outs = list(outs)
    for i, a in enumerate(operands):
        shown.append(not isinstance(a, Carry))
        if isinstance(a, Carry):
            arrays.append(hold(a.array, pltpu.VMEM))
            specs.append(in_vmem())
            windows.append(None)
            outs.append(Copy(i))
        elif isinstance(a, Scalar):
            arrays.append(a.array)
            specs.append(scalars())
            windows.append(None)
        elif isinstance(a, Window):
            arrays.append(hold(a.array, pltpu.HBM))
            specs.append(in_hbm())
            windows.append(a)
        else:
            arrays.append(hold(a, pltpu.VMEM))
            specs.append(in_vmem())
            windows.append(None)
    aliases, out_shapes, out_specs, out_parts, owners = {}, [], [], [], []
    extra = []
    for o in outs:
        if isinstance(o, Into):
            if o.shared not in owners:
                if o.shared.array is not None:
                    aliases[len(arrays) + len(extra)] = len(out_shapes)
                    extra.append(o.shared.array)
                out_shapes.append(pltpu.HBM(o.shared.full.shape, o.shared.full.dtype))
                out_specs.append(in_hbm())
                owners.append(o.shared)
            out_parts.append(("put", o.shape, o.shared.full.dtype, o.pick, owners.index(o.shared)))
            continue
        if isinstance(o, Flow):
            out_parts.append(("flow", None, None, None, len(out_shapes)))
            out_shapes.append(pltpu.VMEM(o.shape.shape, o.shape.dtype))
            out_specs.append(in_vmem())
        elif isinstance(o, Copy):
            a = arrays[o.i]
            out_parts.append(("copy", o.i, None, None, len(out_shapes)))
            out_shapes.append(pltpu.HBM(a.shape, a.dtype))
            out_specs.append(in_hbm())
        else:
            out_parts.append(("put", o.shape, o.dtype, everything, len(out_shapes)))
            out_shapes.append(pltpu.HBM(o.shape, o.dtype))
            out_specs.append(in_hbm())
        owners.append(None)
    moved = [w for w in windows if w is not None]
    made = [p for p in out_parts if p[0] == "put"]
    count_in, count_extra, count_after = len(arrays), len(extra), len(after)
    count_out, count_moved, count_arrays = len(outs), len(moved), len(out_shapes)

    def run_body(*refs):
        refs = list(refs)
        ins = refs[:count_in]
        at = count_in + count_extra + count_after
        out_refs = refs[at : at + count_arrays]
        at += count_arrays
        in_buffers = refs[at : at + count_moved]
        at += count_moved
        made_buffers = refs[at : at + len(made)]
        at += len(made)
        in_sems, out_sems = refs[at], refs[at + 1]
        rest = refs[at + 2 :]
        views, copies, waited = [], {}, set()
        n = 0
        for i, (ref, w) in enumerate(zip(ins, windows)):
            if not shown[i]:
                continue
            if w is None:
                views.append(ref)
            else:
                copies[i] = pltpu.make_async_copy(w.pick(ref), in_buffers[n], in_sems.at[n])
                copies[i].start()
                views.append(in_buffers[n])
                n += 1
        sent, sources = {}, {}

        def need(*which):
            for i in which:
                if i in copies and i not in waited:
                    waited.add(i)
                    copies[i].wait()

        def put(*which):
            for j in which:
                if j in sources:
                    source, target = sources[j]
                    sent[j] = pltpu.make_async_copy(source, target, out_sems.at[j])
                    sent[j].start()

        body_outs = []
        n = 0
        for j, (kind, what, _, pick, owner) in enumerate(out_parts):
            if kind == "put":
                sources[j] = (made_buffers[n], pick(out_refs[owner]))
                body_outs.append(made_buffers[n])
                n += 1
            elif kind == "copy":
                sources[j] = (ins[what], out_refs[owner])
                put(j)
            else:
                body_outs.append(out_refs[owner])
        body(need, put, *views, *body_outs, *rest)
        need(*copies)
        put(*(j for j in sources if j not in sent))
        for copy in sent.values():
            copy.wait()

    nbytes = sum(nbytes_of(w.shape, w.array.dtype) for w in moved)
    nbytes += sum(nbytes_of(p[1], p[2]) for p in made)
    held = nbytes + sum(nbytes_of(m.shape, m.dtype) for m in scratch)
    results = pl.pallas_call(
        run_body,
        out_shape=tuple(out_shapes),
        in_specs=specs + [anywhere()] * (count_extra + count_after),
        out_specs=tuple(out_specs),
        input_output_aliases=aliases,
        scratch_shapes=[pltpu.VMEM(w.shape, w.array.dtype) for w in moved]
        + [pltpu.VMEM(p[1], p[2]) for p in made]
        + [
            pltpu.SemaphoreType.DMA((max(1, count_moved),)),
            pltpu.SemaphoreType.DMA((max(1, count_out),)),
        ]
        + list(scratch),
        compiler_params=pltpu.CompilerParams(vmem_limit_bytes=held + (margin << 20)),
        cost_estimate=pl.CostEstimate(
            flops=int(flops), bytes_accessed=int(nbytes), transcendentals=int(exps)
        ),
        name=name,
    )(*arrays, *extra, *after)
    for owner, result in zip(owners, results):
        if owner is not None:
            owner.array = result
    return [r for owner, r in zip(owners, results) if owner is None] or [results[-1]]


def flat(ref):
    w = ref[...]
    return w.reshape(-1, w.shape[-1])


def half_rows(core, height):
    return (
        pl.ds(pl.multiple_of(core * height, height), height),
        pl.ds(pl.multiple_of((1 - core) * height, height), height),
    )


def attend_block(query, keys, values, head_masks, diagonal, bias):
    rows, width = query.shape
    lane = lax.broadcasted_iota(jnp.int32, (rows, 128), 1)
    column = lax.broadcasted_iota(jnp.int32, (rows, width), 1) // HEAD_DIM
    mixed = jnp.zeros((rows, width), F32)
    totals = jnp.zeros((rows, 128), F32)
    count = keys.shape[0]
    for h, mask in enumerate(head_masks):
        s = nt(query * mask, keys)
        if diagonal is not None:
            last = jnp.where(diagonal, s[:, count - rows :], NEG)
            s = last if count == rows else jnp.concatenate([s[:, : count - rows], last], axis=1)
        if bias is not None:
            s = s + bias
        top = jnp.max(s, axis=1, keepdims=True)
        e = jnp.exp(s - top)
        total = jnp.sum(e, axis=1, keepdims=True)
        p = (e * (1.0 / total)).astype(LOW)
        mixed = jnp.where(column == h, nn(p, values), mixed)
        totals = jnp.where(lane == h, top + jnp.log(total), totals)
    return mixed, totals


def masks_of(width):
    head = lax.broadcasted_iota(jnp.int32, (1, width), 1) // HEAD_DIM
    return [(head == h).astype(F32).astype(LOW) for h in range(width // HEAD_DIM)]


def triangle(size):
    row = lax.broadcasted_iota(jnp.int32, (size, size), 0)
    col = lax.broadcasted_iota(jnp.int32, (size, size), 1)
    return row >= col


def self_forward_body(
    need, put, core_ref, own_ref, wq_ref, got_ref, wk_ref, wv_ref, wo_ref,
    q_ref, k_ref, v_ref, o_ref, lse_ref, keep_ref, send_ref, tot_ref,
):
    height = own_ref.shape[0]
    frames, width = q_ref.shape
    mine, other = half_rows(core_ref[0], height)
    need(1)
    for i, w_ref, to_ref in ((2, wq_ref, q_ref), (4, wk_ref, k_ref), (5, wv_ref, v_ref)):
        need(i)
        w = flat(w_ref)
        to_ref[mine, :] = nn(own_ref[...], w).astype(LOW)
        need(3)
        to_ref[other, :] = nn(got_ref[...], w).astype(LOW)
    put(0, 1, 2)
    scale = jnp.asarray(HEAD_DIM**-0.5, LOW)
    head_masks = masks_of(width)
    diagonal = triangle(BLOCK)
    for i in range(frames // BLOCK):
        rows = slice(i * BLOCK, (i + 1) * BLOCK)
        mixed, totals = attend_block(
            q_ref[rows, :] * scale,
            k_ref[: (i + 1) * BLOCK, :],
            v_ref[: (i + 1) * BLOCK, :],
            head_masks,
            diagonal,
            None,
        )
        o_ref[rows, :] = mixed.astype(LOW)
        tot_ref[rows, :] = totals
    put(3)
    need(6)
    wo = flat(wo_ref)
    send_ref[...] = nt(o_ref[other, :], wo).astype(LOW)
    put(6)
    keep_ref[...] = nt(o_ref[mine, :], wo).astype(LOW)
    put(5)
    lse_ref[...] = jnp.transpose(tot_ref[...])[:8, :]


def cross_forward_body(
    need, put, core_ref, own_ref, wq_ref, got_ref, bias_ref, k_ref, v_ref, wo_ref,
    q_ref, o_ref, lse_ref, keep_ref, send_ref, tot_ref,
):
    height = own_ref.shape[0]
    frames, width = q_ref.shape
    mine, other = half_rows(core_ref[0], height)
    need(1, 2)
    w = flat(wq_ref)
    q_ref[mine, :] = nn(own_ref[...], w).astype(LOW)
    need(3)
    q_ref[other, :] = nn(got_ref[...], w).astype(LOW)
    put(0)
    scale = jnp.asarray(HEAD_DIM**-0.5, LOW)
    head_masks = masks_of(width)
    need(4, 5, 6)
    for i in range(frames // BLOCK):
        rows = slice(i * BLOCK, (i + 1) * BLOCK)
        mixed, totals = attend_block(
            q_ref[rows, :] * scale, k_ref[...], v_ref[...], head_masks, None, bias_ref[...]
        )
        o_ref[rows, :] = mixed.astype(LOW)
        tot_ref[rows, :] = totals
    put(1)
    need(7)
    wo = flat(wo_ref)
    send_ref[...] = nt(o_ref[other, :], wo).astype(LOW)
    put(4)
    keep_ref[...] = nt(o_ref[mine, :], wo).astype(LOW)
    put(3)
    lse_ref[...] = jnp.transpose(tot_ref[...])[:8, :]


def ffn_forward_body(
    need, put, core_ref, own_ref, got_ref, w1_ref, w2_ref,
    act_ref, slope_ref, keep_ref, send_ref,
):
    height = own_ref.shape[0]
    mine, other = half_rows(core_ref[0], height)
    need(1, 2, 3)
    w1 = flat(w1_ref)
    for j, source, rows, to_ref in (
        (3, got_ref, other, send_ref),
        (2, own_ref, mine, keep_ref),
    ):
        u = nn(source[...], w1)
        phi = 0.5 * (1.0 + lax.erf(u * (2.0**-0.5)))
        act = (u * phi).astype(LOW)
        density = jnp.exp(-0.5 * u * u) * ((2.0 * math.pi) ** -0.5)
        act_ref[rows, :] = act
        slope_ref[rows, :] = (phi + u * density).astype(LOW)
        need(4)
        to_ref[...] = nt(act, flat(w2_ref)).astype(to_ref.dtype)
        put(j)


def head_forward_body(
    need, put, core_ref, own_ref, target_ref, got_ref, *refs
):
    *w_refs, logits_ref, stats_ref, tot_ref = refs
    height = own_ref.shape[0]
    books = len(w_refs)
    vocab = w_refs[0].shape[2]
    halves = half_rows(core_ref[0], height)
    lane = lax.broadcasted_iota(jnp.int32, (height, 128), 1)
    code = lax.broadcasted_iota(jnp.int32, (height, vocab), 1)
    need(1, 2)
    totals = [jnp.zeros((height, 128), F32)] * 2
    for k, w_ref in enumerate(w_refs):
        need(4 + k)
        w = flat(w_ref)
        for j, (source, rows) in enumerate(zip((own_ref, got_ref), halves)):
            need(1 + 2 * j)
            s = nn(source[...], w)
            logits_ref[rows, k * vocab : (k + 1) * vocab] = s
            top = jnp.max(s, axis=1, keepdims=True)
            total = jnp.sum(jnp.exp(s - top), axis=1, keepdims=True)
            hit = code == target_ref[rows, k : k + 1]
            pick = jnp.sum(jnp.where(hit, s, 0.0), axis=1, keepdims=True)
            totals[j] = jnp.where(lane == k, top + jnp.log(total), totals[j])
            totals[j] = jnp.where(lane == books + k, pick, totals[j])
    put(0)
    for rows, t in zip(halves, totals):
        tot_ref[rows, :] = t
    stats_ref[...] = jnp.transpose(tot_ref[...])[: 2 * books, :]


def head_backward_body(
    need, put, core_ref, total_ref, weight_ref, target_ref, logits_ref, *refs
):
    *w_refs, grad_ref, keep_ref, send_ref, loss_ref, col_ref = refs
    height = keep_ref.shape[0]
    books = len(w_refs)
    vocab = w_refs[0].shape[2]
    mine, other = half_rows(core_ref[0], height)
    frames = logits_ref.shape[0]
    need(1, 2, 3)
    wide = jnp.concatenate(
        [total_ref[...], jnp.zeros((128 - total_ref.shape[0], frames), F32)], axis=0
    )
    col_ref[...] = jnp.transpose(wide)
    gap = (col_ref[:, :books] - col_ref[:, books : 2 * books]) * weight_ref[...]
    loss_ref[...] = jnp.broadcast_to(jnp.sum(gap).reshape(1, 1), loss_ref.shape)
    code = lax.broadcasted_iota(jnp.int32, (height, vocab), 1)
    need(4)
    for j, rows, to_ref in ((2, other, send_ref), (1, mine, keep_ref)):
        weight = weight_ref[rows, :]
        total = col_ref[rows, :]
        acc = None
        for k, w_ref in enumerate(w_refs):
            s = logits_ref[rows, k * vocab : (k + 1) * vocab]
            p = jnp.exp(s - total[:, k : k + 1])
            hit = jnp.where(code == target_ref[rows, k : k + 1], 1.0, 0.0)
            g = ((p - hit) * weight[:, k : k + 1]).astype(LOW)
            grad_ref[rows, k * vocab : (k + 1) * vocab] = g
            need(5 + k)
            part = nt(g, flat(w_ref))
            acc = part if acc is None else acc + part
        to_ref[...] = acc.astype(to_ref.dtype)
        put(j)


def ffn_backward_body(
    need, put, core_ref, own_ref, got_ref, w2_ref, slope_ref, w1_ref,
    grad_ref, keep_ref, send_ref,
):
    height = own_ref.shape[0]
    mine, other = half_rows(core_ref[0], height)
    need(1, 2, 3, 4)
    w2 = flat(w2_ref)
    for j, source, rows, to_ref in (
        (2, got_ref, other, send_ref),
        (1, own_ref, mine, keep_ref),
    ):
        g = (nn(source[...], w2) * slope_ref[rows, :].astype(F32)).astype(LOW)
        grad_ref[rows, :] = g
        need(5)
        to_ref[...] = nt(g, flat(w1_ref)).astype(to_ref.dtype)
        put(j)


def attend_back(
    q, k, v, g, lse, head_masks, scale, diagonal, bias, dq_ref, rows, dk_ref, dv_ref, first
):
    count, width = k.shape
    step = q.shape[0]
    dq = jnp.zeros((step, width), F32)
    dk = jnp.zeros((count, width), F32)
    dv = jnp.zeros((count, width), F32)
    for h, mask in enumerate(head_masks):
        qm = q * mask
        gm = g * mask
        s = nt(k, qm)
        if diagonal is not None:
            last = jnp.where(diagonal, s[count - step :, :], NEG)
            s = last if count == step else jnp.concatenate([s[: count - step, :], last], axis=0)
        if bias is not None:
            s = s + bias
        p = jnp.exp(s - lse[h : h + 1, :])
        dp = nt(v, gm)
        inner = jnp.sum(p * dp, axis=0, keepdims=True)
        ds = (p * (dp - inner)).astype(LOW)
        dq = dq + tn(ds, k * mask)
        dk = dk + nn(ds, qm)
        dv = dv + nn(p.astype(LOW), gm)
    dq_ref[rows, :width] = (dq * scale).astype(LOW)
    dk_ref[:count, :] = dk if first else dk_ref[:count, :] + dk
    dv_ref[:count, :] = dv if first else dv_ref[:count, :] + dv


def self_backward_body(
    need, put, core_ref, own_ref, wo_ref, got_ref, q_ref, k_ref, v_ref, lse_ref,
    wq_ref, wk_ref, wv_ref, grad_ref, keep_ref, send_ref, g_ref, dk_acc, dv_acc,
):
    height = own_ref.shape[0]
    frames, width = q_ref.shape
    mine, other = half_rows(core_ref[0], height)
    need(1, 2)
    wo = flat(wo_ref)
    g_ref[mine, :] = nn(own_ref[...], wo).astype(LOW)
    need(3)
    g_ref[other, :] = nn(got_ref[...], wo).astype(LOW)
    scale = HEAD_DIM**-0.5
    head_masks = masks_of(width)
    row = lax.broadcasted_iota(jnp.int32, (BLOCK, BLOCK), 0)
    col = lax.broadcasted_iota(jnp.int32, (BLOCK, BLOCK), 1)
    diagonal = col >= row
    blocks = frames // BLOCK
    need(4, 5, 6, 7)
    for i in reversed(range(blocks)):
        rows = slice(i * BLOCK, (i + 1) * BLOCK)
        count = (i + 1) * BLOCK
        attend_back(
            q_ref[rows, :] * jnp.asarray(scale, LOW),
            k_ref[:count, :],
            v_ref[:count, :],
            g_ref[rows, :],
            lse_ref[:, rows],
            head_masks,
            scale,
            diagonal,
            None,
            grad_ref,
            rows,
            dk_acc,
            dv_acc,
            i == blocks - 1,
        )
    grad_ref[:, width : 2 * width] = dk_acc[...].astype(LOW)
    grad_ref[:, 2 * width :] = dv_acc[...].astype(LOW)
    put(0)
    need(8, 9, 10)
    for j, rows, to_ref in ((2, other, send_ref), (1, mine, keep_ref)):
        part = None
        for n, w_ref in enumerate((wq_ref, wk_ref, wv_ref)):
            term = nt(grad_ref[rows, n * width : (n + 1) * width], flat(w_ref))
            part = term if part is None else part + term
        to_ref[...] = part.astype(to_ref.dtype)
        put(j)


def cross_backward_body(
    need, put, core_ref, own_ref, wo_ref, got_ref, bias_ref, q_ref, k_ref, v_ref, lse_ref, wq_ref,
    dq_ref, dk_ref, dv_ref, keep_ref, send_ref, g_ref, dk_acc, dv_acc,
):
    height = own_ref.shape[0]
    frames, width = q_ref.shape
    mine, other = half_rows(core_ref[0], height)
    need(1, 2)
    wo = flat(wo_ref)
    g_ref[mine, :] = nn(own_ref[...], wo).astype(LOW)
    need(3)
    g_ref[other, :] = nn(got_ref[...], wo).astype(LOW)
    scale = HEAD_DIM**-0.5
    head_masks = masks_of(width)
    need(4, 5, 6, 7, 8)
    for i in range(frames // BLOCK):
        rows = slice(i * BLOCK, (i + 1) * BLOCK)
        attend_back(
            q_ref[rows, :] * jnp.asarray(scale, LOW),
            k_ref[...],
            v_ref[...],
            g_ref[rows, :],
            lse_ref[:, rows],
            head_masks,
            scale,
            None,
            bias_ref[...],
            dq_ref,
            rows,
            dk_acc,
            dv_acc,
            i == 0,
        )
    put(0)
    need(9)
    wq = flat(wq_ref)
    for j, rows, to_ref in ((4, other, send_ref), (3, mine, keep_ref)):
        to_ref[...] = nt(dq_ref[rows, :], wq).astype(to_ref.dtype)
        put(j)
    dk_ref[...] = dk_acc[...].astype(LOW)
    dv_ref[...] = dv_acc[...].astype(LOW)


def normalize(values, gain, shift):
    center = values - jnp.mean(values, axis=1, keepdims=True)
    spread = jnp.mean(center * center, axis=1, keepdims=True)
    return center * lax.rsqrt(spread + 1e-05) * gain + shift


def merge_body(books, own_ref, far_ref, out_ref):
    own, far = own_ref[:books, :], far_ref[:books, :]
    high = jnp.maximum(own, far)
    out_ref[:books, :] = high + jnp.log(jnp.exp(own - high) + jnp.exp(far - high))
    out_ref[books:, :] = own_ref[books:, :] + far_ref[books:, :]


def text_in_body(need, put, place_ref, norm_ref, rows_ref, w_ref, out_ref):
    columns = out_ref.shape[1]
    at = pl.ds(pl.multiple_of(place_ref[0] * columns, columns), columns)
    need(2, 3)
    out_ref[...] = (nn(rows_ref[...], flat(w_ref)) + norm_ref[8:9, at]).astype(LOW)


def add_body(keep_ref, got_ref, out_ref):
    out_ref[...] = (keep_ref[...].astype(F32) + got_ref[...].astype(F32)).astype(LOW)


def norm_body(which, hidden_ref, part_ref, far_ref, norm_ref, new_ref, out_ref):
    new = hidden_ref[...] + (part_ref[...].astype(F32) + far_ref[...].astype(F32))
    new_ref[...] = new
    out_ref[...] = normalize(
        new, norm_ref[which : which + 1, :], norm_ref[which + 4 : which + 5, :]
    ).astype(LOW)


def embed_norm_body(need, put, side_ref, place_ref, norm_ref, *refs):
    *part_refs, new_ref, out_ref = refs
    side = side_ref[0]
    rows = part_refs[0].shape[0]
    need(1, 2)
    for s, part in enumerate(part_refs):
        need(3 + s)
        at = pl.ds(pl.multiple_of((side ^ s) * rows, rows), rows)
        new = part[...].astype(F32) + place_ref[at, :]
        new_ref[at, :] = new
        out_ref[at, :] = normalize(new, norm_ref[0:1, :], norm_ref[4:5, :]).astype(LOW)
    put(1, 0)


def norm_back_body(which, hidden_ref, part_ref, far_ref, *refs):
    *before, norm_ref, new_ref, low_ref, sums_ref = refs
    values = hidden_ref[...]
    grad = part_ref[...].astype(F32) + far_ref[...].astype(F32)
    gain = norm_ref[which : which + 1, :]
    center = values - jnp.mean(values, axis=1, keepdims=True)
    spread = jnp.mean(center * center, axis=1, keepdims=True)
    inverse = lax.rsqrt(spread + 1e-05)
    unit = center * inverse
    scaled = grad * gain
    first = jnp.mean(scaled, axis=1, keepdims=True)
    second = jnp.mean(scaled * unit, axis=1, keepdims=True)
    new = inverse * (scaled - first - unit * second)
    if before:
        new = before[0][...] + new
    new_ref[...] = new
    low_ref[...] = new.astype(LOW)
    sums_ref[...] = jnp.concatenate(
        [
            jnp.sum(grad * unit, axis=0, keepdims=True),
            jnp.sum(grad, axis=0, keepdims=True),
            jnp.zeros((6, values.shape[1]), F32),
        ],
        axis=0,
    )


def weight_grad_body(clips, turn_left, need, put, core_ref, *refs):
    lefts = refs[: 2 * clips]
    rights = refs[2 * clips : 3 * clips]
    outs = refs[3 * clips : -1]
    turned = refs[-1]
    height, width = lefts[0].shape
    frames = rights[0].shape[0]
    group = outs[0].shape[2]
    core = core_ref[0]

    def place(c, at):
        return pl.ds(pl.multiple_of(c * frames + at * height, 128), height)

    if turn_left:
        for m, out_ref in enumerate(outs):
            total = None
            for c in range(clips):
                if m == 0:
                    for j, at in ((0, core), (1, 1 - core)):
                        need(1 + 2 * c + j)
                        turned[:, place(c, at)] = jnp.transpose(lefts[2 * c + j][...])
                    need(1 + 2 * clips + c)
                part = nn(
                    turned[:, c * frames : (c + 1) * frames],
                    rights[c][:, m * group : (m + 1) * group],
                )
                total = part if total is None else total + part
            out_ref[...] = total.astype(LOW).reshape(out_ref.shape)
            put(m)
    else:
        total = None
        for c in range(clips):
            need(1 + 2 * clips + c)
            turned[:, c * frames : (c + 1) * frames] = jnp.transpose(rights[c][...])
            for j, at in ((0, core), (1, 1 - core)):
                need(1 + 2 * c + j)
                part = nn(turned[:, place(c, at)], lefts[2 * c + j][...])
                total = part if total is None else total + part
        for m, out_ref in enumerate(outs):
            member = total[m * group : (m + 1) * group, :]
            out_ref[...] = jnp.transpose(member).astype(LOW).reshape(out_ref.shape)
            put(m)


def norm_rows_kernel(body, outs, operands, norm_rows, after, name="norm"):
    height, width = operands[0].shape
    operands = list(operands) + ([] if norm_rows is None else [norm_rows])
    nbytes = sum(nbytes_of(a.shape, a.dtype) for a in operands + list(outs))
    return pl.pallas_call(
        later(body, len(after), len(operands)),
        out_shape=tuple(pltpu.VMEM(o.shape, o.dtype) for o in outs),
        in_specs=[in_vmem()] * len(operands) + [anywhere()] * len(after),
        out_specs=tuple(in_vmem() for _ in outs),
        compiler_params=pltpu.CompilerParams(vmem_limit_bytes=12 << 20),
        cost_estimate=pl.CostEstimate(
            flops=20 * height * width, bytes_accessed=nbytes // 4, transcendentals=0
        ),
        name=name,
    )(*(hold(a, pltpu.VMEM) for a in operands), *after)


def embed_body(base_ref, codes_ref, *refs):
    *table_refs, out_ref = refs
    books, features, vocab = table_refs[0].shape
    rows = codes_ref.shape[1]
    chunk = min(256, vocab)
    code = lax.broadcasted_iota(jnp.int32, (rows, chunk), 1)
    acc = jnp.zeros((rows, features), F32)
    for k in range(books):
        column = codes_ref[0, :, k : k + 1]
        for b, table in enumerate(table_refs):
            local = column - base_ref[b]
            for v in range(0, vocab, chunk):
                hit = jnp.where(code == local - v, 1.0, 0.0).astype(LOW)
                acc = acc + nt(hit, table[k, :, v : v + chunk])
    out_ref[0] = acc.astype(LOW)


def embed(base, codes, tables, after):
    blocks, rows, books = codes.shape
    features = tables[0].shape[1]
    vocab = tables[0].shape[2] * len(tables)
    return pl.pallas_call(
        later(embed_body, len(after), 2 + len(tables)),
        out_shape=sds((blocks, rows, features), LOW),
        grid=(blocks,),
        in_specs=[scalars(), pl.BlockSpec((1, rows, books), lambda i: (i, 0, 0))]
        + [in_vmem() for t in tables]
        + [anywhere()] * len(after),
        out_specs=pl.BlockSpec((1, rows, features), lambda i: (i, 0, 0)),
        compiler_params=pltpu.CompilerParams(vmem_limit_bytes=12 << 20),
        cost_estimate=pl.CostEstimate(
            flops=4 * blocks * rows * books * vocab * features,
            bytes_accessed=2 * books * vocab * features + blocks * rows * (features + 512),
            transcendentals=0,
        ),
        name="embed",
    )(base, codes, *tables, *after)


def embed_back_body(base_ref, codes_ref, *refs):
    *grad_refs, out_ref, all_ref = refs
    rows, features = grad_refs[0].shape
    vocab = out_ref.shape[3]
    book = pl.program_id(1)
    chunk = min(256, vocab)

    @pl.when((pl.program_id(0) == 0) & (book == 0))
    def _():
        for j, g in enumerate(grad_refs):
            all_ref[j * rows : (j + 1) * rows, :] = g[...]

    base = base_ref[pl.program_id(0)]
    line = codes_ref[0]
    line = line[0:1, :]
    code = lax.broadcasted_iota(jnp.int32, (chunk, line.shape[1]), 0)
    for v in range(0, vocab, chunk):
        hit = jnp.where(code == line - (base + v), 1.0, 0.0).astype(LOW)
        out_ref[0, 0, :, v : v + chunk] = jnp.transpose(nn(hit, all_ref[...])).astype(LOW)


def embed_back(base, lines, grads, vocab):
    parts = base.shape[0]
    books, _, total = lines.shape
    features = grads[0].shape[1]
    return pl.pallas_call(
        embed_back_body,
        out_shape=sds((parts, books, features, vocab), LOW),
        grid=(parts, books),
        in_specs=[scalars(), pl.BlockSpec((1, 8, total), lambda i, k: (k, 0, 0))]
        + [pl.BlockSpec(g.shape, lambda i, k: (0, 0)) for g in grads],
        out_specs=pl.BlockSpec((1, 1, features, vocab), lambda i, k: (i, k, 0, 0)),
        scratch_shapes=[pltpu.VMEM((total, features), LOW)],
        compiler_params=pltpu.CompilerParams(vmem_limit_bytes=12 << 20),
        cost_estimate=pl.CostEstimate(
            flops=4 * parts * books * vocab * features * total,
            bytes_accessed=2 * parts * books * features * vocab + 2 * total * features,
            transcendentals=0,
        ),
        name="embed_back",
    )(base, lines, *grads)


def gather_features_body(need, put, where_ref, *refs):
    clips = sum(r.shape[1] != refs[0].shape[1] for r in refs)
    part_refs, outs = refs[:-clips], refs[-clips:]
    features = part_refs[0].shape[1]
    strip = outs[0].shape[0]
    for m, part in enumerate(part_refs):
        at = pl.ds(pl.multiple_of(where_ref[m] * features, features), features)
        for c, out_ref in enumerate(outs):
            out_ref[:, at] = part[c * strip : (c + 1) * strip, :]


def split_features_body(need, put, where_ref, side_ref, *refs):
    clips = side_ref.shape[0] - 1
    grads, outs = refs[:clips], refs[clips:]
    features = outs[0].shape[1]
    rows = outs[0].shape[0] // clips
    at_rows = pl.ds(pl.multiple_of(side_ref[0] * rows, rows), rows)
    need(*range(2, 2 + clips))
    for m, out_ref in reversed(list(enumerate(outs))):
        at = pl.ds(pl.multiple_of(where_ref[m] * features, features), features)
        for c in range(clips):
            out_ref[c * rows : (c + 1) * rows, :] = grads[c][at_rows, at]
        put(m)


def text_body(need, put, where_ref, *refs):
    *part_refs, wk_ref, wv_ref, tp_ref, k_ref, v_ref = refs
    columns = part_refs[0].shape[1]
    for m, part in enumerate(part_refs):
        need(1 + m)
        at = pl.ds(pl.multiple_of(where_ref[m] * columns, columns), columns)
        tp_ref[:, at] = part[...]
    put(0)
    for j, w_ref, to_ref in ((1, wk_ref, k_ref), (2, wv_ref, v_ref)):
        need(len(part_refs) + j)
        to_ref[...] = nn(tp_ref[...], flat(w_ref)).astype(LOW)
        put(j)


def text_back_body(clips, need, put, where_ref, *refs):
    dks, dvs = refs[:clips], refs[clips : 2 * clips]
    wk_ref, wv_ref, tp_ref = refs[2 * clips : 2 * clips + 3]
    *part_refs, gk_ref, gv_ref, full_ref = refs[2 * clips + 3 :]
    columns = part_refs[0].shape[1]
    length = dks[0].shape[0]
    need(*range(1, 1 + 2 * clips + 2))
    wk, wv = flat(wk_ref), flat(wv_ref)
    for c in range(clips):
        tp_rows = slice(c * length, (c + 1) * length)
        full_ref[tp_rows, :] = (nt(dks[c][...], wk) + nt(dvs[c][...], wv)).astype(LOW)
    for m, part_ref in enumerate(part_refs):
        at = pl.ds(pl.multiple_of(where_ref[m] * columns, columns), columns)
        part_ref[...] = full_ref[:, at]
    put(*range(len(part_refs)))
    need(3 + 2 * clips)
    turned = jnp.transpose(tp_ref[...])
    for j, grads, to_ref in ((0, dks, gk_ref), (1, dvs, gv_ref)):
        total = None
        for c in range(clips):
            part = nn(turned[:, c * length : (c + 1) * length], grads[c][...])
            total = part if total is None else total + part
        to_ref[...] = total.astype(LOW).reshape(to_ref.shape)
        put(len(part_refs) + j)


def text_weight_body(need, put, rows_ref, own_ref, far_ref, out_ref, bias_ref):
    need(0)
    grad = (own_ref[...].astype(F32) + far_ref[...].astype(F32)).astype(LOW)
    out_ref[...] = tn(rows_ref[...], grad).astype(LOW).reshape(out_ref.shape)
    bias_ref[...] = jnp.broadcast_to(
        jnp.sum(grad.astype(F32), axis=0, keepdims=True), bias_ref.shape
    )


def positions_rows(start, count, feature_count):
    half_width = feature_count // 2
    frequency = jnp.exp(
        jnp.arange(half_width, dtype=F32) * (-math.log(10000.0) / (half_width - 1))
    )
    angles = (start + jnp.arange(count, dtype=jnp.int32)).astype(F32)[:, None] * frequency[None, :]
    return jnp.concatenate([jnp.cos(angles), jnp.sin(angles)], axis=1)


def adam_update(weight, gradient, first_moment, second_moment, step_rate, factor):
    clipped = gradient * factor
    new_first = moment_decay * first_moment + (1.0 - moment_decay) * clipped
    new_second = moment_decay * second_moment + (1.0 - moment_decay) * clipped * clipped
    first_hat = new_first / (1.0 - moment_decay**STEP)
    second_hat = new_second / (1.0 - moment_decay**STEP)
    new_weight = weight * (1.0 - step_rate * weight_decay) - step_rate * first_hat / (
        jnp.sqrt(second_hat) + stability_offset
    )
    return (new_weight, new_first, new_second)


def swap(values, axis, mask):
    size = lax.axis_size(axis)
    return lax.ppermute(values, axis, [(i, i ^ mask) for i in range(size)])


def on_device(
    audio_codes,
    delay_mask,
    frame_mask,
    text_states,
    text_mask,
    attention,
    feedforward,
    tables,
    text_proj,
    norm_params,
    attention_first,
    attention_second,
    feedforward_first,
    feedforward_second,
    tables_first,
    tables_second,
    text_first,
    text_second,
    norm_first,
    norm_second,
):
    clips, frames, books = audio_codes.shape
    text_len, text_width = text_states.shape[1:]
    dp = lax.axis_size("dp")
    tensor = lax.axis_size("tensor")
    group = lax.axis_index("dp")
    place = lax.axis_index("tensor")
    core = place & 1
    side = place >> 1
    sides = tensor // 2
    height = frames // 2
    strip = height // sides
    share = attention.shape[1]
    columns = attention.shape[2]
    width = share * dp
    vocab = tables.shape[2]
    text_share = text_proj.shape[1]
    core_arg = Scalar(core.astype(jnp.int32).reshape(1))
    side_arg = Scalar(side.astype(jnp.int32).reshape(1))
    swap_core = partial(swap, axis="tensor", mask=1)

    def spread_tensor(values):
        held = [values]
        mask = tensor // 2
        order = [0]
        while mask:
            held = held + [swap(v, "tensor", mask) for v in held]
            order = order + [o | mask for o in order]
            mask //= 2
        return [v for _, v in sorted(zip(order, held), key=lambda t: t[0])]

    def collect_tensor(parts):
        mask = 1
        live = {m: p for m, p in enumerate(parts)}
        while mask < tensor:
            fresh = {}
            for m in live:
                if not m & mask:
                    got = swap(live[m | mask].astype(LOW), "tensor", mask)
                    fresh[m] = live[m].astype(F32) + got.astype(F32)
            live = fresh
            mask *= 2
        return live[0]

    def across(values):
        own = values
        mask = 2
        rest = None
        while mask < tensor:
            got = swap(own, "tensor", mask)
            mask *= 2
            if mask < tensor:
                own = (own.astype(F32) + got.astype(F32)).astype(LOW)
            rest = got
        if rest is None:
            rest = jnp.zeros_like(own)
        return own, rest

    def total_over(values, axes):
        for axis in axes:
            mask = 1
            while mask < lax.axis_size(axis):
                values = values + swap(values, axis, mask)
                mask *= 2
        return values

    last = []

    def run(body, outs, operands, **rest):
        shared = [o.shared.array for o in outs if isinstance(o, Into)]
        wait_for = [a for a in last if not any(a is b for b in shared)]
        results = kernel(body, outs, operands, after=wait_for, **rest)
        last[:] = [results[-1]]
        return results

    norm_pad = jnp.pad(norm_params.astype(LOW), ((0, 16 - norm_params.shape[0]), (0, columns - share)))
    attn_flat = jnp.concatenate(
        [attention.astype(LOW).reshape(-1, columns), text_proj.astype(LOW).T, norm_pad], axis=0
    )
    attn_all = lax.all_gather(attn_flat, "dp", axis=0)
    ffn_all = lax.all_gather(feedforward.astype(LOW), "dp", axis=0)
    head_all = lax.all_gather(tables[books:].astype(LOW), "dp", axis=0)

    frame_live = (jnp.arange(frames, dtype=jnp.int32) < frames - 1).astype(jnp.int32)
    weight_int = delay_mask * frame_mask[:, :, None] * frame_live[None, :, None]
    start = core * height + side * strip
    strip_codes = lax.dynamic_slice_in_dim(audio_codes, start, strip, 1)
    lines = jnp.transpose(strip_codes, (2, 0, 1)).reshape(books, clips * strip)
    count_line = jnp.broadcast_to(jnp.sum(weight_int), (1, clips * strip))
    packet = jnp.concatenate([lines, count_line], axis=0)[None]
    mask = 1
    while mask < dp:
        packet = jnp.concatenate([packet, swap(packet, "dp", mask)], axis=0)
        mask *= 2
    valid_count = jnp.sum(packet[:, books, 0]).astype(F32)
    all_lines = packet[:, :books]
    all_codes = jnp.transpose(all_lines, (0, 2, 1))
    back_lines = jnp.broadcast_to(
        jnp.transpose(all_lines, (1, 0, 2)).reshape(books, 1, dp * clips * strip),
        (books, 8, dp * clips * strip),
    )
    vocab_base = (place ^ jnp.arange(tensor, dtype=jnp.int32)) * vocab
    group_order = group ^ jnp.arange(dp, dtype=jnp.int32)
    place_order = place ^ jnp.arange(tensor, dtype=jnp.int32)

    text_bias_row = jnp.where(text_mask > 0, 0.0, NEG).astype(F32)
    bias_lines = [text_bias_row[c : c + 1] for c in range(clips)]
    bias_columns = [jnp.transpose(line) for line in bias_lines]
    targets = (jnp.roll(audio_codes, -1, axis=1) - place * vocab).astype(jnp.int32)
    targets = [targets[c] for c in range(clips)]
    grad_weight = weight_int.astype(F32) / valid_count
    grad_weight = [grad_weight[c] for c in range(clips)]
    placed = positions_rows(core * height, height, width)
    last[:] = bias_lines + bias_columns + targets + grad_weight + [placed, back_lines]

    table_parts = spread_tensor(tables[:books].astype(LOW))
    step = max(1, dp // 4)
    arrived = [None] * dp
    for low_end in reversed(range(0, dp, step)):
        embedded = embed(
            vocab_base, all_codes[low_end : low_end + step], table_parts, list(last)
        )
        last[:] = [embedded]
        for m in range(low_end, low_end + step):
            piece = embedded[m - low_end]
            arrived[m] = swap(piece, "dp", m) if m else piece
    aligned = share % 128 == 0
    if aligned:
        strips = run(
            gather_features_body,
            [Flow(sds((strip, width), LOW))] * clips,
            [Scalar(group_order)] + arrived,
            name="gather_features",
        )
        strips = [free(a) for a in strips]
    else:
        strips = jnp.take(jnp.stack(arrived), group_order, axis=0)
        strips = jnp.transpose(strips, (1, 0, 2)).reshape(clips, strip, width)

    norm_rows = attn_all[:, 8 * share + text_share :, :share]
    norm_rows = jnp.transpose(norm_rows, (1, 0, 2)).reshape(16, width).astype(F32)

    def w_attn(n):
        return Window(
            attn_all, (dp, share, columns), lambda ref: ref.at[:, pl.ds(n * share, share), :]
        )

    def w_member(array, n):
        return Window(array, (dp,) + array.shape[2:], lambda ref: ref.at[:, n])

    half_sds = sds((height, width), F32)
    half_low = sds((height, width), LOW)
    flow = Flow(half_low)

    def fetch(a):
        return Window(a, a.shape, everything)


    def norm_step(which, hidden, parts):
        new, out = norm_rows_kernel(
            partial(norm_body, which), [half_sds, half_low], [hidden, *parts], norm_rows, last
        )
        last[:] = [out]
        return new, (out, swap_core(free(out)))

    def norm_back(which, hidden, parts, before):
        operands = [hidden, *parts] + ([before] if before is not None else [])
        new, out, sums = norm_rows_kernel(
            partial(norm_back_body, which),
            [half_sds, half_low, sds((8, width), F32)],
            operands,
            norm_rows,
            last,
        )
        last[:] = [out]
        return new, (out, swap_core(free(out))), free(sums)

    waiting = []
    moving = [None] * clips

    def flush():
        if waiting:
            c, keep, got = waiting.pop()
            (part,) = norm_rows_kernel(add_body, [half_low], [keep, got], None, last, name="add")
            last[:] = [part]
            moving[c] = (part, *across(free(part))[1:])

    def reduce_rows(c, keep, send):
        waiting.append((c, keep, swap_core(free(send))))

    text_rows = text_states.reshape(clips * text_len, text_width)
    def text_in_step():
        (result,) = run(
            text_in_body,
            [Flow(sds((clips * text_len, columns), LOW))],
            [
                Scalar(place.astype(jnp.int32).reshape(1)),
                norm_rows,
                fetch(text_rows),
                Window(
                    attn_all,
                    (dp, text_share, columns),
                    lambda ref: ref.at[:, pl.ds(8 * share, text_share), :],
                ),
            ],
            flops=2 * clips * text_len * text_width * columns,
            name="text_in",
        )
        return spread_tensor(free(result))

    full = sds((frames, columns), LOW)
    lse_sds = sds((8, frames), F32)
    tot = [pltpu.VMEM((frames, 128), F32)]
    heads = columns // HEAD_DIM
    score_flops = 2 * heads * frames * HEAD_DIM
    units = feedforward.shape[2]
    inner = sds((frames, units), LOW)
    every = range(clips)

    def embed_step(c):
        mine = strips[c]
        parts = [mine] + [swap(mine, "tensor", 2 * s) for s in range(1, sides)]
        new, out = run(
            embed_norm_body,
            [Flow(half_sds), Flow(half_low)],
            [side_arg, placed, norm_rows] + parts,
            flops=10 * height * width,
            name="embed_norm",
        )
        return new, (out, swap_core(free(out)))

    def self_step(c, pair):
        own, got = pair
        *saved, keep, send, left, right, hidden[0][c] = run(
            self_forward_body,
            [full, full, full, full, lse_sds, flow, flow, Copy(1), Copy(3)],
            [core_arg, own, w_attn(0), got, w_attn(1), w_attn(2), w_attn(6)]
            + [Carry(hidden[0][c])],
            flops=8 * frames * width * columns + 4 * score_flops * frames,
            scratch=tot,
            name="self_forward",
        )
        pairs[0][c] = (left, right)
        reduce_rows(c, keep, send)
        return saved

    text_full = sds((clips * text_len, width), LOW)
    text_cols = sds((clips * text_len, columns), LOW)

    def text_step():
        return run(
            text_body,
            [text_full, text_cols, text_cols],
            [Scalar(place_order)] + text_parts + [w_attn(4), w_attn(5)],
            flops=4 * clips * text_len * width * columns,
            name="text",
        )

    def text_rows_of(array, c):
        return Window(
            array, (text_len, columns), lambda ref: ref.at[pl.ds(c * text_len, text_len), :]
        )

    def cross_step(c, pair):
        own, got = pair
        k, v = text_rows_of(text_key, c), text_rows_of(text_value, c)
        q, o, lse, keep, send, left, right, hidden[1][c] = run(
            cross_forward_body,
            [full, full, lse_sds, flow, flow, Copy(1), Copy(3)],
            [core_arg, own, w_attn(3), got, bias_lines[c], k, v, w_attn(7)]
            + [Carry(hidden[1][c])],
            flops=4 * frames * width * columns + 4 * score_flops * text_len,
            scratch=tot,
            name="cross_forward",
        )
        pairs[1][c] = (left, right)
        reduce_rows(c, keep, send)
        return (q, k, v, o, lse)

    def ffn_step(c, pair):
        *saved, keep, send, left, right, hidden[2][c] = run(
            ffn_forward_body,
            [inner, inner, flow, flow, Copy(1), Copy(2)],
            [core_arg, *pair, w_member(ffn_all, 0), w_member(ffn_all, 1), Carry(hidden[2][c])],
            flops=4 * frames * width * units,
            name="ffn_forward",
        )
        pairs[2][c] = (left, right)
        reduce_rows(c, keep, send)
        return saved

    hidden = [[None] * clips for _ in range(4)]
    pairs = [[None] * clips for _ in range(4)]
    kept = [[None] * clips for _ in range(3)]
    for c in every:
        hidden[0][c], pairs[0][c] = embed_step(c)
        flush()
        kept[0][c] = self_step(c, pairs[0][c])
        if c == 0:
            text_parts = text_in_step()
    text_hidden, text_key, text_value = text_step()
    for c in every:
        hidden[1][c], pairs[1][c] = norm_step(1, hidden[0][c], moving[c])
        flush()
        kept[1][c] = cross_step(c, pairs[1][c])
    for c in every:
        hidden[2][c], pairs[2][c] = norm_step(2, hidden[1][c], moving[c])
        flush()
        kept[2][c] = ffn_step(c, pairs[2][c])

    loss_part = [None] * clips
    sums = [[], [], [], []]

    def head_step(c, pair):
        own, got = pair
        logits, stats, left, right, hidden[3][c] = run(
            head_forward_body,
            [
                sds((frames, books * vocab), F32),
                Flow(sds((2 * books, frames), F32)),
                Copy(1),
                Copy(3),
            ],
            [core_arg, own, targets[c], got]
            + [w_member(head_all, k) for k in range(books)]
            + [Carry(hidden[3][c])],
            flops=2 * frames * width * books * vocab,
            scratch=tot,
            name="head_forward",
        )
        pairs[3][c] = (left, right)
        return logits, stats

    def merge_step(stats):
        mask = 1
        while mask < tensor:
            far = swap(free(stats), "tensor", mask)
            (stats,) = norm_rows_kernel(
                partial(merge_body, books),
                [sds((2 * books, frames), F32)],
                [stats, far],
                None,
                last,
                name="merge",
            )
            last[:] = [stats]
            mask *= 2
        return stats

    def head_back_step(c, logits, total):
        grad, keep, send, loss = run(
            head_backward_body,
            [sds((frames, books * vocab), LOW), flow, flow, Flow(sds((8, 128), F32))],
            [core_arg, total, grad_weight[c], targets[c], fetch(logits)]
            + [w_member(head_all, k) for k in range(books)],
            flops=2 * frames * width * books * vocab,
            scratch=tot,
            name="head_backward",
        )
        loss_part[c] = free(loss)[0, 0]
        reduce_rows(c, keep, send)
        return grad

    attn_shared = Shared((dp, 8 * share + text_share, columns), LOW)
    ffn_shared = Shared((dp,) + feedforward.shape, LOW)
    head_shared = Shared((dp, books, share, vocab), LOW)

    def attn_into(n):
        return Into(
            attn_shared,
            (dp, share, columns),
            lambda ref: ref.at[:, pl.ds(n * share, share), :],
        )

    def member_into(shared, n):
        return Into(shared, (dp,) + shared.full.shape[2:], lambda ref: ref.at[:, n])

    def weights(lefts, rights, outs, name):
        total = rights[0].shape[1]
        turn_left = 2 * total > width
        run(
            partial(weight_grad_body, clips, turn_left),
            outs,
            [core_arg] + [fetch(half) for pair in lefts for half in pair] + [fetch(a) for a in rights],
            flops=2 * clips * frames * width * total,
            scratch=[pltpu.VMEM((width if turn_left else total, clips * frames), LOW)],
            name=name,
            margin=26,
        )

    logit_grads = [None] * clips
    ready = [None] * clips
    for c in every:
        hidden[3][c], pairs[3][c] = norm_step(3, hidden[2][c], moving[c])
        flush()
        ready[c] = head_step(c, pairs[3][c])
        if c:
            flush()
            logits, stats = ready[c - 1]
            logit_grads[c - 1] = head_back_step(c - 1, logits, merge_step(stats))
    logits, stats = ready[-1]
    stats = merge_step(stats)
    flush()
    logit_grads[-1] = head_back_step(clips - 1, logits, stats)

    def ffn_back_step(c, pair):
        own, got = pair
        grad, keep, send, left, right, grads[c] = run(
            ffn_backward_body,
            [inner, flow, flow, Copy(1), Copy(2)],
            [core_arg, own, got, w_member(ffn_all, 1), fetch(kept[2][c][1]), w_member(ffn_all, 0)]
            + [Carry(grads[c])],
            flops=4 * frames * width * units,
            name="ffn_backward",
        )
        back_pairs[3][c] = (left, right)
        reduce_rows(c, keep, send)
        return grad

    grads = [None] * clips
    back_pairs = [[None] * clips for _ in range(4)]
    inner_grads = [None] * clips
    for c in every:
        grads[c], back_pairs[3][c], s = norm_back(3, hidden[3][c], moving[c], None)
        sums[3].append(s)
        flush()
        inner_grads[c] = ffn_back_step(c, back_pairs[3][c])
        if c == 0:
            head_into = [member_into(head_shared, k) for k in range(books)]
            weights(pairs[3], logit_grads, head_into, "head_weights")
    head_sum = lax.psum_scatter(free(head_shared.array), "dp", scatter_dimension=0, tiled=False)

    acc_text = [pltpu.VMEM((text_len, columns), F32)] * 2
    small = sds((text_len, columns), LOW)

    def cross_back_step(c, pair):
        own, got = pair
        q, k, v, o, lse = kept[1][c]
        bias = bias_columns[c]
        dq, dk, dv, keep, send, left, right, grads[c] = run(
            cross_backward_body,
            [full, small, small, flow, flow, Copy(1), Copy(3)],
            [core_arg, own, w_attn(7), got, bias, fetch(q), k, v, fetch(lse), w_attn(3)]
            + [Carry(grads[c])],
            flops=4 * frames * width * columns + 10 * score_flops * text_len,
            scratch=[pltpu.VMEM((frames, columns), LOW)] + acc_text,
            name="cross_backward",
        )
        back_pairs[2][c] = (left, right)
        reduce_rows(c, keep, send)
        return (dq, dk, dv)

    cross_grads = [None] * clips
    for c in every:
        grads[c], back_pairs[2][c], s = norm_back(2, hidden[2][c], moving[c], grads[c])
        sums[2].append(s)
        flush()
        cross_grads[c] = cross_back_step(c, back_pairs[2][c])
        if c == 0:
            weights(
                back_pairs[3], [k[0] for k in kept[2]], [member_into(ffn_shared, 1)], "ffn_two"
            )
        if c == min(1, clips - 1):
            weights(pairs[2], inner_grads, [member_into(ffn_shared, 0)], "ffn_one")
    ffn_sum = lax.psum_scatter(free(ffn_shared.array), "dp", scatter_dimension=0, tiled=False)

    def text_back_step():
        results = run(
            partial(text_back_body, clips),
            [Flow(text_cols)] * tensor + [attn_into(4), attn_into(5)],
            [Scalar(place_order)]
            + [fetch(g[1]) for g in cross_grads]
            + [fetch(g[2]) for g in cross_grads]
            + [w_attn(4), w_attn(5), fetch(text_hidden)],
            flops=8 * clips * text_len * width * columns,
            scratch=[pltpu.VMEM((clips * text_len, width), LOW)],
            name="text_back",
        )
        live = dict(enumerate(results))
        mask = 1
        while mask < tensor:
            fresh = {}
            for m in live:
                if not m & mask:
                    fresh[m] = (live[m], swap(free(live[m | mask]), "tensor", mask))
            mask *= 2
            if mask < tensor:
                for m, both in fresh.items():
                    (fresh[m],) = norm_rows_kernel(
                        add_body, [text_cols], list(both), None, last, name="add"
                    )
                    last[:] = [fresh[m]]
            live = fresh
        return live[0]

    acc_self = [pltpu.VMEM((frames, columns), F32)] * 2

    def self_back_step(c, pair):
        own, got = pair
        q, k, v, o, lse = kept[0][c]
        grad, keep, send, left, right, grads[c] = run(
            self_backward_body,
            [sds((frames, 3 * columns), LOW), flow, flow, Copy(1), Copy(3)],
            [core_arg, own, w_attn(6), got]
            + [fetch(a) for a in (q, k, v, lse)]
            + [w_attn(0), w_attn(1), w_attn(2), Carry(grads[c])],
            flops=8 * frames * width * columns + 10 * score_flops * frames,
            scratch=[pltpu.VMEM((frames, columns), LOW)] + acc_self,
            name="self_backward",
        )
        back_pairs[1][c] = (left, right)
        reduce_rows(c, keep, send)
        return grad

    self_grads = [None] * clips
    for c in every:
        grads[c], back_pairs[1][c], s = norm_back(1, hidden[1][c], moving[c], grads[c])
        sums[1].append(s)
        flush()
        self_grads[c] = self_back_step(c, back_pairs[1][c])
        if c == 0:
            text_grad = text_back_step()
            weights(back_pairs[2], [k[3] for k in kept[1]], [attn_into(7)], "cross_out")
        if c == min(1, clips - 1):
            weights(pairs[1], [g[0] for g in cross_grads], [attn_into(3)], "cross_query")

    zero_lows = [None] * clips

    def zero_step(c):
        _, (zero_lows[c], _), s = norm_back(0, hidden[0][c], moving[c], grads[c])
        sums[0].append(s)

    zero_step(0)
    flush()
    text_into = Into(
        attn_shared,
        (dp, text_share, columns),
        lambda ref: ref.at[:, pl.ds(8 * share, text_share), :],
    )
    (bias_grad,) = run(
        text_weight_body,
        [text_into, Flow(sds((8, columns), F32))],
        [fetch(text_rows), *text_grad],
        flops=2 * clips * text_len * text_width * columns,
        name="text_weight",
    )
    weights(back_pairs[1], [k[3] for k in kept[0]], [attn_into(6)], "self_out")
    weights(pairs[0], self_grads, [attn_into(n) for n in range(3)], "self_in")
    attn_sum = lax.psum_scatter(free(attn_shared.array), "dp", scatter_dimension=0, tiled=False)
    for c in range(1, clips):
        zero_step(c)

    if aligned:
        pieces = list(map(free, run(
            split_features_body,
            [Flow(sds((clips * strip, share), LOW))] * dp,
            [
                Scalar(group_order),
                Scalar(jnp.broadcast_to(side.astype(jnp.int32), (clips + 1,))),
            ]
            + zero_lows,
            name="split_features",
        )))
    else:
        rows = jnp.concatenate(
            [lax.dynamic_slice_in_dim(free(a), side * strip, strip, 0) for a in zero_lows], axis=0
        )
        rows = jnp.transpose(rows.reshape(clips * strip, dp, share), (1, 0, 2))
        pieces = list(jnp.take(rows, group_order, axis=0))
    rows_all = [pieces[0]] + [swap(pieces[m], "dp", m) for m in range(1, dp)]
    embed_parts = embed_back(vocab_base, back_lines, rows_all, vocab)
    grad_embed = collect_tensor([embed_parts[m] for m in range(tensor)])

    norm_part = jnp.concatenate(
        [sum(s)[0:1] for s in sums] + [sum(s)[1:2] for s in sums], axis=0
    ) * (1.0 / sides)
    bias_row = lax.dynamic_update_slice_in_dim(
        jnp.zeros((width,), F32), free(bias_grad)[0], place * columns, 0
    )
    norm_total = total_over(
        jnp.concatenate([norm_part, bias_row[None]], axis=0), ("tensor", "dp")
    )
    grad_norm_rows = lax.dynamic_slice_in_dim(norm_total, group * share, share, 1)

    grad_attention = attn_sum[: 8 * share].reshape(attention.shape).astype(F32)
    grad_text_proj = jnp.transpose(attn_sum[8 * share :]).astype(F32)
    grad_feedforward = ffn_sum.astype(F32)
    grad_heads = head_sum.astype(F32)
    local_square = (
        jnp.sum(grad_attention * grad_attention)
        + jnp.sum(grad_feedforward * grad_feedforward)
        + jnp.sum(grad_heads * grad_heads)
        + jnp.sum(grad_embed * grad_embed)
        + jnp.sum(grad_text_proj * grad_text_proj)
        + jnp.sum(grad_norm_rows * grad_norm_rows) / tensor
    )
    both = total_over(
        jnp.stack([local_square, sum(loss_part) / tensor]).reshape(1, 2), ("tensor", "dp")
    )[0]
    grad_norm = jnp.sqrt(both[0])
    mean_loss = both[1]
    factor = clip_limit / jnp.maximum(grad_norm, clip_limit)
    grad_tables = jnp.concatenate([grad_embed, grad_heads], 0)
    attn_new, attn_first_new, attn_second_new = adam_update(
        attention, grad_attention, attention_first, attention_second, rate_matrix, factor
    )
    ffn_new, ffn_first_new, ffn_second_new = adam_update(
        feedforward, grad_feedforward, feedforward_first, feedforward_second, rate_matrix, factor
    )
    table_new, table_first_new, table_second_new = adam_update(
        tables, grad_tables, tables_first, tables_second, rate_table, factor
    )
    text_new, text_first_new, text_second_new = adam_update(
        text_proj, grad_text_proj, text_first, text_second, rate_matrix, factor
    )
    norm_new, norm_first_new, norm_second_new = adam_update(
        norm_params, grad_norm_rows, norm_first, norm_second, rate_norm, factor
    )
    return (
        mean_loss,
        valid_count,
        grad_norm,
        attn_new,
        attn_new.astype(LOW),
        attn_first_new,
        attn_second_new,
        ffn_new,
        ffn_new.astype(LOW),
        ffn_first_new,
        ffn_second_new,
        table_new,
        table_new.astype(LOW),
        table_first_new,
        table_second_new,
        text_new,
        text_new.astype(LOW),
        text_first_new,
        text_second_new,
        norm_new,
        norm_first_new,
        norm_second_new,
    )


def solution(mesh):
    clip3 = P("dp", None, None)
    clip2 = P("dp", None)
    matrix = P(None, "dp", "tensor")
    text = P("tensor", "dp")
    norm = P(None, "dp")
    placed = (
        (clip3, clip3, clip2, clip3, clip2)
        + (matrix, matrix, matrix, text, norm)
        + (matrix,) * 6
        + (text, text, norm, norm)
    )
    return jax.shard_map(
        on_device,
        mesh=mesh,
        in_specs=placed,
        out_specs=(P(), P(), P()) + (matrix,) * 12 + (text,) * 4 + (norm,) * 3,
        check_vma=False,
    )
```

```python
from functools import partial
import math

import jax
import jax.numpy as jnp
from jax import lax
from jax.experimental import pallas as pl
from jax.experimental.pallas import tpu as pltpu
from jax.sharding import PartitionSpec as P

HEAD_DIM = 64
STEP = 5
BLOCK = 256
NEG = -1e30
LOW = jnp.bfloat16
F32 = jnp.float32

SMALL = pl.CostEstimate(flops=1024, bytes_accessed=1024, transcendentals=0)

PIECES = 2

clip_limit = 0.004
stability_offset = 1e-08
weight_decay = 0.01
moment_decay = 0.5
rate_matrix = 0.03
rate_table = 0.05
rate_norm = 0.2


def nn(a, b):
    return lax.dot_general(a, b, (((1,), (0,)), ((), ())), preferred_element_type=F32)


def nt(a, b):
    return lax.dot_general(a, b, (((1,), (1,)), ((), ())), preferred_element_type=F32)


def tn(a, b):
    return lax.dot_general(a, b, (((0,), (0,)), ((), ())), preferred_element_type=F32)


def sds(shape, kind):
    return jax.ShapeDtypeStruct(shape, kind)


def scalars():
    return pl.BlockSpec(memory_space=pltpu.SMEM)


def anywhere():
    return pl.BlockSpec(memory_space=pl.ANY)


def in_hbm():
    return pl.BlockSpec(memory_space=pltpu.HBM)


def in_vmem():
    return pl.BlockSpec(memory_space=pltpu.VMEM)


def whole(a):
    rank = len(a.shape)
    return pl.BlockSpec(a.shape, lambda i: (0,) * rank)


def later(body, count, at):
    def ordered(*refs):
        return body(*refs[:at], *refs[at + count :])

    return ordered


class Scalar:
    def __init__(self, array):
        self.array = array


class Window:
    def __init__(self, array, shape, pick):
        self.array, self.shape, self.pick = array, tuple(shape), pick


def hold(array, space):
    return pltpu.with_memory_space_constraint(array, space)


def free(array):
    return pltpu.with_memory_space_constraint(array, pl.ANY)


class Flow:
    def __init__(self, shape):
        self.shape = shape


class Copy:
    def __init__(self, i):
        self.i = i


class Carry:
    def __init__(self, array):
        self.array = array


class Shared:
    def __init__(self, shape, kind):
        self.full, self.array = sds(shape, kind), None


class Into:
    def __init__(self, shared, shape, pick):
        self.shared, self.shape, self.pick = shared, tuple(shape), pick


def everything(ref):
    return ref


def nbytes_of(shape, kind):
    return math.prod(shape) * jnp.dtype(kind).itemsize


def kernel(body, outs, operands, flops=0, scratch=(), name=None, exps=0, after=(), margin=12):
    arrays, specs, windows, shown = [], [], [], []
    outs = list(outs)
    for i, a in enumerate(operands):
        shown.append(not isinstance(a, Carry))
        if isinstance(a, Carry):
            arrays.append(hold(a.array, pltpu.VMEM))
            specs.append(in_vmem())
            windows.append(None)
            outs.append(Copy(i))
        elif isinstance(a, Scalar):
            arrays.append(a.array)
            specs.append(scalars())
            windows.append(None)
        elif isinstance(a, Window):
            arrays.append(hold(a.array, pltpu.HBM))
            specs.append(in_hbm())
            windows.append(a)
        else:
            arrays.append(hold(a, pltpu.VMEM))
            specs.append(in_vmem())
            windows.append(None)
    aliases, out_shapes, out_specs, out_parts, owners = {}, [], [], [], []
    extra = []
    for o in outs:
        if isinstance(o, Into):
            if o.shared not in owners:
                if o.shared.array is not None:
                    aliases[len(arrays) + len(extra)] = len(out_shapes)
                    extra.append(o.shared.array)
                out_shapes.append(pltpu.HBM(o.shared.full.shape, o.shared.full.dtype))
                out_specs.append(in_hbm())
                owners.append(o.shared)
            out_parts.append(("put", o.shape, o.shared.full.dtype, o.pick, owners.index(o.shared)))
            continue
        if isinstance(o, Flow):
            out_parts.append(("flow", None, None, None, len(out_shapes)))
            out_shapes.append(pltpu.VMEM(o.shape.shape, o.shape.dtype))
            out_specs.append(in_vmem())
        elif isinstance(o, Copy):
            a = arrays[o.i]
            out_parts.append(("copy", o.i, None, None, len(out_shapes)))
            out_shapes.append(pltpu.HBM(a.shape, a.dtype))
            out_specs.append(in_hbm())
        else:
            out_parts.append(("put", o.shape, o.dtype, everything, len(out_shapes)))
            out_shapes.append(pltpu.HBM(o.shape, o.dtype))
            out_specs.append(in_hbm())
        owners.append(None)
    moved = [w for w in windows if w is not None]
    made = [p for p in out_parts if p[0] == "put"]
    count_in, count_extra, count_after = len(arrays), len(extra), len(after)
    count_out, count_moved, count_arrays = len(outs), len(moved), len(out_shapes)

    def run_body(*refs):
        refs = list(refs)
        ins = refs[:count_in]
        at = count_in + count_extra + count_after
        out_refs = refs[at : at + count_arrays]
        at += count_arrays
        in_buffers = refs[at : at + count_moved]
        at += count_moved
        made_buffers = refs[at : at + len(made)]
        at += len(made)
        in_sems, out_sems = refs[at], refs[at + 1]
        rest = refs[at + 2 :]
        views, copies, waited = [], {}, set()
        n = 0
        for i, (ref, w) in enumerate(zip(ins, windows)):
            if not shown[i]:
                continue
            if w is None:
                views.append(ref)
            else:
                copies[i] = pltpu.make_async_copy(w.pick(ref), in_buffers[n], in_sems.at[n])
                copies[i].start()
                views.append(in_buffers[n])
                n += 1
        sent, sources = {}, {}

        def need(*which):
            for i in which:
                if i in copies and i not in waited:
                    waited.add(i)
                    copies[i].wait()

        def put(*which):
            for j in which:
                if j in sources:
                    source, target = sources[j]
                    sent[j] = pltpu.make_async_copy(source, target, out_sems.at[j])
                    sent[j].start()

        body_outs = []
        n = 0
        for j, (kind, what, _, pick, owner) in enumerate(out_parts):
            if kind == "put":
                sources[j] = (made_buffers[n], pick(out_refs[owner]))
                body_outs.append(made_buffers[n])
                n += 1
            elif kind == "copy":
                sources[j] = (ins[what], out_refs[owner])
                put(j)
            else:
                body_outs.append(out_refs[owner])
        body(need, put, *views, *body_outs, *rest)
        need(*copies)
        put(*(j for j in sources if j not in sent))
        for copy in sent.values():
            copy.wait()

    nbytes = sum(nbytes_of(w.shape, w.array.dtype) for w in moved)
    nbytes += sum(nbytes_of(p[1], p[2]) for p in made)
    held = nbytes + sum(nbytes_of(m.shape, m.dtype) for m in scratch)
    results = pl.pallas_call(
        run_body,
        out_shape=tuple(out_shapes),
        in_specs=specs + [anywhere()] * (count_extra + count_after),
        out_specs=tuple(out_specs),
        input_output_aliases=aliases,
        scratch_shapes=[pltpu.VMEM(w.shape, w.array.dtype) for w in moved]
        + [pltpu.VMEM(p[1], p[2]) for p in made]
        + [
            pltpu.SemaphoreType.DMA((max(1, count_moved),)),
            pltpu.SemaphoreType.DMA((max(1, count_out),)),
        ]
        + list(scratch),
        compiler_params=pltpu.CompilerParams(vmem_limit_bytes=held + (margin << 20)),
        cost_estimate=SMALL,
        name=name,
    )(*arrays, *extra, *after)
    for owner, result in zip(owners, results):
        if owner is not None:
            owner.array = result
    return [r for owner, r in zip(owners, results) if owner is None] or [results[-1]]


def flat(ref):
    w = ref[...]
    return w.reshape(-1, w.shape[-1])


def half_rows(core, height):
    return (
        pl.ds(pl.multiple_of(core * height, height), height),
        pl.ds(pl.multiple_of((1 - core) * height, height), height),
    )


def attend_block(query, keys, values, head_masks, diagonal, bias):
    rows, width = query.shape
    lane = lax.broadcasted_iota(jnp.int32, (rows, 128), 1)
    column = lax.broadcasted_iota(jnp.int32, (rows, width), 1) // HEAD_DIM
    mixed = jnp.zeros((rows, width), F32)
    totals = jnp.zeros((rows, 128), F32)
    count = keys.shape[0]
    for h, mask in enumerate(head_masks):
        s = nt(query * mask, keys)
        if diagonal is not None:
            last = jnp.where(diagonal, s[:, count - rows :], NEG)
            s = last if count == rows else jnp.concatenate([s[:, : count - rows], last], axis=1)
        if bias is not None:
            s = s + bias
        top = jnp.max(s, axis=1, keepdims=True)
        e = jnp.exp(s - top)
        total = jnp.sum(e, axis=1, keepdims=True)
        p = (e * (1.0 / total)).astype(LOW)
        mixed = jnp.where(column == h, nn(p, values), mixed)
        totals = jnp.where(lane == h, top + jnp.log(total), totals)
    return mixed, totals


def masks_of(width):
    head = lax.broadcasted_iota(jnp.int32, (1, width), 1) // HEAD_DIM
    return [(head == h).astype(F32).astype(LOW) for h in range(width // HEAD_DIM)]


def triangle(size):
    row = lax.broadcasted_iota(jnp.int32, (size, size), 0)
    col = lax.broadcasted_iota(jnp.int32, (size, size), 1)
    return row >= col


def self_forward_body(
    need, put, core_ref, own_ref, wq_ref, got_ref, wk_ref, wv_ref, wo_ref,
    q_ref, k_ref, v_ref, o_ref, lse_ref, keep_ref, send_ref, tot_ref,
):
    height = own_ref.shape[0]
    frames, width = q_ref.shape
    mine, other = half_rows(core_ref[0], height)
    need(1)
    for i, w_ref, to_ref in ((2, wq_ref, q_ref), (4, wk_ref, k_ref), (5, wv_ref, v_ref)):
        need(i)
        w = flat(w_ref)
        to_ref[mine, :] = nn(own_ref[...], w).astype(LOW)
        need(3)
        to_ref[other, :] = nn(got_ref[...], w).astype(LOW)
    put(0, 1, 2)
    scale = jnp.asarray(HEAD_DIM**-0.5, LOW)
    head_masks = masks_of(width)
    diagonal = triangle(BLOCK)
    for i in range(frames // BLOCK):
        rows = slice(i * BLOCK, (i + 1) * BLOCK)
        mixed, totals = attend_block(
            q_ref[rows, :] * scale,
            k_ref[: (i + 1) * BLOCK, :],
            v_ref[: (i + 1) * BLOCK, :],
            head_masks,
            diagonal,
            None,
        )
        o_ref[rows, :] = mixed.astype(LOW)
        tot_ref[rows, :] = totals
    put(3)
    need(6)
    wo = flat(wo_ref)
    send_ref[...] = nt(o_ref[other, :], wo).astype(LOW)
    put(6)
    keep_ref[...] = nt(o_ref[mine, :], wo).astype(LOW)
    put(5)
    lse_ref[...] = jnp.transpose(tot_ref[...])[:8, :]


def cross_forward_body(
    need, put, core_ref, own_ref, wq_ref, got_ref, bias_ref, k_ref, v_ref, wo_ref,
    q_ref, o_ref, lse_ref, keep_ref, send_ref, tot_ref,
):
    height = own_ref.shape[0]
    frames, width = q_ref.shape
    mine, other = half_rows(core_ref[0], height)
    need(1, 2)
    w = flat(wq_ref)
    q_ref[mine, :] = nn(own_ref[...], w).astype(LOW)
    need(3)
    q_ref[other, :] = nn(got_ref[...], w).astype(LOW)
    put(0)
    scale = jnp.asarray(HEAD_DIM**-0.5, LOW)
    head_masks = masks_of(width)
    need(4, 5, 6)
    for i in range(frames // BLOCK):
        rows = slice(i * BLOCK, (i + 1) * BLOCK)
        mixed, totals = attend_block(
            q_ref[rows, :] * scale, k_ref[...], v_ref[...], head_masks, None, bias_ref[...]
        )
        o_ref[rows, :] = mixed.astype(LOW)
        tot_ref[rows, :] = totals
    put(1)
    need(7)
    wo = flat(wo_ref)
    send_ref[...] = nt(o_ref[other, :], wo).astype(LOW)
    put(4)
    keep_ref[...] = nt(o_ref[mine, :], wo).astype(LOW)
    put(3)
    lse_ref[...] = jnp.transpose(tot_ref[...])[:8, :]


def ffn_forward_body(
    need, put, core_ref, own_ref, got_ref, w1_ref, w2_ref,
    act_ref, slope_ref, keep_ref, send_ref,
):
    height = own_ref.shape[0]
    mine, other = half_rows(core_ref[0], height)
    need(1, 2, 3)
    w1 = flat(w1_ref)
    for j, source, rows, to_ref in (
        (3, got_ref, other, send_ref),
        (2, own_ref, mine, keep_ref),
    ):
        u = nn(source[...], w1)
        phi = 0.5 * (1.0 + lax.erf(u * (2.0**-0.5)))
        act = (u * phi).astype(LOW)
        density = jnp.exp(-0.5 * u * u) * ((2.0 * math.pi) ** -0.5)
        act_ref[rows, :] = act
        slope_ref[rows, :] = (phi + u * density).astype(LOW)
        need(4)
        to_ref[...] = nt(act, flat(w2_ref)).astype(to_ref.dtype)
        put(j)


def head_forward_body(
    need, put, core_ref, own_ref, target_ref, got_ref, *refs
):
    *w_refs, logits_ref, stats_ref, tot_ref = refs
    height = own_ref.shape[0]
    books = len(w_refs)
    vocab = w_refs[0].shape[2]
    halves = half_rows(core_ref[0], height)
    lane = lax.broadcasted_iota(jnp.int32, (height, 128), 1)
    code = lax.broadcasted_iota(jnp.int32, (height, vocab), 1)
    need(1, 2)
    totals = [jnp.zeros((height, 128), F32)] * 2
    for k, w_ref in enumerate(w_refs):
        need(4 + k)
        w = flat(w_ref)
        for j, (source, rows) in enumerate(zip((own_ref, got_ref), halves)):
            need(1 + 2 * j)
            s = nn(source[...], w)
            logits_ref[rows, k * vocab : (k + 1) * vocab] = s
            top = jnp.max(s, axis=1, keepdims=True)
            total = jnp.sum(jnp.exp(s - top), axis=1, keepdims=True)
            hit = code == target_ref[rows, k : k + 1]
            pick = jnp.sum(jnp.where(hit, s, 0.0), axis=1, keepdims=True)
            totals[j] = jnp.where(lane == k, top + jnp.log(total), totals[j])
            totals[j] = jnp.where(lane == books + k, pick, totals[j])
    put(0)
    for rows, t in zip(halves, totals):
        tot_ref[rows, :] = t
    stats_ref[...] = jnp.transpose(tot_ref[...])[: 2 * books, :]


def head_backward_body(
    need, put, core_ref, total_ref, weight_ref, target_ref, logits_ref, *refs
):
    *w_refs, valid_ref, grad_ref, keep_ref, send_ref, loss_ref, col_ref = refs
    height = keep_ref.shape[0]
    books = len(w_refs)
    vocab = w_refs[0].shape[2]
    mine, other = half_rows(core_ref[0], height)
    frames = logits_ref.shape[0]
    need(1, 2, 3)
    wide = jnp.concatenate(
        [total_ref[...], jnp.zeros((128 - total_ref.shape[0], frames), F32)], axis=0
    )
    col_ref[...] = jnp.transpose(wide)
    share = 1.0 / valid_ref[0]
    gap = (col_ref[:, :books] - col_ref[:, books : 2 * books]) * (weight_ref[...] * share)
    loss_ref[...] = jnp.broadcast_to(jnp.sum(gap).reshape(1, 1), loss_ref.shape)
    code = lax.broadcasted_iota(jnp.int32, (height, vocab), 1)
    need(4)
    for j, rows, to_ref in ((2, other, send_ref), (1, mine, keep_ref)):
        weight = weight_ref[rows, :] * share
        total = col_ref[rows, :]
        acc = None
        for k, w_ref in enumerate(w_refs):
            s = logits_ref[rows, k * vocab : (k + 1) * vocab]
            p = jnp.exp(s - total[:, k : k + 1])
            hit = jnp.where(code == target_ref[rows, k : k + 1], 1.0, 0.0)
            g = ((p - hit) * weight[:, k : k + 1]).astype(LOW)
            grad_ref[rows, k * vocab : (k + 1) * vocab] = g
            need(5 + k)
            part = nt(g, flat(w_ref))
            acc = part if acc is None else acc + part
        to_ref[...] = acc.astype(to_ref.dtype)
        put(j)


def ffn_backward_body(
    need, put, core_ref, own_ref, got_ref, w2_ref, slope_ref, w1_ref,
    grad_ref, keep_ref, send_ref,
):
    height = own_ref.shape[0]
    mine, other = half_rows(core_ref[0], height)
    need(1, 2, 3, 4)
    w2 = flat(w2_ref)
    for j, source, rows, to_ref in (
        (2, got_ref, other, send_ref),
        (1, own_ref, mine, keep_ref),
    ):
        g = (nn(source[...], w2) * slope_ref[rows, :].astype(F32)).astype(LOW)
        grad_ref[rows, :] = g
        need(5)
        to_ref[...] = nt(g, flat(w1_ref)).astype(to_ref.dtype)
        put(j)


def attend_back(
    q, k, v, g, lse, head_masks, scale, diagonal, bias, dq_ref, rows, dk_ref, dv_ref, first
):
    count, width = k.shape
    step = q.shape[0]
    dq = jnp.zeros((step, width), F32)
    dk = jnp.zeros((count, width), F32)
    dv = jnp.zeros((count, width), F32)
    for h, mask in enumerate(head_masks):
        qm = q * mask
        gm = g * mask
        s = nt(k, qm)
        if diagonal is not None:
            last = jnp.where(diagonal, s[count - step :, :], NEG)
            s = last if count == step else jnp.concatenate([s[: count - step, :], last], axis=0)
        if bias is not None:
            s = s + bias
        p = jnp.exp(s - lse[h : h + 1, :])
        dp = nt(v, gm)
        inner = jnp.sum(p * dp, axis=0, keepdims=True)
        ds = (p * (dp - inner)).astype(LOW)
        dq = dq + tn(ds, k * mask)
        dk = dk + nn(ds, qm)
        dv = dv + nn(p.astype(LOW), gm)
    dq_ref[rows, :width] = (dq * scale).astype(LOW)
    dk_ref[:count, :] = dk if first else dk_ref[:count, :] + dk
    dv_ref[:count, :] = dv if first else dv_ref[:count, :] + dv


def self_backward_body(
    need, put, core_ref, own_ref, wo_ref, got_ref, q_ref, k_ref, v_ref, lse_ref,
    wq_ref, wk_ref, wv_ref, grad_ref, keep_ref, send_ref, g_ref, dk_acc, dv_acc,
):
    height = own_ref.shape[0]
    frames, width = q_ref.shape
    mine, other = half_rows(core_ref[0], height)
    need(1, 2)
    wo = flat(wo_ref)
    g_ref[mine, :] = nn(own_ref[...], wo).astype(LOW)
    need(3)
    g_ref[other, :] = nn(got_ref[...], wo).astype(LOW)
    scale = HEAD_DIM**-0.5
    head_masks = masks_of(width)
    row = lax.broadcasted_iota(jnp.int32, (BLOCK, BLOCK), 0)
    col = lax.broadcasted_iota(jnp.int32, (BLOCK, BLOCK), 1)
    diagonal = col >= row
    blocks = frames // BLOCK
    need(4, 5, 6, 7)
    for i in reversed(range(blocks)):
        rows = slice(i * BLOCK, (i + 1) * BLOCK)
        count = (i + 1) * BLOCK
        attend_back(
            q_ref[rows, :] * jnp.asarray(scale, LOW),
            k_ref[:count, :],
            v_ref[:count, :],
            g_ref[rows, :],
            lse_ref[:, rows],
            head_masks,
            scale,
            diagonal,
            None,
            grad_ref,
            rows,
            dk_acc,
            dv_acc,
            i == blocks - 1,
        )
    grad_ref[:, width : 2 * width] = dk_acc[...].astype(LOW)
    grad_ref[:, 2 * width :] = dv_acc[...].astype(LOW)
    put(0)
    need(8, 9, 10)
    for j, rows, to_ref in ((2, other, send_ref), (1, mine, keep_ref)):
        part = None
        for n, w_ref in enumerate((wq_ref, wk_ref, wv_ref)):
            term = nt(grad_ref[rows, n * width : (n + 1) * width], flat(w_ref))
            part = term if part is None else part + term
        to_ref[...] = part.astype(to_ref.dtype)
        put(j)


def cross_backward_body(
    need, put, core_ref, own_ref, wo_ref, got_ref, bias_ref, q_ref, k_ref, v_ref, lse_ref, wq_ref,
    dq_ref, dk_ref, dv_ref, keep_ref, send_ref, g_ref, dk_acc, dv_acc,
):
    height = own_ref.shape[0]
    frames, width = q_ref.shape
    mine, other = half_rows(core_ref[0], height)
    need(1, 2)
    wo = flat(wo_ref)
    g_ref[mine, :] = nn(own_ref[...], wo).astype(LOW)
    need(3)
    g_ref[other, :] = nn(got_ref[...], wo).astype(LOW)
    scale = HEAD_DIM**-0.5
    head_masks = masks_of(width)
    need(4, 5, 6, 7, 8)
    for i in range(frames // BLOCK):
        rows = slice(i * BLOCK, (i + 1) * BLOCK)
        attend_back(
            q_ref[rows, :] * jnp.asarray(scale, LOW),
            k_ref[...],
            v_ref[...],
            g_ref[rows, :],
            lse_ref[:, rows],
            head_masks,
            scale,
            None,
            bias_ref[...],
            dq_ref,
            rows,
            dk_acc,
            dv_acc,
            i == 0,
        )
    put(0)
    need(9)
    wq = flat(wq_ref)
    for j, rows, to_ref in ((4, other, send_ref), (3, mine, keep_ref)):
        to_ref[...] = nt(dq_ref[rows, :], wq).astype(to_ref.dtype)
        put(j)
    dk_ref[...] = dk_acc[...].astype(LOW)
    dv_ref[...] = dv_acc[...].astype(LOW)


def normalize(values, gain, shift):
    center = values - jnp.mean(values, axis=1, keepdims=True)
    spread = jnp.mean(center * center, axis=1, keepdims=True)
    return center * lax.rsqrt(spread + 1e-05) * gain + shift


def merge_body(books, own_ref, far_ref, out_ref):
    own, far = own_ref[:books, :], far_ref[:books, :]
    high = jnp.maximum(own, far)
    out_ref[:books, :] = high + jnp.log(jnp.exp(own - high) + jnp.exp(far - high))
    out_ref[books:, :] = own_ref[books:, :] + far_ref[books:, :]


def text_in_body(need, put, place_ref, norm_ref, rows_ref, w_ref, out_ref):
    columns = out_ref.shape[1]
    at = pl.ds(pl.multiple_of(place_ref[0] * columns, columns), columns)
    need(2, 3)
    out_ref[...] = (nn(rows_ref[...], flat(w_ref)) + norm_ref[8:9, at]).astype(LOW)


def add_body(keep_ref, got_ref, out_ref):
    out_ref[...] = (keep_ref[...].astype(F32) + got_ref[...].astype(F32)).astype(LOW)


def add_parts_body(keep_ref, got_ref, *out_refs):
    rows = out_refs[0].shape[0]
    for j, out_ref in enumerate(out_refs):
        at = slice(j * rows, (j + 1) * rows)
        out_ref[...] = (keep_ref[at, :].astype(F32) + got_ref[at, :].astype(F32)).astype(LOW)


def joined(refs):
    half = len(refs) // 2
    sums = [a[...].astype(F32) + b[...].astype(F32) for a, b in zip(refs[:half], refs[half:])]
    return jnp.concatenate(sums, axis=0)


def norm_body(which, hidden_ref, *refs):
    *part_refs, norm_ref, new_ref, out_ref = refs
    new = hidden_ref[...] + joined(part_refs)
    new_ref[...] = new
    out_ref[...] = normalize(
        new, norm_ref[which : which + 1, :], norm_ref[which + 4 : which + 5, :]
    ).astype(LOW)


def embed_norm_body(need, put, side_ref, place_ref, norm_ref, *refs):
    *part_refs, new_ref, out_ref = refs
    side = side_ref[0]
    rows = part_refs[0].shape[0]
    need(1, 2)
    for s, part in enumerate(part_refs):
        need(3 + s)
        at = pl.ds(pl.multiple_of((side ^ s) * rows, rows), rows)
        new = part[...].astype(F32) + place_ref[at, :]
        new_ref[at, :] = new
        out_ref[at, :] = normalize(new, norm_ref[0:1, :], norm_ref[4:5, :]).astype(LOW)
    put(1, 0)


def norm_back_body(which, parts, hidden_ref, *refs):
    *before, norm_ref, new_ref, low_ref, sums_ref = refs[parts:]
    values = hidden_ref[...]
    grad = joined(refs[:parts])
    gain = norm_ref[which : which + 1, :]
    center = values - jnp.mean(values, axis=1, keepdims=True)
    spread = jnp.mean(center * center, axis=1, keepdims=True)
    inverse = lax.rsqrt(spread + 1e-05)
    unit = center * inverse
    scaled = grad * gain
    first = jnp.mean(scaled, axis=1, keepdims=True)
    second = jnp.mean(scaled * unit, axis=1, keepdims=True)
    new = inverse * (scaled - first - unit * second)
    if before:
        new = before[0][...] + new
    new_ref[...] = new
    low_ref[...] = new.astype(LOW)
    sums_ref[...] = jnp.concatenate(
        [
            jnp.sum(grad * unit, axis=0, keepdims=True),
            jnp.sum(grad, axis=0, keepdims=True),
            jnp.zeros((6, values.shape[1]), F32),
        ],
        axis=0,
    )


def weight_grad_body(clips, turn_left, need, put, core_ref, *refs):
    lefts = refs[: 2 * clips]
    rights = refs[2 * clips : 3 * clips]
    outs = refs[3 * clips : -1]
    turned = refs[-1]
    height, width = lefts[0].shape
    frames = rights[0].shape[0]
    group = outs[0].shape[2]
    core = core_ref[0]

    def place(c, at):
        return pl.ds(pl.multiple_of(c * frames + at * height, 128), height)

    if turn_left:
        for m, out_ref in enumerate(outs):
            total = None
            for c in range(clips):
                if m == 0:
                    for j, at in ((0, core), (1, 1 - core)):
                        need(1 + 2 * c + j)
                        turned[:, place(c, at)] = jnp.transpose(lefts[2 * c + j][...])
                    need(1 + 2 * clips + c)
                part = nn(
                    turned[:, c * frames : (c + 1) * frames],
                    rights[c][:, m * group : (m + 1) * group],
                )
                total = part if total is None else total + part
            out_ref[...] = total.astype(LOW).reshape(out_ref.shape)
            put(m)
    else:
        total = None
        for c in range(clips):
            need(1 + 2 * clips + c)
            turned[:, c * frames : (c + 1) * frames] = jnp.transpose(rights[c][...])
            for j, at in ((0, core), (1, 1 - core)):
                need(1 + 2 * c + j)
                part = nn(turned[:, place(c, at)], lefts[2 * c + j][...])
                total = part if total is None else total + part
        for m, out_ref in enumerate(outs):
            member = total[m * group : (m + 1) * group, :]
            out_ref[...] = jnp.transpose(member).astype(LOW).reshape(out_ref.shape)
            put(m)


def norm_rows_kernel(body, outs, operands, norm_rows, after, name="norm"):
    height, width = operands[0].shape
    operands = list(operands) + ([] if norm_rows is None else [norm_rows])
    nbytes = sum(nbytes_of(a.shape, a.dtype) for a in operands + list(outs))
    return pl.pallas_call(
        later(body, len(after), len(operands)),
        out_shape=tuple(pltpu.VMEM(o.shape, o.dtype) for o in outs),
        in_specs=[in_vmem()] * len(operands) + [anywhere()] * len(after),
        out_specs=tuple(in_vmem() for _ in outs),
        compiler_params=pltpu.CompilerParams(vmem_limit_bytes=12 << 20),
        cost_estimate=SMALL,
        name=name,
    )(*(hold(a, pltpu.VMEM) for a in operands), *after)


def turned_codes(packet):
    lines = packet.astype(F32)
    wide = jnp.concatenate([lines, jnp.zeros((120, lines.shape[1]), F32)], axis=0)
    return jnp.transpose(wide)


def embed_body(count, books, base_ref, *refs):
    packets, tables, outs = refs[:count], refs[count : len(refs) - count], refs[len(refs) - count :]
    features, vocab = tables[0].shape[1:]
    rows = outs[0].shape[0]
    chunk = min(256, vocab)
    code = lax.broadcasted_iota(jnp.int32, (rows, chunk), 1).astype(F32)
    for packet, out_ref in zip(packets, outs):
        columns = turned_codes(packet[...])
        acc = jnp.zeros((rows, features), F32)
        for k in range(books):
            column = columns[:rows, k : k + 1]
            for b, table in enumerate(tables):
                local = column - base_ref[b].astype(F32)
                for v in range(0, vocab, chunk):
                    hit = jnp.where(code == local - float(v), 1.0, 0.0).astype(LOW)
                    acc = acc + nt(hit, table[k, :, v : v + chunk])
        out_ref[...] = acc.astype(LOW)


def embed(base, packets, tables, rows, after):
    books, features = tables[0].shape[:2]
    count = len(packets)
    return pl.pallas_call(
        later(partial(embed_body, count, books), len(after), 1 + count + len(tables)),
        out_shape=[sds((rows, features), LOW)] * count,
        in_specs=[scalars()]
        + [in_vmem()] * (count + len(tables))
        + [anywhere()] * len(after),
        out_specs=[in_vmem()] * count,
        compiler_params=pltpu.CompilerParams(vmem_limit_bytes=16 << 20),
        cost_estimate=SMALL,
        name="embed",
    )(base, *packets, *tables, *after)


def embed_back_body(groups, base_ref, *refs):
    packets, grads = refs[:groups], refs[groups : 2 * groups]
    out_ref, all_ref = refs[-2:]
    rows, features = grads[0].shape
    padded = packets[0].shape[1]
    vocab = out_ref.shape[3]
    chunk = min(256, vocab)
    book = pl.program_id(1)

    @pl.when((pl.program_id(0) == 0) & (book == 0))
    def _():
        for j, g in enumerate(grads):
            all_ref[j * padded : j * padded + rows, :] = g[...]
            if padded > rows:
                all_ref[j * padded + rows : (j + 1) * padded, :] = jnp.zeros(
                    (padded - rows, features), LOW
                )

    base = base_ref[pl.program_id(0)]
    line = jnp.concatenate([p[pl.ds(book, 1), :] for p in packets], axis=1)
    code = lax.broadcasted_iota(jnp.int32, (chunk, line.shape[1]), 0)
    for v in range(0, vocab, chunk):
        hit = jnp.where(code == line - (base + v), 1.0, 0.0).astype(LOW)
        out_ref[0, 0, :, v : v + chunk] = jnp.transpose(nn(hit, all_ref[...])).astype(LOW)


def embed_back(base, packets, grads, books, vocab, after):
    parts = base.shape[0]
    groups = len(packets)
    features = grads[0].shape[1]
    return pl.pallas_call(
        later(partial(embed_back_body, groups), len(after), 1 + 2 * groups),
        out_shape=sds((parts, books, features, vocab), LOW),
        grid=(parts, books),
        in_specs=[scalars()] + [in_vmem()] * (2 * groups) + [anywhere()] * len(after),
        out_specs=pl.BlockSpec((1, 1, features, vocab), lambda i, k: (i, k, 0, 0)),
        scratch_shapes=[pltpu.VMEM((groups * packets[0].shape[1], features), LOW)],
        compiler_params=pltpu.CompilerParams(vmem_limit_bytes=24 << 20),
        cost_estimate=SMALL,
        name="embed_back",
    )(base, *packets, *grads, *after)


def gather_features_body(need, put, where_ref, *refs):
    clips = sum(r.shape[1] != refs[0].shape[1] for r in refs)
    part_refs, outs = refs[:-clips], refs[-clips:]
    features = part_refs[0].shape[1]
    strip = outs[0].shape[0]
    for m, part in enumerate(part_refs):
        at = pl.ds(pl.multiple_of(where_ref[m] * features, features), features)
        for c, out_ref in enumerate(outs):
            out_ref[:, at] = part[c * strip : (c + 1) * strip, :]


def split_features_body(need, put, where_ref, side_ref, *refs):
    clips = side_ref.shape[0] - 1
    grads, outs = refs[:clips], refs[clips:]
    features = outs[0].shape[1]
    rows = outs[0].shape[0] // clips
    at_rows = pl.ds(pl.multiple_of(side_ref[0] * rows, rows), rows)
    need(*range(2, 2 + clips))
    for m, out_ref in reversed(list(enumerate(outs))):
        at = pl.ds(pl.multiple_of(where_ref[m] * features, features), features)
        for c in range(clips):
            out_ref[c * rows : (c + 1) * rows, :] = grads[c][at_rows, at]
        put(m)


def text_body(need, put, where_ref, *refs):
    *part_refs, wk_ref, wv_ref, tp_ref, k_ref, v_ref = refs
    columns = part_refs[0].shape[1]
    for m, part in enumerate(part_refs):
        need(1 + m)
        at = pl.ds(pl.multiple_of(where_ref[m] * columns, columns), columns)
        tp_ref[:, at] = part[...]
    put(0)
    for j, w_ref, to_ref in ((1, wk_ref, k_ref), (2, wv_ref, v_ref)):
        need(len(part_refs) + j)
        to_ref[...] = nn(tp_ref[...], flat(w_ref)).astype(LOW)
        put(j)


def text_back_body(clips, need, put, where_ref, *refs):
    dks, dvs = refs[:clips], refs[clips : 2 * clips]
    wk_ref, wv_ref, tp_ref = refs[2 * clips : 2 * clips + 3]
    *part_refs, gk_ref, gv_ref, full_ref = refs[2 * clips + 3 :]
    columns = part_refs[0].shape[1]
    length = dks[0].shape[0]
    need(*range(1, 1 + 2 * clips + 2))
    wk, wv = flat(wk_ref), flat(wv_ref)
    for c in range(clips):
        tp_rows = slice(c * length, (c + 1) * length)
        full_ref[tp_rows, :] = (nt(dks[c][...], wk) + nt(dvs[c][...], wv)).astype(LOW)
    for m, part_ref in enumerate(part_refs):
        at = pl.ds(pl.multiple_of(where_ref[m] * columns, columns), columns)
        part_ref[...] = full_ref[:, at]
    put(*range(len(part_refs)))
    need(3 + 2 * clips)
    turned = jnp.transpose(tp_ref[...])
    for j, grads, to_ref in ((0, dks, gk_ref), (1, dvs, gv_ref)):
        total = None
        for c in range(clips):
            part = nn(turned[:, c * length : (c + 1) * length], grads[c][...])
            total = part if total is None else total + part
        to_ref[...] = total.astype(LOW).reshape(to_ref.shape)
        put(len(part_refs) + j)


def text_weight_body(need, put, rows_ref, own_ref, far_ref, out_ref, bias_ref):
    need(0)
    grad = (own_ref[...].astype(F32) + far_ref[...].astype(F32)).astype(LOW)
    out_ref[...] = tn(rows_ref[...], grad).astype(LOW).reshape(out_ref.shape)
    bias_ref[...] = jnp.broadcast_to(
        jnp.sum(grad.astype(F32), axis=0, keepdims=True), bias_ref.shape
    )


def positions_rows(start, count, feature_count):
    half_width = feature_count // 2
    frequency = jnp.exp(
        jnp.arange(half_width, dtype=F32) * (-math.log(10000.0) / (half_width - 1))
    )
    angles = (start + jnp.arange(count, dtype=jnp.int32)).astype(F32)[:, None] * frequency[None, :]
    return jnp.concatenate([jnp.cos(angles), jnp.sin(angles)], axis=1)


def adam_update(weight, gradient, first_moment, second_moment, step_rate, factor):
    clipped = gradient * factor
    new_first = moment_decay * first_moment + (1.0 - moment_decay) * clipped
    new_second = moment_decay * second_moment + (1.0 - moment_decay) * clipped * clipped
    first_hat = new_first / (1.0 - moment_decay**STEP)
    second_hat = new_second / (1.0 - moment_decay**STEP)
    new_weight = weight * (1.0 - step_rate * weight_decay) - step_rate * first_hat / (
        jnp.sqrt(second_hat) + stability_offset
    )
    return (new_weight, new_first, new_second)


def swap(values, axis, mask):
    size = lax.axis_size(axis)
    return lax.ppermute(values, axis, [(i, i ^ mask) for i in range(size)])


def on_device(
    audio_codes,
    delay_mask,
    frame_mask,
    text_states,
    text_mask,
    attention,
    feedforward,
    tables,
    text_proj,
    norm_params,
    attention_first,
    attention_second,
    feedforward_first,
    feedforward_second,
    tables_first,
    tables_second,
    text_first,
    text_second,
    norm_first,
    norm_second,
):
    clips, frames, books = audio_codes.shape
    text_len, text_width = text_states.shape[1:]
    dp = lax.axis_size("dp")
    tensor = lax.axis_size("tensor")
    group = lax.axis_index("dp")
    place = lax.axis_index("tensor")
    core = place & 1
    side = place >> 1
    sides = tensor // 2
    height = frames // 2
    strip = height // sides
    share = attention.shape[1]
    columns = attention.shape[2]
    width = share * dp
    vocab = tables.shape[2]
    text_share = text_proj.shape[1]
    core_arg = Scalar(core.astype(jnp.int32).reshape(1))
    side_arg = Scalar(side.astype(jnp.int32).reshape(1))
    swap_core = partial(swap, axis="tensor", mask=1)

    def spread_tensor(values):
        held = [values]
        mask = tensor // 2
        order = [0]
        while mask:
            held = held + [swap(v, "tensor", mask) for v in held]
            order = order + [o | mask for o in order]
            mask //= 2
        return [v for _, v in sorted(zip(order, held), key=lambda t: t[0])]

    def collect_tensor(parts):
        mask = 1
        live = {m: p for m, p in enumerate(parts)}
        while mask < tensor:
            fresh = {}
            for m in live:
                if not m & mask:
                    got = swap(live[m | mask].astype(LOW), "tensor", mask)
                    fresh[m] = live[m].astype(F32) + got.astype(F32)
            live = fresh
            mask *= 2
        return live[0]

    def across(values):
        own = values
        mask = 2
        rest = None
        while mask < tensor:
            got = swap(own, "tensor", mask)
            mask *= 2
            if mask < tensor:
                own = (own.astype(F32) + got.astype(F32)).astype(LOW)
            rest = got
        if rest is None:
            rest = jnp.zeros_like(own)
        return own, rest

    def total_over(values, axes):
        for axis in axes:
            mask = 1
            while mask < lax.axis_size(axis):
                values = values + swap(values, axis, mask)
                mask *= 2
        return values

    last = []

    def run(body, outs, operands, **rest):
        shared = [o.shared.array for o in outs if isinstance(o, Into)]
        wait_for = [a for a in last if not any(a is b for b in shared)]
        results = kernel(body, outs, operands, after=wait_for, **rest)
        last[:] = [results[-1]]
        return results

    norm_pad = jnp.pad(norm_params.astype(LOW), ((0, 16 - norm_params.shape[0]), (0, columns - share)))
    attn_flat = jnp.concatenate(
        [attention.astype(LOW).reshape(-1, columns), text_proj.astype(LOW).T, norm_pad], axis=0
    )
    attn_all = lax.all_gather(attn_flat, "dp", axis=0)
    ffn_all = lax.all_gather(feedforward.astype(LOW), "dp", axis=0)
    head_all = lax.all_gather(tables[books:].astype(LOW), "dp", axis=0)

    frame_live = (jnp.arange(frames, dtype=jnp.int32) < frames - 1).astype(jnp.int32)
    weight_int = delay_mask * frame_mask[:, :, None] * frame_live[None, :, None]
    start = core * height + side * strip
    strip_codes = lax.dynamic_slice_in_dim(audio_codes, start, strip, 1)
    count = clips * strip
    padded = -(-count // 128) * 128
    lines = jnp.transpose(strip_codes, (2, 0, 1)).reshape(books, count)
    lines = jnp.pad(lines, ((0, 0), (0, padded - count)), constant_values=-1)
    count_line = jnp.broadcast_to(jnp.sum(weight_int), (8 - books, padded))
    packet = jnp.concatenate([lines, count_line], axis=0)
    packets = [packet] + [swap(packet, "dp", m) for m in range(1, dp)]
    valid_count = sum(p[books, 0] for p in packets).astype(F32)
    vocab_base = (place ^ jnp.arange(tensor, dtype=jnp.int32)) * vocab
    group_order = group ^ jnp.arange(dp, dtype=jnp.int32)
    place_order = place ^ jnp.arange(tensor, dtype=jnp.int32)

    text_bias_row = jnp.where(text_mask > 0, 0.0, NEG).astype(F32)
    bias_lines = [text_bias_row[c : c + 1] for c in range(clips)]
    bias_columns = [jnp.transpose(line) for line in bias_lines]
    targets = (jnp.roll(audio_codes, -1, axis=1) - place * vocab).astype(jnp.int32)
    targets = [targets[c] for c in range(clips)]
    valid_arg = Scalar(valid_count.reshape(1))
    loss_weight = [weight_int[c].astype(F32) for c in range(clips)]
    placed = positions_rows(core * height, height, width)

    table_parts = spread_tensor(tables[:books].astype(LOW))
    step = max(1, dp // 4)
    arrived = [None] * dp
    for low_end in reversed(range(0, dp, step)):
        embedded = embed(
            vocab_base, packets[low_end : low_end + step], table_parts, count, list(last)
        )
        last[:] = [embedded[-1]]
        for m, piece in enumerate(embedded, low_end):
            arrived[m] = swap(piece, "dp", m) if m else piece
        last += [a for a in arrived[low_end + step : low_end + 2 * step] if a is not None]
    last += bias_lines + bias_columns + targets + loss_weight + [placed]
    aligned = share % 128 == 0
    if aligned:
        strips = run(
            gather_features_body,
            [Flow(sds((strip, width), LOW))] * clips,
            [Scalar(group_order)] + arrived,
            name="gather_features",
        )
        strips = [free(a) for a in strips]
    else:
        strips = jnp.take(jnp.stack(arrived), group_order, axis=0)
        strips = jnp.transpose(strips, (1, 0, 2)).reshape(clips, strip, width)

    norm_rows = attn_all[:, 8 * share + text_share :, :share]
    norm_rows = jnp.transpose(norm_rows, (1, 0, 2)).reshape(16, width).astype(F32)

    def w_attn(n):
        return Window(
            attn_all, (dp, share, columns), lambda ref: ref.at[:, pl.ds(n * share, share), :]
        )

    def w_member(array, n):
        return Window(array, (dp,) + array.shape[2:], lambda ref: ref.at[:, n])

    half_sds = sds((height, width), F32)
    half_low = sds((height, width), LOW)
    flow = Flow(half_low)

    def fetch(a):
        return Window(a, a.shape, everything)


    def norm_step(which, hidden, parts):
        new, out = norm_rows_kernel(
            partial(norm_body, which),
            [half_sds, half_low],
            [hidden, *parts],
            norm_rows,
            last + soon,
        )
        soon[:] = []
        last[:] = [out]
        return new, (out, swap_core(free(out)))

    def norm_back(which, hidden, parts, before):
        operands = [hidden, *parts] + ([before] if before is not None else [])
        new, out, sums = norm_rows_kernel(
            partial(norm_back_body, which, len(parts)),
            [half_sds, half_low, sds((8, width), F32)],
            operands,
            norm_rows,
            last + soon,
        )
        soon[:] = []
        last[:] = [out]
        return new, (out, swap_core(free(out))), free(sums)

    waiting, soon = [], []
    moving = [None] * clips

    def flush():
        if waiting:
            c, keep, got = waiting.pop()
            parts = norm_rows_kernel(
                add_parts_body,
                [sds((height // PIECES, width), LOW)] * PIECES,
                [keep, got],
                None,
                last,
                name="add",
            )
            last[:] = [parts[-1]]
            fars = [across(free(part))[1] for part in parts]
            moving[c] = (*parts, *fars)
            soon[:] = fars[:-1]

    def reduce_rows(c, keep, send):
        waiting.append((c, keep, swap_core(free(send))))

    text_rows = text_states.reshape(clips * text_len, text_width)
    def text_in_step():
        (result,) = run(
            text_in_body,
            [Flow(sds((clips * text_len, columns), LOW))],
            [
                Scalar(place.astype(jnp.int32).reshape(1)),
                norm_rows,
                fetch(text_rows),
                Window(
                    attn_all,
                    (dp, text_share, columns),
                    lambda ref: ref.at[:, pl.ds(8 * share, text_share), :],
                ),
            ],
            flops=2 * clips * text_len * text_width * columns,
            name="text_in",
        )
        return spread_tensor(free(result))

    full = sds((frames, columns), LOW)
    lse_sds = sds((8, frames), F32)
    tot = [pltpu.VMEM((frames, 128), F32)]
    heads = columns // HEAD_DIM
    score_flops = 2 * heads * frames * HEAD_DIM
    units = feedforward.shape[2]
    inner = sds((frames, units), LOW)
    every = range(clips)

    def embed_step(c):
        mine = strips[c]
        parts = [mine] + [swap(mine, "tensor", 2 * s) for s in range(1, sides)]
        new, out = run(
            embed_norm_body,
            [Flow(half_sds), Flow(half_low)],
            [side_arg, placed, norm_rows] + parts,
            flops=10 * height * width,
            name="embed_norm",
        )
        return new, (out, swap_core(free(out)))

    def self_step(c, pair):
        own, got = pair
        *saved, keep, send, left, right, hidden[0][c] = run(
            self_forward_body,
            [full, full, full, full, lse_sds, flow, flow, Copy(1), Copy(3)],
            [core_arg, own, w_attn(0), got, w_attn(1), w_attn(2), w_attn(6)]
            + [Carry(hidden[0][c])],
            flops=8 * frames * width * columns + 4 * score_flops * frames,
            scratch=tot,
            name="self_forward",
        )
        pairs[0][c] = (left, right)
        reduce_rows(c, keep, send)
        return saved

    text_full = sds((clips * text_len, width), LOW)
    text_cols = sds((clips * text_len, columns), LOW)

    def text_step():
        return run(
            text_body,
            [text_full, text_cols, text_cols],
            [Scalar(place_order)] + text_parts + [w_attn(4), w_attn(5)],
            flops=4 * clips * text_len * width * columns,
            name="text",
        )

    def text_rows_of(array, c):
        return Window(
            array, (text_len, columns), lambda ref: ref.at[pl.ds(c * text_len, text_len), :]
        )

    def cross_step(c, pair):
        own, got = pair
        k, v = text_rows_of(text_key, c), text_rows_of(text_value, c)
        q, o, lse, keep, send, left, right, hidden[1][c] = run(
            cross_forward_body,
            [full, full, lse_sds, flow, flow, Copy(1), Copy(3)],
            [core_arg, own, w_attn(3), got, bias_lines[c], k, v, w_attn(7)]
            + [Carry(hidden[1][c])],
            flops=4 * frames * width * columns + 4 * score_flops * text_len,
            scratch=tot,
            name="cross_forward",
        )
        pairs[1][c] = (left, right)
        reduce_rows(c, keep, send)
        return (q, k, v, o, lse)

    def ffn_step(c, pair):
        *saved, keep, send, left, right, hidden[2][c] = run(
            ffn_forward_body,
            [inner, inner, flow, flow, Copy(1), Copy(2)],
            [core_arg, *pair, w_member(ffn_all, 0), w_member(ffn_all, 1), Carry(hidden[2][c])],
            flops=4 * frames * width * units,
            name="ffn_forward",
        )
        pairs[2][c] = (left, right)
        reduce_rows(c, keep, send)
        return saved

    hidden = [[None] * clips for _ in range(4)]
    pairs = [[None] * clips for _ in range(4)]
    kept = [[None] * clips for _ in range(3)]
    for c in every:
        hidden[0][c], pairs[0][c] = embed_step(c)
        flush()
        kept[0][c] = self_step(c, pairs[0][c])
        if c == 0:
            text_parts = text_in_step()
    text_hidden, text_key, text_value = text_step()
    for c in every:
        hidden[1][c], pairs[1][c] = norm_step(1, hidden[0][c], moving[c])
        flush()
        kept[1][c] = cross_step(c, pairs[1][c])
    for c in every:
        hidden[2][c], pairs[2][c] = norm_step(2, hidden[1][c], moving[c])
        flush()
        kept[2][c] = ffn_step(c, pairs[2][c])

    loss_part = [None] * clips
    sums = [[], [], [], []]

    def head_step(c, pair):
        own, got = pair
        logits, stats, left, right, hidden[3][c] = run(
            head_forward_body,
            [
                sds((frames, books * vocab), F32),
                Flow(sds((2 * books, frames), F32)),
                Copy(1),
                Copy(3),
            ],
            [core_arg, own, targets[c], got]
            + [w_member(head_all, k) for k in range(books)]
            + [Carry(hidden[3][c])],
            flops=2 * frames * width * books * vocab,
            scratch=tot,
            name="head_forward",
        )
        pairs[3][c] = (left, right)
        return logits, stats

    def merge_step(stats):
        mask = 1
        while mask < tensor:
            far = swap(free(stats), "tensor", mask)
            (stats,) = norm_rows_kernel(
                partial(merge_body, books),
                [sds((2 * books, frames), F32)],
                [stats, far],
                None,
                last,
                name="merge",
            )
            last[:] = [stats]
            mask *= 2
        return stats

    def head_back_step(c, logits, stats):
        grad, keep, send, loss = run(
            head_backward_body,
            [sds((frames, books * vocab), LOW), flow, flow, Flow(sds((8, 128), F32))],
            [core_arg, stats, loss_weight[c], targets[c], fetch(logits)]
            + [w_member(head_all, k) for k in range(books)]
            + [valid_arg],
            flops=2 * frames * width * books * vocab,
            scratch=tot,
            name="head_backward",
        )
        loss_part[c] = free(loss)[0, 0]
        reduce_rows(c, keep, send)
        return grad

    attn_shared = Shared((dp, 8 * share + text_share, columns), LOW)
    ffn_shared = Shared((dp,) + feedforward.shape, LOW)
    head_shared = Shared((dp, books, share, vocab), LOW)

    def attn_into(n):
        return Into(
            attn_shared,
            (dp, share, columns),
            lambda ref: ref.at[:, pl.ds(n * share, share), :],
        )

    def member_into(shared, n):
        return Into(shared, (dp,) + shared.full.shape[2:], lambda ref: ref.at[:, n])

    def weights(lefts, rights, outs, name):
        total = rights[0].shape[1]
        turn_left = 2 * total > width
        run(
            partial(weight_grad_body, clips, turn_left),
            outs,
            [core_arg] + [fetch(half) for pair in lefts for half in pair] + [fetch(a) for a in rights],
            flops=2 * clips * frames * width * total,
            scratch=[pltpu.VMEM((width if turn_left else total, clips * frames), LOW)],
            name=name,
            margin=26,
        )

    logit_grads = [None] * clips
    ready = [None] * clips
    for c in every:
        hidden[3][c], pairs[3][c] = norm_step(3, hidden[2][c], moving[c])
        flush()
        ready[c] = head_step(c, pairs[3][c])
        if c:
            flush()
            logits, stats = ready[c - 1]
            logit_grads[c - 1] = head_back_step(c - 1, logits, merge_step(stats))
    logits, stats = ready[-1]
    stats = merge_step(stats)
    flush()
    logit_grads[-1] = head_back_step(clips - 1, logits, stats)

    def ffn_back_step(c, pair):
        own, got = pair
        grad, keep, send, left, right, grads[c] = run(
            ffn_backward_body,
            [inner, flow, flow, Copy(1), Copy(2)],
            [core_arg, own, got, w_member(ffn_all, 1), fetch(kept[2][c][1]), w_member(ffn_all, 0)]
            + [Carry(grads[c])],
            flops=4 * frames * width * units,
            name="ffn_backward",
        )
        back_pairs[3][c] = (left, right)
        reduce_rows(c, keep, send)
        return grad

    grads = [None] * clips
    back_pairs = [[None] * clips for _ in range(4)]
    inner_grads = [None] * clips
    for c in every:
        grads[c], back_pairs[3][c], s = norm_back(3, hidden[3][c], moving[c], None)
        sums[3].append(s)
        flush()
        inner_grads[c] = ffn_back_step(c, back_pairs[3][c])
        if c == 0:
            head_into = [member_into(head_shared, k) for k in range(books)]
            weights(pairs[3], logit_grads, head_into, "head_weights")
    head_sum = lax.psum_scatter(free(head_shared.array), "dp", scatter_dimension=0, tiled=False)

    acc_text = [pltpu.VMEM((text_len, columns), F32)] * 2
    small = sds((text_len, columns), LOW)

    def cross_back_step(c, pair):
        own, got = pair
        q, k, v, o, lse = kept[1][c]
        bias = bias_columns[c]
        dq, dk, dv, keep, send, left, right, grads[c] = run(
            cross_backward_body,
            [full, small, small, flow, flow, Copy(1), Copy(3)],
            [core_arg, own, w_attn(7), got, bias, fetch(q), k, v, fetch(lse), w_attn(3)]
            + [Carry(grads[c])],
            flops=4 * frames * width * columns + 10 * score_flops * text_len,
            scratch=[pltpu.VMEM((frames, columns), LOW)] + acc_text,
            name="cross_backward",
        )
        back_pairs[2][c] = (left, right)
        reduce_rows(c, keep, send)
        return (dq, dk, dv)

    cross_grads = [None] * clips
    for c in every:
        grads[c], back_pairs[2][c], s = norm_back(2, hidden[2][c], moving[c], grads[c])
        sums[2].append(s)
        flush()
        cross_grads[c] = cross_back_step(c, back_pairs[2][c])
        if c == 0:
            weights(
                back_pairs[3], [k[0] for k in kept[2]], [member_into(ffn_shared, 1)], "ffn_two"
            )
        if c == min(1, clips - 1):
            weights(pairs[2], inner_grads, [member_into(ffn_shared, 0)], "ffn_one")
    ffn_sum = lax.psum_scatter(free(ffn_shared.array), "dp", scatter_dimension=0, tiled=False)

    def text_back_step():
        results = run(
            partial(text_back_body, clips),
            [Flow(text_cols)] * tensor + [attn_into(4), attn_into(5)],
            [Scalar(place_order)]
            + [fetch(g[1]) for g in cross_grads]
            + [fetch(g[2]) for g in cross_grads]
            + [w_attn(4), w_attn(5), fetch(text_hidden)],
            flops=8 * clips * text_len * width * columns,
            scratch=[pltpu.VMEM((clips * text_len, width), LOW)],
            name="text_back",
        )
        live = dict(enumerate(results))
        mask = 1
        while mask < tensor:
            fresh = {}
            for m in live:
                if not m & mask:
                    fresh[m] = (live[m], swap(free(live[m | mask]), "tensor", mask))
            mask *= 2
            if mask < tensor:
                for m, both in fresh.items():
                    (fresh[m],) = norm_rows_kernel(
                        add_body, [text_cols], list(both), None, last, name="add"
                    )
                    last[:] = [fresh[m]]
            live = fresh
        return live[0]

    acc_self = [pltpu.VMEM((frames, columns), F32)] * 2

    def self_back_step(c, pair):
        own, got = pair
        q, k, v, o, lse = kept[0][c]
        grad, keep, send, left, right, grads[c] = run(
            self_backward_body,
            [sds((frames, 3 * columns), LOW), flow, flow, Copy(1), Copy(3)],
            [core_arg, own, w_attn(6), got]
            + [fetch(a) for a in (q, k, v, lse)]
            + [w_attn(0), w_attn(1), w_attn(2), Carry(grads[c])],
            flops=8 * frames * width * columns + 10 * score_flops * frames,
            scratch=[pltpu.VMEM((frames, columns), LOW)] + acc_self,
            name="self_backward",
        )
        back_pairs[1][c] = (left, right)
        reduce_rows(c, keep, send)
        return grad

    self_grads = [None] * clips
    for c in every:
        grads[c], back_pairs[1][c], s = norm_back(1, hidden[1][c], moving[c], grads[c])
        sums[1].append(s)
        flush()
        self_grads[c] = self_back_step(c, back_pairs[1][c])
        if c == 0:
            text_grad = text_back_step()
            weights(back_pairs[2], [k[3] for k in kept[1]], [attn_into(7)], "cross_out")
        if c == min(1, clips - 1):
            weights(pairs[1], [g[0] for g in cross_grads], [attn_into(3)], "cross_query")

    zero_lows = [None] * clips

    def zero_step(c):
        _, (zero_lows[c], _), s = norm_back(0, hidden[0][c], moving[c], grads[c])
        sums[0].append(s)

    zero_step(0)
    flush()
    text_into = Into(
        attn_shared,
        (dp, text_share, columns),
        lambda ref: ref.at[:, pl.ds(8 * share, text_share), :],
    )
    (bias_grad,) = run(
        text_weight_body,
        [text_into, Flow(sds((8, columns), F32))],
        [fetch(text_rows), *text_grad],
        flops=2 * clips * text_len * text_width * columns,
        name="text_weight",
    )
    weights(back_pairs[1], [k[3] for k in kept[0]], [attn_into(6)], "self_out")
    weights(pairs[0], self_grads, [attn_into(n) for n in range(3)], "self_in")
    attn_sum = lax.psum_scatter(free(attn_shared.array), "dp", scatter_dimension=0, tiled=False)
    for c in range(1, clips):
        zero_step(c)

    if aligned:
        pieces = list(map(free, run(
            split_features_body,
            [Flow(sds((clips * strip, share), LOW))] * dp,
            [
                Scalar(group_order),
                Scalar(jnp.broadcast_to(side.astype(jnp.int32), (clips + 1,))),
            ]
            + zero_lows,
            name="split_features",
        )))
    else:
        rows = jnp.concatenate(
            [lax.dynamic_slice_in_dim(free(a), side * strip, strip, 0) for a in zero_lows], axis=0
        )
        rows = jnp.transpose(rows.reshape(clips * strip, dp, share), (1, 0, 2))
        pieces = list(jnp.take(rows, group_order, axis=0))
    rows_all = [pieces[0]] + [swap(pieces[m], "dp", m) for m in range(1, dp)]
    embed_parts = embed_back(vocab_base, packets, rows_all, books, vocab, list(last))
    grad_embed = collect_tensor([embed_parts[m] for m in range(tensor)])

    norm_part = jnp.concatenate(
        [sum(s)[0:1] for s in sums] + [sum(s)[1:2] for s in sums], axis=0
    ) * (1.0 / sides)
    bias_row = lax.dynamic_update_slice_in_dim(
        jnp.zeros((width,), F32), free(bias_grad)[0], place * columns, 0
    )
    norm_total = total_over(
        jnp.concatenate([norm_part, bias_row[None]], axis=0), ("tensor", "dp")
    )
    grad_norm_rows = lax.dynamic_slice_in_dim(norm_total, group * share, share, 1)

    grad_attention = attn_sum[: 8 * share].reshape(attention.shape).astype(F32)
    grad_text_proj = jnp.transpose(attn_sum[8 * share :]).astype(F32)
    grad_feedforward = ffn_sum.astype(F32)
    grad_heads = head_sum.astype(F32)
    local_square = (
        jnp.sum(grad_attention * grad_attention)
        + jnp.sum(grad_feedforward * grad_feedforward)
        + jnp.sum(grad_heads * grad_heads)
        + jnp.sum(grad_embed * grad_embed)
        + jnp.sum(grad_text_proj * grad_text_proj)
        + jnp.sum(grad_norm_rows * grad_norm_rows) / tensor
    )
    both = total_over(
        jnp.stack([local_square, sum(loss_part) / tensor]).reshape(1, 2), ("tensor", "dp")
    )[0]
    grad_norm = jnp.sqrt(both[0])
    mean_loss = both[1]
    factor = clip_limit / jnp.maximum(grad_norm, clip_limit)
    grad_tables = jnp.concatenate([grad_embed, grad_heads], 0)
    attn_new, attn_first_new, attn_second_new = adam_update(
        attention, grad_attention, attention_first, attention_second, rate_matrix, factor
    )
    ffn_new, ffn_first_new, ffn_second_new = adam_update(
        feedforward, grad_feedforward, feedforward_first, feedforward_second, rate_matrix, factor
    )
    table_new, table_first_new, table_second_new = adam_update(
        tables, grad_tables, tables_first, tables_second, rate_table, factor
    )
    text_new, text_first_new, text_second_new = adam_update(
        text_proj, grad_text_proj, text_first, text_second, rate_matrix, factor
    )
    norm_new, norm_first_new, norm_second_new = adam_update(
        norm_params, grad_norm_rows, norm_first, norm_second, rate_norm, factor
    )
    return (
        mean_loss,
        valid_count,
        grad_norm,
        attn_new,
        attn_new.astype(LOW),
        attn_first_new,
        attn_second_new,
        ffn_new,
        ffn_new.astype(LOW),
        ffn_first_new,
        ffn_second_new,
        table_new,
        table_new.astype(LOW),
        table_first_new,
        table_second_new,
        text_new,
        text_new.astype(LOW),
        text_first_new,
        text_second_new,
        norm_new,
        norm_first_new,
        norm_second_new,
    )


def solution(mesh):
    clip3 = P("dp", None, None)
    clip2 = P("dp", None)
    matrix = P(None, "dp", "tensor")
    text = P("tensor", "dp")
    norm = P(None, "dp")
    placed = (
        (clip3, clip3, clip2, clip3, clip2)
        + (matrix, matrix, matrix, text, norm)
        + (matrix,) * 6
        + (text, text, norm, norm)
    )
    return jax.shard_map(
        on_device,
        mesh=mesh,
        in_specs=placed,
        out_specs=(P(), P(), P()) + (matrix,) * 12 + (text,) * 4 + (norm,) * 3,
        check_vma=False,
    )
```

```python
from functools import partial
import math

import jax
import jax.numpy as jnp
from jax import lax
from jax.experimental import pallas as pl
from jax.experimental.pallas import tpu as pltpu
from jax.sharding import PartitionSpec as P

HEAD_DIM = 64
STEP = 5
BLOCK = 256
NEG = -1e30
LOW = jnp.bfloat16
F32 = jnp.float32

SELF = (0, 1, 2, 6)
CROSS = (3, 4, 5, 7)

SMALL = pl.CostEstimate(flops=1024, bytes_accessed=1024, transcendentals=0)

PIECES = (2, 1)
MORE_PIECES = (1, 1, 1)

clip_limit = 0.004
stability_offset = 1e-08
weight_decay = 0.01
moment_decay = 0.5
rate_matrix = 0.03
rate_table = 0.05
rate_norm = 0.2


def nn(a, b):
    return lax.dot_general(a, b, (((1,), (0,)), ((), ())), preferred_element_type=F32)


def nt(a, b):
    return lax.dot_general(a, b, (((1,), (1,)), ((), ())), preferred_element_type=F32)


def tn(a, b):
    return lax.dot_general(a, b, (((0,), (0,)), ((), ())), preferred_element_type=F32)


def sds(shape, kind):
    return jax.ShapeDtypeStruct(shape, kind)


def scalars():
    return pl.BlockSpec(memory_space=pltpu.SMEM)


def anywhere():
    return pl.BlockSpec(memory_space=pl.ANY)


def in_hbm():
    return pl.BlockSpec(memory_space=pltpu.HBM)


def in_vmem():
    return pl.BlockSpec(memory_space=pltpu.VMEM)


def whole(a):
    rank = len(a.shape)
    return pl.BlockSpec(a.shape, lambda i: (0,) * rank)


def later(body, count, at):
    def ordered(*refs):
        return body(*refs[:at], *refs[at + count :])

    return ordered


class Scalar:
    def __init__(self, array):
        self.array = array


class Window:
    def __init__(self, array, shape, pick):
        self.array, self.shape, self.pick = array, tuple(shape), pick


def hold(array, space):
    return pltpu.with_memory_space_constraint(array, space)


def free(array):
    return pltpu.with_memory_space_constraint(array, pl.ANY)


class Flow:
    def __init__(self, shape):
        self.shape = shape


class Copy:
    def __init__(self, i):
        self.i = i


class Carry:
    def __init__(self, array):
        self.array = array


class Ahead:
    def __init__(self, array):
        self.array = array


class Shared:
    def __init__(self, shape, kind):
        self.full, self.array = sds(shape, kind), None


class Into:
    def __init__(self, shared, shape, pick):
        self.shared, self.shape, self.pick = shared, tuple(shape), pick


def everything(ref):
    return ref


def nbytes_of(shape, kind):
    return math.prod(shape) * jnp.dtype(kind).itemsize


def kernel(body, outs, operands, flops=0, scratch=(), name=None, exps=0, after=(), margin=12):
    arrays, specs, windows, shown, fetched = [], [], [], [], {}
    outs = list(outs)
    for i, a in enumerate(operands):
        shown.append(not isinstance(a, (Carry, Ahead)))
        if isinstance(a, Ahead):
            arrays.append(hold(a.array, pltpu.HBM))
            specs.append(in_hbm())
            windows.append(None)
            outs.append(Flow(sds(a.array.shape, a.array.dtype)))
            fetched[len(outs) - 1] = i
        elif isinstance(a, Carry):
            arrays.append(hold(a.array, pltpu.VMEM))
            specs.append(in_vmem())
            windows.append(None)
            outs.append(Copy(i))
        elif isinstance(a, Scalar):
            arrays.append(a.array)
            specs.append(scalars())
            windows.append(None)
        elif isinstance(a, Window):
            arrays.append(hold(a.array, pltpu.HBM))
            specs.append(in_hbm())
            windows.append(a)
        else:
            arrays.append(hold(a, pltpu.VMEM))
            specs.append(in_vmem())
            windows.append(None)
    aliases, out_shapes, out_specs, out_parts, owners = {}, [], [], [], []
    extra = []
    for o in outs:
        if isinstance(o, Into):
            if o.shared not in owners:
                if o.shared.array is not None:
                    aliases[len(arrays) + len(extra)] = len(out_shapes)
                    extra.append(o.shared.array)
                out_shapes.append(pltpu.HBM(o.shared.full.shape, o.shared.full.dtype))
                out_specs.append(in_hbm())
                owners.append(o.shared)
            out_parts.append(("put", o.shape, o.shared.full.dtype, o.pick, owners.index(o.shared)))
            continue
        if isinstance(o, Flow):
            out_parts.append(("flow", None, None, None, len(out_shapes)))
            out_shapes.append(pltpu.VMEM(o.shape.shape, o.shape.dtype))
            out_specs.append(in_vmem())
        elif isinstance(o, Copy):
            a = arrays[o.i]
            out_parts.append(("copy", o.i, None, None, len(out_shapes)))
            out_shapes.append(pltpu.HBM(a.shape, a.dtype))
            out_specs.append(in_hbm())
        else:
            out_parts.append(("put", o.shape, o.dtype, everything, len(out_shapes)))
            out_shapes.append(pltpu.HBM(o.shape, o.dtype))
            out_specs.append(in_hbm())
        owners.append(None)
    out_parts.append(("token", None, None, None, len(out_shapes)))
    out_shapes.append(pltpu.VMEM((8, 128), F32))
    out_specs.append(in_vmem())
    owners.append(None)
    moved = [w for w in windows if w is not None]
    made = [p for p in out_parts if p[0] == "put"]
    count_in, count_extra, count_after = len(arrays), len(extra), len(after)
    count_out, count_moved, count_arrays = len(out_parts), len(moved), len(out_shapes)

    def run_body(*refs):
        refs = list(refs)
        ins = refs[:count_in]
        at = count_in + count_extra + count_after
        out_refs = refs[at : at + count_arrays]
        at += count_arrays
        in_buffers = refs[at : at + count_moved]
        at += count_moved
        made_buffers = refs[at : at + len(made)]
        at += len(made)
        in_sems, out_sems = refs[at], refs[at + 1]
        rest = refs[at + 2 :]
        views, copies, waited = [], {}, set()
        n = 0
        for i, (ref, w) in enumerate(zip(ins, windows)):
            if not shown[i]:
                continue
            if w is None:
                views.append(ref)
            else:
                copies[i] = pltpu.make_async_copy(w.pick(ref), in_buffers[n], in_sems.at[n])
                copies[i].start()
                views.append(in_buffers[n])
                n += 1
        sent, sources = {}, {}

        def need(*which):
            for i in which:
                if i in copies and i not in waited:
                    waited.add(i)
                    copies[i].wait()

        def put(*which):
            for j in which:
                if j in sources:
                    source, target = sources[j]
                    sent[j] = pltpu.make_async_copy(source, target, out_sems.at[j])
                    sent[j].start()

        body_outs = []
        n = 0
        for j, (kind, what, _, pick, owner) in enumerate(out_parts):
            if kind == "put":
                sources[j] = (made_buffers[n], pick(out_refs[owner]))
                body_outs.append(made_buffers[n])
                n += 1
            elif kind == "copy":
                sources[j] = (ins[what], out_refs[owner])
                put(j)
            elif kind == "token":
                out_refs[owner][...] = jnp.zeros((8, 128), F32)
            elif j in fetched:
                sources[j] = (ins[fetched[j]], out_refs[owner])
                put(j)
            else:
                body_outs.append(out_refs[owner])
        body(need, put, *views, *body_outs, *rest)
        need(*copies)
        put(*(j for j in sources if j not in sent))
        for copy in sent.values():
            copy.wait()

    nbytes = sum(nbytes_of(w.shape, w.array.dtype) for w in moved)
    nbytes += sum(nbytes_of(p[1], p[2]) for p in made)
    held = nbytes + sum(nbytes_of(m.shape, m.dtype) for m in scratch)
    results = pl.pallas_call(
        run_body,
        out_shape=tuple(out_shapes),
        in_specs=specs + [anywhere()] * (count_extra + count_after),
        out_specs=tuple(out_specs),
        input_output_aliases=aliases,
        scratch_shapes=[pltpu.VMEM(w.shape, w.array.dtype) for w in moved]
        + [pltpu.VMEM(p[1], p[2]) for p in made]
        + [
            pltpu.SemaphoreType.DMA((max(1, count_moved),)),
            pltpu.SemaphoreType.DMA((max(1, count_out),)),
        ]
        + list(scratch),
        compiler_params=pltpu.CompilerParams(vmem_limit_bytes=held + (margin << 20)),
        cost_estimate=SMALL,
        name=name,
    )(*arrays, *extra, *after)
    for owner, result in zip(owners, results):
        if owner is not None:
            owner.array = result
    return [r for owner, r in zip(owners, results) if owner is None]


def flat(ref):
    w = ref[...]
    return w.reshape(-1, w.shape[-1])


def half_rows(core, height):
    return (
        pl.ds(pl.multiple_of(core * height, height), height),
        pl.ds(pl.multiple_of((1 - core) * height, height), height),
    )


def attend_block(query, keys, values, head_masks, diagonal, bias):
    rows, width = query.shape
    lane = lax.broadcasted_iota(jnp.int32, (rows, 128), 1)
    column = lax.broadcasted_iota(jnp.int32, (rows, width), 1) // HEAD_DIM
    mixed = jnp.zeros((rows, width), F32)
    totals = jnp.zeros((rows, 128), F32)
    count = keys.shape[0]
    for h, mask in enumerate(head_masks):
        s = nt(query * mask, keys)
        if diagonal is not None:
            last = jnp.where(diagonal, s[:, count - rows :], NEG)
            s = last if count == rows else jnp.concatenate([s[:, : count - rows], last], axis=1)
        if bias is not None:
            s = s + bias
        top = jnp.max(s, axis=1, keepdims=True)
        e = jnp.exp(s - top)
        total = jnp.sum(e, axis=1, keepdims=True)
        p = (e * (1.0 / total)).astype(LOW)
        mixed = jnp.where(column == h, nn(p, values), mixed)
        totals = jnp.where(lane == h, top + jnp.log(total), totals)
    return mixed, totals


def masks_of(width):
    head = lax.broadcasted_iota(jnp.int32, (1, width), 1) // HEAD_DIM
    return [(head == h).astype(F32).astype(LOW) for h in range(width // HEAD_DIM)]


def triangle(size):
    row = lax.broadcasted_iota(jnp.int32, (size, size), 0)
    col = lax.broadcasted_iota(jnp.int32, (size, size), 1)
    return row >= col


def self_forward_body(
    need, put, core_ref, own_ref, wq_ref, got_ref, wk_ref, wv_ref, wo_ref,
    q_ref, k_ref, v_ref, o_ref, lse_ref, keep_ref, send_ref, tot_ref,
):
    height = own_ref.shape[0]
    frames, width = q_ref.shape
    mine, other = half_rows(core_ref[0], height)
    need(1)
    for i, w_ref, to_ref in ((2, wq_ref, q_ref), (4, wk_ref, k_ref), (5, wv_ref, v_ref)):
        need(i)
        w = flat(w_ref)
        to_ref[mine, :] = nn(own_ref[...], w).astype(LOW)
        need(3)
        to_ref[other, :] = nn(got_ref[...], w).astype(LOW)
    put(0, 1, 2)
    scale = jnp.asarray(HEAD_DIM**-0.5, LOW)
    head_masks = masks_of(width)
    diagonal = triangle(BLOCK)
    for i in range(frames // BLOCK):
        rows = slice(i * BLOCK, (i + 1) * BLOCK)
        mixed, totals = attend_block(
            q_ref[rows, :] * scale,
            k_ref[: (i + 1) * BLOCK, :],
            v_ref[: (i + 1) * BLOCK, :],
            head_masks,
            diagonal,
            None,
        )
        o_ref[rows, :] = mixed.astype(LOW)
        tot_ref[rows, :] = totals
    put(3)
    need(6)
    wo = flat(wo_ref)
    send_ref[...] = nt(o_ref[other, :], wo).astype(LOW)
    put(6)
    keep_ref[...] = nt(o_ref[mine, :], wo).astype(LOW)
    put(5)
    lse_ref[...] = jnp.transpose(tot_ref[...])[:8, :]


def cross_forward_body(
    need, put, core_ref, own_ref, wq_ref, got_ref, bias_ref, k_ref, v_ref, wo_ref,
    q_ref, o_ref, lse_ref, keep_ref, send_ref, tot_ref,
):
    height = own_ref.shape[0]
    frames, width = q_ref.shape
    mine, other = half_rows(core_ref[0], height)
    need(1, 2)
    w = flat(wq_ref)
    q_ref[mine, :] = nn(own_ref[...], w).astype(LOW)
    need(3)
    q_ref[other, :] = nn(got_ref[...], w).astype(LOW)
    put(0)
    scale = jnp.asarray(HEAD_DIM**-0.5, LOW)
    head_masks = masks_of(width)
    need(4, 5, 6)
    for i in range(frames // BLOCK):
        rows = slice(i * BLOCK, (i + 1) * BLOCK)
        mixed, totals = attend_block(
            q_ref[rows, :] * scale, k_ref[...], v_ref[...], head_masks, None, bias_ref[...]
        )
        o_ref[rows, :] = mixed.astype(LOW)
        tot_ref[rows, :] = totals
    put(1)
    need(7)
    wo = flat(wo_ref)
    send_ref[...] = nt(o_ref[other, :], wo).astype(LOW)
    put(4)
    keep_ref[...] = nt(o_ref[mine, :], wo).astype(LOW)
    put(3)
    lse_ref[...] = jnp.transpose(tot_ref[...])[:8, :]


def ffn_forward_body(
    need, put, core_ref, own_ref, got_ref, w1_ref, w2_ref,
    act_ref, slope_ref, keep_ref, send_ref,
):
    height = own_ref.shape[0]
    mine, other = half_rows(core_ref[0], height)
    need(1, 2, 3)
    w1 = flat(w1_ref)
    for j, source, rows, to_ref in (
        (3, got_ref, other, send_ref),
        (2, own_ref, mine, keep_ref),
    ):
        u = nn(source[...], w1)
        phi = 0.5 * (1.0 + lax.erf(u * (2.0**-0.5)))
        act = (u * phi).astype(LOW)
        density = jnp.exp(-0.5 * u * u) * ((2.0 * math.pi) ** -0.5)
        act_ref[rows, :] = act
        slope_ref[rows, :] = (phi + u * density).astype(LOW)
        need(4)
        to_ref[...] = nt(act, flat(w2_ref)).astype(to_ref.dtype)
        put(j)


def head_forward_body(
    need, put, core_ref, own_ref, target_ref, got_ref, *refs
):
    *w_refs, logits_ref, stats_ref, tot_ref = refs
    height = own_ref.shape[0]
    books = len(w_refs)
    vocab = w_refs[0].shape[2]
    halves = half_rows(core_ref[0], height)
    lane = lax.broadcasted_iota(jnp.int32, (height, 128), 1)
    code = lax.broadcasted_iota(jnp.int32, (height, vocab), 1)
    need(1, 2)
    totals = [jnp.zeros((height, 128), F32)] * 2
    for k, w_ref in enumerate(w_refs):
        need(4 + k)
        w = flat(w_ref)
        for j, (source, rows) in enumerate(zip((own_ref, got_ref), halves)):
            need(1 + 2 * j)
            s = nn(source[...], w)
            logits_ref[rows, k * vocab : (k + 1) * vocab] = s
            top = jnp.max(s, axis=1, keepdims=True)
            total = jnp.sum(jnp.exp(s - top), axis=1, keepdims=True)
            hit = code == target_ref[rows, k : k + 1]
            pick = jnp.sum(jnp.where(hit, s, 0.0), axis=1, keepdims=True)
            totals[j] = jnp.where(lane == k, top + jnp.log(total), totals[j])
            totals[j] = jnp.where(lane == books + k, pick, totals[j])
    put(0)
    for rows, t in zip(halves, totals):
        tot_ref[rows, :] = t
    stats_ref[...] = jnp.transpose(tot_ref[...])[: 2 * books, :]


def head_backward_body(
    need, put, core_ref, total_ref, weight_ref, target_ref, logits_ref, *refs
):
    *w_refs, valid_ref, grad_ref, keep_ref, send_ref, loss_ref, col_ref = refs
    height = keep_ref.shape[0]
    books = len(w_refs)
    vocab = w_refs[0].shape[2]
    mine, other = half_rows(core_ref[0], height)
    frames = logits_ref.shape[0]
    need(1, 2, 3)
    wide = jnp.concatenate(
        [total_ref[...], jnp.zeros((128 - total_ref.shape[0], frames), F32)], axis=0
    )
    col_ref[...] = jnp.transpose(wide)
    share = 1.0 / valid_ref[0:1, 0:1]
    gap = (col_ref[:, :books] - col_ref[:, books : 2 * books]) * (weight_ref[...] * share)
    loss_ref[...] = jnp.broadcast_to(jnp.sum(gap).reshape(1, 1), loss_ref.shape)
    code = lax.broadcasted_iota(jnp.int32, (height, vocab), 1)
    need(4)
    for j, rows, to_ref in ((2, other, send_ref), (1, mine, keep_ref)):
        weight = weight_ref[rows, :] * share
        total = col_ref[rows, :]
        acc = None
        for k, w_ref in enumerate(w_refs):
            s = logits_ref[rows, k * vocab : (k + 1) * vocab]
            p = jnp.exp(s - total[:, k : k + 1])
            hit = jnp.where(code == target_ref[rows, k : k + 1], 1.0, 0.0)
            g = ((p - hit) * weight[:, k : k + 1]).astype(LOW)
            grad_ref[rows, k * vocab : (k + 1) * vocab] = g
            need(5 + k)
            part = nt(g, flat(w_ref))
            acc = part if acc is None else acc + part
        to_ref[...] = acc.astype(to_ref.dtype)
        put(j)


def ffn_backward_body(
    need, put, core_ref, own_ref, got_ref, w2_ref, slope_ref, w1_ref,
    grad_ref, keep_ref, send_ref,
):
    height = own_ref.shape[0]
    mine, other = half_rows(core_ref[0], height)
    need(1, 2, 3, 4)
    w2 = flat(w2_ref)
    for j, source, rows, to_ref in (
        (2, got_ref, other, send_ref),
        (1, own_ref, mine, keep_ref),
    ):
        g = (nn(source[...], w2) * slope_ref[rows, :].astype(F32)).astype(LOW)
        grad_ref[rows, :] = g
        need(5)
        to_ref[...] = nt(g, flat(w1_ref)).astype(to_ref.dtype)
        put(j)


def attend_back(
    q, k, v, g, lse, head_masks, scale, diagonal, bias, dq_ref, rows, dk_ref, dv_ref, first
):
    count, width = k.shape
    step = q.shape[0]
    dq = jnp.zeros((step, width), F32)
    dk = jnp.zeros((count, width), F32)
    dv = jnp.zeros((count, width), F32)
    for h, mask in enumerate(head_masks):
        qm = q * mask
        gm = g * mask
        s = nt(k, qm)
        if diagonal is not None:
            last = jnp.where(diagonal, s[count - step :, :], NEG)
            s = last if count == step else jnp.concatenate([s[: count - step, :], last], axis=0)
        if bias is not None:
            s = s + bias
        p = jnp.exp(s - lse[h : h + 1, :])
        dp = nt(v, gm)
        inner = jnp.sum(p * dp, axis=0, keepdims=True)
        ds = (p * (dp - inner)).astype(LOW)
        dq = dq + tn(ds, k * mask)
        dk = dk + nn(ds, qm)
        dv = dv + nn(p.astype(LOW), gm)
    dq_ref[rows, :width] = (dq * scale).astype(LOW)
    dk_ref[:count, :] = dk if first else dk_ref[:count, :] + dk
    dv_ref[:count, :] = dv if first else dv_ref[:count, :] + dv


def self_backward_body(
    need, put, core_ref, own_ref, wo_ref, got_ref, q_ref, k_ref, v_ref, lse_ref,
    wq_ref, wk_ref, wv_ref, grad_ref, keep_ref, send_ref, g_ref, dk_acc, dv_acc,
):
    height = own_ref.shape[0]
    frames, width = q_ref.shape
    mine, other = half_rows(core_ref[0], height)
    need(1, 2)
    wo = flat(wo_ref)
    g_ref[mine, :] = nn(own_ref[...], wo).astype(LOW)
    need(3)
    g_ref[other, :] = nn(got_ref[...], wo).astype(LOW)
    scale = HEAD_DIM**-0.5
    head_masks = masks_of(width)
    row = lax.broadcasted_iota(jnp.int32, (BLOCK, BLOCK), 0)
    col = lax.broadcasted_iota(jnp.int32, (BLOCK, BLOCK), 1)
    diagonal = col >= row
    blocks = frames // BLOCK
    need(4, 5, 6, 7)
    for i in reversed(range(blocks)):
        rows = slice(i * BLOCK, (i + 1) * BLOCK)
        count = (i + 1) * BLOCK
        attend_back(
            q_ref[rows, :] * jnp.asarray(scale, LOW),
            k_ref[:count, :],
            v_ref[:count, :],
            g_ref[rows, :],
            lse_ref[:, rows],
            head_masks,
            scale,
            diagonal,
            None,
            grad_ref,
            rows,
            dk_acc,
            dv_acc,
            i == blocks - 1,
        )
    grad_ref[:, width : 2 * width] = dk_acc[...].astype(LOW)
    grad_ref[:, 2 * width :] = dv_acc[...].astype(LOW)
    put(0)
    need(8, 9, 10)
    for j, rows, to_ref in ((2, other, send_ref), (1, mine, keep_ref)):
        part = None
        for n, w_ref in enumerate((wq_ref, wk_ref, wv_ref)):
            term = nt(grad_ref[rows, n * width : (n + 1) * width], flat(w_ref))
            part = term if part is None else part + term
        to_ref[...] = part.astype(to_ref.dtype)
        put(j)


def cross_backward_body(
    need, put, core_ref, own_ref, wo_ref, got_ref, bias_ref, q_ref, k_ref, v_ref, lse_ref, wq_ref,
    dq_ref, dk_ref, dv_ref, keep_ref, send_ref, g_ref, dk_acc, dv_acc,
):
    height = own_ref.shape[0]
    frames, width = q_ref.shape
    mine, other = half_rows(core_ref[0], height)
    need(1, 2)
    wo = flat(wo_ref)
    g_ref[mine, :] = nn(own_ref[...], wo).astype(LOW)
    need(3)
    g_ref[other, :] = nn(got_ref[...], wo).astype(LOW)
    scale = HEAD_DIM**-0.5
    head_masks = masks_of(width)
    need(4, 5, 6, 7, 8)
    for i in range(frames // BLOCK):
        rows = slice(i * BLOCK, (i + 1) * BLOCK)
        attend_back(
            q_ref[rows, :] * jnp.asarray(scale, LOW),
            k_ref[...],
            v_ref[...],
            g_ref[rows, :],
            lse_ref[:, rows],
            head_masks,
            scale,
            None,
            bias_ref[...],
            dq_ref,
            rows,
            dk_acc,
            dv_acc,
            i == 0,
        )
    put(0)
    need(9)
    wq = flat(wq_ref)
    for j, rows, to_ref in ((4, other, send_ref), (3, mine, keep_ref)):
        to_ref[...] = nt(dq_ref[rows, :], wq).astype(to_ref.dtype)
        put(j)
    dk_ref[...] = dk_acc[...].astype(LOW)
    dv_ref[...] = dv_acc[...].astype(LOW)


def normalize(values, gain, shift):
    center = values - jnp.mean(values, axis=1, keepdims=True)
    spread = jnp.mean(center * center, axis=1, keepdims=True)
    return center * lax.rsqrt(spread + 1e-05) * gain + shift


def count_body(books, *refs):
    *packet_refs, out_ref = refs
    total = sum(p[books : books + 1, 0:128] for p in packet_refs)
    out_ref[...] = jnp.broadcast_to(total, out_ref.shape).astype(F32)


def merge_body(books, own_ref, far_ref, out_ref):
    own, far = own_ref[:books, :], far_ref[:books, :]
    high = jnp.maximum(own, far)
    out_ref[:books, :] = high + jnp.log(jnp.exp(own - high) + jnp.exp(far - high))
    out_ref[books:, :] = own_ref[books:, :] + far_ref[books:, :]


def text_in_body(need, put, place_ref, norm_ref, rows_ref, w_ref, out_ref):
    columns = out_ref.shape[1]
    at = pl.ds(pl.multiple_of(place_ref[0] * columns, columns), columns)
    need(2, 3)
    out_ref[...] = (nn(rows_ref[...], flat(w_ref)) + norm_ref[8:9, at]).astype(LOW)


def add_body(keep_ref, got_ref, out_ref):
    out_ref[...] = (keep_ref[...].astype(F32) + got_ref[...].astype(F32)).astype(LOW)


def add_parts_body(keep_ref, got_ref, *out_refs):
    start = 0
    for out_ref in out_refs:
        at = slice(start, start + out_ref.shape[0])
        start += out_ref.shape[0]
        out_ref[...] = (keep_ref[at, :].astype(F32) + got_ref[at, :].astype(F32)).astype(LOW)


def joined(refs):
    half = len(refs) // 2
    sums = [a[...].astype(F32) + b[...].astype(F32) for a, b in zip(refs[:half], refs[half:])]
    return jnp.concatenate(sums, axis=0)


def norm_body(which, hidden_ref, *refs):
    *part_refs, norm_ref, new_ref, out_ref = refs
    new = hidden_ref[...] + joined(part_refs)
    new_ref[...] = new
    out_ref[...] = normalize(
        new, norm_ref[which : which + 1, :], norm_ref[which + 4 : which + 5, :]
    ).astype(LOW)


def embed_norm_body(need, put, side_ref, place_ref, norm_ref, *refs):
    *part_refs, new_ref, out_ref = refs
    side = side_ref[0]
    rows = part_refs[0].shape[0]
    need(1, 2)
    for s, part in enumerate(part_refs):
        need(3 + s)
        at = pl.ds(pl.multiple_of((side ^ s) * rows, rows), rows)
        new = part[...].astype(F32) + place_ref[at, :]
        new_ref[at, :] = new
        out_ref[at, :] = normalize(new, norm_ref[0:1, :], norm_ref[4:5, :]).astype(LOW)
    put(1, 0)


def norm_back_body(which, parts, hidden_ref, *refs):
    *before, norm_ref, new_ref, low_ref, sums_ref = refs[parts:]
    values = hidden_ref[...]
    grad = joined(refs[:parts])
    gain = norm_ref[which : which + 1, :]
    center = values - jnp.mean(values, axis=1, keepdims=True)
    spread = jnp.mean(center * center, axis=1, keepdims=True)
    inverse = lax.rsqrt(spread + 1e-05)
    unit = center * inverse
    scaled = grad * gain
    first = jnp.mean(scaled, axis=1, keepdims=True)
    second = jnp.mean(scaled * unit, axis=1, keepdims=True)
    new = inverse * (scaled - first - unit * second)
    if before:
        new = before[0][...] + new
    new_ref[...] = new
    low_ref[...] = new.astype(LOW)
    sums_ref[...] = jnp.concatenate(
        [
            jnp.sum(grad * unit, axis=0, keepdims=True),
            jnp.sum(grad, axis=0, keepdims=True),
            jnp.zeros((6, values.shape[1]), F32),
        ],
        axis=0,
    )


def weight_grad_body(clips, turn_left, need, put, core_ref, *refs):
    lefts = refs[: 2 * clips]
    rights = refs[2 * clips : 3 * clips]
    outs = refs[3 * clips : -1]
    turned = refs[-1]
    height, width = lefts[0].shape
    frames = rights[0].shape[0]
    group = outs[0].shape[2]
    core = core_ref[0]

    def place(c, at):
        return pl.ds(pl.multiple_of(c * frames + at * height, 128), height)

    if turn_left:
        for m, out_ref in enumerate(outs):
            total = None
            for c in range(clips):
                if m == 0:
                    for j, at in ((0, core), (1, 1 - core)):
                        need(1 + 2 * c + j)
                        turned[:, place(c, at)] = jnp.transpose(lefts[2 * c + j][...])
                    need(1 + 2 * clips + c)
                part = nn(
                    turned[:, c * frames : (c + 1) * frames],
                    rights[c][:, m * group : (m + 1) * group],
                )
                total = part if total is None else total + part
            out_ref[...] = total.astype(LOW).reshape(out_ref.shape)
            put(m)
    else:
        total = None
        for c in range(clips):
            need(1 + 2 * clips + c)
            turned[:, c * frames : (c + 1) * frames] = jnp.transpose(rights[c][...])
            for j, at in ((0, core), (1, 1 - core)):
                need(1 + 2 * c + j)
                part = nn(turned[:, place(c, at)], lefts[2 * c + j][...])
                total = part if total is None else total + part
        for m, out_ref in enumerate(outs):
            member = total[m * group : (m + 1) * group, :]
            out_ref[...] = jnp.transpose(member).astype(LOW).reshape(out_ref.shape)
            put(m)


def norm_rows_kernel(body, outs, operands, norm_rows, after, name="norm"):
    height, width = operands[0].shape
    operands = list(operands) + ([] if norm_rows is None else [norm_rows])
    nbytes = sum(nbytes_of(a.shape, a.dtype) for a in operands + list(outs))
    return pl.pallas_call(
        later(body, len(after), len(operands)),
        out_shape=tuple(pltpu.VMEM(o.shape, o.dtype) for o in outs),
        in_specs=[in_vmem()] * len(operands) + [anywhere()] * len(after),
        out_specs=tuple(in_vmem() for _ in outs),
        compiler_params=pltpu.CompilerParams(vmem_limit_bytes=12 << 20),
        cost_estimate=SMALL,
        name=name,
    )(*(hold(a, pltpu.VMEM) for a in operands), *after)


def turned_codes(packet):
    lines = packet.astype(F32)
    wide = jnp.concatenate([lines, jnp.zeros((120, lines.shape[1]), F32)], axis=0)
    return jnp.transpose(wide)


def embed_body(count, books, base_ref, *refs):
    packets, tables, outs = refs[:count], refs[count : len(refs) - count], refs[len(refs) - count :]
    features, vocab = tables[0].shape[1:]
    rows = outs[0].shape[0]
    chunk = min(256, vocab)
    code = lax.broadcasted_iota(jnp.int32, (rows, chunk), 1).astype(F32)
    for packet, out_ref in zip(packets, outs):
        columns = turned_codes(packet[...])
        acc = jnp.zeros((rows, features), F32)
        for k in range(books):
            column = columns[:rows, k : k + 1]
            for b, table in enumerate(tables):
                local = column - base_ref[b].astype(F32)
                for v in range(0, vocab, chunk):
                    hit = jnp.where(code == local - float(v), 1.0, 0.0).astype(LOW)
                    acc = acc + nt(hit, table[k, :, v : v + chunk])
        out_ref[...] = acc.astype(LOW)


def embed(base, packets, tables, rows, after):
    books, features = tables[0].shape[:2]
    count = len(packets)
    return pl.pallas_call(
        later(partial(embed_body, count, books), len(after), 1 + count + len(tables)),
        out_shape=[sds((rows, features), LOW)] * count,
        in_specs=[scalars()]
        + [in_vmem()] * (count + len(tables))
        + [anywhere()] * len(after),
        out_specs=[in_vmem()] * count,
        compiler_params=pltpu.CompilerParams(vmem_limit_bytes=16 << 20),
        cost_estimate=SMALL,
        name="embed",
    )(base, *packets, *tables, *after)


def embed_back_body(groups, base_ref, *refs):
    packets, grads = refs[:groups], refs[groups : 2 * groups]
    out_ref, all_ref = refs[-2:]
    rows, features = grads[0].shape
    padded = packets[0].shape[1]
    vocab = out_ref.shape[3]
    chunk = min(256, vocab)
    book = pl.program_id(1)

    @pl.when((pl.program_id(0) == 0) & (book == 0))
    def _():
        for j, g in enumerate(grads):
            all_ref[j * padded : j * padded + rows, :] = g[...]
            if padded > rows:
                all_ref[j * padded + rows : (j + 1) * padded, :] = jnp.zeros(
                    (padded - rows, features), LOW
                )

    base = base_ref[pl.program_id(0)]
    line = jnp.concatenate([p[pl.ds(book, 1), :] for p in packets], axis=1)
    code = lax.broadcasted_iota(jnp.int32, (chunk, line.shape[1]), 0)
    for v in range(0, vocab, chunk):
        hit = jnp.where(code == line - (base + v), 1.0, 0.0).astype(LOW)
        out_ref[0, 0, :, v : v + chunk] = jnp.transpose(nn(hit, all_ref[...])).astype(LOW)


def embed_back(base, packets, grads, books, vocab, after):
    parts = base.shape[0]
    groups = len(packets)
    features = grads[0].shape[1]
    return pl.pallas_call(
        later(partial(embed_back_body, groups), len(after), 1 + 2 * groups),
        out_shape=sds((parts, books, features, vocab), LOW),
        grid=(parts, books),
        in_specs=[scalars()] + [in_vmem()] * (2 * groups) + [anywhere()] * len(after),
        out_specs=pl.BlockSpec((1, 1, features, vocab), lambda i, k: (i, k, 0, 0)),
        scratch_shapes=[pltpu.VMEM((groups * packets[0].shape[1], features), LOW)],
        compiler_params=pltpu.CompilerParams(vmem_limit_bytes=24 << 20),
        cost_estimate=SMALL,
        name="embed_back",
    )(base, *packets, *grads, *after)


def gather_features_body(need, put, where_ref, *refs):
    clips = sum(r.shape[1] != refs[0].shape[1] for r in refs)
    part_refs, outs = refs[:-clips], refs[-clips:]
    features = part_refs[0].shape[1]
    strip = outs[0].shape[0]
    for m, part in enumerate(part_refs):
        at = pl.ds(pl.multiple_of(where_ref[m] * features, features), features)
        for c, out_ref in enumerate(outs):
            out_ref[:, at] = part[c * strip : (c + 1) * strip, :]


def split_features_body(need, put, where_ref, side_ref, *refs):
    clips = side_ref.shape[0] - 1
    grads, outs = refs[:clips], refs[clips:]
    features = outs[0].shape[1]
    rows = outs[0].shape[0] // clips
    at_rows = pl.ds(pl.multiple_of(side_ref[0] * rows, rows), rows)
    need(*range(2, 2 + clips))
    for m, out_ref in reversed(list(enumerate(outs))):
        at = pl.ds(pl.multiple_of(where_ref[m] * features, features), features)
        for c in range(clips):
            out_ref[c * rows : (c + 1) * rows, :] = grads[c][at_rows, at]
        put(m)


def text_body(need, put, where_ref, *refs):
    *part_refs, wk_ref, wv_ref, tp_ref, k_ref, v_ref = refs
    columns = part_refs[0].shape[1]
    for m, part in enumerate(part_refs):
        need(1 + m)
        at = pl.ds(pl.multiple_of(where_ref[m] * columns, columns), columns)
        tp_ref[:, at] = part[...]
    put(0)
    for j, w_ref, to_ref in ((1, wk_ref, k_ref), (2, wv_ref, v_ref)):
        need(len(part_refs) + j)
        to_ref[...] = nn(tp_ref[...], flat(w_ref)).astype(LOW)
        put(j)


def text_back_body(clips, need, put, where_ref, *refs):
    dks, dvs = refs[:clips], refs[clips : 2 * clips]
    wk_ref, wv_ref, tp_ref = refs[2 * clips : 2 * clips + 3]
    *part_refs, gk_ref, gv_ref, full_ref = refs[2 * clips + 3 :]
    columns = part_refs[0].shape[1]
    length = dks[0].shape[0]
    need(*range(1, 1 + 2 * clips + 2))
    wk, wv = flat(wk_ref), flat(wv_ref)
    for c in range(clips):
        tp_rows = slice(c * length, (c + 1) * length)
        full_ref[tp_rows, :] = (nt(dks[c][...], wk) + nt(dvs[c][...], wv)).astype(LOW)
    for m, part_ref in enumerate(part_refs):
        at = pl.ds(pl.multiple_of(where_ref[m] * columns, columns), columns)
        part_ref[...] = full_ref[:, at]
    put(*range(len(part_refs)))
    need(3 + 2 * clips)
    turned = jnp.transpose(tp_ref[...])
    for j, grads, to_ref in ((0, dks, gk_ref), (1, dvs, gv_ref)):
        total = None
        for c in range(clips):
            part = nn(turned[:, c * length : (c + 1) * length], grads[c][...])
            total = part if total is None else total + part
        to_ref[...] = total.astype(LOW).reshape(to_ref.shape)
        put(len(part_refs) + j)


def text_weight_body(need, put, rows_ref, own_ref, far_ref, out_ref, bias_ref):
    need(0)
    grad = (own_ref[...].astype(F32) + far_ref[...].astype(F32)).astype(LOW)
    out_ref[...] = tn(rows_ref[...], grad).astype(LOW).reshape(out_ref.shape)
    bias_ref[...] = jnp.broadcast_to(
        jnp.sum(grad.astype(F32), axis=0, keepdims=True), bias_ref.shape
    )


def positions_rows(start, count, feature_count):
    half_width = feature_count // 2
    frequency = jnp.exp(
        jnp.arange(half_width, dtype=F32) * (-math.log(10000.0) / (half_width - 1))
    )
    angles = (start + jnp.arange(count, dtype=jnp.int32)).astype(F32)[:, None] * frequency[None, :]
    return jnp.concatenate([jnp.cos(angles), jnp.sin(angles)], axis=1)


def adam_update(weight, gradient, first_moment, second_moment, step_rate, factor):
    clipped = gradient * factor
    new_first = moment_decay * first_moment + (1.0 - moment_decay) * clipped
    new_second = moment_decay * second_moment + (1.0 - moment_decay) * clipped * clipped
    first_hat = new_first / (1.0 - moment_decay**STEP)
    second_hat = new_second / (1.0 - moment_decay**STEP)
    new_weight = weight * (1.0 - step_rate * weight_decay) - step_rate * first_hat / (
        jnp.sqrt(second_hat) + stability_offset
    )
    return (new_weight, new_first, new_second)


def swap(values, axis, mask):
    size = lax.axis_size(axis)
    return lax.ppermute(values, axis, [(i, i ^ mask) for i in range(size)])


def on_device(
    audio_codes,
    delay_mask,
    frame_mask,
    text_states,
    text_mask,
    attention,
    feedforward,
    tables,
    text_proj,
    norm_params,
    attention_first,
    attention_second,
    feedforward_first,
    feedforward_second,
    tables_first,
    tables_second,
    text_first,
    text_second,
    norm_first,
    norm_second,
):
    clips, frames, books = audio_codes.shape
    text_len, text_width = text_states.shape[1:]
    dp = lax.axis_size("dp")
    tensor = lax.axis_size("tensor")
    group = lax.axis_index("dp")
    place = lax.axis_index("tensor")
    core = place & 1
    side = place >> 1
    sides = tensor // 2
    height = frames // 2
    strip = height // sides
    share = attention.shape[1]
    columns = attention.shape[2]
    width = share * dp
    vocab = tables.shape[2]
    text_share = text_proj.shape[1]
    core_arg = Scalar(core.astype(jnp.int32).reshape(1))
    side_arg = Scalar(side.astype(jnp.int32).reshape(1))
    swap_core = partial(swap, axis="tensor", mask=1)

    def spread_tensor(values):
        held = [values]
        mask = tensor // 2
        order = [0]
        while mask:
            held = held + [swap(v, "tensor", mask) for v in held]
            order = order + [o | mask for o in order]
            mask //= 2
        return [v for _, v in sorted(zip(order, held), key=lambda t: t[0])]

    def collect_tensor(parts):
        mask = 1
        live = {m: p for m, p in enumerate(parts)}
        while mask < tensor:
            fresh = {}
            for m in live:
                if not m & mask:
                    got = swap(live[m | mask].astype(LOW), "tensor", mask)
                    fresh[m] = live[m].astype(F32) + got.astype(F32)
            live = fresh
            mask *= 2
        return live[0]

    def across(values):
        own = values
        mask = 2
        rest = None
        while mask < tensor:
            got = swap(own, "tensor", mask)
            mask *= 2
            if mask < tensor:
                own = (own.astype(F32) + got.astype(F32)).astype(LOW)
            rest = got
        if rest is None:
            rest = jnp.zeros_like(own)
        return own, rest

    def total_over(values, axes):
        for axis in axes:
            mask = 1
            while mask < lax.axis_size(axis):
                values = values + swap(values, axis, mask)
                mask *= 2
        return values

    last = []

    def run(body, outs, operands, after=(), **rest):
        *results, token = kernel(body, outs, operands, after=last + list(after), **rest)
        last[:] = [token]
        return results

    def run_block(*args, **rest):
        return run(*args, **rest)

    def run_weight(*args, **rest):
        results = run(*args, after=soon[:1], **rest)
        del soon[:1]
        return results

    norm_pad = jnp.pad(norm_params.astype(LOW), ((0, 16 - norm_params.shape[0]), (0, columns - share)))
    attn_rows = attention.astype(LOW)
    self_flat = jnp.concatenate([attn_rows[n] for n in SELF] + [norm_pad], axis=0)
    cross_flat = jnp.concatenate([attn_rows[n] for n in CROSS] + [text_proj.astype(LOW).T], axis=0)
    self_all = lax.all_gather(self_flat, "dp", axis=0)
    cross_all = lax.all_gather(cross_flat, "dp", axis=0)
    ffn_all = lax.all_gather(feedforward.astype(LOW), "dp", axis=0)
    head_all = lax.all_gather(tables[books:].astype(LOW), "dp", axis=0)

    frame_live = (jnp.arange(frames, dtype=jnp.int32) < frames - 1).astype(jnp.int32)
    weight_int = delay_mask * frame_mask[:, :, None] * frame_live[None, :, None]
    start = core * height + side * strip
    strip_codes = lax.dynamic_slice_in_dim(audio_codes, start, strip, 1)
    count = clips * strip
    padded = -(-count // 128) * 128
    lines = jnp.transpose(strip_codes, (2, 0, 1)).reshape(books, count)
    lines = jnp.pad(lines, ((0, 0), (0, padded - count)), constant_values=-1)
    count_line = jnp.broadcast_to(jnp.sum(weight_int), (8 - books, padded))
    packet = jnp.concatenate([lines, count_line], axis=0)
    packets = [packet] + [swap(packet, "dp", m) for m in range(1, dp)]
    vocab_base = (place ^ jnp.arange(tensor, dtype=jnp.int32)) * vocab
    group_order = group ^ jnp.arange(dp, dtype=jnp.int32)
    place_order = place ^ jnp.arange(tensor, dtype=jnp.int32)

    text_bias_row = jnp.where(text_mask > 0, 0.0, NEG).astype(F32)
    bias_lines = [text_bias_row[c : c + 1] for c in range(clips)]
    bias_columns = [jnp.transpose(line) for line in bias_lines]
    targets = (jnp.roll(audio_codes, -1, axis=1) - place * vocab).astype(jnp.int32)
    targets = [targets[c] for c in range(clips)]
    loss_weight = [weight_int[c].astype(F32) for c in range(clips)]
    placed = positions_rows(core * height, height, width)

    table_parts = spread_tensor(tables[:books].astype(LOW))
    step = max(1, dp // 4)
    arrived = [None] * dp
    for low_end in reversed(range(0, dp, step)):
        embedded = embed(
            vocab_base, packets[low_end : low_end + step], table_parts, count, list(last)
        )
        last[:] = [embedded[-1]]
        for m, piece in enumerate(embedded, low_end):
            arrived[m] = swap(piece, "dp", m) if m else piece
        last += [a for a in arrived[low_end + step : low_end + 2 * step] if a is not None]
    (counted,) = norm_rows_kernel(
        partial(count_body, books), [sds((8, 128), F32)], packets, None, last, name="count"
    )
    last[:] = bias_lines + bias_columns + targets + loss_weight + [placed, counted]
    last += [a for a in arrived if a is not None]
    aligned = share % 128 == 0
    if aligned:
        strips = run(
            gather_features_body,
            [Flow(sds((strip, width), LOW))] * clips,
            [Scalar(group_order)] + arrived,
            name="gather_features",
        )
        strips = [free(a) for a in strips]
    else:
        strips = jnp.take(jnp.stack(arrived), group_order, axis=0)
        strips = jnp.transpose(strips, (1, 0, 2)).reshape(clips, strip, width)

    norm_rows = self_all[:, 4 * share :, :share]
    norm_rows = jnp.transpose(norm_rows, (1, 0, 2)).reshape(16, width).astype(F32)

    def w_attn(n):
        array, at = (self_all, SELF.index(n)) if n in SELF else (cross_all, CROSS.index(n))
        return Window(
            array, (dp, share, columns), lambda ref: ref.at[:, pl.ds(at * share, share), :]
        )

    def w_member(array, n):
        return Window(array, (dp,) + array.shape[2:], lambda ref: ref.at[:, n])

    half_sds = sds((height, width), F32)
    half_low = sds((height, width), LOW)
    flow = Flow(half_low)

    def fetch(a):
        return Window(a, a.shape, everything)


    def norm_step(which, hidden, parts):
        new, out = norm_rows_kernel(
            partial(norm_body, which),
            [half_sds, half_low],
            [hidden, *parts],
            norm_rows,
            last + soon,
        )
        soon[:] = []
        last[:] = [out]
        return new, (out, swap_core(free(out)))

    def norm_back(which, c, parts, before):
        rows = near.get((which, c, "back"), hidden[which][c])
        if before is not None:
            before = near_grad.get((which, c), before)
        operands = [rows, *parts] + ([before] if before is not None else [])
        new, out, sums = norm_rows_kernel(
            partial(norm_back_body, which, len(parts)),
            [half_sds, half_low, sds((8, width), F32)],
            operands,
            norm_rows,
            last + soon,
        )
        soon[:] = []
        last[:] = [out]
        return new, (out, swap_core(free(out))), free(sums)

    waiting, soon, middle = [], [], []
    moving = [None] * clips

    def flush(pieces=PIECES):
        if waiting:
            c, keep, got = waiting.pop()
            parts = norm_rows_kernel(
                add_parts_body,
                [sds((height * part // sum(pieces), width), LOW) for part in pieces],
                [keep, got],
                None,
                last + middle,
                name="add",
            )
            last[:] = [parts[-1]]
            fars = [across(free(part))[1] for part in parts]
            moving[c] = (*parts, *fars)
            soon[:] = fars[:-1]
            middle[:] = fars[-1:]

    def reduce_rows(c, keep, send):
        waiting.append((c, keep, swap_core(free(send))))

    text_rows = text_states.reshape(clips * text_len, text_width)
    def text_in_step():
        (result,) = run(
            text_in_body,
            [Flow(sds((clips * text_len, columns), LOW))],
            [
                Scalar(place.astype(jnp.int32).reshape(1)),
                norm_rows,
                fetch(text_rows),
                Window(
                    cross_all,
                    (dp, text_share, columns),
                    lambda ref: ref.at[:, pl.ds(4 * share, text_share), :],
                ),
            ],
            flops=2 * clips * text_len * text_width * columns,
            name="text_in",
        )
        return spread_tensor(free(result))

    full = sds((frames, columns), LOW)
    lse_sds = sds((8, frames), F32)
    tot = [pltpu.VMEM((frames, 128), F32)]
    heads = columns // HEAD_DIM
    score_flops = 2 * heads * frames * HEAD_DIM
    units = feedforward.shape[2]
    inner = sds((frames, units), LOW)
    every = range(clips)

    near, near_grad = {}, {}

    def ahead(phase, c):
        at, clip = (phase - 1, c + 1) if c + 1 < clips else (phase, 0)
        if at < 0 or (phase == 3 and clip == 0) or (clip == c):
            return []
        return [Ahead(hidden[at][clip])]

    def took(phase, c, results):
        at, clip = (phase - 1, c + 1) if c + 1 < clips else (phase, 0)
        if ahead(phase, c):
            *results, near[at, clip] = results
        return results

    def ahead_back(phase, c):
        at, clip = (phase, c + 1) if c + 1 < clips else (phase - 1, 0)
        if clip == c:
            return []
        found = [Ahead(hidden[at][clip])]
        if at < 3:
            found.append(Ahead(grads[clip]))
        return found

    def took_back(phase, c, results):
        at, clip = (phase, c + 1) if c + 1 < clips else (phase - 1, 0)
        count = len(ahead_back(phase, c))
        if count == 2:
            near_grad[at, clip] = results[-1]
        if count:
            near[at, clip, "back"] = results[len(results) - count]
        return results[: len(results) - count]

    def embed_step(c):
        mine = strips[c]
        parts = [mine] + [swap(mine, "tensor", 2 * s) for s in range(1, sides)]
        new, out = run(
            embed_norm_body,
            [Flow(half_sds), Flow(half_low)],
            [side_arg, placed, norm_rows] + parts,
            flops=10 * height * width,
            name="embed_norm",
        )
        return new, (out, swap_core(free(out)))

    def self_step(c, pair):
        own, got = pair
        *saved, keep, send, left, right, hidden[0][c] = took(0, c, run_block(
            self_forward_body,
            [full, full, full, full, lse_sds, flow, flow, Copy(1), Copy(3)],
            [core_arg, own, w_attn(0), got, w_attn(1), w_attn(2), w_attn(6)]
            + [Carry(hidden[0][c])]
            + ahead(0, c),
            flops=8 * frames * width * columns + 4 * score_flops * frames,
            scratch=tot,
            name="self_forward",
        ))
        pairs[0][c] = (left, right)
        reduce_rows(c, keep, send)
        return saved

    text_full = sds((clips * text_len, width), LOW)
    text_cols = sds((clips * text_len, columns), LOW)

    def text_step():
        return run(
            text_body,
            [text_full, text_cols, text_cols],
            [Scalar(place_order)] + text_parts + [w_attn(4), w_attn(5)],
            flops=4 * clips * text_len * width * columns,
            name="text",
        )

    def text_rows_of(array, c):
        return Window(
            array, (text_len, columns), lambda ref: ref.at[pl.ds(c * text_len, text_len), :]
        )

    def cross_step(c, pair):
        own, got = pair
        k, v = text_rows_of(text_key, c), text_rows_of(text_value, c)
        q, o, lse, keep, send, left, right, hidden[1][c] = took(1, c, run_block(
            cross_forward_body,
            [full, full, lse_sds, flow, flow, Copy(1), Copy(3)],
            [core_arg, own, w_attn(3), got, bias_lines[c], k, v, w_attn(7)]
            + [Carry(hidden[1][c])]
            + ahead(1, c),
            flops=4 * frames * width * columns + 4 * score_flops * text_len,
            scratch=tot,
            name="cross_forward",
        ))
        pairs[1][c] = (left, right)
        reduce_rows(c, keep, send)
        return (q, k, v, o, lse)

    def ffn_step(c, pair):
        *saved, keep, send, left, right, hidden[2][c] = took(2, c, run_block(
            ffn_forward_body,
            [inner, inner, flow, flow, Copy(1), Copy(2)],
            [core_arg, *pair, w_member(ffn_all, 0), w_member(ffn_all, 1), Carry(hidden[2][c])]
            + ahead(2, c),
            flops=4 * frames * width * units,
            name="ffn_forward",
        ))
        pairs[2][c] = (left, right)
        reduce_rows(c, keep, send)
        return saved

    hidden = [[None] * clips for _ in range(4)]
    pairs = [[None] * clips for _ in range(4)]
    kept = [[None] * clips for _ in range(3)]
    for c in every:
        hidden[0][c], pairs[0][c] = embed_step(c)
        flush()
        kept[0][c] = self_step(c, pairs[0][c])
        if c == 0:
            text_parts = text_in_step()
    text_hidden, text_key, text_value = text_step()
    for c in every:
        hidden[1][c], pairs[1][c] = norm_step(1, near.get((0, c), hidden[0][c]), moving[c])
        flush()
        kept[1][c] = cross_step(c, pairs[1][c])
    for c in every:
        hidden[2][c], pairs[2][c] = norm_step(2, near.get((1, c), hidden[1][c]), moving[c])
        flush()
        kept[2][c] = ffn_step(c, pairs[2][c])

    loss_part = [None] * clips
    sums = [[], [], [], []]

    def head_step(c, pair):
        own, got = pair
        logits, stats, left, right, hidden[3][c] = took(3, c, run_block(
            head_forward_body,
            [
                sds((frames, books * vocab), F32),
                Flow(sds((2 * books, frames), F32)),
                Copy(1),
                Copy(3),
            ],
            [core_arg, own, targets[c], got]
            + [w_member(head_all, k) for k in range(books)]
            + [Carry(hidden[3][c])]
            + ahead(3, c),
            flops=2 * frames * width * books * vocab,
            scratch=tot,
            name="head_forward",
        ))
        pairs[3][c] = (left, right)
        return logits, stats

    def merge_step(stats):
        mask = 1
        while mask < tensor:
            far = swap(free(stats), "tensor", mask)
            (stats,) = norm_rows_kernel(
                partial(merge_body, books),
                [sds((2 * books, frames), F32)],
                [stats, far],
                None,
                last,
                name="merge",
            )
            last[:] = [stats]
            mask *= 2
        return stats

    def head_back_step(c, logits, stats):
        grad, keep, send, loss = run_block(
            head_backward_body,
            [sds((frames, books * vocab), LOW), flow, flow, Flow(sds((8, 128), F32))],
            [core_arg, stats, loss_weight[c], targets[c], fetch(logits)]
            + [w_member(head_all, k) for k in range(books)]
            + [counted],
            flops=2 * frames * width * books * vocab,
            scratch=tot,
            name="head_backward",
        )
        loss_part[c] = free(loss)[0, 0]
        reduce_rows(c, keep, send)
        return grad

    self_shared = Shared((dp, 4 * share + text_share, columns), LOW)
    cross_shared = Shared((dp, 4 * share, columns), LOW)
    ffn_shared = Shared((dp,) + feedforward.shape, LOW)
    head_shared = Shared((dp, books, share, vocab), LOW)

    def attn_into(n):
        shared, at = (
            (self_shared, SELF.index(n)) if n in SELF else (cross_shared, CROSS.index(n))
        )
        return Into(
            shared, (dp, share, columns), lambda ref: ref.at[:, pl.ds(at * share, share), :]
        )

    def member_into(shared, n):
        return Into(shared, (dp,) + shared.full.shape[2:], lambda ref: ref.at[:, n])

    def weights(lefts, rights, outs, name):
        total = rights[0].shape[1]
        turn_left = 2 * total > width
        run_weight(
            partial(weight_grad_body, clips, turn_left),
            outs,
            [core_arg] + [fetch(half) for pair in lefts for half in pair] + [fetch(a) for a in rights],
            flops=2 * clips * frames * width * total,
            scratch=[pltpu.VMEM((width if turn_left else total, clips * frames), LOW)],
            name=name,
            margin=26,
        )

    logit_grads = [None] * clips
    ready = [None] * clips
    for c in every:
        hidden[3][c], pairs[3][c] = norm_step(3, near.get((2, c), hidden[2][c]), moving[c])
        flush()
        ready[c] = head_step(c, pairs[3][c])
        if c:
            flush()
            logits, stats = ready[c - 1]
            logit_grads[c - 1] = head_back_step(c - 1, logits, merge_step(stats))
    logits, stats = ready[-1]
    stats = merge_step(stats)
    flush()
    logit_grads[-1] = head_back_step(clips - 1, logits, stats)

    def ffn_back_step(c, pair):
        own, got = pair
        grad, keep, send, left, right, grads[c] = took_back(3, c, run_block(
            ffn_backward_body,
            [inner, flow, flow, Copy(1), Copy(2)],
            [core_arg, own, got, w_member(ffn_all, 1), fetch(kept[2][c][1]), w_member(ffn_all, 0)]
            + [Carry(grads[c])]
            + ahead_back(3, c),
            flops=4 * frames * width * units,
            name="ffn_backward",
        ))
        back_pairs[3][c] = (left, right)
        reduce_rows(c, keep, send)
        return grad

    grads = [None] * clips
    back_pairs = [[None] * clips for _ in range(4)]
    inner_grads = [None] * clips
    for c in every:
        grads[c], back_pairs[3][c], s = norm_back(3, c, moving[c], None)
        sums[3].append(s)
        flush(MORE_PIECES if c == 0 else PIECES)
        inner_grads[c] = ffn_back_step(c, back_pairs[3][c])
        if c == 0:
            head_into = [member_into(head_shared, k) for k in range(books)]
            weights(pairs[3], logit_grads, head_into, "head_weights")
    head_sum = lax.psum_scatter(free(head_shared.array), "dp", scatter_dimension=0, tiled=False)

    acc_text = [pltpu.VMEM((text_len, columns), F32)] * 2
    small = sds((text_len, columns), LOW)

    def cross_back_step(c, pair):
        own, got = pair
        q, k, v, o, lse = kept[1][c]
        bias = bias_columns[c]
        dq, dk, dv, keep, send, left, right, grads[c] = took_back(2, c, run_block(
            cross_backward_body,
            [full, small, small, flow, flow, Copy(1), Copy(3)],
            [core_arg, own, w_attn(7), got, bias, fetch(q), k, v, fetch(lse), w_attn(3)]
            + [Carry(grads[c])]
            + ahead_back(2, c),
            flops=4 * frames * width * columns + 10 * score_flops * text_len,
            scratch=[pltpu.VMEM((frames, columns), LOW)] + acc_text,
            name="cross_backward",
        ))
        back_pairs[2][c] = (left, right)
        reduce_rows(c, keep, send)
        return (dq, dk, dv)

    cross_grads = [None] * clips
    for c in every:
        grads[c], back_pairs[2][c], s = norm_back(2, c, moving[c], grads[c])
        sums[2].append(s)
        flush(MORE_PIECES if c < 2 else PIECES)
        cross_grads[c] = cross_back_step(c, back_pairs[2][c])
        if c == 0:
            weights(
                back_pairs[3], [k[0] for k in kept[2]], [member_into(ffn_shared, 1)], "ffn_two"
            )
        if c == min(1, clips - 1):
            weights(pairs[2], inner_grads, [member_into(ffn_shared, 0)], "ffn_one")
    ffn_sum = lax.psum_scatter(free(ffn_shared.array), "dp", scatter_dimension=0, tiled=False)

    def text_back_step():
        results = run(
            partial(text_back_body, clips),
            [Flow(text_cols)] * tensor + [attn_into(4), attn_into(5)],
            [Scalar(place_order)]
            + [fetch(g[1]) for g in cross_grads]
            + [fetch(g[2]) for g in cross_grads]
            + [w_attn(4), w_attn(5), fetch(text_hidden)],
            flops=8 * clips * text_len * width * columns,
            scratch=[pltpu.VMEM((clips * text_len, width), LOW)],
            name="text_back",
        )
        live = dict(enumerate(results))
        mask = 1
        while mask < tensor:
            fresh = {}
            for m in live:
                if not m & mask:
                    fresh[m] = (live[m], swap(free(live[m | mask]), "tensor", mask))
            mask *= 2
            if mask < tensor:
                for m, both in fresh.items():
                    (fresh[m],) = norm_rows_kernel(
                        add_body, [text_cols], list(both), None, last, name="add"
                    )
                    last[:] = [fresh[m]]
            live = fresh
        return live[0]

    acc_self = [pltpu.VMEM((frames, columns), F32)] * 2

    def self_back_step(c, pair):
        own, got = pair
        q, k, v, o, lse = kept[0][c]
        grad, keep, send, left, right, grads[c] = took_back(1, c, run_block(
            self_backward_body,
            [sds((frames, 3 * columns), LOW), flow, flow, Copy(1), Copy(3)],
            [core_arg, own, w_attn(6), got]
            + [fetch(a) for a in (q, k, v, lse)]
            + [w_attn(0), w_attn(1), w_attn(2), Carry(grads[c])]
            + ahead_back(1, c),
            flops=8 * frames * width * columns + 10 * score_flops * frames,
            scratch=[pltpu.VMEM((frames, columns), LOW)] + acc_self,
            name="self_backward",
        ))
        back_pairs[1][c] = (left, right)
        reduce_rows(c, keep, send)
        return grad

    self_grads = [None] * clips
    for c in every:
        grads[c], back_pairs[1][c], s = norm_back(1, c, moving[c], grads[c])
        sums[1].append(s)
        flush(MORE_PIECES if c < 2 else PIECES)
        self_grads[c] = self_back_step(c, back_pairs[1][c])
        if c == 0:
            text_grad = text_back_step()
            weights(back_pairs[2], [k[3] for k in kept[1]], [attn_into(7)], "cross_out")
        if c == min(1, clips - 1):
            weights(pairs[1], [g[0] for g in cross_grads], [attn_into(3)], "cross_query")
            cross_sum = lax.psum_scatter(
                free(cross_shared.array), "dp", scatter_dimension=0, tiled=False
            )

    zero_lows = [None] * clips

    def zero_step(c):
        _, (zero_lows[c], _), s = norm_back(0, c, moving[c], grads[c])
        sums[0].append(s)

    zero_step(0)
    flush(MORE_PIECES)
    text_into = Into(
        self_shared,
        (dp, text_share, columns),
        lambda ref: ref.at[:, pl.ds(4 * share, text_share), :],
    )
    (bias_grad,) = run(
        text_weight_body,
        [text_into, Flow(sds((8, columns), F32))],
        [fetch(text_rows), *text_grad],
        flops=2 * clips * text_len * text_width * columns,
        name="text_weight",
    )
    weights(back_pairs[1], [k[3] for k in kept[0]], [attn_into(6)], "self_out")
    weights(pairs[0], self_grads, [attn_into(n) for n in range(3)], "self_in")
    self_sum = lax.psum_scatter(free(self_shared.array), "dp", scatter_dimension=0, tiled=False)
    for c in range(1, clips):
        zero_step(c)

    if aligned:
        pieces = list(map(free, run(
            split_features_body,
            [Flow(sds((clips * strip, share), LOW))] * dp,
            [
                Scalar(group_order),
                Scalar(jnp.broadcast_to(side.astype(jnp.int32), (clips + 1,))),
            ]
            + zero_lows,
            name="split_features",
        )))
    else:
        rows = jnp.concatenate(
            [lax.dynamic_slice_in_dim(free(a), side * strip, strip, 0) for a in zero_lows], axis=0
        )
        rows = jnp.transpose(rows.reshape(clips * strip, dp, share), (1, 0, 2))
        pieces = list(jnp.take(rows, group_order, axis=0))
    rows_all = [pieces[0]] + [swap(pieces[m], "dp", m) for m in range(1, dp)]
    embed_parts = embed_back(vocab_base, packets, rows_all, books, vocab, list(last))
    grad_embed = collect_tensor([embed_parts[m] for m in range(tensor)])

    norm_part = jnp.concatenate(
        [sum(s)[0:1] for s in sums] + [sum(s)[1:2] for s in sums], axis=0
    ) * (1.0 / sides)
    bias_row = lax.dynamic_update_slice_in_dim(
        jnp.zeros((width,), F32), free(bias_grad)[0], place * columns, 0
    )
    norm_total = total_over(
        jnp.concatenate([norm_part, bias_row[None]], axis=0), ("tensor", "dp")
    )
    grad_norm_rows = lax.dynamic_slice_in_dim(norm_total, group * share, share, 1)

    parts = [None] * attention.shape[0]
    for at, n in enumerate(SELF):
        parts[n] = self_sum[at * share : (at + 1) * share]
    for at, n in enumerate(CROSS):
        parts[n] = cross_sum[at * share : (at + 1) * share]
    grad_attention = jnp.stack(parts).astype(F32)
    grad_text_proj = jnp.transpose(self_sum[4 * share :]).astype(F32)
    grad_feedforward = ffn_sum.astype(F32)
    grad_heads = head_sum.astype(F32)
    local_square = (
        jnp.sum(grad_attention * grad_attention)
        + jnp.sum(grad_feedforward * grad_feedforward)
        + jnp.sum(grad_heads * grad_heads)
        + jnp.sum(grad_embed * grad_embed)
        + jnp.sum(grad_text_proj * grad_text_proj)
        + jnp.sum(grad_norm_rows * grad_norm_rows) / tensor
    )
    both = total_over(
        jnp.stack([local_square, sum(loss_part) / tensor]).reshape(1, 2), ("tensor", "dp")
    )[0]
    grad_norm = jnp.sqrt(both[0])
    mean_loss = both[1]
    factor = clip_limit / jnp.maximum(grad_norm, clip_limit)
    grad_tables = jnp.concatenate([grad_embed, grad_heads], 0)
    attn_new, attn_first_new, attn_second_new = adam_update(
        attention, grad_attention, attention_first, attention_second, rate_matrix, factor
    )
    ffn_new, ffn_first_new, ffn_second_new = adam_update(
        feedforward, grad_feedforward, feedforward_first, feedforward_second, rate_matrix, factor
    )
    table_new, table_first_new, table_second_new = adam_update(
        tables, grad_tables, tables_first, tables_second, rate_table, factor
    )
    text_new, text_first_new, text_second_new = adam_update(
        text_proj, grad_text_proj, text_first, text_second, rate_matrix, factor
    )
    norm_new, norm_first_new, norm_second_new = adam_update(
        norm_params, grad_norm_rows, norm_first, norm_second, rate_norm, factor
    )
    return (
        mean_loss,
        free(counted)[0, 0],
        grad_norm,
        attn_new,
        attn_new.astype(LOW),
        attn_first_new,
        attn_second_new,
        ffn_new,
        ffn_new.astype(LOW),
        ffn_first_new,
        ffn_second_new,
        table_new,
        table_new.astype(LOW),
        table_first_new,
        table_second_new,
        text_new,
        text_new.astype(LOW),
        text_first_new,
        text_second_new,
        norm_new,
        norm_first_new,
        norm_second_new,
    )


def solution(mesh):
    clip3 = P("dp", None, None)
    clip2 = P("dp", None)
    matrix = P(None, "dp", "tensor")
    text = P("tensor", "dp")
    norm = P(None, "dp")
    placed = (
        (clip3, clip3, clip2, clip3, clip2)
        + (matrix, matrix, matrix, text, norm)
        + (matrix,) * 6
        + (text, text, norm, norm)
    )
    return jax.shard_map(
        on_device,
        mesh=mesh,
        in_specs=placed,
        out_specs=(P(), P(), P()) + (matrix,) * 12 + (text,) * 4 + (norm,) * 3,
        check_vma=False,
    )
```

```python
from functools import partial
import math

import jax
import jax.numpy as jnp
from jax import lax
from jax.experimental import pallas as pl
from jax.experimental.pallas import tpu as pltpu
from jax.sharding import PartitionSpec as P

HEAD_DIM = 64
STEP = 5
BLOCK = 256
NEG = -1e30
LOW = jnp.bfloat16
F32 = jnp.float32

SELF = (0, 1, 2, 6)
CROSS = (3, 4, 5, 7)

SMALL = pl.CostEstimate(flops=1024, bytes_accessed=1024, transcendentals=0)

PIECES = (1, 1)

clip_limit = 0.004
stability_offset = 1e-08
weight_decay = 0.01
moment_decay = 0.5
rate_matrix = 0.03
rate_table = 0.05
rate_norm = 0.2


def nn(a, b):
    return lax.dot_general(a, b, (((1,), (0,)), ((), ())), preferred_element_type=F32)


def nt(a, b):
    return lax.dot_general(a, b, (((1,), (1,)), ((), ())), preferred_element_type=F32)


def tn(a, b):
    return lax.dot_general(a, b, (((0,), (0,)), ((), ())), preferred_element_type=F32)


def sds(shape, kind):
    return jax.ShapeDtypeStruct(shape, kind)


def scalars():
    return pl.BlockSpec(memory_space=pltpu.SMEM)


def anywhere():
    return pl.BlockSpec(memory_space=pl.ANY)


def in_hbm():
    return pl.BlockSpec(memory_space=pltpu.HBM)


def in_vmem():
    return pl.BlockSpec(memory_space=pltpu.VMEM)


def whole(a):
    rank = len(a.shape)
    return pl.BlockSpec(a.shape, lambda i: (0,) * rank)


def later(body, count, at):
    def ordered(*refs):
        return body(*refs[:at], *refs[at + count :])

    return ordered


class Scalar:
    def __init__(self, array):
        self.array = array


class Window:
    def __init__(self, array, shape, pick):
        self.array, self.shape, self.pick = array, tuple(shape), pick


def hold(array, space):
    return pltpu.with_memory_space_constraint(array, space)


def free(array):
    return pltpu.with_memory_space_constraint(array, pl.ANY)


class Flow:
    def __init__(self, shape):
        self.shape = shape


class Copy:
    def __init__(self, i):
        self.i = i


class Carry:
    def __init__(self, array):
        self.array = array


class Ahead:
    def __init__(self, array):
        self.array = array


class Shared:
    def __init__(self, shape, kind):
        self.full, self.array = sds(shape, kind), None


class Into:
    def __init__(self, shared, shape, pick):
        self.shared, self.shape, self.pick = shared, tuple(shape), pick


def everything(ref):
    return ref


def nbytes_of(shape, kind):
    return math.prod(shape) * jnp.dtype(kind).itemsize


def kernel(body, outs, operands, flops=0, scratch=(), name=None, exps=0, after=(), margin=12):
    arrays, specs, windows, shown, fetched = [], [], [], [], {}
    outs = list(outs)
    for i, a in enumerate(operands):
        shown.append(not isinstance(a, (Carry, Ahead)))
        if isinstance(a, Ahead):
            arrays.append(hold(a.array, pltpu.HBM))
            specs.append(in_hbm())
            windows.append(None)
            outs.append(Flow(sds(a.array.shape, a.array.dtype)))
            fetched[len(outs) - 1] = i
        elif isinstance(a, Carry):
            arrays.append(hold(a.array, pltpu.VMEM))
            specs.append(in_vmem())
            windows.append(None)
            outs.append(Copy(i))
        elif isinstance(a, Scalar):
            arrays.append(a.array)
            specs.append(scalars())
            windows.append(None)
        elif isinstance(a, Window):
            arrays.append(hold(a.array, pltpu.HBM))
            specs.append(in_hbm())
            windows.append(a)
        else:
            arrays.append(hold(a, pltpu.VMEM))
            specs.append(in_vmem())
            windows.append(None)
    aliases, out_shapes, out_specs, out_parts, owners = {}, [], [], [], []
    extra = []
    for o in outs:
        if isinstance(o, Into):
            if o.shared not in owners:
                if o.shared.array is not None:
                    aliases[len(arrays) + len(extra)] = len(out_shapes)
                    extra.append(o.shared.array)
                out_shapes.append(pltpu.HBM(o.shared.full.shape, o.shared.full.dtype))
                out_specs.append(in_hbm())
                owners.append(o.shared)
            out_parts.append(("put", o.shape, o.shared.full.dtype, o.pick, owners.index(o.shared)))
            continue
        if isinstance(o, Flow):
            out_parts.append(("flow", None, None, None, len(out_shapes)))
            out_shapes.append(pltpu.VMEM(o.shape.shape, o.shape.dtype))
            out_specs.append(in_vmem())
        elif isinstance(o, Copy):
            a = arrays[o.i]
            out_parts.append(("copy", o.i, None, None, len(out_shapes)))
            out_shapes.append(pltpu.HBM(a.shape, a.dtype))
            out_specs.append(in_hbm())
        else:
            out_parts.append(("put", o.shape, o.dtype, everything, len(out_shapes)))
            out_shapes.append(pltpu.HBM(o.shape, o.dtype))
            out_specs.append(in_hbm())
        owners.append(None)
    out_parts.append(("token", None, None, None, len(out_shapes)))
    out_shapes.append(pltpu.VMEM((8, 128), F32))
    out_specs.append(in_vmem())
    owners.append(None)
    moved = [w for w in windows if w is not None]
    made = [p for p in out_parts if p[0] == "put"]
    count_in, count_extra, count_after = len(arrays), len(extra), len(after)
    count_out, count_moved, count_arrays = len(out_parts), len(moved), len(out_shapes)

    def run_body(*refs):
        refs = list(refs)
        ins = refs[:count_in]
        at = count_in + count_extra + count_after
        out_refs = refs[at : at + count_arrays]
        at += count_arrays
        in_buffers = refs[at : at + count_moved]
        at += count_moved
        made_buffers = refs[at : at + len(made)]
        at += len(made)
        in_sems, out_sems = refs[at], refs[at + 1]
        rest = refs[at + 2 :]
        views, copies, waited = [], {}, set()
        n = 0
        for i, (ref, w) in enumerate(zip(ins, windows)):
            if not shown[i]:
                continue
            if w is None:
                views.append(ref)
            else:
                copies[i] = pltpu.make_async_copy(w.pick(ref), in_buffers[n], in_sems.at[n])
                copies[i].start()
                views.append(in_buffers[n])
                n += 1
        sent, sources = {}, {}

        def need(*which):
            for i in which:
                if i in copies and i not in waited:
                    waited.add(i)
                    copies[i].wait()

        def put(*which):
            for j in which:
                if j in sources:
                    source, target = sources[j]
                    sent[j] = pltpu.make_async_copy(source, target, out_sems.at[j])
                    sent[j].start()

        body_outs = []
        n = 0
        for j, (kind, what, _, pick, owner) in enumerate(out_parts):
            if kind == "put":
                sources[j] = (made_buffers[n], pick(out_refs[owner]))
                body_outs.append(made_buffers[n])
                n += 1
            elif kind == "copy":
                sources[j] = (ins[what], out_refs[owner])
                put(j)
            elif kind == "token":
                out_refs[owner][...] = jnp.zeros((8, 128), F32)
            elif j in fetched:
                sources[j] = (ins[fetched[j]], out_refs[owner])
                put(j)
            else:
                body_outs.append(out_refs[owner])
        body(need, put, *views, *body_outs, *rest)
        need(*copies)
        put(*(j for j in sources if j not in sent))
        for copy in sent.values():
            copy.wait()

    nbytes = sum(nbytes_of(w.shape, w.array.dtype) for w in moved)
    nbytes += sum(nbytes_of(p[1], p[2]) for p in made)
    held = nbytes + sum(nbytes_of(m.shape, m.dtype) for m in scratch)
    results = pl.pallas_call(
        run_body,
        out_shape=tuple(out_shapes),
        in_specs=specs + [anywhere()] * (count_extra + count_after),
        out_specs=tuple(out_specs),
        input_output_aliases=aliases,
        scratch_shapes=[pltpu.VMEM(w.shape, w.array.dtype) for w in moved]
        + [pltpu.VMEM(p[1], p[2]) for p in made]
        + [
            pltpu.SemaphoreType.DMA((max(1, count_moved),)),
            pltpu.SemaphoreType.DMA((max(1, count_out),)),
        ]
        + list(scratch),
        compiler_params=pltpu.CompilerParams(vmem_limit_bytes=held + (margin << 20)),
        cost_estimate=SMALL,
        name=name,
    )(*arrays, *extra, *after)
    for owner, result in zip(owners, results):
        if owner is not None:
            owner.array = result
    return [r for owner, r in zip(owners, results) if owner is None]


def flat(ref):
    w = ref[...]
    return w.reshape(-1, w.shape[-1])


def half_rows(core, height):
    return (
        pl.ds(pl.multiple_of(core * height, height), height),
        pl.ds(pl.multiple_of((1 - core) * height, height), height),
    )


def attend_block(query, keys, values, head_masks, diagonal, bias):
    rows, width = query.shape
    lane = lax.broadcasted_iota(jnp.int32, (rows, 128), 1)
    column = lax.broadcasted_iota(jnp.int32, (rows, width), 1) // HEAD_DIM
    mixed = jnp.zeros((rows, width), F32)
    totals = jnp.zeros((rows, 128), F32)
    count = keys.shape[0]
    for h, mask in enumerate(head_masks):
        s = nt(query * mask, keys)
        if diagonal is not None:
            last = jnp.where(diagonal, s[:, count - rows :], NEG)
            s = last if count == rows else jnp.concatenate([s[:, : count - rows], last], axis=1)
        if bias is not None:
            s = s + bias
        top = jnp.max(s, axis=1, keepdims=True)
        e = jnp.exp(s - top)
        total = jnp.sum(e, axis=1, keepdims=True)
        p = (e * (1.0 / total)).astype(LOW)
        mixed = jnp.where(column == h, nn(p, values), mixed)
        totals = jnp.where(lane == h, top + jnp.log(total), totals)
    return mixed, totals


def masks_of(width):
    head = lax.broadcasted_iota(jnp.int32, (1, width), 1) // HEAD_DIM
    return [(head == h).astype(F32).astype(LOW) for h in range(width // HEAD_DIM)]


def triangle(size):
    row = lax.broadcasted_iota(jnp.int32, (size, size), 0)
    col = lax.broadcasted_iota(jnp.int32, (size, size), 1)
    return row >= col


def self_forward_body(
    need, put, core_ref, own_ref, wq_ref, got_ref, wk_ref, wv_ref, wo_ref,
    q_ref, k_ref, v_ref, o_ref, lse_ref, keep_ref, send_ref, tot_ref,
):
    height = own_ref.shape[0]
    frames, width = q_ref.shape
    mine, other = half_rows(core_ref[0], height)
    need(1)
    for i, w_ref, to_ref in ((2, wq_ref, q_ref), (4, wk_ref, k_ref), (5, wv_ref, v_ref)):
        need(i)
        w = flat(w_ref)
        to_ref[mine, :] = nn(own_ref[...], w).astype(LOW)
        need(3)
        to_ref[other, :] = nn(got_ref[...], w).astype(LOW)
    put(0, 1, 2)
    scale = jnp.asarray(HEAD_DIM**-0.5, LOW)
    head_masks = masks_of(width)
    diagonal = triangle(BLOCK)
    for i in range(frames // BLOCK):
        rows = slice(i * BLOCK, (i + 1) * BLOCK)
        mixed, totals = attend_block(
            q_ref[rows, :] * scale,
            k_ref[: (i + 1) * BLOCK, :],
            v_ref[: (i + 1) * BLOCK, :],
            head_masks,
            diagonal,
            None,
        )
        o_ref[rows, :] = mixed.astype(LOW)
        tot_ref[rows, :] = totals
    put(3)
    need(6)
    wo = flat(wo_ref)
    send_ref[...] = nt(o_ref[other, :], wo).astype(LOW)
    put(6)
    keep_ref[...] = nt(o_ref[mine, :], wo).astype(LOW)
    put(5)
    lse_ref[...] = jnp.transpose(tot_ref[...])[:8, :]


def cross_forward_body(
    need, put, core_ref, own_ref, wq_ref, got_ref, bias_ref, k_ref, v_ref, wo_ref,
    q_ref, o_ref, lse_ref, keep_ref, send_ref, tot_ref,
):
    height = own_ref.shape[0]
    frames, width = q_ref.shape
    mine, other = half_rows(core_ref[0], height)
    need(1, 2)
    w = flat(wq_ref)
    q_ref[mine, :] = nn(own_ref[...], w).astype(LOW)
    need(3)
    q_ref[other, :] = nn(got_ref[...], w).astype(LOW)
    put(0)
    scale = jnp.asarray(HEAD_DIM**-0.5, LOW)
    head_masks = masks_of(width)
    need(4, 5, 6)
    for i in range(frames // BLOCK):
        rows = slice(i * BLOCK, (i + 1) * BLOCK)
        mixed, totals = attend_block(
            q_ref[rows, :] * scale, k_ref[...], v_ref[...], head_masks, None, bias_ref[...]
        )
        o_ref[rows, :] = mixed.astype(LOW)
        tot_ref[rows, :] = totals
    put(1)
    need(7)
    wo = flat(wo_ref)
    send_ref[...] = nt(o_ref[other, :], wo).astype(LOW)
    put(4)
    keep_ref[...] = nt(o_ref[mine, :], wo).astype(LOW)
    put(3)
    lse_ref[...] = jnp.transpose(tot_ref[...])[:8, :]


def ffn_forward_body(
    need, put, core_ref, own_ref, got_ref, w1_ref, w2_ref,
    act_ref, slope_ref, keep_ref, send_ref,
):
    height = own_ref.shape[0]
    mine, other = half_rows(core_ref[0], height)
    need(1, 2, 3)
    w1 = flat(w1_ref)
    for j, source, rows, to_ref in (
        (3, got_ref, other, send_ref),
        (2, own_ref, mine, keep_ref),
    ):
        u = nn(source[...], w1)
        phi = 0.5 * (1.0 + lax.erf(u * (2.0**-0.5)))
        act = (u * phi).astype(LOW)
        density = jnp.exp(-0.5 * u * u) * ((2.0 * math.pi) ** -0.5)
        act_ref[rows, :] = act
        slope_ref[rows, :] = (phi + u * density).astype(LOW)
        need(4)
        to_ref[...] = nt(act, flat(w2_ref)).astype(to_ref.dtype)
        put(j)


def head_forward_body(
    need, put, core_ref, own_ref, target_ref, got_ref, *refs
):
    *w_refs, logits_ref, stats_ref, tot_ref = refs
    height = own_ref.shape[0]
    books = len(w_refs)
    vocab = w_refs[0].shape[2]
    halves = half_rows(core_ref[0], height)
    lane = lax.broadcasted_iota(jnp.int32, (height, 128), 1)
    code = lax.broadcasted_iota(jnp.int32, (height, vocab), 1)
    need(1, 2)
    totals = [jnp.zeros((height, 128), F32)] * 2
    for k, w_ref in enumerate(w_refs):
        need(4 + k)
        w = flat(w_ref)
        for j, (source, rows) in enumerate(zip((own_ref, got_ref), halves)):
            need(1 + 2 * j)
            s = nn(source[...], w)
            logits_ref[rows, k * vocab : (k + 1) * vocab] = s
            top = jnp.max(s, axis=1, keepdims=True)
            total = jnp.sum(jnp.exp(s - top), axis=1, keepdims=True)
            hit = code == target_ref[rows, k : k + 1]
            pick = jnp.sum(jnp.where(hit, s, 0.0), axis=1, keepdims=True)
            totals[j] = jnp.where(lane == k, top + jnp.log(total), totals[j])
            totals[j] = jnp.where(lane == books + k, pick, totals[j])
    put(0)
    for rows, t in zip(halves, totals):
        tot_ref[rows, :] = t
    stats_ref[...] = jnp.transpose(tot_ref[...])[: 2 * books, :]


def head_backward_body(
    need, put, core_ref, total_ref, weight_ref, target_ref, logits_ref, *refs
):
    *w_refs, valid_ref, grad_ref, keep_ref, send_ref, loss_ref, col_ref = refs
    height = keep_ref.shape[0]
    books = len(w_refs)
    vocab = w_refs[0].shape[2]
    mine, other = half_rows(core_ref[0], height)
    frames = logits_ref.shape[0]
    need(1, 2, 3)
    wide = jnp.concatenate(
        [total_ref[...], jnp.zeros((128 - total_ref.shape[0], frames), F32)], axis=0
    )
    col_ref[...] = jnp.transpose(wide)
    share = 1.0 / valid_ref[0:1, 0:1]
    gap = (col_ref[:, :books] - col_ref[:, books : 2 * books]) * (weight_ref[...] * share)
    loss_ref[...] = jnp.broadcast_to(jnp.sum(gap).reshape(1, 1), loss_ref.shape)
    code = lax.broadcasted_iota(jnp.int32, (height, vocab), 1)
    need(4)
    for j, rows, to_ref in ((2, other, send_ref), (1, mine, keep_ref)):
        weight = weight_ref[rows, :] * share
        total = col_ref[rows, :]
        acc = None
        for k, w_ref in enumerate(w_refs):
            s = logits_ref[rows, k * vocab : (k + 1) * vocab]
            p = jnp.exp(s - total[:, k : k + 1])
            hit = jnp.where(code == target_ref[rows, k : k + 1], 1.0, 0.0)
            g = ((p - hit) * weight[:, k : k + 1]).astype(LOW)
            grad_ref[rows, k * vocab : (k + 1) * vocab] = g
            need(5 + k)
            part = nt(g, flat(w_ref))
            acc = part if acc is None else acc + part
        to_ref[...] = acc.astype(to_ref.dtype)
        put(j)


def ffn_backward_body(
    need, put, core_ref, own_ref, got_ref, w2_ref, slope_ref, w1_ref,
    grad_ref, keep_ref, send_ref,
):
    height = own_ref.shape[0]
    mine, other = half_rows(core_ref[0], height)
    need(1, 2, 3, 4)
    w2 = flat(w2_ref)
    for j, source, rows, to_ref in (
        (2, got_ref, other, send_ref),
        (1, own_ref, mine, keep_ref),
    ):
        g = (nn(source[...], w2) * slope_ref[rows, :].astype(F32)).astype(LOW)
        grad_ref[rows, :] = g
        need(5)
        to_ref[...] = nt(g, flat(w1_ref)).astype(to_ref.dtype)
        put(j)


def attend_back(
    q, k, v, g, lse, head_masks, scale, diagonal, bias, dq_ref, rows, dk_ref, dv_ref, first
):
    count, width = k.shape
    step = q.shape[0]
    dq = jnp.zeros((step, width), F32)
    dk = jnp.zeros((count, width), F32)
    dv = jnp.zeros((count, width), F32)
    for h, mask in enumerate(head_masks):
        qm = q * mask
        gm = g * mask
        s = nt(k, qm)
        if diagonal is not None:
            last = jnp.where(diagonal, s[count - step :, :], NEG)
            s = last if count == step else jnp.concatenate([s[: count - step, :], last], axis=0)
        if bias is not None:
            s = s + bias
        p = jnp.exp(s - lse[h : h + 1, :])
        dp = nt(v, gm)
        inner = jnp.sum(p * dp, axis=0, keepdims=True)
        ds = (p * (dp - inner)).astype(LOW)
        dq = dq + tn(ds, k * mask)
        dk = dk + nn(ds, qm)
        dv = dv + nn(p.astype(LOW), gm)
    dq_ref[rows, :width] = (dq * scale).astype(LOW)
    dk_ref[:count, :] = dk if first else dk_ref[:count, :] + dk
    dv_ref[:count, :] = dv if first else dv_ref[:count, :] + dv


def self_backward_body(
    need, put, core_ref, own_ref, wo_ref, got_ref, q_ref, k_ref, v_ref, lse_ref,
    wq_ref, wk_ref, wv_ref, grad_ref, keep_ref, send_ref, g_ref, dk_acc, dv_acc,
):
    height = own_ref.shape[0]
    frames, width = q_ref.shape
    mine, other = half_rows(core_ref[0], height)
    need(1, 2)
    wo = flat(wo_ref)
    g_ref[mine, :] = nn(own_ref[...], wo).astype(LOW)
    need(3)
    g_ref[other, :] = nn(got_ref[...], wo).astype(LOW)
    scale = HEAD_DIM**-0.5
    head_masks = masks_of(width)
    row = lax.broadcasted_iota(jnp.int32, (BLOCK, BLOCK), 0)
    col = lax.broadcasted_iota(jnp.int32, (BLOCK, BLOCK), 1)
    diagonal = col >= row
    blocks = frames // BLOCK
    need(4, 5, 6, 7)
    for i in reversed(range(blocks)):
        rows = slice(i * BLOCK, (i + 1) * BLOCK)
        count = (i + 1) * BLOCK
        attend_back(
            q_ref[rows, :] * jnp.asarray(scale, LOW),
            k_ref[:count, :],
            v_ref[:count, :],
            g_ref[rows, :],
            lse_ref[:, rows],
            head_masks,
            scale,
            diagonal,
            None,
            grad_ref,
            rows,
            dk_acc,
            dv_acc,
            i == blocks - 1,
        )
    grad_ref[:, width : 2 * width] = dk_acc[...].astype(LOW)
    grad_ref[:, 2 * width :] = dv_acc[...].astype(LOW)
    put(0)
    need(8, 9, 10)
    for j, rows, to_ref in ((2, other, send_ref), (1, mine, keep_ref)):
        part = None
        for n, w_ref in enumerate((wq_ref, wk_ref, wv_ref)):
            term = nt(grad_ref[rows, n * width : (n + 1) * width], flat(w_ref))
            part = term if part is None else part + term
        to_ref[...] = part.astype(to_ref.dtype)
        put(j)


def cross_backward_body(
    need, put, core_ref, own_ref, wo_ref, got_ref, bias_ref, q_ref, k_ref, v_ref, lse_ref, wq_ref,
    dq_ref, dk_ref, dv_ref, keep_ref, send_ref, g_ref, dk_acc, dv_acc,
):
    height = own_ref.shape[0]
    frames, width = q_ref.shape
    mine, other = half_rows(core_ref[0], height)
    need(1, 2)
    wo = flat(wo_ref)
    g_ref[mine, :] = nn(own_ref[...], wo).astype(LOW)
    need(3)
    g_ref[other, :] = nn(got_ref[...], wo).astype(LOW)
    scale = HEAD_DIM**-0.5
    head_masks = masks_of(width)
    need(4, 5, 6, 7, 8)
    for i in range(frames // BLOCK):
        rows = slice(i * BLOCK, (i + 1) * BLOCK)
        attend_back(
            q_ref[rows, :] * jnp.asarray(scale, LOW),
            k_ref[...],
            v_ref[...],
            g_ref[rows, :],
            lse_ref[:, rows],
            head_masks,
            scale,
            None,
            bias_ref[...],
            dq_ref,
            rows,
            dk_acc,
            dv_acc,
            i == 0,
        )
    put(0)
    need(9)
    wq = flat(wq_ref)
    for j, rows, to_ref in ((4, other, send_ref), (3, mine, keep_ref)):
        to_ref[...] = nt(dq_ref[rows, :], wq).astype(to_ref.dtype)
        put(j)
    dk_ref[...] = dk_acc[...].astype(LOW)
    dv_ref[...] = dv_acc[...].astype(LOW)


def normalize(values, gain, shift):
    center = values - jnp.mean(values, axis=1, keepdims=True)
    spread = jnp.mean(center * center, axis=1, keepdims=True)
    return center * lax.rsqrt(spread + 1e-05) * gain + shift


def count_body(books, *refs):
    *packet_refs, out_ref = refs
    total = sum(p[books : books + 1, 0:128] for p in packet_refs)
    out_ref[...] = jnp.broadcast_to(total, out_ref.shape).astype(F32)


def merge_body(books, own_ref, far_ref, out_ref):
    own, far = own_ref[:books, :], far_ref[:books, :]
    high = jnp.maximum(own, far)
    out_ref[:books, :] = high + jnp.log(jnp.exp(own - high) + jnp.exp(far - high))
    out_ref[books:, :] = own_ref[books:, :] + far_ref[books:, :]


def text_in_body(need, put, place_ref, norm_ref, rows_ref, w_ref, out_ref):
    columns = out_ref.shape[1]
    at = pl.ds(pl.multiple_of(place_ref[0] * columns, columns), columns)
    need(2, 3)
    out_ref[...] = (nn(rows_ref[...], flat(w_ref)) + norm_ref[8:9, at]).astype(LOW)


def add_body(keep_ref, got_ref, out_ref):
    out_ref[...] = (keep_ref[...].astype(F32) + got_ref[...].astype(F32)).astype(LOW)


def add_parts_body(keep_ref, got_ref, *out_refs):
    start = 0
    for out_ref in out_refs:
        at = slice(start, start + out_ref.shape[0])
        start += out_ref.shape[0]
        out_ref[...] = (keep_ref[at, :].astype(F32) + got_ref[at, :].astype(F32)).astype(LOW)


def joined(refs):
    half = len(refs) // 2
    sums = [a[...].astype(F32) + b[...].astype(F32) for a, b in zip(refs[:half], refs[half:])]
    return jnp.concatenate(sums, axis=0)


def norm_body(which, hidden_ref, *refs):
    *part_refs, norm_ref, new_ref, out_ref = refs
    new = hidden_ref[...] + joined(part_refs)
    new_ref[...] = new
    out_ref[...] = normalize(
        new, norm_ref[which : which + 1, :], norm_ref[which + 4 : which + 5, :]
    ).astype(LOW)


def embed_norm_body(need, put, side_ref, place_ref, norm_ref, *refs):
    *part_refs, new_ref, out_ref = refs
    side = side_ref[0]
    rows = part_refs[0].shape[0]
    need(1, 2)
    for s, part in enumerate(part_refs):
        need(3 + s)
        at = pl.ds(pl.multiple_of((side ^ s) * rows, rows), rows)
        new = part[...].astype(F32) + place_ref[at, :]
        new_ref[at, :] = new
        out_ref[at, :] = normalize(new, norm_ref[0:1, :], norm_ref[4:5, :]).astype(LOW)
    put(1, 0)


def norm_back_body(which, parts, hidden_ref, *refs):
    *before, norm_ref, new_ref, low_ref, sums_ref = refs[parts:]
    values = hidden_ref[...]
    grad = joined(refs[:parts])
    gain = norm_ref[which : which + 1, :]
    center = values - jnp.mean(values, axis=1, keepdims=True)
    spread = jnp.mean(center * center, axis=1, keepdims=True)
    inverse = lax.rsqrt(spread + 1e-05)
    unit = center * inverse
    scaled = grad * gain
    first = jnp.mean(scaled, axis=1, keepdims=True)
    second = jnp.mean(scaled * unit, axis=1, keepdims=True)
    new = inverse * (scaled - first - unit * second)
    if before:
        new = before[0][...] + new
    new_ref[...] = new
    low_ref[...] = new.astype(LOW)
    sums_ref[...] = jnp.concatenate(
        [
            jnp.sum(grad * unit, axis=0, keepdims=True),
            jnp.sum(grad, axis=0, keepdims=True),
            jnp.zeros((6, values.shape[1]), F32),
        ],
        axis=0,
    )


def weight_grad_body(clips, turn_left, need, put, core_ref, *refs):
    lefts = refs[: 2 * clips]
    rights = refs[2 * clips : 3 * clips]
    outs = refs[3 * clips : -1]
    turned = refs[-1]
    height, width = lefts[0].shape
    frames = rights[0].shape[0]
    group = outs[0].shape[2]
    core = core_ref[0]

    def place(c, at):
        return pl.ds(pl.multiple_of(c * frames + at * height, 128), height)

    if turn_left:
        step = min(group, 512)
        for m, v in [(m, v) for m in range(len(outs)) for v in range(0, group, step)]:
            total = None
            for c in range(clips):
                if m == 0 and v == 0:
                    for j, at in ((0, core), (1, 1 - core)):
                        need(1 + 2 * c + j)
                        turned[:, place(c, at)] = jnp.transpose(lefts[2 * c + j][...])
                    need(1 + 2 * clips + c)
                part = nn(
                    turned[:, c * frames : (c + 1) * frames],
                    rights[c][:, m * group + v : m * group + v + step],
                )
                total = part if total is None else total + part
            outs[m][:, :, v : v + step] = total.astype(LOW).reshape(-1, outs[m].shape[1], step)
            if v + step == group:
                put(m)
    else:
        total = None
        for c in range(clips):
            need(1 + 2 * clips + c)
            turned[:, c * frames : (c + 1) * frames] = jnp.transpose(rights[c][...])
            for j, at in ((0, core), (1, 1 - core)):
                need(1 + 2 * c + j)
                part = nn(turned[:, place(c, at)], lefts[2 * c + j][...])
                total = part if total is None else total + part
        for m, out_ref in enumerate(outs):
            member = total[m * group : (m + 1) * group, :]
            out_ref[...] = jnp.transpose(member).astype(LOW).reshape(out_ref.shape)
            put(m)


def norm_rows_kernel(body, outs, operands, norm_rows, after, name="norm"):
    height, width = operands[0].shape
    operands = list(operands) + ([] if norm_rows is None else [norm_rows])
    nbytes = sum(nbytes_of(a.shape, a.dtype) for a in operands + list(outs))
    return pl.pallas_call(
        later(body, len(after), len(operands)),
        out_shape=tuple(pltpu.VMEM(o.shape, o.dtype) for o in outs),
        in_specs=[in_vmem()] * len(operands) + [anywhere()] * len(after),
        out_specs=tuple(in_vmem() for _ in outs),
        compiler_params=pltpu.CompilerParams(vmem_limit_bytes=12 << 20),
        cost_estimate=SMALL,
        name=name,
    )(*(hold(a, pltpu.VMEM) for a in operands), *after)


def equal_to(code, local):
    local = jnp.clip(local, -1.0, 256.0).astype(LOW)
    return jnp.where(code == local, jnp.asarray(1, LOW), jnp.asarray(0, LOW))


def embed_body(count, books, base_ref, *refs):
    packets, tables, outs = refs[:count], refs[count : len(refs) - count], refs[len(refs) - count :]
    features, vocab = tables[0].shape[1:]
    rows = outs[0].shape[0]
    padded = packets[0].shape[1]
    chunk = min(256, vocab)
    code = lax.broadcasted_iota(jnp.int32, (chunk, padded), 0).astype(F32).astype(LOW)
    for packet, out_ref in zip(packets, outs):
        lines = packet[...].astype(F32)
        acc = jnp.zeros((features, padded), F32)
        for k in range(books):
            for b, table in enumerate(tables):
                local = lines[k : k + 1, :] - base_ref[b].astype(F32)
                for v in range(0, vocab, chunk):
                    acc = acc + nn(table[k, :, v : v + chunk], equal_to(code, local - float(v)))
        out_ref[...] = jnp.transpose(acc)[:rows, :].astype(LOW)


def embed(base, packets, tables, rows, after):
    books, features = tables[0].shape[:2]
    count = len(packets)
    return pl.pallas_call(
        later(partial(embed_body, count, books), len(after), 1 + count + len(tables)),
        out_shape=[sds((rows, features), LOW)] * count,
        in_specs=[scalars()]
        + [in_vmem()] * (count + len(tables))
        + [anywhere()] * len(after),
        out_specs=[in_vmem()] * count,
        compiler_params=pltpu.CompilerParams(vmem_limit_bytes=16 << 20),
        cost_estimate=SMALL,
        name="embed",
    )(base, *packets, *tables, *after)


def embed_back_body(groups, base_ref, line_ref, *refs):
    grads, (out_ref, turned, columns) = refs[:groups], refs[groups:]
    rows, features = grads[0].shape
    vocab = out_ref.shape[3]
    chunk = min(256, vocab)
    total = line_ref.shape[1]

    @pl.when((pl.program_id(0) == 0) & (pl.program_id(1) == 0))
    def _():
        whole_rows = jnp.concatenate([g[...] for g in grads], axis=0)
        turned[...] = jnp.transpose(whole_rows)
        wide = jnp.concatenate(
            [line_ref[...].astype(F32), jnp.zeros((128 - line_ref.shape[0], total), F32)], axis=0
        )
        columns[...] = jnp.transpose(wide)

    base = base_ref[pl.program_id(0)].astype(F32)
    lane = lax.broadcasted_iota(jnp.int32, (total, 128), 1)
    column = jnp.sum(
        jnp.where(lane == pl.program_id(1), columns[...], 0.0), axis=1, keepdims=True
    )
    code = lax.broadcasted_iota(jnp.int32, (total, chunk), 1).astype(F32).astype(LOW)
    for v in range(0, vocab, chunk):
        hit = equal_to(code, column - (base + float(v)))
        out_ref[0, 0, :, v : v + chunk] = nn(turned[...], hit).astype(LOW)


def embed_back(base, lines, grads, books, vocab, after):
    parts = base.shape[0]
    groups = len(grads)
    rows, features = grads[0].shape
    return pl.pallas_call(
        later(partial(embed_back_body, groups), len(after), 2 + groups),
        out_shape=sds((parts, books, features, vocab), LOW),
        grid=(parts, books),
        in_specs=[scalars()] + [in_vmem()] * (1 + groups) + [anywhere()] * len(after),
        out_specs=pl.BlockSpec((1, 1, features, vocab), lambda i, k: (i, k, 0, 0)),
        scratch_shapes=[
            pltpu.VMEM((features, groups * rows), LOW),
            pltpu.VMEM((groups * rows, 128), F32),
        ],
        compiler_params=pltpu.CompilerParams(vmem_limit_bytes=32 << 20),
        cost_estimate=SMALL,
        name="embed_back",
    )(base, lines, *grads, *after)


def gather_features_body(need, put, where_ref, *refs):
    clips = sum(r.shape[1] != refs[0].shape[1] for r in refs)
    part_refs, outs = refs[:-clips], refs[-clips:]
    features = part_refs[0].shape[1]
    strip = outs[0].shape[0]
    for m, part in enumerate(part_refs):
        at = pl.ds(pl.multiple_of(where_ref[m] * features, features), features)
        for c, out_ref in enumerate(outs):
            out_ref[:, at] = part[c * strip : (c + 1) * strip, :]


def split_features_body(need, put, where_ref, side_ref, *refs):
    clips = side_ref.shape[0] - 1
    grads, outs = refs[:clips], refs[clips:]
    features = outs[0].shape[1]
    rows = outs[0].shape[0] // clips
    at_rows = pl.ds(pl.multiple_of(side_ref[0] * rows, rows), rows)
    need(*range(2, 2 + clips))
    for m, out_ref in reversed(list(enumerate(outs))):
        at = pl.ds(pl.multiple_of(where_ref[m] * features, features), features)
        for c in range(clips):
            out_ref[c * rows : (c + 1) * rows, :] = grads[c][at_rows, at]
        put(m)


def text_body(need, put, where_ref, *refs):
    *part_refs, wk_ref, wv_ref, tp_ref, k_ref, v_ref = refs
    columns = part_refs[0].shape[1]
    for m, part in enumerate(part_refs):
        need(1 + m)
        at = pl.ds(pl.multiple_of(where_ref[m] * columns, columns), columns)
        tp_ref[:, at] = part[...]
    put(0)
    for j, w_ref, to_ref in ((1, wk_ref, k_ref), (2, wv_ref, v_ref)):
        need(len(part_refs) + j)
        to_ref[...] = nn(tp_ref[...], flat(w_ref)).astype(LOW)
        put(j)


def text_back_body(clips, need, put, where_ref, *refs):
    dks, dvs = refs[:clips], refs[clips : 2 * clips]
    wk_ref, wv_ref, tp_ref = refs[2 * clips : 2 * clips + 3]
    *part_refs, gk_ref, gv_ref, full_ref = refs[2 * clips + 3 :]
    columns = part_refs[0].shape[1]
    length = dks[0].shape[0]
    need(*range(1, 1 + 2 * clips + 2))
    wk, wv = flat(wk_ref), flat(wv_ref)
    for c in range(clips):
        tp_rows = slice(c * length, (c + 1) * length)
        full_ref[tp_rows, :] = (nt(dks[c][...], wk) + nt(dvs[c][...], wv)).astype(LOW)
    for m, part_ref in enumerate(part_refs):
        at = pl.ds(pl.multiple_of(where_ref[m] * columns, columns), columns)
        part_ref[...] = full_ref[:, at]
    put(*range(len(part_refs)))
    need(3 + 2 * clips)
    turned = jnp.transpose(tp_ref[...])
    for j, grads, to_ref in ((0, dks, gk_ref), (1, dvs, gv_ref)):
        total = None
        for c in range(clips):
            part = nn(turned[:, c * length : (c + 1) * length], grads[c][...])
            total = part if total is None else total + part
        to_ref[...] = total.astype(LOW).reshape(to_ref.shape)
        put(len(part_refs) + j)


def text_weight_body(need, put, rows_ref, own_ref, far_ref, out_ref, bias_ref):
    need(0)
    grad = (own_ref[...].astype(F32) + far_ref[...].astype(F32)).astype(LOW)
    out_ref[...] = tn(rows_ref[...], grad).astype(LOW).reshape(out_ref.shape)
    bias_ref[...] = jnp.broadcast_to(
        jnp.sum(grad.astype(F32), axis=0, keepdims=True), bias_ref.shape
    )


def positions_rows(start, count, feature_count):
    half_width = feature_count // 2
    frequency = jnp.exp(
        jnp.arange(half_width, dtype=F32) * (-math.log(10000.0) / (half_width - 1))
    )
    angles = (start + jnp.arange(count, dtype=jnp.int32)).astype(F32)[:, None] * frequency[None, :]
    return jnp.concatenate([jnp.cos(angles), jnp.sin(angles)], axis=1)


def adam_update(weight, gradient, first_moment, second_moment, step_rate, factor):
    clipped = gradient * factor
    new_first = moment_decay * first_moment + (1.0 - moment_decay) * clipped
    new_second = moment_decay * second_moment + (1.0 - moment_decay) * clipped * clipped
    first_hat = new_first / (1.0 - moment_decay**STEP)
    second_hat = new_second / (1.0 - moment_decay**STEP)
    new_weight = weight * (1.0 - step_rate * weight_decay) - step_rate * first_hat / (
        jnp.sqrt(second_hat) + stability_offset
    )
    return (new_weight, new_first, new_second)


def swap(values, axis, mask):
    size = lax.axis_size(axis)
    return lax.ppermute(values, axis, [(i, i ^ mask) for i in range(size)])


def on_device(
    audio_codes,
    delay_mask,
    frame_mask,
    text_states,
    text_mask,
    attention,
    feedforward,
    tables,
    text_proj,
    norm_params,
    attention_first,
    attention_second,
    feedforward_first,
    feedforward_second,
    tables_first,
    tables_second,
    text_first,
    text_second,
    norm_first,
    norm_second,
):
    clips, frames, books = audio_codes.shape
    text_len, text_width = text_states.shape[1:]
    dp = lax.axis_size("dp")
    tensor = lax.axis_size("tensor")
    group = lax.axis_index("dp")
    place = lax.axis_index("tensor")
    core = place & 1
    side = place >> 1
    sides = tensor // 2
    height = frames // 2
    strip = height // sides
    share = attention.shape[1]
    columns = attention.shape[2]
    width = share * dp
    vocab = tables.shape[2]
    text_share = text_proj.shape[1]
    core_arg = Scalar(core.astype(jnp.int32).reshape(1))
    side_arg = Scalar(side.astype(jnp.int32).reshape(1))
    swap_core = partial(swap, axis="tensor", mask=1)

    def spread_tensor(values):
        held = [values]
        mask = tensor // 2
        order = [0]
        while mask:
            held = held + [swap(v, "tensor", mask) for v in held]
            order = order + [o | mask for o in order]
            mask //= 2
        return [v for _, v in sorted(zip(order, held), key=lambda t: t[0])]

    def collect_tensor(parts):
        mask = 1
        live = {m: p for m, p in enumerate(parts)}
        while mask < tensor:
            fresh = {}
            for m in live:
                if not m & mask:
                    got = swap(live[m | mask].astype(LOW), "tensor", mask)
                    fresh[m] = live[m].astype(F32) + got.astype(F32)
            live = fresh
            mask *= 2
        return live[0]

    def across(values):
        own = values
        mask = 2
        rest = None
        while mask < tensor:
            got = swap(own, "tensor", mask)
            mask *= 2
            if mask < tensor:
                own = (own.astype(F32) + got.astype(F32)).astype(LOW)
            rest = got
        if rest is None:
            rest = jnp.zeros_like(own)
        return own, rest

    def total_over(values, axes):
        for axis in axes:
            mask = 1
            while mask < lax.axis_size(axis):
                values = values + swap(values, axis, mask)
                mask *= 2
        return values

    last = []

    def run(body, outs, operands, after=(), **rest):
        *results, token = kernel(body, outs, operands, after=last + list(after), **rest)
        last[:] = [token]
        return results

    def run_block(*args, **rest):
        return run(*args, **rest)

    def run_weight(*args, **rest):
        results = run(*args, after=soon[:1], **rest)
        del soon[:1]
        return results

    norm_pad = jnp.pad(norm_params.astype(LOW), ((0, 16 - norm_params.shape[0]), (0, columns - share)))
    attn_rows = attention.astype(LOW)
    self_flat = jnp.concatenate([attn_rows[n] for n in SELF] + [norm_pad], axis=0)
    cross_flat = jnp.concatenate([attn_rows[n] for n in CROSS] + [text_proj.astype(LOW).T], axis=0)
    self_all = lax.all_gather(self_flat, "dp", axis=0)
    cross_all = lax.all_gather(cross_flat, "dp", axis=0)
    ffn_all = lax.all_gather(feedforward.astype(LOW), "dp", axis=0)
    head_all = lax.all_gather(tables[books:].astype(LOW), "dp", axis=0)

    frame_live = (jnp.arange(frames, dtype=jnp.int32) < frames - 1).astype(jnp.int32)
    weight_int = delay_mask * frame_mask[:, :, None] * frame_live[None, :, None]
    start = core * height + side * strip
    strip_codes = lax.dynamic_slice_in_dim(audio_codes, start, strip, 1)
    count = clips * strip
    padded = -(-count // 128) * 128
    lines = jnp.transpose(strip_codes, (2, 0, 1)).reshape(books, count)
    lines = jnp.pad(lines, ((0, 0), (0, padded - count)), constant_values=-1)
    count_line = jnp.broadcast_to(jnp.sum(weight_int), (8 - books, padded))
    packet = jnp.concatenate([lines, count_line], axis=0)
    packets = [packet] + [swap(packet, "dp", m) for m in range(1, dp)]
    vocab_base = (place ^ jnp.arange(tensor, dtype=jnp.int32)) * vocab
    group_order = group ^ jnp.arange(dp, dtype=jnp.int32)
    place_order = place ^ jnp.arange(tensor, dtype=jnp.int32)

    text_bias_row = jnp.where(text_mask > 0, 0.0, NEG).astype(F32)
    bias_lines = [text_bias_row[c : c + 1] for c in range(clips)]
    bias_columns = [jnp.transpose(line) for line in bias_lines]
    targets = (jnp.roll(audio_codes, -1, axis=1) - place * vocab).astype(jnp.int32)
    targets = [targets[c] for c in range(clips)]
    loss_weight = [weight_int[c].astype(F32) for c in range(clips)]
    placed = positions_rows(core * height, height, width)

    table_parts = spread_tensor(tables[:books].astype(LOW))
    step = max(1, dp // 4)
    arrived = [None] * dp
    for low_end in reversed(range(0, dp, step)):
        embedded = embed(
            vocab_base, packets[low_end : low_end + step], table_parts, count, list(last)
        )
        last[:] = [embedded[-1]]
        for m, piece in enumerate(embedded, low_end):
            arrived[m] = swap(piece, "dp", m) if m else piece
        last += [a for a in arrived[low_end + step : low_end + 2 * step] if a is not None]
    (counted,) = norm_rows_kernel(
        partial(count_body, books), [sds((8, 128), F32)], packets, None, last, name="count"
    )
    back_lines = jnp.concatenate([p[:, :count] for p in packets], axis=1)
    last[:] = bias_lines + bias_columns + targets + loss_weight + [placed, counted, back_lines]
    last += [a for a in arrived if a is not None]
    aligned = share % 128 == 0
    if aligned:
        strips = run(
            gather_features_body,
            [Flow(sds((strip, width), LOW))] * clips,
            [Scalar(group_order)] + arrived,
            name="gather_features",
        )
        strips = [free(a) for a in strips]
    else:
        strips = jnp.take(jnp.stack(arrived), group_order, axis=0)
        strips = jnp.transpose(strips, (1, 0, 2)).reshape(clips, strip, width)

    norm_rows = self_all[:, 4 * share :, :share]
    norm_rows = jnp.transpose(norm_rows, (1, 0, 2)).reshape(16, width).astype(F32)

    def w_attn(n):
        array, at = (self_all, SELF.index(n)) if n in SELF else (cross_all, CROSS.index(n))
        return Window(
            array, (dp, share, columns), lambda ref: ref.at[:, pl.ds(at * share, share), :]
        )

    def w_member(array, n):
        return Window(array, (dp,) + array.shape[2:], lambda ref: ref.at[:, n])

    half_sds = sds((height, width), F32)
    half_low = sds((height, width), LOW)
    flow = Flow(half_low)

    def fetch(a):
        return Window(a, a.shape, everything)


    def norm_step(which, hidden, parts):
        new, out = norm_rows_kernel(
            partial(norm_body, which),
            [half_sds, half_low],
            [hidden, *parts],
            norm_rows,
            last + soon,
        )
        soon[:] = []
        last[:] = [out]
        return new, (out, swap_core(free(out)))

    def norm_back(which, c, parts, before):
        rows = near.get((which, c, "back"), hidden[which][c])
        if before is not None:
            before = near_grad.get((which, c), before)
        operands = [rows, *parts] + ([before] if before is not None else [])
        new, out, sums = norm_rows_kernel(
            partial(norm_back_body, which, len(parts)),
            [half_sds, half_low, sds((8, width), F32)],
            operands,
            norm_rows,
            last + soon,
        )
        soon[:] = []
        last[:] = [out]
        return new, (out, swap_core(free(out))), free(sums)

    waiting, soon = [], []
    moving = [None] * clips

    def flush():
        if waiting:
            c, keep, got = waiting.pop()
            parts = norm_rows_kernel(
                add_parts_body,
                [sds((height * part // sum(PIECES), width), LOW) for part in PIECES],
                [keep, got],
                None,
                last,
                name="add",
            )
            last[:] = [parts[-1]]
            fars = [across(free(part))[1] for part in parts]
            moving[c] = (*parts, *fars)
            soon[:] = fars[:-1]

    def reduce_rows(c, keep, send):
        waiting.append((c, keep, swap_core(free(send))))

    text_rows = text_states.reshape(clips * text_len, text_width)
    def text_in_step():
        (result,) = run(
            text_in_body,
            [Flow(sds((clips * text_len, columns), LOW))],
            [
                Scalar(place.astype(jnp.int32).reshape(1)),
                norm_rows,
                fetch(text_rows),
                Window(
                    cross_all,
                    (dp, text_share, columns),
                    lambda ref: ref.at[:, pl.ds(4 * share, text_share), :],
                ),
            ],
            flops=2 * clips * text_len * text_width * columns,
            name="text_in",
        )
        return spread_tensor(free(result))

    full = sds((frames, columns), LOW)
    lse_sds = sds((8, frames), F32)
    tot = [pltpu.VMEM((frames, 128), F32)]
    heads = columns // HEAD_DIM
    score_flops = 2 * heads * frames * HEAD_DIM
    units = feedforward.shape[2]
    inner = sds((frames, units), LOW)
    every = range(clips)

    near, near_grad = {}, {}

    def ahead(phase, c):
        at, clip = (phase - 1, c + 1) if c + 1 < clips else (phase, 0)
        if at < 0 or (phase == 3 and clip == 0) or (clip == c):
            return []
        return [Ahead(hidden[at][clip])]

    def took(phase, c, results):
        at, clip = (phase - 1, c + 1) if c + 1 < clips else (phase, 0)
        if ahead(phase, c):
            *results, near[at, clip] = results
        return results

    def ahead_back(phase, c):
        at, clip = (phase, c + 1) if c + 1 < clips else (phase - 1, 0)
        if clip == c:
            return []
        found = [Ahead(hidden[at][clip])]
        if at < 3:
            found.append(Ahead(grads[clip]))
        return found

    def took_back(phase, c, results):
        at, clip = (phase, c + 1) if c + 1 < clips else (phase - 1, 0)
        count = len(ahead_back(phase, c))
        if count == 2:
            near_grad[at, clip] = results[-1]
        if count:
            near[at, clip, "back"] = results[len(results) - count]
        return results[: len(results) - count]

    def embed_step(c):
        mine = strips[c]
        parts = [mine] + [swap(mine, "tensor", 2 * s) for s in range(1, sides)]
        new, out = run(
            embed_norm_body,
            [Flow(half_sds), Flow(half_low)],
            [side_arg, placed, norm_rows] + parts,
            flops=10 * height * width,
            name="embed_norm",
        )
        return new, (out, swap_core(free(out)))

    def self_step(c, pair):
        own, got = pair
        *saved, keep, send, left, right, hidden[0][c] = took(0, c, run_block(
            self_forward_body,
            [full, full, full, full, lse_sds, flow, flow, Copy(1), Copy(3)],
            [core_arg, own, w_attn(0), got, w_attn(1), w_attn(2), w_attn(6)]
            + [Carry(hidden[0][c])]
            + ahead(0, c),
            flops=8 * frames * width * columns + 4 * score_flops * frames,
            scratch=tot,
            name="self_forward",
        ))
        pairs[0][c] = (left, right)
        reduce_rows(c, keep, send)
        return saved

    text_full = sds((clips * text_len, width), LOW)
    text_cols = sds((clips * text_len, columns), LOW)

    def text_step():
        return run(
            text_body,
            [text_full, text_cols, text_cols],
            [Scalar(place_order)] + text_parts + [w_attn(4), w_attn(5)],
            flops=4 * clips * text_len * width * columns,
            name="text",
        )

    def text_rows_of(array, c):
        return Window(
            array, (text_len, columns), lambda ref: ref.at[pl.ds(c * text_len, text_len), :]
        )

    def cross_step(c, pair):
        own, got = pair
        k, v = text_rows_of(text_key, c), text_rows_of(text_value, c)
        q, o, lse, keep, send, left, right, hidden[1][c] = took(1, c, run_block(
            cross_forward_body,
            [full, full, lse_sds, flow, flow, Copy(1), Copy(3)],
            [core_arg, own, w_attn(3), got, bias_lines[c], k, v, w_attn(7)]
            + [Carry(hidden[1][c])]
            + ahead(1, c),
            flops=4 * frames * width * columns + 4 * score_flops * text_len,
            scratch=tot,
            name="cross_forward",
        ))
        pairs[1][c] = (left, right)
        reduce_rows(c, keep, send)
        return (q, k, v, o, lse)

    def ffn_step(c, pair):
        *saved, keep, send, left, right, hidden[2][c] = took(2, c, run_block(
            ffn_forward_body,
            [inner, inner, flow, flow, Copy(1), Copy(2)],
            [core_arg, *pair, w_member(ffn_all, 0), w_member(ffn_all, 1), Carry(hidden[2][c])]
            + ahead(2, c),
            flops=4 * frames * width * units,
            name="ffn_forward",
        ))
        pairs[2][c] = (left, right)
        reduce_rows(c, keep, send)
        return saved

    hidden = [[None] * clips for _ in range(4)]
    pairs = [[None] * clips for _ in range(4)]
    kept = [[None] * clips for _ in range(3)]
    for c in every:
        hidden[0][c], pairs[0][c] = embed_step(c)
        flush()
        kept[0][c] = self_step(c, pairs[0][c])
        if c == 0:
            text_parts = text_in_step()
    text_hidden, text_key, text_value = text_step()
    for c in every:
        hidden[1][c], pairs[1][c] = norm_step(1, near.get((0, c), hidden[0][c]), moving[c])
        flush()
        kept[1][c] = cross_step(c, pairs[1][c])
    for c in every:
        hidden[2][c], pairs[2][c] = norm_step(2, near.get((1, c), hidden[1][c]), moving[c])
        flush()
        kept[2][c] = ffn_step(c, pairs[2][c])

    loss_part = [None] * clips
    sums = [[], [], [], []]

    def head_step(c, pair):
        own, got = pair
        logits, stats, left, right, hidden[3][c] = took(3, c, run_block(
            head_forward_body,
            [
                sds((frames, books * vocab), F32),
                Flow(sds((2 * books, frames), F32)),
                Copy(1),
                Copy(3),
            ],
            [core_arg, own, targets[c], got]
            + [w_member(head_all, k) for k in range(books)]
            + [Carry(hidden[3][c])]
            + ahead(3, c),
            flops=2 * frames * width * books * vocab,
            scratch=tot,
            name="head_forward",
        ))
        pairs[3][c] = (left, right)
        return logits, stats

    def merge_step(stats):
        mask = 1
        while mask < tensor:
            far = swap(free(stats), "tensor", mask)
            (stats,) = norm_rows_kernel(
                partial(merge_body, books),
                [sds((2 * books, frames), F32)],
                [stats, far],
                None,
                last,
                name="merge",
            )
            last[:] = [stats]
            mask *= 2
        return stats

    def head_back_step(c, logits, stats):
        grad, keep, send, loss = run_block(
            head_backward_body,
            [sds((frames, books * vocab), LOW), flow, flow, Flow(sds((8, 128), F32))],
            [core_arg, stats, loss_weight[c], targets[c], fetch(logits)]
            + [w_member(head_all, k) for k in range(books)]
            + [counted],
            flops=2 * frames * width * books * vocab,
            scratch=tot,
            name="head_backward",
        )
        loss_part[c] = free(loss)[0, 0]
        reduce_rows(c, keep, send)
        return grad

    self_shared = Shared((dp, 4 * share + text_share, columns), LOW)
    cross_shared = Shared((dp, 4 * share, columns), LOW)
    ffn_shared = Shared((dp,) + feedforward.shape, LOW)
    head_shared = Shared((dp, books, share, vocab), LOW)

    def attn_into(n):
        shared, at = (
            (self_shared, SELF.index(n)) if n in SELF else (cross_shared, CROSS.index(n))
        )
        return Into(
            shared, (dp, share, columns), lambda ref: ref.at[:, pl.ds(at * share, share), :]
        )

    def member_into(shared, n):
        return Into(shared, (dp,) + shared.full.shape[2:], lambda ref: ref.at[:, n])

    def weights(lefts, rights, outs, name):
        total = rights[0].shape[1]
        turn_left = 2 * total > width
        run_weight(
            partial(weight_grad_body, clips, turn_left),
            outs,
            [core_arg] + [fetch(half) for pair in lefts for half in pair] + [fetch(a) for a in rights],
            flops=2 * clips * frames * width * total,
            scratch=[pltpu.VMEM((width if turn_left else total, clips * frames), LOW)],
            name=name,
            margin=16,
        )

    logit_grads = [None] * clips
    ready = [None] * clips
    for c in every:
        hidden[3][c], pairs[3][c] = norm_step(3, near.get((2, c), hidden[2][c]), moving[c])
        flush()
        ready[c] = head_step(c, pairs[3][c])
        if c:
            flush()
            logits, stats = ready[c - 1]
            logit_grads[c - 1] = head_back_step(c - 1, logits, merge_step(stats))
    logits, stats = ready[-1]
    stats = merge_step(stats)
    flush()
    logit_grads[-1] = head_back_step(clips - 1, logits, stats)

    def ffn_back_step(c, pair):
        own, got = pair
        grad, keep, send, left, right, grads[c] = took_back(3, c, run_block(
            ffn_backward_body,
            [inner, flow, flow, Copy(1), Copy(2)],
            [core_arg, own, got, w_member(ffn_all, 1), fetch(kept[2][c][1]), w_member(ffn_all, 0)]
            + [Carry(grads[c])]
            + ahead_back(3, c),
            flops=4 * frames * width * units,
            name="ffn_backward",
        ))
        back_pairs[3][c] = (left, right)
        reduce_rows(c, keep, send)
        return grad

    grads = [None] * clips
    back_pairs = [[None] * clips for _ in range(4)]
    inner_grads = [None] * clips
    for c in every:
        grads[c], back_pairs[3][c], s = norm_back(3, c, moving[c], None)
        sums[3].append(s)
        flush()
        inner_grads[c] = ffn_back_step(c, back_pairs[3][c])
        if c == 0:
            head_into = [member_into(head_shared, k) for k in range(books)]
            weights(pairs[3], logit_grads, head_into, "head_weights")
    head_sum = lax.psum_scatter(free(head_shared.array), "dp", scatter_dimension=0, tiled=False)

    acc_text = [pltpu.VMEM((text_len, columns), F32)] * 2
    small = sds((text_len, columns), LOW)

    def cross_back_step(c, pair):
        own, got = pair
        q, k, v, o, lse = kept[1][c]
        bias = bias_columns[c]
        dq, dk, dv, keep, send, left, right, grads[c] = took_back(2, c, run_block(
            cross_backward_body,
            [full, small, small, flow, flow, Copy(1), Copy(3)],
            [core_arg, own, w_attn(7), got, bias, fetch(q), k, v, fetch(lse), w_attn(3)]
            + [Carry(grads[c])]
            + ahead_back(2, c),
            flops=4 * frames * width * columns + 10 * score_flops * text_len,
            scratch=[pltpu.VMEM((frames, columns), LOW)] + acc_text,
            name="cross_backward",
        ))
        back_pairs[2][c] = (left, right)
        reduce_rows(c, keep, send)
        return (dq, dk, dv)

    cross_grads = [None] * clips
    for c in every:
        grads[c], back_pairs[2][c], s = norm_back(2, c, moving[c], grads[c])
        sums[2].append(s)
        flush()
        cross_grads[c] = cross_back_step(c, back_pairs[2][c])
        if c == 0:
            weights(
                back_pairs[3], [k[0] for k in kept[2]], [member_into(ffn_shared, 1)], "ffn_two"
            )
        if c == min(1, clips - 1):
            weights(pairs[2], inner_grads, [member_into(ffn_shared, 0)], "ffn_one")
    ffn_sum = lax.psum_scatter(free(ffn_shared.array), "dp", scatter_dimension=0, tiled=False)

    def text_back_step():
        results = run(
            partial(text_back_body, clips),
            [Flow(text_cols)] * tensor + [attn_into(4), attn_into(5)],
            [Scalar(place_order)]
            + [fetch(g[1]) for g in cross_grads]
            + [fetch(g[2]) for g in cross_grads]
            + [w_attn(4), w_attn(5), fetch(text_hidden)],
            flops=8 * clips * text_len * width * columns,
            scratch=[pltpu.VMEM((clips * text_len, width), LOW)],
            name="text_back",
        )
        live = dict(enumerate(results))
        mask = 1
        while mask < tensor:
            fresh = {}
            for m in live:
                if not m & mask:
                    fresh[m] = (live[m], swap(free(live[m | mask]), "tensor", mask))
            mask *= 2
            if mask < tensor:
                for m, both in fresh.items():
                    (fresh[m],) = norm_rows_kernel(
                        add_body, [text_cols], list(both), None, last, name="add"
                    )
                    last[:] = [fresh[m]]
            live = fresh
        return live[0]

    acc_self = [pltpu.VMEM((frames, columns), F32)] * 2

    def self_back_step(c, pair):
        own, got = pair
        q, k, v, o, lse = kept[0][c]
        grad, keep, send, left, right, grads[c] = took_back(1, c, run_block(
            self_backward_body,
            [sds((frames, 3 * columns), LOW), flow, flow, Copy(1), Copy(3)],
            [core_arg, own, w_attn(6), got]
            + [fetch(a) for a in (q, k, v, lse)]
            + [w_attn(0), w_attn(1), w_attn(2), Carry(grads[c])]
            + ahead_back(1, c),
            flops=8 * frames * width * columns + 10 * score_flops * frames,
            scratch=[pltpu.VMEM((frames, columns), LOW)] + acc_self,
            name="self_backward",
        ))
        back_pairs[1][c] = (left, right)
        reduce_rows(c, keep, send)
        return grad

    self_grads = [None] * clips
    last.append(head_sum)
    for c in every:
        grads[c], back_pairs[1][c], s = norm_back(1, c, moving[c], grads[c])
        sums[1].append(s)
        flush()
        self_grads[c] = self_back_step(c, back_pairs[1][c])
        if c == 0:
            text_grad = text_back_step()
            weights(back_pairs[2], [k[3] for k in kept[1]], [attn_into(7)], "cross_out")
        if c == min(1, clips - 1):
            weights(pairs[1], [g[0] for g in cross_grads], [attn_into(3)], "cross_query")
            cross_sum = lax.psum_scatter(
                free(cross_shared.array), "dp", scatter_dimension=0, tiled=False
            )

    zero_lows = [None] * clips

    def zero_step(c):
        _, (zero_lows[c], _), s = norm_back(0, c, moving[c], grads[c])
        sums[0].append(s)

    zero_step(0)
    flush()
    text_into = Into(
        self_shared,
        (dp, text_share, columns),
        lambda ref: ref.at[:, pl.ds(4 * share, text_share), :],
    )
    (bias_grad,) = run(
        text_weight_body,
        [text_into, Flow(sds((8, columns), F32))],
        [fetch(text_rows), *text_grad],
        after=[ffn_sum],
        flops=2 * clips * text_len * text_width * columns,
        name="text_weight",
    )
    weights(back_pairs[1], [k[3] for k in kept[0]], [attn_into(6)], "self_out")
    for c in range(1, clips):
        zero_step(c)

    if aligned:
        pieces = list(map(free, run(
            split_features_body,
            [Flow(sds((clips * strip, share), LOW))] * dp,
            [
                Scalar(group_order),
                Scalar(jnp.broadcast_to(side.astype(jnp.int32), (clips + 1,))),
            ]
            + zero_lows,
            after=[cross_sum],
            name="split_features",
        )))
    else:
        rows = jnp.concatenate(
            [lax.dynamic_slice_in_dim(free(a), side * strip, strip, 0) for a in zero_lows], axis=0
        )
        rows = jnp.transpose(rows.reshape(clips * strip, dp, share), (1, 0, 2))
        pieces = list(jnp.take(rows, group_order, axis=0))
    weights(pairs[0], self_grads, [attn_into(n) for n in range(3)], "self_in")
    self_sum = lax.psum_scatter(free(self_shared.array), "dp", scatter_dimension=0, tiled=False)
    rows_all = [pieces[0]] + [swap(pieces[m], "dp", m) for m in range(1, dp)]
    embed_parts = embed_back(vocab_base, back_lines, rows_all, books, vocab, list(last))
    grad_embed = collect_tensor([embed_parts[m] for m in range(tensor)])

    norm_part = jnp.concatenate(
        [sum(s)[0:1] for s in sums] + [sum(s)[1:2] for s in sums], axis=0
    ) * (1.0 / sides)
    bias_row = lax.dynamic_update_slice_in_dim(
        jnp.zeros((width,), F32), free(bias_grad)[0], place * columns, 0
    )
    norm_total = total_over(
        jnp.concatenate([norm_part, bias_row[None]], axis=0), ("tensor", "dp")
    )
    grad_norm_rows = lax.dynamic_slice_in_dim(norm_total, group * share, share, 1)

    own_self = self_sum[: 4 * share].reshape(4, share, columns)
    own_cross = cross_sum.reshape(4, share, columns)
    grad_attention = jnp.concatenate(
        [own_self[:3], own_cross[:3], own_self[3:], own_cross[3:]], axis=0
    ).astype(F32)
    grad_text_proj = jnp.transpose(self_sum[4 * share :]).astype(F32)
    grad_feedforward = ffn_sum.astype(F32)
    grad_heads = head_sum.astype(F32)
    local_square = (
        jnp.sum(jnp.square(self_sum.astype(F32)))
        + jnp.sum(jnp.square(cross_sum.astype(F32)))
        + jnp.sum(grad_feedforward * grad_feedforward)
        + jnp.sum(grad_heads * grad_heads)
        + jnp.sum(grad_embed * grad_embed)
        + jnp.sum(grad_norm_rows * grad_norm_rows) / tensor
    )
    both = total_over(
        jnp.stack([local_square, sum(loss_part) / tensor]).reshape(1, 2), ("tensor", "dp")
    )[0]
    grad_norm = jnp.sqrt(both[0])
    mean_loss = both[1]
    factor = clip_limit / jnp.maximum(grad_norm, clip_limit)
    grad_tables = jnp.concatenate([grad_embed, grad_heads], 0)
    attn_new, attn_first_new, attn_second_new = adam_update(
        attention, grad_attention, attention_first, attention_second, rate_matrix, factor
    )
    ffn_new, ffn_first_new, ffn_second_new = adam_update(
        feedforward, grad_feedforward, feedforward_first, feedforward_second, rate_matrix, factor
    )
    table_new, table_first_new, table_second_new = adam_update(
        tables, grad_tables, tables_first, tables_second, rate_table, factor
    )
    text_new, text_first_new, text_second_new = adam_update(
        text_proj, grad_text_proj, text_first, text_second, rate_matrix, factor
    )
    norm_new, norm_first_new, norm_second_new = adam_update(
        norm_params, grad_norm_rows, norm_first, norm_second, rate_norm, factor
    )
    return (
        mean_loss,
        free(counted)[0, 0],
        grad_norm,
        attn_new,
        attn_new.astype(LOW),
        attn_first_new,
        attn_second_new,
        ffn_new,
        ffn_new.astype(LOW),
        ffn_first_new,
        ffn_second_new,
        table_new,
        table_new.astype(LOW),
        table_first_new,
        table_second_new,
        text_new,
        text_new.astype(LOW),
        text_first_new,
        text_second_new,
        norm_new,
        norm_first_new,
        norm_second_new,
    )


def solution(mesh):
    clip3 = P("dp", None, None)
    clip2 = P("dp", None)
    matrix = P(None, "dp", "tensor")
    text = P("tensor", "dp")
    norm = P(None, "dp")
    placed = (
        (clip3, clip3, clip2, clip3, clip2)
        + (matrix, matrix, matrix, text, norm)
        + (matrix,) * 6
        + (text, text, norm, norm)
    )
    return jax.shard_map(
        on_device,
        mesh=mesh,
        in_specs=placed,
        out_specs=(P(), P(), P()) + (matrix,) * 12 + (text,) * 4 + (norm,) * 3,
        check_vma=False,
    )
```

```python
from functools import partial
import math

import jax
import jax.numpy as jnp
from jax import lax
from jax.experimental import pallas as pl
from jax.experimental.pallas import tpu as pltpu
from jax.sharding import PartitionSpec as P

HEAD_DIM = 64
STEP = 5
BLOCK = 256
NEG = -1e30
LOW = jnp.bfloat16
F32 = jnp.float32

SELF = (0, 1, 2, 6)
CROSS = (3, 4, 5, 7)

SMALL = pl.CostEstimate(flops=1024, bytes_accessed=1024, transcendentals=0)

PIECES = (1, 1)

clip_limit = 0.004
stability_offset = 1e-08
weight_decay = 0.01
moment_decay = 0.5
rate_matrix = 0.03
rate_table = 0.05
rate_norm = 0.2


def nn(a, b):
    return lax.dot_general(a, b, (((1,), (0,)), ((), ())), preferred_element_type=F32)


def nt(a, b):
    return lax.dot_general(a, b, (((1,), (1,)), ((), ())), preferred_element_type=F32)


def tn(a, b):
    return lax.dot_general(a, b, (((0,), (0,)), ((), ())), preferred_element_type=F32)


def sds(shape, kind):
    return jax.ShapeDtypeStruct(shape, kind)


def scalars():
    return pl.BlockSpec(memory_space=pltpu.SMEM)


def anywhere():
    return pl.BlockSpec(memory_space=pl.ANY)


def in_hbm():
    return pl.BlockSpec(memory_space=pltpu.HBM)


def in_vmem():
    return pl.BlockSpec(memory_space=pltpu.VMEM)


def whole(a):
    rank = len(a.shape)
    return pl.BlockSpec(a.shape, lambda i: (0,) * rank)


def later(body, count, at):
    def ordered(*refs):
        return body(*refs[:at], *refs[at + count :])

    return ordered


class Scalar:
    def __init__(self, array):
        self.array = array


class Window:
    def __init__(self, array, shape, pick):
        self.array, self.shape, self.pick = array, tuple(shape), pick


def hold(array, space):
    return pltpu.with_memory_space_constraint(array, space)


def free(array):
    return pltpu.with_memory_space_constraint(array, pl.ANY)


class Flow:
    def __init__(self, shape):
        self.shape = shape


class Copy:
    def __init__(self, i):
        self.i = i


class Carry:
    def __init__(self, array):
        self.array = array


class Ahead:
    def __init__(self, array):
        self.array = array


class Shared:
    def __init__(self, shape, kind):
        self.full, self.array = sds(shape, kind), None


class Into:
    def __init__(self, shared, shape, pick):
        self.shared, self.shape, self.pick = shared, tuple(shape), pick


def everything(ref):
    return ref


def nbytes_of(shape, kind):
    return math.prod(shape) * jnp.dtype(kind).itemsize


def kernel(body, outs, operands, flops=0, scratch=(), name=None, exps=0, after=(), margin=12):
    arrays, specs, windows, shown, fetched = [], [], [], [], {}
    outs = list(outs)
    for i, a in enumerate(operands):
        shown.append(not isinstance(a, (Carry, Ahead)))
        if isinstance(a, Ahead):
            arrays.append(hold(a.array, pltpu.HBM))
            specs.append(in_hbm())
            windows.append(None)
            outs.append(Flow(sds(a.array.shape, a.array.dtype)))
            fetched[len(outs) - 1] = i
        elif isinstance(a, Carry):
            arrays.append(hold(a.array, pltpu.VMEM))
            specs.append(in_vmem())
            windows.append(None)
            outs.append(Copy(i))
        elif isinstance(a, Scalar):
            arrays.append(a.array)
            specs.append(scalars())
            windows.append(None)
        elif isinstance(a, Window):
            arrays.append(hold(a.array, pltpu.HBM))
            specs.append(in_hbm())
            windows.append(a)
        else:
            arrays.append(hold(a, pltpu.VMEM))
            specs.append(in_vmem())
            windows.append(None)
    aliases, out_shapes, out_specs, out_parts, owners = {}, [], [], [], []
    extra = []
    for o in outs:
        if isinstance(o, Into):
            if o.shared not in owners:
                if o.shared.array is not None:
                    aliases[len(arrays) + len(extra)] = len(out_shapes)
                    extra.append(o.shared.array)
                out_shapes.append(pltpu.HBM(o.shared.full.shape, o.shared.full.dtype))
                out_specs.append(in_hbm())
                owners.append(o.shared)
            out_parts.append(("put", o.shape, o.shared.full.dtype, o.pick, owners.index(o.shared)))
            continue
        if isinstance(o, Flow):
            out_parts.append(("flow", None, None, None, len(out_shapes)))
            out_shapes.append(pltpu.VMEM(o.shape.shape, o.shape.dtype))
            out_specs.append(in_vmem())
        elif isinstance(o, Copy):
            a = arrays[o.i]
            out_parts.append(("copy", o.i, None, None, len(out_shapes)))
            out_shapes.append(pltpu.HBM(a.shape, a.dtype))
            out_specs.append(in_hbm())
        else:
            out_parts.append(("put", o.shape, o.dtype, everything, len(out_shapes)))
            out_shapes.append(pltpu.HBM(o.shape, o.dtype))
            out_specs.append(in_hbm())
        owners.append(None)
    out_parts.append(("token", None, None, None, len(out_shapes)))
    out_shapes.append(pltpu.VMEM((8, 128), F32))
    out_specs.append(in_vmem())
    owners.append(None)
    moved = [w for w in windows if w is not None]
    made = [p for p in out_parts if p[0] == "put"]
    count_in, count_extra, count_after = len(arrays), len(extra), len(after)
    count_out, count_moved, count_arrays = len(out_parts), len(moved), len(out_shapes)

    def run_body(*refs):
        refs = list(refs)
        ins = refs[:count_in]
        at = count_in + count_extra + count_after
        out_refs = refs[at : at + count_arrays]
        at += count_arrays
        in_buffers = refs[at : at + count_moved]
        at += count_moved
        made_buffers = refs[at : at + len(made)]
        at += len(made)
        in_sems, out_sems = refs[at], refs[at + 1]
        rest = refs[at + 2 :]
        views, copies, waited = [], {}, set()
        n = 0
        for i, (ref, w) in enumerate(zip(ins, windows)):
            if not shown[i]:
                continue
            if w is None:
                views.append(ref)
            else:
                copies[i] = pltpu.make_async_copy(w.pick(ref), in_buffers[n], in_sems.at[n])
                copies[i].start()
                views.append(in_buffers[n])
                n += 1
        sent, sources = {}, {}

        def need(*which):
            for i in which:
                if i in copies and i not in waited:
                    waited.add(i)
                    copies[i].wait()

        def put(*which):
            for j in which:
                if j in sources:
                    source, target = sources[j]
                    sent[j] = pltpu.make_async_copy(source, target, out_sems.at[j])
                    sent[j].start()

        body_outs = []
        n = 0
        for j, (kind, what, _, pick, owner) in enumerate(out_parts):
            if kind == "put":
                sources[j] = (made_buffers[n], pick(out_refs[owner]))
                body_outs.append(made_buffers[n])
                n += 1
            elif kind == "copy":
                sources[j] = (ins[what], out_refs[owner])
                put(j)
            elif kind == "token":
                out_refs[owner][...] = jnp.zeros((8, 128), F32)
            elif j in fetched:
                sources[j] = (ins[fetched[j]], out_refs[owner])
                put(j)
            else:
                body_outs.append(out_refs[owner])
        body(need, put, *views, *body_outs, *rest)
        need(*copies)
        put(*(j for j in sources if j not in sent))
        for copy in sent.values():
            copy.wait()

    nbytes = sum(nbytes_of(w.shape, w.array.dtype) for w in moved)
    nbytes += sum(nbytes_of(p[1], p[2]) for p in made)
    held = nbytes + sum(nbytes_of(m.shape, m.dtype) for m in scratch)
    results = pl.pallas_call(
        run_body,
        out_shape=tuple(out_shapes),
        in_specs=specs + [anywhere()] * (count_extra + count_after),
        out_specs=tuple(out_specs),
        input_output_aliases=aliases,
        scratch_shapes=[pltpu.VMEM(w.shape, w.array.dtype) for w in moved]
        + [pltpu.VMEM(p[1], p[2]) for p in made]
        + [
            pltpu.SemaphoreType.DMA((max(1, count_moved),)),
            pltpu.SemaphoreType.DMA((max(1, count_out),)),
        ]
        + list(scratch),
        compiler_params=pltpu.CompilerParams(vmem_limit_bytes=held + (margin << 20)),
        cost_estimate=SMALL,
        name=name,
    )(*arrays, *extra, *after)
    for owner, result in zip(owners, results):
        if owner is not None:
            owner.array = result
    return [r for owner, r in zip(owners, results) if owner is None]


def flat(ref):
    w = ref[...]
    return w.reshape(-1, w.shape[-1])


def half_rows(core, height):
    return (
        pl.ds(pl.multiple_of(core * height, height), height),
        pl.ds(pl.multiple_of((1 - core) * height, height), height),
    )


def attend_block(query, keys, values, head_masks, diagonal, bias):
    rows, width = query.shape
    lane = lax.broadcasted_iota(jnp.int32, (rows, 128), 1)
    column = lax.broadcasted_iota(jnp.int32, (rows, width), 1) // HEAD_DIM
    mixed = jnp.zeros((rows, width), F32)
    totals = jnp.zeros((rows, 128), F32)
    count = keys.shape[0]
    for h, mask in enumerate(head_masks):
        s = nt(query * mask, keys)
        if diagonal is not None:
            last = jnp.where(diagonal, s[:, count - rows :], NEG)
            s = last if count == rows else jnp.concatenate([s[:, : count - rows], last], axis=1)
        if bias is not None:
            s = s + bias
        top = jnp.max(s, axis=1, keepdims=True)
        e = jnp.exp(s - top)
        total = jnp.sum(e, axis=1, keepdims=True)
        p = (e * (1.0 / total)).astype(LOW)
        mixed = jnp.where(column == h, nn(p, values), mixed)
        totals = jnp.where(lane == h, top + jnp.log(total), totals)
    return mixed, totals


def masks_of(width):
    head = lax.broadcasted_iota(jnp.int32, (1, width), 1) // HEAD_DIM
    return [(head == h).astype(F32).astype(LOW) for h in range(width // HEAD_DIM)]


def triangle(size):
    row = lax.broadcasted_iota(jnp.int32, (size, size), 0)
    col = lax.broadcasted_iota(jnp.int32, (size, size), 1)
    return row >= col


def self_forward_body(
    need, put, core_ref, own_ref, wq_ref, got_ref, wk_ref, wv_ref, wo_ref,
    q_ref, k_ref, v_ref, o_ref, lse_ref, keep_ref, send_ref, tot_ref,
):
    height = own_ref.shape[0]
    frames, width = q_ref.shape
    mine, other = half_rows(core_ref[0], height)
    need(1)
    for i, w_ref, to_ref in ((2, wq_ref, q_ref), (4, wk_ref, k_ref), (5, wv_ref, v_ref)):
        need(i)
        w = flat(w_ref)
        to_ref[mine, :] = nn(own_ref[...], w).astype(LOW)
        need(3)
        to_ref[other, :] = nn(got_ref[...], w).astype(LOW)
    put(0, 1, 2)
    scale = jnp.asarray(HEAD_DIM**-0.5, LOW)
    head_masks = masks_of(width)
    diagonal = triangle(BLOCK)
    for i in range(frames // BLOCK):
        rows = slice(i * BLOCK, (i + 1) * BLOCK)
        mixed, totals = attend_block(
            q_ref[rows, :] * scale,
            k_ref[: (i + 1) * BLOCK, :],
            v_ref[: (i + 1) * BLOCK, :],
            head_masks,
            diagonal,
            None,
        )
        o_ref[rows, :] = mixed.astype(LOW)
        tot_ref[rows, :] = totals
    put(3)
    need(6)
    wo = flat(wo_ref)
    send_ref[...] = nt(o_ref[other, :], wo).astype(LOW)
    put(6)
    keep_ref[...] = nt(o_ref[mine, :], wo).astype(LOW)
    put(5)
    lse_ref[...] = jnp.transpose(tot_ref[...])[:8, :]


def cross_forward_body(
    need, put, core_ref, own_ref, wq_ref, got_ref, bias_ref, k_ref, v_ref, wo_ref,
    q_ref, o_ref, lse_ref, keep_ref, send_ref, tot_ref,
):
    height = own_ref.shape[0]
    frames, width = q_ref.shape
    mine, other = half_rows(core_ref[0], height)
    need(1, 2)
    w = flat(wq_ref)
    q_ref[mine, :] = nn(own_ref[...], w).astype(LOW)
    need(3)
    q_ref[other, :] = nn(got_ref[...], w).astype(LOW)
    put(0)
    scale = jnp.asarray(HEAD_DIM**-0.5, LOW)
    head_masks = masks_of(width)
    need(4, 5, 6)
    for i in range(frames // BLOCK):
        rows = slice(i * BLOCK, (i + 1) * BLOCK)
        mixed, totals = attend_block(
            q_ref[rows, :] * scale, k_ref[...], v_ref[...], head_masks, None, bias_ref[...]
        )
        o_ref[rows, :] = mixed.astype(LOW)
        tot_ref[rows, :] = totals
    put(1)
    need(7)
    wo = flat(wo_ref)
    send_ref[...] = nt(o_ref[other, :], wo).astype(LOW)
    put(4)
    keep_ref[...] = nt(o_ref[mine, :], wo).astype(LOW)
    put(3)
    lse_ref[...] = jnp.transpose(tot_ref[...])[:8, :]


def ffn_forward_body(
    need, put, core_ref, own_ref, got_ref, w1_ref, w2_ref,
    act_ref, slope_ref, keep_ref, send_ref,
):
    height = own_ref.shape[0]
    mine, other = half_rows(core_ref[0], height)
    need(1, 2, 3)
    w1 = flat(w1_ref)
    for j, source, rows, to_ref in (
        (3, got_ref, other, send_ref),
        (2, own_ref, mine, keep_ref),
    ):
        u = nn(source[...], w1)
        phi = 0.5 * (1.0 + lax.erf(u * (2.0**-0.5)))
        act = (u * phi).astype(LOW)
        density = jnp.exp(-0.5 * u * u) * ((2.0 * math.pi) ** -0.5)
        act_ref[rows, :] = act
        slope_ref[rows, :] = (phi + u * density).astype(LOW)
        need(4)
        to_ref[...] = nt(act, flat(w2_ref)).astype(to_ref.dtype)
        put(j)


def head_forward_body(
    need, put, core_ref, own_ref, target_ref, got_ref, *refs
):
    *w_refs, logits_ref, stats_ref, tot_ref = refs
    height = own_ref.shape[0]
    books = len(w_refs)
    vocab = w_refs[0].shape[2]
    halves = half_rows(core_ref[0], height)
    lane = lax.broadcasted_iota(jnp.int32, (height, 128), 1)
    code = lax.broadcasted_iota(jnp.int32, (height, vocab), 1)
    need(1, 2)
    totals = [jnp.zeros((height, 128), F32)] * 2
    for k, w_ref in enumerate(w_refs):
        need(4 + k)
        w = flat(w_ref)
        for j, (source, rows) in enumerate(zip((own_ref, got_ref), halves)):
            need(1 + 2 * j)
            s = nn(source[...], w)
            logits_ref[rows, k * vocab : (k + 1) * vocab] = s
            top = jnp.max(s, axis=1, keepdims=True)
            total = jnp.sum(jnp.exp(s - top), axis=1, keepdims=True)
            hit = code == target_ref[rows, k : k + 1]
            pick = jnp.sum(jnp.where(hit, s, 0.0), axis=1, keepdims=True)
            totals[j] = jnp.where(lane == k, top + jnp.log(total), totals[j])
            totals[j] = jnp.where(lane == books + k, pick, totals[j])
    put(0)
    for rows, t in zip(halves, totals):
        tot_ref[rows, :] = t
    stats_ref[...] = jnp.transpose(tot_ref[...])[: 2 * books, :]


def head_backward_body(
    need, put, core_ref, total_ref, weight_ref, target_ref, logits_ref, *refs
):
    *w_refs, valid_ref, grad_ref, keep_ref, send_ref, loss_ref, col_ref = refs
    height = keep_ref.shape[0]
    books = len(w_refs)
    vocab = w_refs[0].shape[2]
    mine, other = half_rows(core_ref[0], height)
    frames = logits_ref.shape[0]
    need(1, 2, 3)
    wide = jnp.concatenate(
        [total_ref[...], jnp.zeros((128 - total_ref.shape[0], frames), F32)], axis=0
    )
    col_ref[...] = jnp.transpose(wide)
    share = 1.0 / valid_ref[0:1, 0:1]
    gap = (col_ref[:, :books] - col_ref[:, books : 2 * books]) * (weight_ref[...] * share)
    loss_ref[...] = jnp.broadcast_to(jnp.sum(gap).reshape(1, 1), loss_ref.shape)
    code = lax.broadcasted_iota(jnp.int32, (height, vocab), 1)
    need(4)
    for j, rows, to_ref in ((2, other, send_ref), (1, mine, keep_ref)):
        weight = weight_ref[rows, :] * share
        total = col_ref[rows, :]
        acc = None
        for k, w_ref in enumerate(w_refs):
            s = logits_ref[rows, k * vocab : (k + 1) * vocab]
            p = jnp.exp(s - total[:, k : k + 1])
            hit = jnp.where(code == target_ref[rows, k : k + 1], 1.0, 0.0)
            g = ((p - hit) * weight[:, k : k + 1]).astype(LOW)
            grad_ref[rows, k * vocab : (k + 1) * vocab] = g
            need(5 + k)
            part = nt(g, flat(w_ref))
            acc = part if acc is None else acc + part
        to_ref[...] = acc.astype(to_ref.dtype)
        put(j)


def ffn_backward_body(
    need, put, core_ref, own_ref, got_ref, w2_ref, slope_ref, w1_ref,
    grad_ref, keep_ref, send_ref,
):
    height = own_ref.shape[0]
    mine, other = half_rows(core_ref[0], height)
    need(1, 2, 3, 4)
    w2 = flat(w2_ref)
    for j, source, rows, to_ref in (
        (2, got_ref, other, send_ref),
        (1, own_ref, mine, keep_ref),
    ):
        g = (nn(source[...], w2) * slope_ref[rows, :].astype(F32)).astype(LOW)
        grad_ref[rows, :] = g
        need(5)
        to_ref[...] = nt(g, flat(w1_ref)).astype(to_ref.dtype)
        put(j)


def attend_back(
    q, k, v, g, lse, head_masks, scale, diagonal, bias, dq_ref, rows, dk_ref, dv_ref, first
):
    count, width = k.shape
    step = q.shape[0]
    dq = jnp.zeros((step, width), F32)
    dk = jnp.zeros((count, width), F32)
    dv = jnp.zeros((count, width), F32)
    for h, mask in enumerate(head_masks):
        qm = q * mask
        gm = g * mask
        s = nt(k, qm)
        if diagonal is not None:
            last = jnp.where(diagonal, s[count - step :, :], NEG)
            s = last if count == step else jnp.concatenate([s[: count - step, :], last], axis=0)
        if bias is not None:
            s = s + bias
        p = jnp.exp(s - lse[h : h + 1, :])
        dp = nt(v, gm)
        inner = jnp.sum(p * dp, axis=0, keepdims=True)
        ds = (p * (dp - inner)).astype(LOW)
        dq = dq + tn(ds, k * mask)
        dk = dk + nn(ds, qm)
        dv = dv + nn(p.astype(LOW), gm)
    dq_ref[rows, :width] = (dq * scale).astype(LOW)
    dk_ref[:count, :] = dk if first else dk_ref[:count, :] + dk
    dv_ref[:count, :] = dv if first else dv_ref[:count, :] + dv


def self_backward_body(
    need, put, core_ref, own_ref, wo_ref, got_ref, q_ref, k_ref, v_ref, lse_ref,
    wq_ref, wk_ref, wv_ref, grad_ref, keep_ref, send_ref, g_ref, dk_acc, dv_acc,
):
    height = own_ref.shape[0]
    frames, width = q_ref.shape
    mine, other = half_rows(core_ref[0], height)
    need(1, 2)
    wo = flat(wo_ref)
    g_ref[mine, :] = nn(own_ref[...], wo).astype(LOW)
    need(3)
    g_ref[other, :] = nn(got_ref[...], wo).astype(LOW)
    scale = HEAD_DIM**-0.5
    head_masks = masks_of(width)
    row = lax.broadcasted_iota(jnp.int32, (BLOCK, BLOCK), 0)
    col = lax.broadcasted_iota(jnp.int32, (BLOCK, BLOCK), 1)
    diagonal = col >= row
    blocks = frames // BLOCK
    need(4, 5, 6, 7)
    for i in reversed(range(blocks)):
        rows = slice(i * BLOCK, (i + 1) * BLOCK)
        count = (i + 1) * BLOCK
        attend_back(
            q_ref[rows, :] * jnp.asarray(scale, LOW),
            k_ref[:count, :],
            v_ref[:count, :],
            g_ref[rows, :],
            lse_ref[:, rows],
            head_masks,
            scale,
            diagonal,
            None,
            grad_ref,
            rows,
            dk_acc,
            dv_acc,
            i == blocks - 1,
        )
    grad_ref[:, width : 2 * width] = dk_acc[...].astype(LOW)
    grad_ref[:, 2 * width :] = dv_acc[...].astype(LOW)
    put(0)
    need(8, 9, 10)
    for j, rows, to_ref in ((2, other, send_ref), (1, mine, keep_ref)):
        part = None
        for n, w_ref in enumerate((wq_ref, wk_ref, wv_ref)):
            term = nt(grad_ref[rows, n * width : (n + 1) * width], flat(w_ref))
            part = term if part is None else part + term
        to_ref[...] = part.astype(to_ref.dtype)
        put(j)


def cross_backward_body(
    need, put, core_ref, own_ref, wo_ref, got_ref, bias_ref, q_ref, k_ref, v_ref, lse_ref, wq_ref,
    dq_ref, dk_ref, dv_ref, keep_ref, send_ref, g_ref, dk_acc, dv_acc,
):
    height = own_ref.shape[0]
    frames, width = q_ref.shape
    mine, other = half_rows(core_ref[0], height)
    need(1, 2)
    wo = flat(wo_ref)
    g_ref[mine, :] = nn(own_ref[...], wo).astype(LOW)
    need(3)
    g_ref[other, :] = nn(got_ref[...], wo).astype(LOW)
    scale = HEAD_DIM**-0.5
    head_masks = masks_of(width)
    need(4, 5, 6, 7, 8)
    for i in range(frames // BLOCK):
        rows = slice(i * BLOCK, (i + 1) * BLOCK)
        attend_back(
            q_ref[rows, :] * jnp.asarray(scale, LOW),
            k_ref[...],
            v_ref[...],
            g_ref[rows, :],
            lse_ref[:, rows],
            head_masks,
            scale,
            None,
            bias_ref[...],
            dq_ref,
            rows,
            dk_acc,
            dv_acc,
            i == 0,
        )
    put(0)
    need(9)
    wq = flat(wq_ref)
    for j, rows, to_ref in ((4, other, send_ref), (3, mine, keep_ref)):
        to_ref[...] = nt(dq_ref[rows, :], wq).astype(to_ref.dtype)
        put(j)
    dk_ref[...] = dk_acc[...].astype(LOW)
    dv_ref[...] = dv_acc[...].astype(LOW)


def normalize(values, gain, shift):
    center = values - jnp.mean(values, axis=1, keepdims=True)
    spread = jnp.mean(center * center, axis=1, keepdims=True)
    return center * lax.rsqrt(spread + 1e-05) * gain + shift


def count_body(books, *refs):
    *packet_refs, out_ref = refs
    total = sum(p[books : books + 1, 0:128] for p in packet_refs)
    out_ref[...] = jnp.broadcast_to(total, out_ref.shape).astype(F32)


def merge_body(books, own_ref, far_ref, out_ref):
    own, far = own_ref[:books, :], far_ref[:books, :]
    high = jnp.maximum(own, far)
    out_ref[:books, :] = high + jnp.log(jnp.exp(own - high) + jnp.exp(far - high))
    out_ref[books:, :] = own_ref[books:, :] + far_ref[books:, :]


def text_in_body(need, put, place_ref, norm_ref, rows_ref, w_ref, out_ref):
    columns = out_ref.shape[1]
    at = pl.ds(pl.multiple_of(place_ref[0] * columns, columns), columns)
    need(2, 3)
    out_ref[...] = (nn(rows_ref[...], flat(w_ref)) + norm_ref[8:9, at]).astype(LOW)


def add_body(keep_ref, got_ref, out_ref):
    out_ref[...] = (keep_ref[...].astype(F32) + got_ref[...].astype(F32)).astype(LOW)


def add_parts_body(keep_ref, got_ref, *out_refs):
    start = 0
    for out_ref in out_refs:
        at = slice(start, start + out_ref.shape[0])
        start += out_ref.shape[0]
        out_ref[...] = (keep_ref[at, :].astype(F32) + got_ref[at, :].astype(F32)).astype(LOW)


def joined(refs):
    half = len(refs) // 2
    sums = [a[...].astype(F32) + b[...].astype(F32) for a, b in zip(refs[:half], refs[half:])]
    return jnp.concatenate(sums, axis=0)


def norm_body(which, hidden_ref, *refs):
    *part_refs, norm_ref, new_ref, out_ref = refs
    new = hidden_ref[...] + joined(part_refs)
    new_ref[...] = new
    out_ref[...] = normalize(
        new, norm_ref[which : which + 1, :], norm_ref[which + 4 : which + 5, :]
    ).astype(LOW)


def embed_norm_body(need, put, side_ref, place_ref, norm_ref, *refs):
    *part_refs, new_ref, out_ref = refs
    side = side_ref[0]
    rows = part_refs[0].shape[0]
    need(1, 2)
    for s, part in enumerate(part_refs):
        need(3 + s)
        at = pl.ds(pl.multiple_of((side ^ s) * rows, rows), rows)
        new = part[...].astype(F32) + place_ref[at, :]
        new_ref[at, :] = new
        out_ref[at, :] = normalize(new, norm_ref[0:1, :], norm_ref[4:5, :]).astype(LOW)
    put(1, 0)


def norm_back_body(which, parts, hidden_ref, *refs):
    *before, norm_ref, new_ref, low_ref, sums_ref = refs[parts:]
    sums = before.pop() if before and before[-1].shape[0] == sums_ref.shape[0] else None
    values = hidden_ref[...]
    grad = joined(refs[:parts])
    gain = norm_ref[which : which + 1, :]
    center = values - jnp.mean(values, axis=1, keepdims=True)
    spread = jnp.mean(center * center, axis=1, keepdims=True)
    inverse = lax.rsqrt(spread + 1e-05)
    unit = center * inverse
    scaled = grad * gain
    first = jnp.mean(scaled, axis=1, keepdims=True)
    second = jnp.mean(scaled * unit, axis=1, keepdims=True)
    new = inverse * (scaled - first - unit * second)
    if before:
        new = before[0][...] + new
    new_ref[...] = new
    low_ref[...] = new.astype(LOW)
    sums_ref[...] = jnp.zeros(sums_ref.shape, F32) if sums is None else sums[...]
    sums_ref[which : which + 1, :] += jnp.sum(grad * unit, axis=0, keepdims=True)
    sums_ref[which + 4 : which + 5, :] += jnp.sum(grad, axis=0, keepdims=True)


def weight_grad_body(clips, turn_left, need, put, core_ref, *refs):
    lefts = refs[: 2 * clips]
    rights = refs[2 * clips : 3 * clips]
    outs = refs[3 * clips : -1]
    turned = refs[-1]
    height, width = lefts[0].shape
    frames = rights[0].shape[0]
    group = outs[0].shape[2]
    core = core_ref[0]

    def place(c, at):
        return pl.ds(pl.multiple_of(c * frames + at * height, 128), height)

    if turn_left:
        step = min(group, 512)
        for m, v in [(m, v) for m in range(len(outs)) for v in range(0, group, step)]:
            total = None
            for c in range(clips):
                if m == 0 and v == 0:
                    for j, at in ((0, core), (1, 1 - core)):
                        need(1 + 2 * c + j)
                        turned[:, place(c, at)] = jnp.transpose(lefts[2 * c + j][...])
                    need(1 + 2 * clips + c)
                part = nn(
                    turned[:, c * frames : (c + 1) * frames],
                    rights[c][:, m * group + v : m * group + v + step],
                )
                total = part if total is None else total + part
            outs[m][:, :, v : v + step] = total.astype(LOW).reshape(-1, outs[m].shape[1], step)
            if v + step == group:
                put(m)
    else:
        total = None
        for c in range(clips):
            need(1 + 2 * clips + c)
            turned[:, c * frames : (c + 1) * frames] = jnp.transpose(rights[c][...])
            for j, at in ((0, core), (1, 1 - core)):
                need(1 + 2 * c + j)
                part = nn(turned[:, place(c, at)], lefts[2 * c + j][...])
                total = part if total is None else total + part
        for m, out_ref in enumerate(outs):
            member = total[m * group : (m + 1) * group, :]
            out_ref[...] = jnp.transpose(member).astype(LOW).reshape(out_ref.shape)
            put(m)


def norm_rows_kernel(body, outs, operands, norm_rows, after, name="norm"):
    height, width = operands[0].shape
    operands = list(operands) + ([] if norm_rows is None else [norm_rows])
    nbytes = sum(nbytes_of(a.shape, a.dtype) for a in operands + list(outs))
    return pl.pallas_call(
        later(body, len(after), len(operands)),
        out_shape=tuple(pltpu.VMEM(o.shape, o.dtype) for o in outs),
        in_specs=[in_vmem()] * len(operands) + [anywhere()] * len(after),
        out_specs=tuple(in_vmem() for _ in outs),
        compiler_params=pltpu.CompilerParams(vmem_limit_bytes=12 << 20),
        cost_estimate=SMALL,
        name=name,
    )(*(hold(a, pltpu.VMEM) for a in operands), *after)


def equal_to(code, local):
    local = jnp.clip(local, -1.0, 256.0).astype(LOW)
    return jnp.where(code == local, jnp.asarray(1, LOW), jnp.asarray(0, LOW))


def embed_body(count, books, base_ref, *refs):
    packets, tables, outs = refs[:count], refs[count : len(refs) - count], refs[len(refs) - count :]
    features, vocab = tables[0].shape[1:]
    rows = outs[0].shape[0]
    padded = packets[0].shape[1]
    chunk = min(256, vocab)
    code = lax.broadcasted_iota(jnp.int32, (chunk, padded), 0).astype(F32).astype(LOW)
    for packet, out_ref in zip(packets, outs):
        lines = packet[...].astype(F32)
        acc = jnp.zeros((features, padded), F32)
        for k in range(books):
            for b, table in enumerate(tables):
                local = lines[k : k + 1, :] - base_ref[b].astype(F32)
                for v in range(0, vocab, chunk):
                    acc = acc + nn(table[k, :, v : v + chunk], equal_to(code, local - float(v)))
        out_ref[...] = jnp.transpose(acc)[:rows, :].astype(LOW)


def embed(base, packets, tables, rows, after):
    books, features = tables[0].shape[:2]
    count = len(packets)
    return pl.pallas_call(
        later(partial(embed_body, count, books), len(after), 1 + count + len(tables)),
        out_shape=[sds((rows, features), LOW)] * count,
        in_specs=[scalars()]
        + [in_vmem()] * (count + len(tables))
        + [anywhere()] * len(after),
        out_specs=[in_vmem()] * count,
        compiler_params=pltpu.CompilerParams(vmem_limit_bytes=16 << 20),
        cost_estimate=SMALL,
        name="embed",
    )(base, *packets, *tables, *after)


def embed_back_body(groups, base_ref, line_ref, *refs):
    grads, (out_ref, turned, columns) = refs[:groups], refs[groups:]
    rows, features = grads[0].shape
    vocab = out_ref.shape[3]
    chunk = min(256, vocab)
    total = line_ref.shape[1]

    @pl.when((pl.program_id(0) == 0) & (pl.program_id(1) == 0))
    def _():
        whole_rows = jnp.concatenate([g[...] for g in grads], axis=0)
        turned[...] = jnp.transpose(whole_rows)
        wide = jnp.concatenate(
            [line_ref[...].astype(F32), jnp.zeros((128 - line_ref.shape[0], total), F32)], axis=0
        )
        columns[...] = jnp.transpose(wide)

    base = base_ref[pl.program_id(0)].astype(F32)
    lane = lax.broadcasted_iota(jnp.int32, (total, 128), 1)
    column = jnp.sum(
        jnp.where(lane == pl.program_id(1), columns[...], 0.0), axis=1, keepdims=True
    )
    code = lax.broadcasted_iota(jnp.int32, (total, chunk), 1).astype(F32).astype(LOW)
    for v in range(0, vocab, chunk):
        hit = equal_to(code, column - (base + float(v)))
        out_ref[0, 0, :, v : v + chunk] = nn(turned[...], hit).astype(LOW)


def embed_back(base, lines, grads, books, vocab, after):
    parts = base.shape[0]
    groups = len(grads)
    rows, features = grads[0].shape
    return pl.pallas_call(
        later(partial(embed_back_body, groups), len(after), 2 + groups),
        out_shape=sds((parts, books, features, vocab), LOW),
        grid=(parts, books),
        in_specs=[scalars()] + [in_vmem()] * (1 + groups) + [anywhere()] * len(after),
        out_specs=pl.BlockSpec((1, 1, features, vocab), lambda i, k: (i, k, 0, 0)),
        scratch_shapes=[
            pltpu.VMEM((features, groups * rows), LOW),
            pltpu.VMEM((groups * rows, 128), F32),
        ],
        compiler_params=pltpu.CompilerParams(vmem_limit_bytes=32 << 20),
        cost_estimate=SMALL,
        name="embed_back",
    )(base, lines, *grads, *after)


def gather_features_body(need, put, where_ref, *refs):
    clips = sum(r.shape[1] != refs[0].shape[1] for r in refs)
    part_refs, outs = refs[:-clips], refs[-clips:]
    features = part_refs[0].shape[1]
    strip = outs[0].shape[0]
    for m, part in enumerate(part_refs):
        at = pl.ds(pl.multiple_of(where_ref[m] * features, features), features)
        for c, out_ref in enumerate(outs):
            out_ref[:, at] = part[c * strip : (c + 1) * strip, :]


def split_features_body(need, put, where_ref, side_ref, *refs):
    clips = side_ref.shape[0] - 1
    grads, outs = refs[:clips], refs[clips:]
    features = outs[0].shape[1]
    rows = outs[0].shape[0] // clips
    at_rows = pl.ds(pl.multiple_of(side_ref[0] * rows, rows), rows)
    need(*range(2, 2 + clips))
    for m, out_ref in reversed(list(enumerate(outs))):
        at = pl.ds(pl.multiple_of(where_ref[m] * features, features), features)
        for c in range(clips):
            out_ref[c * rows : (c + 1) * rows, :] = grads[c][at_rows, at]
        put(m)


def text_body(need, put, where_ref, *refs):
    *part_refs, wk_ref, wv_ref, tp_ref, k_ref, v_ref = refs
    columns = part_refs[0].shape[1]
    for m, part in enumerate(part_refs):
        need(1 + m)
        at = pl.ds(pl.multiple_of(where_ref[m] * columns, columns), columns)
        tp_ref[:, at] = part[...]
    put(0)
    for j, w_ref, to_ref in ((1, wk_ref, k_ref), (2, wv_ref, v_ref)):
        need(len(part_refs) + j)
        to_ref[...] = nn(tp_ref[...], flat(w_ref)).astype(LOW)
        put(j)


def text_back_body(clips, need, put, where_ref, *refs):
    dks, dvs = refs[:clips], refs[clips : 2 * clips]
    wk_ref, wv_ref, tp_ref = refs[2 * clips : 2 * clips + 3]
    *part_refs, gk_ref, gv_ref, full_ref = refs[2 * clips + 3 :]
    columns = part_refs[0].shape[1]
    length = dks[0].shape[0]
    need(*range(1, 1 + 2 * clips + 2))
    wk, wv = flat(wk_ref), flat(wv_ref)
    for c in range(clips):
        tp_rows = slice(c * length, (c + 1) * length)
        full_ref[tp_rows, :] = (nt(dks[c][...], wk) + nt(dvs[c][...], wv)).astype(LOW)
    for m, part_ref in enumerate(part_refs):
        at = pl.ds(pl.multiple_of(where_ref[m] * columns, columns), columns)
        part_ref[...] = full_ref[:, at]
    put(*range(len(part_refs)))
    need(3 + 2 * clips)
    turned = jnp.transpose(tp_ref[...])
    for j, grads, to_ref in ((0, dks, gk_ref), (1, dvs, gv_ref)):
        total = None
        for c in range(clips):
            part = nn(turned[:, c * length : (c + 1) * length], grads[c][...])
            total = part if total is None else total + part
        to_ref[...] = total.astype(LOW).reshape(to_ref.shape)
        put(len(part_refs) + j)


def text_weight_body(need, put, rows_ref, own_ref, far_ref, out_ref, bias_ref):
    need(0)
    grad = (own_ref[...].astype(F32) + far_ref[...].astype(F32)).astype(LOW)
    out_ref[...] = tn(rows_ref[...], grad).astype(LOW).reshape(out_ref.shape)
    bias_ref[...] = jnp.broadcast_to(
        jnp.sum(grad.astype(F32), axis=0, keepdims=True), bias_ref.shape
    )


def positions_rows(start, count, feature_count):
    half_width = feature_count // 2
    frequency = jnp.exp(
        jnp.arange(half_width, dtype=F32) * (-math.log(10000.0) / (half_width - 1))
    )
    angles = (start + jnp.arange(count, dtype=jnp.int32)).astype(F32)[:, None] * frequency[None, :]
    return jnp.concatenate([jnp.cos(angles), jnp.sin(angles)], axis=1)


def adam_update(weight, gradient, first_moment, second_moment, step_rate, factor):
    clipped = gradient * factor
    new_first = moment_decay * first_moment + (1.0 - moment_decay) * clipped
    new_second = moment_decay * second_moment + (1.0 - moment_decay) * clipped * clipped
    first_hat = new_first / (1.0 - moment_decay**STEP)
    second_hat = new_second / (1.0 - moment_decay**STEP)
    new_weight = weight * (1.0 - step_rate * weight_decay) - step_rate * first_hat / (
        jnp.sqrt(second_hat) + stability_offset
    )
    return (new_weight, new_first, new_second)


def swap(values, axis, mask):
    size = lax.axis_size(axis)
    return lax.ppermute(values, axis, [(i, i ^ mask) for i in range(size)])


def on_device(
    audio_codes,
    delay_mask,
    frame_mask,
    text_states,
    text_mask,
    attention,
    feedforward,
    tables,
    text_proj,
    norm_params,
    attention_first,
    attention_second,
    feedforward_first,
    feedforward_second,
    tables_first,
    tables_second,
    text_first,
    text_second,
    norm_first,
    norm_second,
):
    clips, frames, books = audio_codes.shape
    text_len, text_width = text_states.shape[1:]
    dp = lax.axis_size("dp")
    tensor = lax.axis_size("tensor")
    group = lax.axis_index("dp")
    place = lax.axis_index("tensor")
    core = place & 1
    side = place >> 1
    sides = tensor // 2
    height = frames // 2
    strip = height // sides
    share = attention.shape[1]
    columns = attention.shape[2]
    width = share * dp
    vocab = tables.shape[2]
    text_share = text_proj.shape[1]
    core_arg = Scalar(core.astype(jnp.int32).reshape(1))
    side_arg = Scalar(side.astype(jnp.int32).reshape(1))
    swap_core = partial(swap, axis="tensor", mask=1)

    def spread_tensor(values):
        held = [values]
        mask = tensor // 2
        order = [0]
        while mask:
            held = held + [swap(v, "tensor", mask) for v in held]
            order = order + [o | mask for o in order]
            mask //= 2
        return [v for _, v in sorted(zip(order, held), key=lambda t: t[0])]

    def collect_tensor(parts):
        mask = 1
        live = {m: p for m, p in enumerate(parts)}
        while mask < tensor:
            fresh = {}
            for m in live:
                if not m & mask:
                    got = swap(live[m | mask].astype(LOW), "tensor", mask)
                    fresh[m] = live[m].astype(F32) + got.astype(F32)
            live = fresh
            mask *= 2
        return live[0]

    def across(values):
        own = values
        mask = 2
        rest = None
        while mask < tensor:
            got = swap(own, "tensor", mask)
            mask *= 2
            if mask < tensor:
                own = (own.astype(F32) + got.astype(F32)).astype(LOW)
            rest = got
        if rest is None:
            rest = jnp.zeros_like(own)
        return own, rest

    def total_over(values, axes):
        for axis in axes:
            mask = 1
            while mask < lax.axis_size(axis):
                values = values + swap(values, axis, mask)
                mask *= 2
        return values

    last = []

    def run(body, outs, operands, after=(), **rest):
        *results, token = kernel(body, outs, operands, after=last + list(after), **rest)
        last[:] = [token]
        return results

    def run_block(*args, **rest):
        return run(*args, **rest)

    def run_weight(*args, **rest):
        results = run(*args, after=older[:1] or soon[:1], **rest)
        if older:
            older.clear()
        else:
            soon.clear()
        return results

    norm_pad = jnp.pad(norm_params.astype(LOW), ((0, 16 - norm_params.shape[0]), (0, columns - share)))
    attn_rows = attention.astype(LOW)
    self_flat = jnp.concatenate([attn_rows[n] for n in SELF] + [norm_pad], axis=0)
    cross_flat = jnp.concatenate([attn_rows[n] for n in CROSS] + [text_proj.astype(LOW).T], axis=0)
    self_all = lax.all_gather(self_flat, "dp", axis=0)
    cross_all = lax.all_gather(cross_flat, "dp", axis=0)
    ffn_all = lax.all_gather(feedforward.astype(LOW), "dp", axis=0)
    head_all = lax.all_gather(tables[books:].astype(LOW), "dp", axis=0)

    frame_live = (jnp.arange(frames, dtype=jnp.int32) < frames - 1).astype(jnp.int32)
    weight_int = delay_mask * frame_mask[:, :, None] * frame_live[None, :, None]
    start = core * height + side * strip
    strip_codes = lax.dynamic_slice_in_dim(audio_codes, start, strip, 1)
    count = clips * strip
    padded = -(-count // 128) * 128
    lines = jnp.transpose(strip_codes, (2, 0, 1)).reshape(books, count)
    lines = jnp.pad(lines, ((0, 0), (0, padded - count)), constant_values=-1)
    count_line = jnp.broadcast_to(jnp.sum(weight_int), (8 - books, padded))
    packet = jnp.concatenate([lines, count_line], axis=0)
    packets = [packet] + [swap(packet, "dp", m) for m in range(1, dp)]
    vocab_base = (place ^ jnp.arange(tensor, dtype=jnp.int32)) * vocab
    group_order = group ^ jnp.arange(dp, dtype=jnp.int32)
    place_order = place ^ jnp.arange(tensor, dtype=jnp.int32)

    text_bias_row = jnp.where(text_mask > 0, 0.0, NEG).astype(F32)
    bias_lines = [text_bias_row[c : c + 1] for c in range(clips)]
    bias_columns = [jnp.transpose(line) for line in bias_lines]
    targets = (jnp.roll(audio_codes, -1, axis=1) - place * vocab).astype(jnp.int32)
    targets = [targets[c] for c in range(clips)]
    loss_weight = [weight_int[c].astype(F32) for c in range(clips)]
    placed = positions_rows(core * height, height, width)

    table_parts = spread_tensor(tables[:books].astype(LOW))
    step = max(1, dp // 4)
    arrived = [None] * dp
    for low_end in reversed(range(0, dp, step)):
        embedded = embed(
            vocab_base, packets[low_end : low_end + step], table_parts, count, list(last)
        )
        last[:] = [embedded[-1]]
        for m, piece in enumerate(embedded, low_end):
            arrived[m] = swap(piece, "dp", m) if m else piece
        last += [a for a in arrived[low_end + step : low_end + 2 * step] if a is not None]
    (counted,) = norm_rows_kernel(
        partial(count_body, books), [sds((8, 128), F32)], packets, None, last, name="count"
    )
    back_lines = jnp.concatenate([p[:, :count] for p in packets], axis=1)
    last[:] = bias_lines + bias_columns + targets + loss_weight + [placed, counted, back_lines]
    last += [a for a in arrived if a is not None]
    aligned = share % 128 == 0
    if aligned:
        strips = run(
            gather_features_body,
            [Flow(sds((strip, width), LOW))] * clips,
            [Scalar(group_order)] + arrived,
            name="gather_features",
        )
        strips = [free(a) for a in strips]
    else:
        strips = jnp.take(jnp.stack(arrived), group_order, axis=0)
        strips = jnp.transpose(strips, (1, 0, 2)).reshape(clips, strip, width)

    norm_rows = self_all[:, 4 * share :, :share]
    norm_rows = jnp.transpose(norm_rows, (1, 0, 2)).reshape(16, width).astype(F32)

    def w_attn(n):
        array, at = (self_all, SELF.index(n)) if n in SELF else (cross_all, CROSS.index(n))
        return Window(
            array, (dp, share, columns), lambda ref: ref.at[:, pl.ds(at * share, share), :]
        )

    def w_member(array, n):
        return Window(array, (dp,) + array.shape[2:], lambda ref: ref.at[:, n])

    half_sds = sds((height, width), F32)
    half_low = sds((height, width), LOW)
    flow = Flow(half_low)

    def fetch(a):
        return Window(a, a.shape, everything)


    def norm_step(which, hidden, parts):
        new, out = norm_rows_kernel(
            partial(norm_body, which),
            [half_sds, half_low],
            [hidden, *parts],
            norm_rows,
            last + soon,
        )
        soon[:] = []
        last[:] = [out]
        return new, (out, swap_core(free(out)))

    def norm_back(which, c, parts, before):
        rows = near.get((which, c, "back"), hidden[which][c])
        if before is not None:
            before = near_grad.get((which, c), before)
        operands = [rows, *parts] + ([before] if before is not None else []) + sums
        new, out, total = norm_rows_kernel(
            partial(norm_back_body, which, len(parts)),
            [half_sds, half_low, sds((8, width), F32)],
            operands,
            norm_rows,
            last + soon,
        )
        soon[:] = []
        last[:] = [out]
        sums[:] = [total]
        return new, (out, swap_core(free(out)))

    sums = []
    waiting, soon, older, newest = [], [], [], []
    moving = [None] * clips

    def flush():
        if waiting:
            c, keep, got = waiting.pop()
            parts = norm_rows_kernel(
                add_parts_body,
                [sds((height * part // sum(PIECES), width), LOW) for part in PIECES],
                [keep, got],
                None,
                last,
                name="add",
            )
            last[:] = [parts[-1]]
            fars = [across(free(part))[1] for part in parts]
            moving[c] = (*parts, *fars)
            soon[:] = fars[:-1]
            older[:] = newest
            newest[:] = fars[-1:]

    def reduce_rows(c, keep, send):
        waiting.append((c, keep, swap_core(free(send))))

    text_rows = text_states.reshape(clips * text_len, text_width)
    def text_in_step():
        (result,) = run(
            text_in_body,
            [Flow(sds((clips * text_len, columns), LOW))],
            [
                Scalar(place.astype(jnp.int32).reshape(1)),
                norm_rows,
                fetch(text_rows),
                Window(
                    cross_all,
                    (dp, text_share, columns),
                    lambda ref: ref.at[:, pl.ds(4 * share, text_share), :],
                ),
            ],
            flops=2 * clips * text_len * text_width * columns,
            name="text_in",
        )
        return spread_tensor(free(result))

    full = sds((frames, columns), LOW)
    lse_sds = sds((8, frames), F32)
    tot = [pltpu.VMEM((frames, 128), F32)]
    heads = columns // HEAD_DIM
    score_flops = 2 * heads * frames * HEAD_DIM
    units = feedforward.shape[2]
    inner = sds((frames, units), LOW)
    every = range(clips)

    near, near_grad = {}, {}

    def ahead(phase, c):
        at, clip = (phase - 1, c + 1) if c + 1 < clips else (phase, 0)
        if at < 0 or (phase == 3 and clip == 0) or (clip == c):
            return []
        return [Ahead(hidden[at][clip])]

    def took(phase, c, results):
        at, clip = (phase - 1, c + 1) if c + 1 < clips else (phase, 0)
        if ahead(phase, c):
            *results, near[at, clip] = results
        return results

    def ahead_back(phase, c):
        at, clip = (phase, c + 1) if c + 1 < clips else (phase - 1, 0)
        if clip == c:
            return []
        found = [Ahead(hidden[at][clip])]
        if at < 3:
            found.append(Ahead(grads[clip]))
        return found

    def took_back(phase, c, results):
        at, clip = (phase, c + 1) if c + 1 < clips else (phase - 1, 0)
        count = len(ahead_back(phase, c))
        if count == 2:
            near_grad[at, clip] = results[-1]
        if count:
            near[at, clip, "back"] = results[len(results) - count]
        return results[: len(results) - count]

    def embed_step(c):
        mine = strips[c]
        parts = [mine] + [swap(mine, "tensor", 2 * s) for s in range(1, sides)]
        new, out = run(
            embed_norm_body,
            [Flow(half_sds), Flow(half_low)],
            [side_arg, placed, norm_rows] + parts,
            flops=10 * height * width,
            name="embed_norm",
        )
        return new, (out, swap_core(free(out)))

    def self_step(c, pair):
        own, got = pair
        *saved, keep, send, left, right, hidden[0][c] = took(0, c, run_block(
            self_forward_body,
            [full, full, full, full, lse_sds, flow, flow, Copy(1), Copy(3)],
            [core_arg, own, w_attn(0), got, w_attn(1), w_attn(2), w_attn(6)]
            + [Carry(hidden[0][c])]
            + ahead(0, c),
            flops=8 * frames * width * columns + 4 * score_flops * frames,
            scratch=tot,
            name="self_forward",
        ))
        pairs[0][c] = (left, right)
        reduce_rows(c, keep, send)
        return saved

    text_full = sds((clips * text_len, width), LOW)
    text_cols = sds((clips * text_len, columns), LOW)

    def text_step():
        return run(
            text_body,
            [text_full, text_cols, text_cols],
            [Scalar(place_order)] + text_parts + [w_attn(4), w_attn(5)],
            flops=4 * clips * text_len * width * columns,
            name="text",
        )

    def text_rows_of(array, c):
        return Window(
            array, (text_len, columns), lambda ref: ref.at[pl.ds(c * text_len, text_len), :]
        )

    def cross_step(c, pair):
        own, got = pair
        k, v = text_rows_of(text_key, c), text_rows_of(text_value, c)
        q, o, lse, keep, send, left, right, hidden[1][c] = took(1, c, run_block(
            cross_forward_body,
            [full, full, lse_sds, flow, flow, Copy(1), Copy(3)],
            [core_arg, own, w_attn(3), got, bias_lines[c], k, v, w_attn(7)]
            + [Carry(hidden[1][c])]
            + ahead(1, c),
            flops=4 * frames * width * columns + 4 * score_flops * text_len,
            scratch=tot,
            name="cross_forward",
        ))
        pairs[1][c] = (left, right)
        reduce_rows(c, keep, send)
        return (q, k, v, o, lse)

    def ffn_step(c, pair):
        *saved, keep, send, left, right, hidden[2][c] = took(2, c, run_block(
            ffn_forward_body,
            [inner, inner, flow, flow, Copy(1), Copy(2)],
            [core_arg, *pair, w_member(ffn_all, 0), w_member(ffn_all, 1), Carry(hidden[2][c])]
            + ahead(2, c),
            flops=4 * frames * width * units,
            name="ffn_forward",
        ))
        pairs[2][c] = (left, right)
        reduce_rows(c, keep, send)
        return saved

    hidden = [[None] * clips for _ in range(4)]
    pairs = [[None] * clips for _ in range(4)]
    kept = [[None] * clips for _ in range(3)]
    for c in every:
        hidden[0][c], pairs[0][c] = embed_step(c)
        flush()
        kept[0][c] = self_step(c, pairs[0][c])
        if c == 0:
            text_parts = text_in_step()
    text_hidden, text_key, text_value = text_step()
    for c in every:
        hidden[1][c], pairs[1][c] = norm_step(1, near.get((0, c), hidden[0][c]), moving[c])
        flush()
        kept[1][c] = cross_step(c, pairs[1][c])
    for c in every:
        hidden[2][c], pairs[2][c] = norm_step(2, near.get((1, c), hidden[1][c]), moving[c])
        flush()
        kept[2][c] = ffn_step(c, pairs[2][c])

    loss_part = [None] * clips

    def head_step(c, pair):
        own, got = pair
        logits, stats, left, right, hidden[3][c] = took(3, c, run_block(
            head_forward_body,
            [
                sds((frames, books * vocab), F32),
                Flow(sds((2 * books, frames), F32)),
                Copy(1),
                Copy(3),
            ],
            [core_arg, own, targets[c], got]
            + [w_member(head_all, k) for k in range(books)]
            + [Carry(hidden[3][c])]
            + ahead(3, c),
            flops=2 * frames * width * books * vocab,
            scratch=tot,
            name="head_forward",
        ))
        pairs[3][c] = (left, right)
        return logits, stats

    def merge_step(stats):
        mask = 1
        while mask < tensor:
            far = swap(free(stats), "tensor", mask)
            (stats,) = norm_rows_kernel(
                partial(merge_body, books),
                [sds((2 * books, frames), F32)],
                [stats, far],
                None,
                last,
                name="merge",
            )
            last[:] = [stats]
            mask *= 2
        return stats

    def head_back_step(c, logits, stats):
        grad, keep, send, loss = run_block(
            head_backward_body,
            [sds((frames, books * vocab), LOW), flow, flow, Flow(sds((8, 128), F32))],
            [core_arg, stats, loss_weight[c], targets[c], fetch(logits)]
            + [w_member(head_all, k) for k in range(books)]
            + [counted],
            flops=2 * frames * width * books * vocab,
            scratch=tot,
            name="head_backward",
        )
        loss_part[c] = free(loss)[0, 0]
        reduce_rows(c, keep, send)
        return grad

    self_shared = Shared((dp, 4 * share + text_share, columns), LOW)
    cross_shared = Shared((dp, 4 * share, columns), LOW)
    ffn_shared = Shared((dp,) + feedforward.shape, LOW)
    head_shared = Shared((dp, books, share, vocab), LOW)

    def attn_into(n):
        shared, at = (
            (self_shared, SELF.index(n)) if n in SELF else (cross_shared, CROSS.index(n))
        )
        return Into(
            shared, (dp, share, columns), lambda ref: ref.at[:, pl.ds(at * share, share), :]
        )

    def member_into(shared, n):
        return Into(shared, (dp,) + shared.full.shape[2:], lambda ref: ref.at[:, n])

    def halves(rights, shared, n):
        step = rights[0].shape[1] // 2
        found = []
        for at in (0, step):
            windows = [
                Window(a, (frames, step), lambda ref, at=at: ref.at[:, pl.ds(at, step)])
                for a in rights
            ]
            into = Into(
                shared, (dp, share, step), lambda ref, at=at: ref.at[:, n, :, pl.ds(at, step)]
            )
            found.append((windows, [into]))
        return found

    def weights(lefts, rights, outs, name):
        rights = [a if isinstance(a, Window) else fetch(a) for a in rights]
        total = rights[0].shape[1]
        turn_left = 2 * total > width
        run_weight(
            partial(weight_grad_body, clips, turn_left),
            outs,
            [core_arg] + [fetch(half) for pair in lefts for half in pair] + rights,
            flops=2 * clips * frames * width * total,
            scratch=[pltpu.VMEM((width if turn_left else total, clips * frames), LOW)],
            name=name,
            margin=16,
        )

    logit_grads = [None] * clips
    ready = [None] * clips
    for c in every:
        hidden[3][c], pairs[3][c] = norm_step(3, near.get((2, c), hidden[2][c]), moving[c])
        flush()
        ready[c] = head_step(c, pairs[3][c])
        if c:
            flush()
            logits, stats = ready[c - 1]
            logit_grads[c - 1] = head_back_step(c - 1, logits, merge_step(stats))
    logits, stats = ready[-1]
    stats = merge_step(stats)
    flush()
    logit_grads[-1] = head_back_step(clips - 1, logits, stats)

    def ffn_back_step(c, pair):
        own, got = pair
        grad, keep, send, left, right, grads[c] = took_back(3, c, run_block(
            ffn_backward_body,
            [inner, flow, flow, Copy(1), Copy(2)],
            [core_arg, own, got, w_member(ffn_all, 1), fetch(kept[2][c][1]), w_member(ffn_all, 0)]
            + [Carry(grads[c])]
            + ahead_back(3, c),
            flops=4 * frames * width * units,
            name="ffn_backward",
        ))
        back_pairs[3][c] = (left, right)
        reduce_rows(c, keep, send)
        return grad

    grads = [None] * clips
    back_pairs = [[None] * clips for _ in range(4)]
    inner_grads = [None] * clips
    for c in every:
        grads[c], back_pairs[3][c] = norm_back(3, c, moving[c], None)
        flush()
        inner_grads[c] = ffn_back_step(c, back_pairs[3][c])
        if c == 0:
            step = books // 2 * vocab
            for at in (0, 1):
                windows = [
                    Window(a, (frames, step), lambda ref, at=at: ref.at[:, pl.ds(at * step, step)])
                    for a in logit_grads
                ]
                into = [
                    member_into(head_shared, k) for k in range(at * books // 2, (at + 1) * books // 2)
                ]
                weights(pairs[3], windows, into, "head_weights")
    head_sum = lax.psum_scatter(free(head_shared.array), "dp", scatter_dimension=0, tiled=False)

    acc_text = [pltpu.VMEM((text_len, columns), F32)] * 2
    small = sds((text_len, columns), LOW)

    def cross_back_step(c, pair):
        own, got = pair
        q, k, v, o, lse = kept[1][c]
        bias = bias_columns[c]
        dq, dk, dv, keep, send, left, right, grads[c] = took_back(2, c, run_block(
            cross_backward_body,
            [full, small, small, flow, flow, Copy(1), Copy(3)],
            [core_arg, own, w_attn(7), got, bias, fetch(q), k, v, fetch(lse), w_attn(3)]
            + [Carry(grads[c])]
            + ahead_back(2, c),
            flops=4 * frames * width * columns + 10 * score_flops * text_len,
            scratch=[pltpu.VMEM((frames, columns), LOW)] + acc_text,
            name="cross_backward",
        ))
        back_pairs[2][c] = (left, right)
        reduce_rows(c, keep, send)
        return (dq, dk, dv)

    cross_grads = [None] * clips
    for c in every:
        grads[c], back_pairs[2][c] = norm_back(2, c, moving[c], grads[c])
        flush()
        cross_grads[c] = cross_back_step(c, back_pairs[2][c])
        if c == 0:
            for windows, into in halves([k[0] for k in kept[2]], ffn_shared, 1):
                weights(back_pairs[3], windows, into, "ffn_two")
        if c == min(1, clips - 1):
            for windows, into in halves(inner_grads, ffn_shared, 0):
                weights(pairs[2], windows, into, "ffn_one")
    ffn_sum = lax.psum_scatter(free(ffn_shared.array), "dp", scatter_dimension=0, tiled=False)

    def text_back_step():
        results = run_weight(
            partial(text_back_body, clips),
            [Flow(text_cols)] * tensor + [attn_into(4), attn_into(5)],
            [Scalar(place_order)]
            + [fetch(g[1]) for g in cross_grads]
            + [fetch(g[2]) for g in cross_grads]
            + [w_attn(4), w_attn(5), fetch(text_hidden)],
            flops=8 * clips * text_len * width * columns,
            scratch=[pltpu.VMEM((clips * text_len, width), LOW)],
            name="text_back",
        )
        live = dict(enumerate(results))
        mask = 1
        while mask < tensor:
            fresh = {}
            for m in live:
                if not m & mask:
                    fresh[m] = (live[m], swap(free(live[m | mask]), "tensor", mask))
            mask *= 2
            if mask < tensor:
                for m, both in fresh.items():
                    (fresh[m],) = norm_rows_kernel(
                        add_body, [text_cols], list(both), None, last, name="add"
                    )
                    last[:] = [fresh[m]]
            live = fresh
        return live[0]

    acc_self = [pltpu.VMEM((frames, columns), F32)] * 2

    def self_back_step(c, pair):
        own, got = pair
        q, k, v, o, lse = kept[0][c]
        grad, keep, send, left, right, grads[c] = took_back(1, c, run_block(
            self_backward_body,
            [sds((frames, 3 * columns), LOW), flow, flow, Copy(1), Copy(3)],
            [core_arg, own, w_attn(6), got]
            + [fetch(a) for a in (q, k, v, lse)]
            + [w_attn(0), w_attn(1), w_attn(2), Carry(grads[c])]
            + ahead_back(1, c),
            flops=8 * frames * width * columns + 10 * score_flops * frames,
            scratch=[pltpu.VMEM((frames, columns), LOW)] + acc_self,
            name="self_backward",
        ))
        back_pairs[1][c] = (left, right)
        reduce_rows(c, keep, send)
        return grad

    self_grads = [None] * clips
    last.append(head_sum)
    for c in every:
        grads[c], back_pairs[1][c] = norm_back(1, c, moving[c], grads[c])
        flush()
        self_grads[c] = self_back_step(c, back_pairs[1][c])
        if c == 0:
            text_grad = text_back_step()
            weights(back_pairs[2], [k[3] for k in kept[1]], [attn_into(7)], "cross_out")
            weights(pairs[1], [g[0] for g in cross_grads], [attn_into(3)], "cross_query")
            cross_sum = lax.psum_scatter(
                free(cross_shared.array), "dp", scatter_dimension=0, tiled=False
            )

    zero_lows = [None] * clips

    def zero_step(c):
        _, (zero_lows[c], _) = norm_back(0, c, moving[c], grads[c])

    weights(back_pairs[1], [k[3] for k in kept[0]], [attn_into(6)], "self_out")
    first = list(soon)
    flush()
    text_into = Into(
        self_shared,
        (dp, text_share, columns),
        lambda ref: ref.at[:, pl.ds(4 * share, text_share), :],
    )
    (bias_grad,) = run(
        text_weight_body,
        [text_into, Flow(sds((8, columns), F32))],
        [fetch(text_rows), *text_grad],
        after=[ffn_sum] + first,
        flops=2 * clips * text_len * text_width * columns,
        name="text_weight",
    )
    for members in ((0, 1), (2,)):
        size = len(members) * columns
        windows = [
            Window(
                a, (frames, size), lambda ref: ref.at[:, pl.ds(members[0] * columns, size)]
            )
            for a in self_grads
        ]
        weights(pairs[0], windows, [attn_into(n) for n in members], "self_in")
    soon[:] = newest
    self_sum = lax.psum_scatter(free(self_shared.array), "dp", scatter_dimension=0, tiled=False)
    for c in every:
        zero_step(c)

    if aligned:
        pieces = list(map(free, run(
            split_features_body,
            [Flow(sds((clips * strip, share), LOW))] * dp,
            [
                Scalar(group_order),
                Scalar(jnp.broadcast_to(side.astype(jnp.int32), (clips + 1,))),
            ]
            + zero_lows,
            after=[cross_sum],
            name="split_features",
        )))
    else:
        rows = jnp.concatenate(
            [lax.dynamic_slice_in_dim(free(a), side * strip, strip, 0) for a in zero_lows], axis=0
        )
        rows = jnp.transpose(rows.reshape(clips * strip, dp, share), (1, 0, 2))
        pieces = list(jnp.take(rows, group_order, axis=0))
    rows_all = [pieces[0]] + [swap(pieces[m], "dp", m) for m in range(1, dp)]
    embed_parts = embed_back(vocab_base, back_lines, rows_all, books, vocab, list(last))
    grad_embed = collect_tensor([embed_parts[m] for m in range(tensor)])

    norm_part = free(sums[0]) * (1.0 / sides)
    bias_row = lax.dynamic_update_slice_in_dim(
        jnp.zeros((width,), F32), free(bias_grad)[0], place * columns, 0
    )
    norm_total = total_over(
        jnp.concatenate([norm_part, bias_row[None]], axis=0), ("tensor", "dp")
    )
    grad_norm_rows = lax.dynamic_slice_in_dim(norm_total, group * share, share, 1)

    own_self = self_sum[: 4 * share].reshape(4, share, columns)
    own_cross = cross_sum.reshape(4, share, columns)
    grad_attention = jnp.concatenate(
        [own_self[:3], own_cross[:3], own_self[3:], own_cross[3:]], axis=0
    ).astype(F32)
    grad_text_proj = jnp.transpose(self_sum[4 * share :]).astype(F32)
    grad_feedforward = ffn_sum.astype(F32)
    grad_heads = head_sum.astype(F32)
    local_square = (
        jnp.sum(jnp.square(self_sum.astype(F32)))
        + jnp.sum(jnp.square(cross_sum.astype(F32)))
        + jnp.sum(grad_feedforward * grad_feedforward)
        + jnp.sum(grad_heads * grad_heads)
        + jnp.sum(grad_embed * grad_embed)
        + jnp.sum(grad_norm_rows * grad_norm_rows) / tensor
    )
    both = total_over(
        jnp.stack([local_square, sum(loss_part) / tensor]).reshape(1, 2), ("tensor", "dp")
    )[0]
    grad_norm = jnp.sqrt(both[0])
    mean_loss = both[1]
    factor = clip_limit / jnp.maximum(grad_norm, clip_limit)
    grad_tables = jnp.concatenate([grad_embed, grad_heads], 0)
    attn_new, attn_first_new, attn_second_new = adam_update(
        attention, grad_attention, attention_first, attention_second, rate_matrix, factor
    )
    ffn_new, ffn_first_new, ffn_second_new = adam_update(
        feedforward, grad_feedforward, feedforward_first, feedforward_second, rate_matrix, factor
    )
    table_new, table_first_new, table_second_new = adam_update(
        tables, grad_tables, tables_first, tables_second, rate_table, factor
    )
    text_new, text_first_new, text_second_new = adam_update(
        text_proj, grad_text_proj, text_first, text_second, rate_matrix, factor
    )
    norm_new, norm_first_new, norm_second_new = adam_update(
        norm_params, grad_norm_rows, norm_first, norm_second, rate_norm, factor
    )
    return (
        mean_loss,
        free(counted)[0, 0],
        grad_norm,
        attn_new,
        attn_new.astype(LOW),
        attn_first_new,
        attn_second_new,
        ffn_new,
        ffn_new.astype(LOW),
        ffn_first_new,
        ffn_second_new,
        table_new,
        table_new.astype(LOW),
        table_first_new,
        table_second_new,
        text_new,
        text_new.astype(LOW),
        text_first_new,
        text_second_new,
        norm_new,
        norm_first_new,
        norm_second_new,
    )


def solution(mesh):
    clip3 = P("dp", None, None)
    clip2 = P("dp", None)
    matrix = P(None, "dp", "tensor")
    text = P("tensor", "dp")
    norm = P(None, "dp")
    placed = (
        (clip3, clip3, clip2, clip3, clip2)
        + (matrix, matrix, matrix, text, norm)
        + (matrix,) * 6
        + (text, text, norm, norm)
    )
    return jax.shard_map(
        on_device,
        mesh=mesh,
        in_specs=placed,
        out_specs=(P(), P(), P()) + (matrix,) * 12 + (text,) * 4 + (norm,) * 3,
        check_vma=False,
    )
```

```python
from functools import partial
import math

import jax
import jax.numpy as jnp
from jax import lax
from jax.experimental import pallas as pl
from jax.experimental.pallas import tpu as pltpu
from jax.sharding import PartitionSpec as P

HEAD_DIM = 64
STEP = 5
BLOCK = 256
NEG = -1e30
LOW = jnp.bfloat16
F32 = jnp.float32

SELF = (0, 1, 2, 6)
CROSS = (3, 4, 5, 7)

SMALL = pl.CostEstimate(flops=1024, bytes_accessed=1024, transcendentals=0)

PIECES = (1, 1)

clip_limit = 0.004
stability_offset = 1e-08
weight_decay = 0.01
moment_decay = 0.5
rate_matrix = 0.03
rate_table = 0.05
rate_norm = 0.2


def nn(a, b):
    return lax.dot_general(a, b, (((1,), (0,)), ((), ())), preferred_element_type=F32)


def nt(a, b):
    return lax.dot_general(a, b, (((1,), (1,)), ((), ())), preferred_element_type=F32)


def tn(a, b):
    return lax.dot_general(a, b, (((0,), (0,)), ((), ())), preferred_element_type=F32)


def sds(shape, kind):
    return jax.ShapeDtypeStruct(shape, kind)


def scalars():
    return pl.BlockSpec(memory_space=pltpu.SMEM)


def anywhere():
    return pl.BlockSpec(memory_space=pl.ANY)


def in_hbm():
    return pl.BlockSpec(memory_space=pltpu.HBM)


def in_vmem():
    return pl.BlockSpec(memory_space=pltpu.VMEM)


def whole(a):
    rank = len(a.shape)
    return pl.BlockSpec(a.shape, lambda i: (0,) * rank)


def later(body, count, at):
    def ordered(*refs):
        return body(*refs[:at], *refs[at + count :])

    return ordered


class Scalar:
    def __init__(self, array):
        self.array = array


class Window:
    def __init__(self, array, shape, pick):
        self.array, self.shape, self.pick = array, tuple(shape), pick


def hold(array, space):
    return pltpu.with_memory_space_constraint(array, space)


def free(array):
    return pltpu.with_memory_space_constraint(array, pl.ANY)


class Flow:
    def __init__(self, shape):
        self.shape = shape


class Copy:
    def __init__(self, i):
        self.i = i


class Carry:
    def __init__(self, array):
        self.array = array


class Ahead:
    def __init__(self, array):
        self.array = array


class Shared:
    def __init__(self, shape, kind):
        self.full, self.array = sds(shape, kind), None


class Into:
    def __init__(self, shared, shape, pick):
        self.shared, self.shape, self.pick = shared, tuple(shape), pick


def everything(ref):
    return ref


def nbytes_of(shape, kind):
    return math.prod(shape) * jnp.dtype(kind).itemsize


def kernel(body, outs, operands, flops=0, scratch=(), name=None, exps=0, after=(), margin=12):
    arrays, specs, windows, shown, fetched = [], [], [], [], {}
    outs = list(outs)
    for i, a in enumerate(operands):
        shown.append(not isinstance(a, (Carry, Ahead)))
        if isinstance(a, Ahead):
            arrays.append(hold(a.array, pltpu.HBM))
            specs.append(in_hbm())
            windows.append(None)
            outs.append(Flow(sds(a.array.shape, a.array.dtype)))
            fetched[len(outs) - 1] = i
        elif isinstance(a, Carry):
            arrays.append(hold(a.array, pltpu.VMEM))
            specs.append(in_vmem())
            windows.append(None)
            outs.append(Copy(i))
        elif isinstance(a, Scalar):
            arrays.append(a.array)
            specs.append(scalars())
            windows.append(None)
        elif isinstance(a, Window):
            arrays.append(hold(a.array, pltpu.HBM))
            specs.append(in_hbm())
            windows.append(a)
        else:
            arrays.append(hold(a, pltpu.VMEM))
            specs.append(in_vmem())
            windows.append(None)
    aliases, out_shapes, out_specs, out_parts, owners = {}, [], [], [], []
    extra = []
    for o in outs:
        if isinstance(o, Into):
            if o.shared not in owners:
                if o.shared.array is not None:
                    aliases[len(arrays) + len(extra)] = len(out_shapes)
                    extra.append(o.shared.array)
                out_shapes.append(pltpu.HBM(o.shared.full.shape, o.shared.full.dtype))
                out_specs.append(in_hbm())
                owners.append(o.shared)
            out_parts.append(("put", o.shape, o.shared.full.dtype, o.pick, owners.index(o.shared)))
            continue
        if isinstance(o, Flow):
            out_parts.append(("flow", None, None, None, len(out_shapes)))
            out_shapes.append(pltpu.VMEM(o.shape.shape, o.shape.dtype))
            out_specs.append(in_vmem())
        elif isinstance(o, Copy):
            a = arrays[o.i]
            out_parts.append(("copy", o.i, None, None, len(out_shapes)))
            out_shapes.append(pltpu.HBM(a.shape, a.dtype))
            out_specs.append(in_hbm())
        else:
            out_parts.append(("put", o.shape, o.dtype, everything, len(out_shapes)))
            out_shapes.append(pltpu.HBM(o.shape, o.dtype))
            out_specs.append(in_hbm())
        owners.append(None)
    out_parts.append(("token", None, None, None, len(out_shapes)))
    out_shapes.append(pltpu.VMEM((8, 128), F32))
    out_specs.append(in_vmem())
    owners.append(None)
    moved = [w for w in windows if w is not None]
    made = [p for p in out_parts if p[0] == "put"]
    count_in, count_extra, count_after = len(arrays), len(extra), len(after)
    count_out, count_moved, count_arrays = len(out_parts), len(moved), len(out_shapes)

    def run_body(*refs):
        refs = list(refs)
        ins = refs[:count_in]
        at = count_in + count_extra + count_after
        out_refs = refs[at : at + count_arrays]
        at += count_arrays
        in_buffers = refs[at : at + count_moved]
        at += count_moved
        made_buffers = refs[at : at + len(made)]
        at += len(made)
        in_sems, out_sems = refs[at], refs[at + 1]
        rest = refs[at + 2 :]
        views, copies, waited = [], {}, set()
        n = 0
        for i, (ref, w) in enumerate(zip(ins, windows)):
            if not shown[i]:
                continue
            if w is None:
                views.append(ref)
            else:
                copies[i] = pltpu.make_async_copy(w.pick(ref), in_buffers[n], in_sems.at[n])
                copies[i].start()
                views.append(in_buffers[n])
                n += 1
        sent, sources = {}, {}

        def need(*which):
            for i in which:
                if i in copies and i not in waited:
                    waited.add(i)
                    copies[i].wait()

        def put(*which):
            for j in which:
                if j in sources:
                    source, target = sources[j]
                    sent[j] = pltpu.make_async_copy(source, target, out_sems.at[j])
                    sent[j].start()

        body_outs = []
        n = 0
        for j, (kind, what, _, pick, owner) in enumerate(out_parts):
            if kind == "put":
                sources[j] = (made_buffers[n], pick(out_refs[owner]))
                body_outs.append(made_buffers[n])
                n += 1
            elif kind == "copy":
                sources[j] = (ins[what], out_refs[owner])
                put(j)
            elif kind == "token":
                out_refs[owner][...] = jnp.zeros((8, 128), F32)
            elif j in fetched:
                sources[j] = (ins[fetched[j]], out_refs[owner])
                put(j)
            else:
                body_outs.append(out_refs[owner])
        body(need, put, *views, *body_outs, *rest)
        need(*copies)
        put(*(j for j in sources if j not in sent))
        for copy in sent.values():
            copy.wait()

    nbytes = sum(nbytes_of(w.shape, w.array.dtype) for w in moved)
    nbytes += sum(nbytes_of(p[1], p[2]) for p in made)
    held = nbytes + sum(nbytes_of(m.shape, m.dtype) for m in scratch)
    results = pl.pallas_call(
        run_body,
        out_shape=tuple(out_shapes),
        in_specs=specs + [anywhere()] * (count_extra + count_after),
        out_specs=tuple(out_specs),
        input_output_aliases=aliases,
        scratch_shapes=[pltpu.VMEM(w.shape, w.array.dtype) for w in moved]
        + [pltpu.VMEM(p[1], p[2]) for p in made]
        + [
            pltpu.SemaphoreType.DMA((max(1, count_moved),)),
            pltpu.SemaphoreType.DMA((max(1, count_out),)),
        ]
        + list(scratch),
        compiler_params=pltpu.CompilerParams(vmem_limit_bytes=held + (margin << 20)),
        cost_estimate=SMALL,
        name=name,
    )(*arrays, *extra, *after)
    for owner, result in zip(owners, results):
        if owner is not None:
            owner.array = result
    return [r for owner, r in zip(owners, results) if owner is None]


def flat(ref):
    w = ref[...]
    return w.reshape(-1, w.shape[-1])


def half_rows(core, height):
    return (
        pl.ds(pl.multiple_of(core * height, height), height),
        pl.ds(pl.multiple_of((1 - core) * height, height), height),
    )


def attend_block(query, keys, values, head_masks, diagonal, bias):
    rows, width = query.shape
    lane = lax.broadcasted_iota(jnp.int32, (rows, 128), 1)
    column = lax.broadcasted_iota(jnp.int32, (rows, width), 1) // HEAD_DIM
    mixed = jnp.zeros((rows, width), F32)
    totals = jnp.zeros((rows, 128), F32)
    count = keys.shape[0]
    for h, mask in enumerate(head_masks):
        s = nt(query * mask, keys)
        if diagonal is not None:
            last = jnp.where(diagonal, s[:, count - rows :], NEG)
            s = last if count == rows else jnp.concatenate([s[:, : count - rows], last], axis=1)
        if bias is not None:
            s = s + bias
        top = jnp.max(s, axis=1, keepdims=True)
        e = jnp.exp(s - top)
        total = jnp.sum(e, axis=1, keepdims=True)
        p = (e * (1.0 / total)).astype(LOW)
        mixed = jnp.where(column == h, nn(p, values), mixed)
        totals = jnp.where(lane == h, top + jnp.log(total), totals)
    return mixed, totals


def masks_of(width):
    head = lax.broadcasted_iota(jnp.int32, (1, width), 1) // HEAD_DIM
    return [(head == h).astype(F32).astype(LOW) for h in range(width // HEAD_DIM)]


def triangle(size):
    row = lax.broadcasted_iota(jnp.int32, (size, size), 0)
    col = lax.broadcasted_iota(jnp.int32, (size, size), 1)
    return row >= col


def self_forward_body(
    need, put, core_ref, own_ref, wq_ref, got_ref, wk_ref, wv_ref, wo_ref,
    q_ref, k_ref, v_ref, o_ref, lse_ref, keep_ref, send_ref, tot_ref,
):
    height = own_ref.shape[0]
    frames, width = q_ref.shape
    mine, other = half_rows(core_ref[0], height)
    need(1)
    for i, w_ref, to_ref in ((2, wq_ref, q_ref), (4, wk_ref, k_ref), (5, wv_ref, v_ref)):
        need(i)
        w = flat(w_ref)
        to_ref[mine, :] = nn(own_ref[...], w).astype(LOW)
        need(3)
        to_ref[other, :] = nn(got_ref[...], w).astype(LOW)
    put(0, 1, 2)
    scale = jnp.asarray(HEAD_DIM**-0.5, LOW)
    head_masks = masks_of(width)
    diagonal = triangle(BLOCK)
    for i in range(frames // BLOCK):
        rows = slice(i * BLOCK, (i + 1) * BLOCK)
        mixed, totals = attend_block(
            q_ref[rows, :] * scale,
            k_ref[: (i + 1) * BLOCK, :],
            v_ref[: (i + 1) * BLOCK, :],
            head_masks,
            diagonal,
            None,
        )
        o_ref[rows, :] = mixed.astype(LOW)
        tot_ref[rows, :] = totals
    put(3)
    need(6)
    wo = flat(wo_ref)
    send_ref[...] = nt(o_ref[other, :], wo).astype(LOW)
    put(6)
    keep_ref[...] = nt(o_ref[mine, :], wo).astype(LOW)
    put(5)
    lse_ref[...] = jnp.transpose(tot_ref[...])[:8, :]


def cross_forward_body(
    need, put, core_ref, own_ref, wq_ref, got_ref, bias_ref, k_ref, v_ref, wo_ref,
    q_ref, o_ref, lse_ref, keep_ref, send_ref, tot_ref,
):
    height = own_ref.shape[0]
    frames, width = q_ref.shape
    mine, other = half_rows(core_ref[0], height)
    need(1, 2)
    w = flat(wq_ref)
    q_ref[mine, :] = nn(own_ref[...], w).astype(LOW)
    need(3)
    q_ref[other, :] = nn(got_ref[...], w).astype(LOW)
    put(0)
    scale = jnp.asarray(HEAD_DIM**-0.5, LOW)
    head_masks = masks_of(width)
    need(4, 5, 6)
    for i in range(frames // BLOCK):
        rows = slice(i * BLOCK, (i + 1) * BLOCK)
        mixed, totals = attend_block(
            q_ref[rows, :] * scale, k_ref[...], v_ref[...], head_masks, None, bias_ref[...]
        )
        o_ref[rows, :] = mixed.astype(LOW)
        tot_ref[rows, :] = totals
    put(1)
    need(7)
    wo = flat(wo_ref)
    send_ref[...] = nt(o_ref[other, :], wo).astype(LOW)
    put(4)
    keep_ref[...] = nt(o_ref[mine, :], wo).astype(LOW)
    put(3)
    lse_ref[...] = jnp.transpose(tot_ref[...])[:8, :]


def ffn_forward_body(
    need, put, core_ref, own_ref, got_ref, w1_ref, w2_ref,
    act_ref, slope_ref, keep_ref, send_ref,
):
    height = own_ref.shape[0]
    mine, other = half_rows(core_ref[0], height)
    need(1, 2, 3)
    w1 = flat(w1_ref)
    for j, source, rows, to_ref in (
        (3, got_ref, other, send_ref),
        (2, own_ref, mine, keep_ref),
    ):
        u = nn(source[...], w1)
        phi = 0.5 * (1.0 + lax.erf(u * (2.0**-0.5)))
        act = (u * phi).astype(LOW)
        density = jnp.exp(-0.5 * u * u) * ((2.0 * math.pi) ** -0.5)
        act_ref[rows, :] = act
        slope_ref[rows, :] = (phi + u * density).astype(LOW)
        need(4)
        to_ref[...] = nt(act, flat(w2_ref)).astype(to_ref.dtype)
        put(j)


def head_forward_body(
    need, put, core_ref, own_ref, target_ref, got_ref, *refs
):
    *w_refs, logits_ref, stats_ref, tot_ref = refs
    height = own_ref.shape[0]
    books = len(w_refs)
    vocab = w_refs[0].shape[2]
    halves = half_rows(core_ref[0], height)
    lane = lax.broadcasted_iota(jnp.int32, (height, 128), 1)
    code = lax.broadcasted_iota(jnp.int32, (height, vocab), 1)
    need(1, 2)
    totals = [jnp.zeros((height, 128), F32)] * 2
    for k, w_ref in enumerate(w_refs):
        need(4 + k)
        w = flat(w_ref)
        for j, (source, rows) in enumerate(zip((own_ref, got_ref), halves)):
            need(1 + 2 * j)
            s = nn(source[...], w)
            logits_ref[rows, k * vocab : (k + 1) * vocab] = s
            top = jnp.max(s, axis=1, keepdims=True)
            total = jnp.sum(jnp.exp(s - top), axis=1, keepdims=True)
            hit = code == target_ref[rows, k : k + 1]
            pick = jnp.sum(jnp.where(hit, s, 0.0), axis=1, keepdims=True)
            totals[j] = jnp.where(lane == k, top + jnp.log(total), totals[j])
            totals[j] = jnp.where(lane == books + k, pick, totals[j])
    put(0)
    for rows, t in zip(halves, totals):
        tot_ref[rows, :] = t
    stats_ref[...] = jnp.transpose(tot_ref[...])[: 2 * books, :]


def head_backward_body(
    need, put, core_ref, total_ref, weight_ref, target_ref, logits_ref, *refs
):
    *w_refs, valid_ref, grad_ref, keep_ref, send_ref, loss_ref, col_ref = refs
    height = keep_ref.shape[0]
    books = len(w_refs)
    vocab = w_refs[0].shape[2]
    mine, other = half_rows(core_ref[0], height)
    frames = logits_ref.shape[0]
    need(1, 2, 3)
    wide = jnp.concatenate(
        [total_ref[...], jnp.zeros((128 - total_ref.shape[0], frames), F32)], axis=0
    )
    col_ref[...] = jnp.transpose(wide)
    share = 1.0 / valid_ref[0:1, 0:1]
    gap = (col_ref[:, :books] - col_ref[:, books : 2 * books]) * (weight_ref[...] * share)
    loss_ref[...] = jnp.broadcast_to(jnp.sum(gap).reshape(1, 1), loss_ref.shape)
    code = lax.broadcasted_iota(jnp.int32, (height, vocab), 1)
    need(4)
    for j, rows, to_ref in ((2, other, send_ref), (1, mine, keep_ref)):
        weight = weight_ref[rows, :] * share
        total = col_ref[rows, :]
        acc = None
        for k, w_ref in enumerate(w_refs):
            s = logits_ref[rows, k * vocab : (k + 1) * vocab]
            p = jnp.exp(s - total[:, k : k + 1])
            hit = jnp.where(code == target_ref[rows, k : k + 1], 1.0, 0.0)
            g = ((p - hit) * weight[:, k : k + 1]).astype(LOW)
            grad_ref[rows, k * vocab : (k + 1) * vocab] = g
            need(5 + k)
            part = nt(g, flat(w_ref))
            acc = part if acc is None else acc + part
        to_ref[...] = acc.astype(to_ref.dtype)
        put(j)


def ffn_backward_body(
    need, put, core_ref, own_ref, got_ref, w2_ref, slope_ref, w1_ref,
    grad_ref, keep_ref, send_ref,
):
    height = own_ref.shape[0]
    mine, other = half_rows(core_ref[0], height)
    need(1, 2, 3, 4)
    w2 = flat(w2_ref)
    for j, source, rows, to_ref in (
        (2, got_ref, other, send_ref),
        (1, own_ref, mine, keep_ref),
    ):
        g = (nn(source[...], w2) * slope_ref[rows, :].astype(F32)).astype(LOW)
        grad_ref[rows, :] = g
        need(5)
        to_ref[...] = nt(g, flat(w1_ref)).astype(to_ref.dtype)
        put(j)


def attend_back(
    q, k, v, g, lse, head_masks, scale, diagonal, bias, dq_ref, rows, dk_ref, dv_ref, first
):
    count, width = k.shape
    step = q.shape[0]
    dq = jnp.zeros((step, width), F32)
    dk = jnp.zeros((count, width), F32)
    dv = jnp.zeros((count, width), F32)
    for h, mask in enumerate(head_masks):
        qm = q * mask
        gm = g * mask
        s = nt(k, qm)
        if diagonal is not None:
            last = jnp.where(diagonal, s[count - step :, :], NEG)
            s = last if count == step else jnp.concatenate([s[: count - step, :], last], axis=0)
        if bias is not None:
            s = s + bias
        p = jnp.exp(s - lse[h : h + 1, :])
        dp = nt(v, gm)
        inner = jnp.sum(p * dp, axis=0, keepdims=True)
        ds = (p * (dp - inner)).astype(LOW)
        dq = dq + tn(ds, k * mask)
        dk = dk + nn(ds, qm)
        dv = dv + nn(p.astype(LOW), gm)
    dq_ref[rows, :width] = (dq * scale).astype(LOW)
    dk_ref[:count, :] = dk if first else dk_ref[:count, :] + dk
    dv_ref[:count, :] = dv if first else dv_ref[:count, :] + dv


def self_backward_body(
    need, put, core_ref, own_ref, wo_ref, got_ref, q_ref, k_ref, v_ref, lse_ref,
    wq_ref, wk_ref, wv_ref, grad_ref, keep_ref, send_ref, g_ref, dk_acc, dv_acc,
):
    height = own_ref.shape[0]
    frames, width = q_ref.shape
    mine, other = half_rows(core_ref[0], height)
    need(1, 2)
    wo = flat(wo_ref)
    g_ref[mine, :] = nn(own_ref[...], wo).astype(LOW)
    need(3)
    g_ref[other, :] = nn(got_ref[...], wo).astype(LOW)
    scale = HEAD_DIM**-0.5
    head_masks = masks_of(width)
    row = lax.broadcasted_iota(jnp.int32, (BLOCK, BLOCK), 0)
    col = lax.broadcasted_iota(jnp.int32, (BLOCK, BLOCK), 1)
    diagonal = col >= row
    blocks = frames // BLOCK
    need(4, 5, 6, 7)
    for i in reversed(range(blocks)):
        rows = slice(i * BLOCK, (i + 1) * BLOCK)
        count = (i + 1) * BLOCK
        attend_back(
            q_ref[rows, :] * jnp.asarray(scale, LOW),
            k_ref[:count, :],
            v_ref[:count, :],
            g_ref[rows, :],
            lse_ref[:, rows],
            head_masks,
            scale,
            diagonal,
            None,
            grad_ref,
            rows,
            dk_acc,
            dv_acc,
            i == blocks - 1,
        )
    grad_ref[:, width : 2 * width] = dk_acc[...].astype(LOW)
    grad_ref[:, 2 * width :] = dv_acc[...].astype(LOW)
    put(0)
    need(8, 9, 10)
    for j, rows, to_ref in ((2, other, send_ref), (1, mine, keep_ref)):
        part = None
        for n, w_ref in enumerate((wq_ref, wk_ref, wv_ref)):
            term = nt(grad_ref[rows, n * width : (n + 1) * width], flat(w_ref))
            part = term if part is None else part + term
        to_ref[...] = part.astype(to_ref.dtype)
        put(j)


def cross_backward_body(
    need, put, core_ref, own_ref, wo_ref, got_ref, bias_ref, q_ref, k_ref, v_ref, lse_ref, wq_ref,
    dq_ref, dk_ref, dv_ref, keep_ref, send_ref, g_ref, dk_acc, dv_acc,
):
    height = own_ref.shape[0]
    frames, width = q_ref.shape
    mine, other = half_rows(core_ref[0], height)
    need(1, 2)
    wo = flat(wo_ref)
    g_ref[mine, :] = nn(own_ref[...], wo).astype(LOW)
    need(3)
    g_ref[other, :] = nn(got_ref[...], wo).astype(LOW)
    scale = HEAD_DIM**-0.5
    head_masks = masks_of(width)
    need(4, 5, 6, 7, 8)
    for i in range(frames // BLOCK):
        rows = slice(i * BLOCK, (i + 1) * BLOCK)
        attend_back(
            q_ref[rows, :] * jnp.asarray(scale, LOW),
            k_ref[...],
            v_ref[...],
            g_ref[rows, :],
            lse_ref[:, rows],
            head_masks,
            scale,
            None,
            bias_ref[...],
            dq_ref,
            rows,
            dk_acc,
            dv_acc,
            i == 0,
        )
    put(0)
    need(9)
    wq = flat(wq_ref)
    for j, rows, to_ref in ((4, other, send_ref), (3, mine, keep_ref)):
        to_ref[...] = nt(dq_ref[rows, :], wq).astype(to_ref.dtype)
        put(j)
    dk_ref[...] = dk_acc[...].astype(LOW)
    dv_ref[...] = dv_acc[...].astype(LOW)


def normalize(values, gain, shift):
    center = values - jnp.mean(values, axis=1, keepdims=True)
    spread = jnp.mean(center * center, axis=1, keepdims=True)
    return center * lax.rsqrt(spread + 1e-05) * gain + shift


def count_body(books, *refs):
    *packet_refs, out_ref = refs
    total = sum(p[books : books + 1, 0:128] for p in packet_refs)
    out_ref[...] = jnp.broadcast_to(total, out_ref.shape).astype(F32)


def merge_body(books, own_ref, far_ref, out_ref):
    own, far = own_ref[:books, :], far_ref[:books, :]
    high = jnp.maximum(own, far)
    out_ref[:books, :] = high + jnp.log(jnp.exp(own - high) + jnp.exp(far - high))
    out_ref[books:, :] = own_ref[books:, :] + far_ref[books:, :]


def text_in_body(need, put, place_ref, norm_ref, rows_ref, w_ref, out_ref):
    columns = out_ref.shape[1]
    at = pl.ds(pl.multiple_of(place_ref[0] * columns, columns), columns)
    need(2, 3)
    out_ref[...] = (nn(rows_ref[...], flat(w_ref)) + norm_ref[8:9, at]).astype(LOW)


def add_body(keep_ref, got_ref, out_ref):
    out_ref[...] = (keep_ref[...].astype(F32) + got_ref[...].astype(F32)).astype(LOW)


def add_parts_body(keep_ref, got_ref, *out_refs):
    start = 0
    for out_ref in out_refs:
        at = slice(start, start + out_ref.shape[0])
        start += out_ref.shape[0]
        out_ref[...] = (keep_ref[at, :].astype(F32) + got_ref[at, :].astype(F32)).astype(LOW)


def joined(refs):
    half = len(refs) // 2
    sums = [a[...].astype(F32) + b[...].astype(F32) for a, b in zip(refs[:half], refs[half:])]
    return jnp.concatenate(sums, axis=0)


def norm_body(which, hidden_ref, *refs):
    *part_refs, norm_ref, new_ref, out_ref = refs
    new = hidden_ref[...] + joined(part_refs)
    new_ref[...] = new
    out_ref[...] = normalize(
        new, norm_ref[which : which + 1, :], norm_ref[which + 4 : which + 5, :]
    ).astype(LOW)


def embed_norm_body(need, put, side_ref, place_ref, norm_ref, *refs):
    *part_refs, new_ref, out_ref = refs
    side = side_ref[0]
    rows = part_refs[0].shape[0]
    need(1, 2)
    for s, part in enumerate(part_refs):
        need(3 + s)
        at = pl.ds(pl.multiple_of((side ^ s) * rows, rows), rows)
        new = part[...].astype(F32) + place_ref[at, :]
        new_ref[at, :] = new
        out_ref[at, :] = normalize(new, norm_ref[0:1, :], norm_ref[4:5, :]).astype(LOW)
    put(1, 0)


def norm_back_body(which, parts, hidden_ref, *refs):
    *before, norm_ref, new_ref, low_ref, sums_ref = refs[parts:]
    sums = before.pop() if before and before[-1].shape[0] == sums_ref.shape[0] else None
    values = hidden_ref[...]
    grad = joined(refs[:parts])
    gain = norm_ref[which : which + 1, :]
    center = values - jnp.mean(values, axis=1, keepdims=True)
    spread = jnp.mean(center * center, axis=1, keepdims=True)
    inverse = lax.rsqrt(spread + 1e-05)
    unit = center * inverse
    scaled = grad * gain
    first = jnp.mean(scaled, axis=1, keepdims=True)
    second = jnp.mean(scaled * unit, axis=1, keepdims=True)
    new = inverse * (scaled - first - unit * second)
    if before:
        new = before[0][...] + new
    new_ref[...] = new
    low_ref[...] = new.astype(LOW)
    sums_ref[...] = jnp.zeros(sums_ref.shape, F32) if sums is None else sums[...]
    sums_ref[which : which + 1, :] += jnp.sum(grad * unit, axis=0, keepdims=True)
    sums_ref[which + 4 : which + 5, :] += jnp.sum(grad, axis=0, keepdims=True)


def weight_grad_body(clips, turn_left, need, put, core_ref, *refs):
    lefts = refs[: 2 * clips]
    rights = refs[2 * clips : 3 * clips]
    outs = refs[3 * clips : -1]
    turned = refs[-1]
    height, width = lefts[0].shape
    frames = rights[0].shape[0]
    group = outs[0].shape[2]
    core = core_ref[0]

    def place(c, at):
        return pl.ds(pl.multiple_of(c * frames + at * height, 128), height)

    if turn_left:
        step = min(group, 512)
        for m, v in [(m, v) for m in range(len(outs)) for v in range(0, group, step)]:
            total = None
            for c in range(clips):
                if m == 0 and v == 0:
                    for j, at in ((0, core), (1, 1 - core)):
                        need(1 + 2 * c + j)
                        turned[:, place(c, at)] = jnp.transpose(lefts[2 * c + j][...])
                    need(1 + 2 * clips + c)
                part = nn(
                    turned[:, c * frames : (c + 1) * frames],
                    rights[c][:, m * group + v : m * group + v + step],
                )
                total = part if total is None else total + part
            outs[m][:, :, v : v + step] = total.astype(LOW).reshape(-1, outs[m].shape[1], step)
            if v + step == group:
                put(m)
    else:
        total = None
        for c in range(clips):
            need(1 + 2 * clips + c)
            turned[:, c * frames : (c + 1) * frames] = jnp.transpose(rights[c][...])
            for j, at in ((0, core), (1, 1 - core)):
                need(1 + 2 * c + j)
                part = nn(turned[:, place(c, at)], lefts[2 * c + j][...])
                total = part if total is None else total + part
        for m, out_ref in enumerate(outs):
            member = total[m * group : (m + 1) * group, :]
            out_ref[...] = jnp.transpose(member).astype(LOW).reshape(out_ref.shape)
            put(m)


def norm_rows_kernel(body, outs, operands, norm_rows, after, name="norm"):
    height, width = operands[0].shape
    operands = list(operands) + ([] if norm_rows is None else [norm_rows])
    nbytes = sum(nbytes_of(a.shape, a.dtype) for a in operands + list(outs))
    return pl.pallas_call(
        later(body, len(after), len(operands)),
        out_shape=tuple(pltpu.VMEM(o.shape, o.dtype) for o in outs),
        in_specs=[in_vmem()] * len(operands) + [anywhere()] * len(after),
        out_specs=tuple(in_vmem() for _ in outs),
        compiler_params=pltpu.CompilerParams(vmem_limit_bytes=12 << 20),
        cost_estimate=SMALL,
        name=name,
    )(*(hold(a, pltpu.VMEM) for a in operands), *after)


def equal_to(code, local):
    local = jnp.clip(local, -1.0, 256.0).astype(LOW)
    return jnp.where(code == local, jnp.asarray(1, LOW), jnp.asarray(0, LOW))


def embed_body(count, books, base_ref, *refs):
    packets, tables, outs = refs[:count], refs[count : len(refs) - count], refs[len(refs) - count :]
    features, vocab = tables[0].shape[1:]
    rows = outs[0].shape[0]
    padded = packets[0].shape[1]
    chunk = min(256, vocab)
    code = lax.broadcasted_iota(jnp.int32, (chunk, padded), 0).astype(F32).astype(LOW)
    for packet, out_ref in zip(packets, outs):
        lines = packet[...].astype(F32)
        acc = jnp.zeros((features, padded), F32)
        for k in range(books):
            for b, table in enumerate(tables):
                local = lines[k : k + 1, :] - base_ref[b].astype(F32)
                for v in range(0, vocab, chunk):
                    acc = acc + nn(table[k, :, v : v + chunk], equal_to(code, local - float(v)))
        out_ref[...] = jnp.transpose(acc)[:rows, :].astype(LOW)


def embed(base, packets, tables, rows, after):
    books, features = tables[0].shape[:2]
    count = len(packets)
    return pl.pallas_call(
        later(partial(embed_body, count, books), len(after), 1 + count + len(tables)),
        out_shape=[sds((rows, features), LOW)] * count,
        in_specs=[scalars()]
        + [in_vmem()] * (count + len(tables))
        + [anywhere()] * len(after),
        out_specs=[in_vmem()] * count,
        compiler_params=pltpu.CompilerParams(vmem_limit_bytes=16 << 20),
        cost_estimate=SMALL,
        name="embed",
    )(base, *packets, *tables, *after)


def embed_back_body(groups, base_ref, line_ref, *refs):
    grads, (out_ref, turned, columns) = refs[:groups], refs[groups:]
    vocab = out_ref.shape[3]
    chunk = min(256, vocab)
    total = line_ref.shape[1]
    rows = total // groups

    @pl.when((pl.program_id(0) == 0) & (pl.program_id(1) == 0))
    def _():
        whole_rows = jnp.concatenate([g[:rows, :] for g in grads], axis=0)
        turned[...] = jnp.transpose(whole_rows)
        wide = jnp.concatenate(
            [line_ref[...].astype(F32), jnp.zeros((128 - line_ref.shape[0], total), F32)], axis=0
        )
        columns[...] = jnp.transpose(wide)

    base = base_ref[pl.program_id(0)].astype(F32)
    lane = lax.broadcasted_iota(jnp.int32, (total, 128), 1)
    column = jnp.sum(
        jnp.where(lane == pl.program_id(1), columns[...], 0.0), axis=1, keepdims=True
    )
    code = lax.broadcasted_iota(jnp.int32, (total, chunk), 1).astype(F32).astype(LOW)
    for v in range(0, vocab, chunk):
        hit = equal_to(code, column - (base + float(v)))
        out_ref[0, 0, :, v : v + chunk] = nn(turned[...], hit).astype(LOW)


def embed_back(base, lines, grads, books, vocab, after):
    parts = base.shape[0]
    groups = len(grads)
    features = grads[0].shape[1]
    rows = lines.shape[1] // groups
    return pl.pallas_call(
        later(partial(embed_back_body, groups), len(after), 2 + groups),
        out_shape=sds((parts, books, features, vocab), LOW),
        grid=(parts, books),
        in_specs=[scalars()] + [in_vmem()] * (1 + groups) + [anywhere()] * len(after),
        out_specs=pl.BlockSpec((1, 1, features, vocab), lambda i, k: (i, k, 0, 0)),
        scratch_shapes=[
            pltpu.VMEM((features, groups * rows), LOW),
            pltpu.VMEM((groups * rows, 128), F32),
        ],
        compiler_params=pltpu.CompilerParams(vmem_limit_bytes=32 << 20),
        cost_estimate=SMALL,
        name="embed_back",
    )(base, lines, *grads, *after)


def gather_features_body(need, put, where_ref, *refs):
    clips = sum(r.shape[1] != refs[0].shape[1] for r in refs)
    part_refs, outs = refs[:-clips], refs[-clips:]
    features = part_refs[0].shape[1]
    strip = outs[0].shape[0]
    for m, part in enumerate(part_refs):
        at = pl.ds(pl.multiple_of(where_ref[m] * features, features), features)
        for c, out_ref in enumerate(outs):
            out_ref[:, at] = part[c * strip : (c + 1) * strip, :]


def split_features_body(scale, need, put, where_ref, side_ref, place_ref, sums_ref, bias_ref, *refs):
    clips = side_ref.shape[0] - 1
    *refs, extra_ref = refs
    grads, outs = refs[:clips], refs[clips:]
    features = outs[0].shape[1]
    columns = bias_ref.shape[1]
    rows = (outs[0].shape[0] - extra_ref.shape[0]) // clips
    at_rows = pl.ds(pl.multiple_of(side_ref[0] * rows, rows), rows)
    extra_ref[...] = jnp.zeros(extra_ref.shape, F32)
    extra_ref[:8, :] = sums_ref[...] * scale
    at = pl.ds(pl.multiple_of(place_ref[0] * columns, columns), columns)
    extra_ref[8:9, at] = bias_ref[0:1, :]
    for m, out_ref in enumerate(outs):
        at = pl.ds(pl.multiple_of(where_ref[m] * features, features), features)
        for c in range(clips):
            out_ref[c * rows : (c + 1) * rows, :] = grads[c][at_rows, at]
        out_ref[clips * rows :, :] = extra_ref[:, at].astype(LOW)


def extra_body(*refs):
    *part_refs, out_ref = refs
    count = out_ref.shape[0]
    out_ref[...] = sum(p[p.shape[0] - count :, :].astype(F32) for p in part_refs)


def text_body(need, put, where_ref, *refs):
    *part_refs, wk_ref, wv_ref, tp_ref, k_ref, v_ref = refs
    columns = part_refs[0].shape[1]
    for m, part in enumerate(part_refs):
        need(1 + m)
        at = pl.ds(pl.multiple_of(where_ref[m] * columns, columns), columns)
        tp_ref[:, at] = part[...]
    put(0)
    for j, w_ref, to_ref in ((1, wk_ref, k_ref), (2, wv_ref, v_ref)):
        need(len(part_refs) + j)
        to_ref[...] = nn(tp_ref[...], flat(w_ref)).astype(LOW)
        put(j)


def text_back_body(clips, need, put, where_ref, *refs):
    dks, dvs = refs[:clips], refs[clips : 2 * clips]
    wk_ref, wv_ref, tp_ref = refs[2 * clips : 2 * clips + 3]
    *part_refs, gk_ref, gv_ref, full_ref = refs[2 * clips + 3 :]
    columns = part_refs[0].shape[1]
    length = dks[0].shape[0]
    need(*range(1, 1 + 2 * clips + 2))
    wk, wv = flat(wk_ref), flat(wv_ref)
    for c in range(clips):
        tp_rows = slice(c * length, (c + 1) * length)
        full_ref[tp_rows, :] = (nt(dks[c][...], wk) + nt(dvs[c][...], wv)).astype(LOW)
    for m, part_ref in enumerate(part_refs):
        at = pl.ds(pl.multiple_of(where_ref[m] * columns, columns), columns)
        part_ref[...] = full_ref[:, at]
    put(*range(len(part_refs)))
    need(3 + 2 * clips)
    turned = jnp.transpose(tp_ref[...])
    for j, grads, to_ref in ((0, dks, gk_ref), (1, dvs, gv_ref)):
        total = None
        for c in range(clips):
            part = nn(turned[:, c * length : (c + 1) * length], grads[c][...])
            total = part if total is None else total + part
        to_ref[...] = total.astype(LOW).reshape(to_ref.shape)
        put(len(part_refs) + j)


def text_weight_body(need, put, rows_ref, own_ref, far_ref, out_ref, bias_ref):
    need(0)
    grad = (own_ref[...].astype(F32) + far_ref[...].astype(F32)).astype(LOW)
    out_ref[...] = tn(rows_ref[...], grad).astype(LOW).reshape(out_ref.shape)
    bias_ref[...] = jnp.broadcast_to(
        jnp.sum(grad.astype(F32), axis=0, keepdims=True), bias_ref.shape
    )


def positions_rows(start, count, feature_count):
    half_width = feature_count // 2
    frequency = jnp.exp(
        jnp.arange(half_width, dtype=F32) * (-math.log(10000.0) / (half_width - 1))
    )
    angles = (start + jnp.arange(count, dtype=jnp.int32)).astype(F32)[:, None] * frequency[None, :]
    return jnp.concatenate([jnp.cos(angles), jnp.sin(angles)], axis=1)


def adam_update(weight, gradient, first_moment, second_moment, step_rate, factor):
    clipped = gradient * factor
    new_first = moment_decay * first_moment + (1.0 - moment_decay) * clipped
    new_second = moment_decay * second_moment + (1.0 - moment_decay) * clipped * clipped
    first_hat = new_first / (1.0 - moment_decay**STEP)
    second_hat = new_second / (1.0 - moment_decay**STEP)
    new_weight = weight * (1.0 - step_rate * weight_decay) - step_rate * first_hat / (
        jnp.sqrt(second_hat) + stability_offset
    )
    return (new_weight, new_first, new_second)


def swap(values, axis, mask):
    size = lax.axis_size(axis)
    return lax.ppermute(values, axis, [(i, i ^ mask) for i in range(size)])


def on_device(
    audio_codes,
    delay_mask,
    frame_mask,
    text_states,
    text_mask,
    attention,
    feedforward,
    tables,
    text_proj,
    norm_params,
    attention_first,
    attention_second,
    feedforward_first,
    feedforward_second,
    tables_first,
    tables_second,
    text_first,
    text_second,
    norm_first,
    norm_second,
):
    clips, frames, books = audio_codes.shape
    text_len, text_width = text_states.shape[1:]
    dp = lax.axis_size("dp")
    tensor = lax.axis_size("tensor")
    group = lax.axis_index("dp")
    place = lax.axis_index("tensor")
    core = place & 1
    side = place >> 1
    sides = tensor // 2
    height = frames // 2
    strip = height // sides
    share = attention.shape[1]
    columns = attention.shape[2]
    width = share * dp
    vocab = tables.shape[2]
    text_share = text_proj.shape[1]
    core_arg = Scalar(core.astype(jnp.int32).reshape(1))
    side_arg = Scalar(side.astype(jnp.int32).reshape(1))
    swap_core = partial(swap, axis="tensor", mask=1)

    def spread_tensor(values):
        held = [values]
        mask = tensor // 2
        order = [0]
        while mask:
            held = held + [swap(v, "tensor", mask) for v in held]
            order = order + [o | mask for o in order]
            mask //= 2
        return [v for _, v in sorted(zip(order, held), key=lambda t: t[0])]

    def collect_tensor(parts):
        mask = 1
        live = {m: p for m, p in enumerate(parts)}
        while mask < tensor:
            fresh = {}
            for m in live:
                if not m & mask:
                    got = swap(live[m | mask].astype(LOW), "tensor", mask)
                    fresh[m] = live[m].astype(F32) + got.astype(F32)
            live = fresh
            mask *= 2
        return live[0]

    def across(values):
        own = values
        mask = 2
        rest = None
        while mask < tensor:
            got = swap(own, "tensor", mask)
            mask *= 2
            if mask < tensor:
                own = (own.astype(F32) + got.astype(F32)).astype(LOW)
            rest = got
        if rest is None:
            rest = jnp.zeros_like(own)
        return own, rest

    def total_over(values, axes):
        for axis in axes:
            mask = 1
            while mask < lax.axis_size(axis):
                values = values + swap(values, axis, mask)
                mask *= 2
        return values

    last = []

    def run(body, outs, operands, after=(), **rest):
        *results, token = kernel(body, outs, operands, after=last + list(after), **rest)
        last[:] = [token]
        return results

    def run_block(*args, **rest):
        return run(*args, **rest)

    def run_weight(*args, **rest):
        results = run(*args, after=older[:1] or soon[:1], **rest)
        if older:
            older.clear()
        else:
            soon.clear()
        return results

    norm_pad = jnp.pad(norm_params.astype(LOW), ((0, 16 - norm_params.shape[0]), (0, columns - share)))
    attn_rows = attention.astype(LOW)
    self_flat = jnp.concatenate([attn_rows[n] for n in SELF] + [norm_pad], axis=0)
    cross_flat = jnp.concatenate([attn_rows[n] for n in CROSS] + [text_proj.astype(LOW).T], axis=0)
    self_all = lax.all_gather(self_flat, "dp", axis=0)
    cross_all = lax.all_gather(cross_flat, "dp", axis=0)
    ffn_all = lax.all_gather(feedforward.astype(LOW), "dp", axis=0)
    head_all = lax.all_gather(tables[books:].astype(LOW), "dp", axis=0)

    frame_live = (jnp.arange(frames, dtype=jnp.int32) < frames - 1).astype(jnp.int32)
    weight_int = delay_mask * frame_mask[:, :, None] * frame_live[None, :, None]
    start = core * height + side * strip
    strip_codes = lax.dynamic_slice_in_dim(audio_codes, start, strip, 1)
    count = clips * strip
    padded = -(-count // 128) * 128
    lines = jnp.transpose(strip_codes, (2, 0, 1)).reshape(books, count)
    lines = jnp.pad(lines, ((0, 0), (0, padded - count)), constant_values=-1)
    count_line = jnp.broadcast_to(jnp.sum(weight_int), (8 - books, padded))
    packet = jnp.concatenate([lines, count_line], axis=0)
    packets = [packet] + [swap(packet, "dp", m) for m in range(1, dp)]
    vocab_base = (place ^ jnp.arange(tensor, dtype=jnp.int32)) * vocab
    group_order = group ^ jnp.arange(dp, dtype=jnp.int32)
    place_order = place ^ jnp.arange(tensor, dtype=jnp.int32)

    text_bias_row = jnp.where(text_mask > 0, 0.0, NEG).astype(F32)
    bias_lines = [text_bias_row[c : c + 1] for c in range(clips)]
    bias_columns = [jnp.transpose(line) for line in bias_lines]
    targets = (jnp.roll(audio_codes, -1, axis=1) - place * vocab).astype(jnp.int32)
    targets = [targets[c] for c in range(clips)]
    loss_weight = [weight_int[c].astype(F32) for c in range(clips)]

    table_parts = spread_tensor(tables[:books].astype(LOW))
    step = max(1, dp // 4)
    arrived = [None] * dp
    for low_end in reversed(range(0, dp, step)):
        embedded = embed(
            vocab_base, packets[low_end : low_end + step], table_parts, count, list(last)
        )
        last[:] = [embedded[-1]]
        if low_end + step == dp:
            begin, _ = lax.optimization_barrier((core * height, embedded[0]))
            placed = positions_rows(begin, height, width)
        for m, piece in enumerate(embedded, low_end):
            arrived[m] = swap(piece, "dp", m) if m else piece
        last += [a for a in arrived[low_end + step : low_end + 2 * step] if a is not None]
    (counted,) = norm_rows_kernel(
        partial(count_body, books), [sds((8, 128), F32)], packets, None, last, name="count"
    )
    back_lines = jnp.concatenate([p[:, :count] for p in packets], axis=1)
    last[:] = bias_lines + bias_columns + targets + loss_weight + [placed, counted, back_lines]
    last += [a for a in arrived if a is not None]
    aligned = share % 128 == 0
    if aligned:
        strips = run(
            gather_features_body,
            [Flow(sds((strip, width), LOW))] * clips,
            [Scalar(group_order)] + arrived,
            name="gather_features",
        )
        strips = [free(a) for a in strips]
    else:
        strips = jnp.take(jnp.stack(arrived), group_order, axis=0)
        strips = jnp.transpose(strips, (1, 0, 2)).reshape(clips, strip, width)

    norm_rows = self_all[:, 4 * share :, :share]
    norm_rows = jnp.transpose(norm_rows, (1, 0, 2)).reshape(16, width).astype(F32)

    def w_attn(n):
        array, at = (self_all, SELF.index(n)) if n in SELF else (cross_all, CROSS.index(n))
        return Window(
            array, (dp, share, columns), lambda ref: ref.at[:, pl.ds(at * share, share), :]
        )

    def w_member(array, n):
        return Window(array, (dp,) + array.shape[2:], lambda ref: ref.at[:, n])

    half_sds = sds((height, width), F32)
    half_low = sds((height, width), LOW)
    flow = Flow(half_low)

    def fetch(a):
        return Window(a, a.shape, everything)


    def norm_step(which, hidden, parts):
        new, out = norm_rows_kernel(
            partial(norm_body, which),
            [half_sds, half_low],
            [hidden, *parts],
            norm_rows,
            last + soon,
        )
        soon[:] = []
        last[:] = [out]
        return new, (out, swap_core(free(out)))

    def norm_back(which, c, parts, before):
        rows = near.get((which, c, "back"), hidden[which][c])
        if before is not None:
            before = near_grad.get((which, c), before)
        operands = [rows, *parts] + ([before] if before is not None else []) + sums
        new, out, total = norm_rows_kernel(
            partial(norm_back_body, which, len(parts)),
            [half_sds, half_low, sds((8, width), F32)],
            operands,
            norm_rows,
            last + soon,
        )
        soon[:] = []
        last[:] = [out]
        sums[:] = [total]
        return new, (out, swap_core(free(out)))

    sums = []
    waiting, soon, older, newest = [], [], [], []
    moving = [None] * clips

    def flush():
        if waiting:
            c, keep, got = waiting.pop()
            parts = norm_rows_kernel(
                add_parts_body,
                [sds((height * part // sum(PIECES), width), LOW) for part in PIECES],
                [keep, got],
                None,
                last,
                name="add",
            )
            last[:] = [parts[-1]]
            fars = [across(free(part))[1] for part in parts]
            moving[c] = (*parts, *fars)
            soon[:] = fars[:-1]
            older[:] = newest
            newest[:] = fars[-1:]

    def reduce_rows(c, keep, send):
        waiting.append((c, keep, swap_core(free(send))))

    text_rows = text_states.reshape(clips * text_len, text_width)
    def text_in_step():
        (result,) = run(
            text_in_body,
            [Flow(sds((clips * text_len, columns), LOW))],
            [
                Scalar(place.astype(jnp.int32).reshape(1)),
                norm_rows,
                fetch(text_rows),
                Window(
                    cross_all,
                    (dp, text_share, columns),
                    lambda ref: ref.at[:, pl.ds(4 * share, text_share), :],
                ),
            ],
            flops=2 * clips * text_len * text_width * columns,
            name="text_in",
        )
        return spread_tensor(free(result))

    full = sds((frames, columns), LOW)
    lse_sds = sds((8, frames), F32)
    tot = [pltpu.VMEM((frames, 128), F32)]
    heads = columns // HEAD_DIM
    score_flops = 2 * heads * frames * HEAD_DIM
    units = feedforward.shape[2]
    inner = sds((frames, units), LOW)
    every = range(clips)

    near, near_grad = {}, {}

    def ahead(phase, c):
        at, clip = (phase - 1, c + 1) if c + 1 < clips else (phase, 0)
        if at < 0 or (phase == 3 and clip == 0) or (clip == c):
            return []
        return [Ahead(hidden[at][clip])]

    def took(phase, c, results):
        at, clip = (phase - 1, c + 1) if c + 1 < clips else (phase, 0)
        if ahead(phase, c):
            *results, near[at, clip] = results
        return results

    def ahead_back(phase, c):
        at, clip = (phase, c + 1) if c + 1 < clips else (phase - 1, 0)
        if clip == c:
            return []
        found = [Ahead(hidden[at][clip])]
        if at < 3:
            found.append(Ahead(grads[clip]))
        return found

    def took_back(phase, c, results):
        at, clip = (phase, c + 1) if c + 1 < clips else (phase - 1, 0)
        count = len(ahead_back(phase, c))
        if count == 2:
            near_grad[at, clip] = results[-1]
        if count:
            near[at, clip, "back"] = results[len(results) - count]
        return results[: len(results) - count]

    def embed_step(c):
        mine = strips[c]
        parts = [mine] + [swap(mine, "tensor", 2 * s) for s in range(1, sides)]
        new, out = run(
            embed_norm_body,
            [Flow(half_sds), Flow(half_low)],
            [side_arg, placed, norm_rows] + parts,
            flops=10 * height * width,
            name="embed_norm",
        )
        return new, (out, swap_core(free(out)))

    def self_step(c, pair):
        own, got = pair
        *saved, keep, send, left, right, hidden[0][c] = took(0, c, run_block(
            self_forward_body,
            [full, full, full, full, lse_sds, flow, flow, Copy(1), Copy(3)],
            [core_arg, own, w_attn(0), got, w_attn(1), w_attn(2), w_attn(6)]
            + [Carry(hidden[0][c])]
            + ahead(0, c),
            flops=8 * frames * width * columns + 4 * score_flops * frames,
            scratch=tot,
            name="self_forward",
        ))
        pairs[0][c] = (left, right)
        reduce_rows(c, keep, send)
        return saved

    text_full = sds((clips * text_len, width), LOW)
    text_cols = sds((clips * text_len, columns), LOW)

    def text_step():
        return run(
            text_body,
            [text_full, text_cols, text_cols],
            [Scalar(place_order)] + text_parts + [w_attn(4), w_attn(5)],
            flops=4 * clips * text_len * width * columns,
            name="text",
        )

    def text_rows_of(array, c):
        return Window(
            array, (text_len, columns), lambda ref: ref.at[pl.ds(c * text_len, text_len), :]
        )

    def cross_step(c, pair):
        own, got = pair
        k, v = text_rows_of(text_key, c), text_rows_of(text_value, c)
        q, o, lse, keep, send, left, right, hidden[1][c] = took(1, c, run_block(
            cross_forward_body,
            [full, full, lse_sds, flow, flow, Copy(1), Copy(3)],
            [core_arg, own, w_attn(3), got, bias_lines[c], k, v, w_attn(7)]
            + [Carry(hidden[1][c])]
            + ahead(1, c),
            flops=4 * frames * width * columns + 4 * score_flops * text_len,
            scratch=tot,
            name="cross_forward",
        ))
        pairs[1][c] = (left, right)
        reduce_rows(c, keep, send)
        return (q, k, v, o, lse)

    def ffn_step(c, pair):
        *saved, keep, send, left, right, hidden[2][c] = took(2, c, run_block(
            ffn_forward_body,
            [inner, inner, flow, flow, Copy(1), Copy(2)],
            [core_arg, *pair, w_member(ffn_all, 0), w_member(ffn_all, 1), Carry(hidden[2][c])]
            + ahead(2, c),
            flops=4 * frames * width * units,
            name="ffn_forward",
        ))
        pairs[2][c] = (left, right)
        reduce_rows(c, keep, send)
        return saved

    hidden = [[None] * clips for _ in range(4)]
    pairs = [[None] * clips for _ in range(4)]
    kept = [[None] * clips for _ in range(3)]
    for c in every:
        hidden[0][c], pairs[0][c] = embed_step(c)
        flush()
        kept[0][c] = self_step(c, pairs[0][c])
        if c == 0:
            text_parts = text_in_step()
    text_hidden, text_key, text_value = text_step()
    for c in every:
        hidden[1][c], pairs[1][c] = norm_step(1, near.get((0, c), hidden[0][c]), moving[c])
        flush()
        kept[1][c] = cross_step(c, pairs[1][c])
    for c in every:
        hidden[2][c], pairs[2][c] = norm_step(2, near.get((1, c), hidden[1][c]), moving[c])
        flush()
        kept[2][c] = ffn_step(c, pairs[2][c])

    loss_part = [None] * clips

    def head_step(c, pair):
        own, got = pair
        logits, stats, left, right, hidden[3][c] = took(3, c, run_block(
            head_forward_body,
            [
                sds((frames, books * vocab), F32),
                Flow(sds((2 * books, frames), F32)),
                Copy(1),
                Copy(3),
            ],
            [core_arg, own, targets[c], got]
            + [w_member(head_all, k) for k in range(books)]
            + [Carry(hidden[3][c])]
            + ahead(3, c),
            flops=2 * frames * width * books * vocab,
            scratch=tot,
            name="head_forward",
        ))
        pairs[3][c] = (left, right)
        return logits, stats

    def merge_step(stats):
        mask = 1
        while mask < tensor:
            far = swap(free(stats), "tensor", mask)
            (stats,) = norm_rows_kernel(
                partial(merge_body, books),
                [sds((2 * books, frames), F32)],
                [stats, far],
                None,
                last,
                name="merge",
            )
            last[:] = [stats]
            mask *= 2
        return stats

    def head_back_step(c, logits, stats, pieces):
        grad, keep, send, loss = run_block(
            head_backward_body,
            [sds((frames, books * vocab), LOW), flow, flow, Flow(sds((8, 128), F32))],
            [core_arg, stats, loss_weight[c], targets[c], fetch(logits)]
            + [w_member(head_all, k) for k in range(books)]
            + [counted],
            flops=2 * frames * width * books * vocab,
            scratch=tot,
            after=pieces,
            name="head_backward",
        )
        loss_part[c] = free(loss)[0, 0]
        reduce_rows(c, keep, send)
        return grad

    self_shared = Shared((dp, 4 * share + text_share, columns), LOW)
    cross_shared = Shared((dp, 4 * share, columns), LOW)
    ffn_shared = Shared((dp,) + feedforward.shape, LOW)
    head_shared = Shared((dp, books, share, vocab), LOW)

    def attn_into(n):
        shared, at = (
            (self_shared, SELF.index(n)) if n in SELF else (cross_shared, CROSS.index(n))
        )
        return Into(
            shared, (dp, share, columns), lambda ref: ref.at[:, pl.ds(at * share, share), :]
        )

    def member_into(shared, n):
        return Into(shared, (dp,) + shared.full.shape[2:], lambda ref: ref.at[:, n])

    def halves(rights, shared, n):
        step = rights[0].shape[1] // 2
        found = []
        for at in (0, step):
            windows = [
                Window(a, (frames, step), lambda ref, at=at: ref.at[:, pl.ds(at, step)])
                for a in rights
            ]
            into = Into(
                shared, (dp, share, step), lambda ref, at=at: ref.at[:, n, :, pl.ds(at, step)]
            )
            found.append((windows, [into]))
        return found

    def weights(lefts, rights, outs, name):
        rights = [a if isinstance(a, Window) else fetch(a) for a in rights]
        total = rights[0].shape[1]
        turn_left = 2 * total > width
        run_weight(
            partial(weight_grad_body, clips, turn_left),
            outs,
            [core_arg] + [fetch(half) for pair in lefts for half in pair] + rights,
            flops=2 * clips * frames * width * total,
            scratch=[pltpu.VMEM((width if turn_left else total, clips * frames), LOW)],
            name=name,
            margin=16,
        )

    logit_grads = [None] * clips
    ready = [None] * clips
    for c in every:
        hidden[3][c], pairs[3][c] = norm_step(3, near.get((2, c), hidden[2][c]), moving[c])
        flush()
        ready[c] = head_step(c, pairs[3][c])
        if c:
            pieces = list(soon)
            flush()
            logits, stats = ready[c - 1]
            logit_grads[c - 1] = head_back_step(c - 1, logits, merge_step(stats), pieces)
    logits, stats = ready[-1]
    stats = merge_step(stats)
    pieces = list(newest)
    flush()
    logit_grads[-1] = head_back_step(clips - 1, logits, stats, pieces)

    def ffn_back_step(c, pair):
        own, got = pair
        grad, keep, send, left, right, grads[c] = took_back(3, c, run_block(
            ffn_backward_body,
            [inner, flow, flow, Copy(1), Copy(2)],
            [core_arg, own, got, w_member(ffn_all, 1), fetch(kept[2][c][1]), w_member(ffn_all, 0)]
            + [Carry(grads[c])]
            + ahead_back(3, c),
            flops=4 * frames * width * units,
            name="ffn_backward",
        ))
        back_pairs[3][c] = (left, right)
        reduce_rows(c, keep, send)
        return grad

    grads = [None] * clips
    back_pairs = [[None] * clips for _ in range(4)]
    inner_grads = [None] * clips
    for c in every:
        grads[c], back_pairs[3][c] = norm_back(3, c, moving[c], None)
        flush()
        inner_grads[c] = ffn_back_step(c, back_pairs[3][c])
        if c == 0:
            step = books // 2 * vocab
            for at in (0, 1):
                windows = [
                    Window(a, (frames, step), lambda ref, at=at: ref.at[:, pl.ds(at * step, step)])
                    for a in logit_grads
                ]
                into = [
                    member_into(head_shared, k) for k in range(at * books // 2, (at + 1) * books // 2)
                ]
                weights(pairs[3], windows, into, "head_weights")
    head_sum = lax.psum_scatter(free(head_shared.array), "dp", scatter_dimension=0, tiled=False)

    acc_text = [pltpu.VMEM((text_len, columns), F32)] * 2
    small = sds((text_len, columns), LOW)

    def cross_back_step(c, pair):
        own, got = pair
        q, k, v, o, lse = kept[1][c]
        bias = bias_columns[c]
        dq, dk, dv, keep, send, left, right, grads[c] = took_back(2, c, run_block(
            cross_backward_body,
            [full, small, small, flow, flow, Copy(1), Copy(3)],
            [core_arg, own, w_attn(7), got, bias, fetch(q), k, v, fetch(lse), w_attn(3)]
            + [Carry(grads[c])]
            + ahead_back(2, c),
            flops=4 * frames * width * columns + 10 * score_flops * text_len,
            scratch=[pltpu.VMEM((frames, columns), LOW)] + acc_text,
            name="cross_backward",
        ))
        back_pairs[2][c] = (left, right)
        reduce_rows(c, keep, send)
        return (dq, dk, dv)

    cross_grads = [None] * clips
    for c in every:
        grads[c], back_pairs[2][c] = norm_back(2, c, moving[c], grads[c])
        flush()
        cross_grads[c] = cross_back_step(c, back_pairs[2][c])
        if c == 0:
            for windows, into in halves([k[0] for k in kept[2]], ffn_shared, 1):
                weights(back_pairs[3], windows, into, "ffn_two")
        if c == min(1, clips - 1):
            for windows, into in halves(inner_grads, ffn_shared, 0):
                weights(pairs[2], windows, into, "ffn_one")
    ffn_sum = lax.psum_scatter(free(ffn_shared.array), "dp", scatter_dimension=0, tiled=False)

    def text_back_step():
        results = run_weight(
            partial(text_back_body, clips),
            [Flow(text_cols)] * tensor + [attn_into(4), attn_into(5)],
            [Scalar(place_order)]
            + [fetch(g[1]) for g in cross_grads]
            + [fetch(g[2]) for g in cross_grads]
            + [w_attn(4), w_attn(5), fetch(text_hidden)],
            flops=8 * clips * text_len * width * columns,
            scratch=[pltpu.VMEM((clips * text_len, width), LOW)],
            name="text_back",
        )
        live = dict(enumerate(results))
        mask = 1
        while mask < tensor:
            fresh = {}
            for m in live:
                if not m & mask:
                    fresh[m] = (live[m], swap(free(live[m | mask]), "tensor", mask))
            mask *= 2
            if mask < tensor:
                for m, both in fresh.items():
                    (fresh[m],) = norm_rows_kernel(
                        add_body, [text_cols], list(both), None, last, name="add"
                    )
                    last[:] = [fresh[m]]
            live = fresh
        return live[0]

    acc_self = [pltpu.VMEM((frames, columns), F32)] * 2

    def self_back_step(c, pair):
        own, got = pair
        q, k, v, o, lse = kept[0][c]
        grad, keep, send, left, right, grads[c] = took_back(1, c, run_block(
            self_backward_body,
            [sds((frames, 3 * columns), LOW), flow, flow, Copy(1), Copy(3)],
            [core_arg, own, w_attn(6), got]
            + [fetch(a) for a in (q, k, v, lse)]
            + [w_attn(0), w_attn(1), w_attn(2), Carry(grads[c])]
            + ahead_back(1, c),
            flops=8 * frames * width * columns + 10 * score_flops * frames,
            scratch=[pltpu.VMEM((frames, columns), LOW)] + acc_self,
            name="self_backward",
        ))
        back_pairs[1][c] = (left, right)
        reduce_rows(c, keep, send)
        return grad

    self_grads = [None] * clips
    last.append(head_sum)
    for c in every:
        grads[c], back_pairs[1][c] = norm_back(1, c, moving[c], grads[c])
        flush()
        self_grads[c] = self_back_step(c, back_pairs[1][c])
        if c == 0:
            text_grad = text_back_step()
            weights(back_pairs[2], [k[3] for k in kept[1]], [attn_into(7)], "cross_out")
            weights(pairs[1], [g[0] for g in cross_grads], [attn_into(3)], "cross_query")
            cross_sum = lax.psum_scatter(
                free(cross_shared.array), "dp", scatter_dimension=0, tiled=False
            )

    zero_lows = [None] * clips

    def zero_step(c):
        _, (zero_lows[c], _) = norm_back(0, c, moving[c], grads[c])

    weights(back_pairs[1], [k[3] for k in kept[0]], [attn_into(6)], "self_out")
    first = list(soon)
    flush()
    text_into = Into(
        self_shared,
        (dp, text_share, columns),
        lambda ref: ref.at[:, pl.ds(4 * share, text_share), :],
    )
    (bias_grad,) = run(
        text_weight_body,
        [text_into, Flow(sds((8, columns), F32))],
        [fetch(text_rows), *text_grad],
        after=[ffn_sum] + first,
        flops=2 * clips * text_len * text_width * columns,
        name="text_weight",
    )
    def self_in(members):
        size = len(members) * columns
        windows = [
            Window(a, (frames, size), lambda ref: ref.at[:, pl.ds(members[0] * columns, size)])
            for a in self_grads
        ]
        weights(pairs[0], windows, [attn_into(n) for n in members], "self_in")

    self_in((0, 1))
    for c in every:
        if c == clips - 1:
            older[:] = newest
            self_in((2,))
            self_sum = lax.psum_scatter(
                free(self_shared.array), "dp", scatter_dimension=0, tiled=False
            )
        zero_step(c)

    if aligned:
        pieces = run(
            partial(split_features_body, 1.0 / sides),
            [Flow(sds((clips * strip + 16, share), LOW))] * dp,
            [
                Scalar(group_order),
                Scalar(jnp.broadcast_to(side.astype(jnp.int32), (clips + 1,))),
                Scalar(place.astype(jnp.int32).reshape(1)),
                sums[0],
                bias_grad,
            ]
            + zero_lows,
            scratch=[pltpu.VMEM((16, width), F32)],
            after=[cross_sum],
            name="split_features",
        )
        pieces = [free(p) for p in pieces]
    else:
        rows = jnp.concatenate(
            [lax.dynamic_slice_in_dim(free(a), side * strip, strip, 0) for a in zero_lows], axis=0
        )
        rows = jnp.transpose(rows.reshape(clips * strip, dp, share), (1, 0, 2))
        pieces = list(jnp.take(rows, group_order, axis=0))
    rows_all = [pieces[0]] + [swap(pieces[m], "dp", m) for m in range(1, dp)]
    embed_parts = embed_back(vocab_base, back_lines, rows_all, books, vocab, list(last))
    grad_embed = collect_tensor([embed_parts[m] for m in range(tensor)])

    if aligned:
        (extra,) = norm_rows_kernel(
            extra_body, [sds((16, share), F32)], rows_all, None, last, name="extra"
        )
        grad_norm_rows = total_over(free(extra), ("tensor",))[: norm_params.shape[0]]
    else:
        norm_part = free(sums[0]) * (1.0 / sides)
        bias_row = lax.dynamic_update_slice_in_dim(
            jnp.zeros((width,), F32), free(bias_grad)[0], place * columns, 0
        )
        norm_total = total_over(
            jnp.concatenate([norm_part, bias_row[None]], axis=0), ("tensor", "dp")
        )
        grad_norm_rows = lax.dynamic_slice_in_dim(norm_total, group * share, share, 1)

    own_self = self_sum[: 4 * share].reshape(4, share, columns)
    own_cross = cross_sum.reshape(4, share, columns)
    grad_attention = jnp.concatenate(
        [own_self[:3], own_cross[:3], own_self[3:], own_cross[3:]], axis=0
    ).astype(F32)
    grad_text_proj = jnp.transpose(self_sum[4 * share :]).astype(F32)
    grad_feedforward = ffn_sum.astype(F32)
    grad_heads = head_sum.astype(F32)
    local_square = (
        jnp.sum(jnp.square(self_sum.astype(F32)))
        + jnp.sum(jnp.square(cross_sum.astype(F32)))
        + jnp.sum(grad_feedforward * grad_feedforward)
        + jnp.sum(grad_heads * grad_heads)
        + jnp.sum(grad_embed * grad_embed)
        + jnp.sum(grad_norm_rows * grad_norm_rows) / tensor
    )
    both = total_over(
        jnp.stack([local_square, sum(loss_part) / tensor]).reshape(1, 2), ("tensor", "dp")
    )[0]
    grad_norm = jnp.sqrt(both[0])
    mean_loss = both[1]
    factor = clip_limit / jnp.maximum(grad_norm, clip_limit)
    grad_tables = jnp.concatenate([grad_embed, grad_heads], 0)
    attn_new, attn_first_new, attn_second_new = adam_update(
        attention, grad_attention, attention_first, attention_second, rate_matrix, factor
    )
    ffn_new, ffn_first_new, ffn_second_new = adam_update(
        feedforward, grad_feedforward, feedforward_first, feedforward_second, rate_matrix, factor
    )
    table_new, table_first_new, table_second_new = adam_update(
        tables, grad_tables, tables_first, tables_second, rate_table, factor
    )
    text_new, text_first_new, text_second_new = adam_update(
        text_proj, grad_text_proj, text_first, text_second, rate_matrix, factor
    )
    norm_new, norm_first_new, norm_second_new = adam_update(
        norm_params, grad_norm_rows, norm_first, norm_second, rate_norm, factor
    )
    return (
        mean_loss,
        free(counted)[0, 0],
        grad_norm,
        attn_new,
        attn_new.astype(LOW),
        attn_first_new,
        attn_second_new,
        ffn_new,
        ffn_new.astype(LOW),
        ffn_first_new,
        ffn_second_new,
        table_new,
        table_new.astype(LOW),
        table_first_new,
        table_second_new,
        text_new,
        text_new.astype(LOW),
        text_first_new,
        text_second_new,
        norm_new,
        norm_first_new,
        norm_second_new,
    )


def solution(mesh):
    clip3 = P("dp", None, None)
    clip2 = P("dp", None)
    matrix = P(None, "dp", "tensor")
    text = P("tensor", "dp")
    norm = P(None, "dp")
    placed = (
        (clip3, clip3, clip2, clip3, clip2)
        + (matrix, matrix, matrix, text, norm)
        + (matrix,) * 6
        + (text, text, norm, norm)
    )
    return jax.shard_map(
        on_device,
        mesh=mesh,
        in_specs=placed,
        out_specs=(P(), P(), P()) + (matrix,) * 12 + (text,) * 4 + (norm,) * 3,
        check_vma=False,
    )
```

```python
from functools import partial
import math

import jax
import jax.numpy as jnp
from jax import lax
from jax.experimental import pallas as pl
from jax.experimental.pallas import tpu as pltpu
from jax.sharding import PartitionSpec as P

HEAD_DIM = 64
STEP = 5
BLOCK = 256
NEG = -1e30
LOW = jnp.bfloat16
F32 = jnp.float32

SELF = (0, 1, 2, 6)
CROSS = (3, 4, 5, 7)

SMALL = pl.CostEstimate(flops=1024, bytes_accessed=1024, transcendentals=0)

PIECES = (1, 1)

clip_limit = 0.004
stability_offset = 1e-08
weight_decay = 0.01
moment_decay = 0.5
rate_matrix = 0.03
rate_table = 0.05
rate_norm = 0.2


def nn(a, b):
    return lax.dot_general(a, b, (((1,), (0,)), ((), ())), preferred_element_type=F32)


def nt(a, b):
    return lax.dot_general(a, b, (((1,), (1,)), ((), ())), preferred_element_type=F32)


def tn(a, b):
    return lax.dot_general(a, b, (((0,), (0,)), ((), ())), preferred_element_type=F32)


def sds(shape, kind):
    return jax.ShapeDtypeStruct(shape, kind)


def scalars():
    return pl.BlockSpec(memory_space=pltpu.SMEM)


def anywhere():
    return pl.BlockSpec(memory_space=pl.ANY)


def in_hbm():
    return pl.BlockSpec(memory_space=pltpu.HBM)


def in_vmem():
    return pl.BlockSpec(memory_space=pltpu.VMEM)


def whole(a):
    rank = len(a.shape)
    return pl.BlockSpec(a.shape, lambda i: (0,) * rank)


def later(body, count, at):
    def ordered(*refs):
        return body(*refs[:at], *refs[at + count :])

    return ordered


class Scalar:
    def __init__(self, array):
        self.array = array


class Window:
    def __init__(self, array, shape, pick):
        self.array, self.shape, self.pick = array, tuple(shape), pick


def hold(array, space):
    return pltpu.with_memory_space_constraint(array, space)


def free(array):
    return pltpu.with_memory_space_constraint(array, pl.ANY)


class Flow:
    def __init__(self, shape):
        self.shape = shape


class Copy:
    def __init__(self, i):
        self.i = i


class Carry:
    def __init__(self, array):
        self.array = array


class Ahead:
    def __init__(self, array):
        self.array = array


class Shared:
    def __init__(self, shape, kind):
        self.full, self.array = sds(shape, kind), None


class Into:
    def __init__(self, shared, shape, pick):
        self.shared, self.shape, self.pick = shared, tuple(shape), pick


def everything(ref):
    return ref


def nbytes_of(shape, kind):
    return math.prod(shape) * jnp.dtype(kind).itemsize


def kernel(body, outs, operands, flops=0, scratch=(), name=None, exps=0, after=(), margin=12):
    arrays, specs, windows, shown, fetched = [], [], [], [], {}
    outs = list(outs)
    for i, a in enumerate(operands):
        shown.append(not isinstance(a, (Carry, Ahead)))
        if isinstance(a, Ahead):
            arrays.append(hold(a.array, pltpu.HBM))
            specs.append(in_hbm())
            windows.append(None)
            outs.append(Flow(sds(a.array.shape, a.array.dtype)))
            fetched[len(outs) - 1] = i
        elif isinstance(a, Carry):
            arrays.append(hold(a.array, pltpu.VMEM))
            specs.append(in_vmem())
            windows.append(None)
            outs.append(Copy(i))
        elif isinstance(a, Scalar):
            arrays.append(a.array)
            specs.append(scalars())
            windows.append(None)
        elif isinstance(a, Window):
            arrays.append(hold(a.array, pltpu.HBM))
            specs.append(in_hbm())
            windows.append(a)
        else:
            arrays.append(hold(a, pltpu.VMEM))
            specs.append(in_vmem())
            windows.append(None)
    aliases, out_shapes, out_specs, out_parts, owners = {}, [], [], [], []
    extra = []
    for o in outs:
        if isinstance(o, Into):
            if o.shared not in owners:
                if o.shared.array is not None:
                    aliases[len(arrays) + len(extra)] = len(out_shapes)
                    extra.append(o.shared.array)
                out_shapes.append(pltpu.HBM(o.shared.full.shape, o.shared.full.dtype))
                out_specs.append(in_hbm())
                owners.append(o.shared)
            out_parts.append(("put", o.shape, o.shared.full.dtype, o.pick, owners.index(o.shared)))
            continue
        if isinstance(o, Flow):
            out_parts.append(("flow", None, None, None, len(out_shapes)))
            out_shapes.append(pltpu.VMEM(o.shape.shape, o.shape.dtype))
            out_specs.append(in_vmem())
        elif isinstance(o, Copy):
            a = arrays[o.i]
            out_parts.append(("copy", o.i, None, None, len(out_shapes)))
            out_shapes.append(pltpu.HBM(a.shape, a.dtype))
            out_specs.append(in_hbm())
        else:
            out_parts.append(("put", o.shape, o.dtype, everything, len(out_shapes)))
            out_shapes.append(pltpu.HBM(o.shape, o.dtype))
            out_specs.append(in_hbm())
        owners.append(None)
    out_parts.append(("token", None, None, None, len(out_shapes)))
    out_shapes.append(pltpu.VMEM((8, 128), F32))
    out_specs.append(in_vmem())
    owners.append(None)
    moved = [w for w in windows if w is not None]
    made = [p for p in out_parts if p[0] == "put"]
    count_in, count_extra, count_after = len(arrays), len(extra), len(after)
    count_out, count_moved, count_arrays = len(out_parts), len(moved), len(out_shapes)

    def run_body(*refs):
        refs = list(refs)
        ins = refs[:count_in]
        at = count_in + count_extra + count_after
        out_refs = refs[at : at + count_arrays]
        at += count_arrays
        in_buffers = refs[at : at + count_moved]
        at += count_moved
        made_buffers = refs[at : at + len(made)]
        at += len(made)
        in_sems, out_sems = refs[at], refs[at + 1]
        rest = refs[at + 2 :]
        views, copies, waited = [], {}, set()
        n = 0
        for i, (ref, w) in enumerate(zip(ins, windows)):
            if not shown[i]:
                continue
            if w is None:
                views.append(ref)
            else:
                copies[i] = pltpu.make_async_copy(w.pick(ref), in_buffers[n], in_sems.at[n])
                copies[i].start()
                views.append(in_buffers[n])
                n += 1
        sent, sources = {}, {}

        def need(*which):
            for i in which:
                if i in copies and i not in waited:
                    waited.add(i)
                    copies[i].wait()

        def put(*which):
            for j in which:
                if j in sources:
                    source, target = sources[j]
                    sent[j] = pltpu.make_async_copy(source, target, out_sems.at[j])
                    sent[j].start()

        body_outs = []
        n = 0
        for j, (kind, what, _, pick, owner) in enumerate(out_parts):
            if kind == "put":
                sources[j] = (made_buffers[n], pick(out_refs[owner]))
                body_outs.append(made_buffers[n])
                n += 1
            elif kind == "copy":
                sources[j] = (ins[what], out_refs[owner])
                put(j)
            elif kind == "token":
                out_refs[owner][...] = jnp.zeros((8, 128), F32)
            elif j in fetched:
                sources[j] = (ins[fetched[j]], out_refs[owner])
                put(j)
            else:
                body_outs.append(out_refs[owner])
        body(need, put, *views, *body_outs, *rest)
        need(*copies)
        put(*(j for j in sources if j not in sent))
        for copy in sent.values():
            copy.wait()

    nbytes = sum(nbytes_of(w.shape, w.array.dtype) for w in moved)
    nbytes += sum(nbytes_of(p[1], p[2]) for p in made)
    held = nbytes + sum(nbytes_of(m.shape, m.dtype) for m in scratch)
    results = pl.pallas_call(
        run_body,
        out_shape=tuple(out_shapes),
        in_specs=specs + [anywhere()] * (count_extra + count_after),
        out_specs=tuple(out_specs),
        input_output_aliases=aliases,
        scratch_shapes=[pltpu.VMEM(w.shape, w.array.dtype) for w in moved]
        + [pltpu.VMEM(p[1], p[2]) for p in made]
        + [
            pltpu.SemaphoreType.DMA((max(1, count_moved),)),
            pltpu.SemaphoreType.DMA((max(1, count_out),)),
        ]
        + list(scratch),
        compiler_params=pltpu.CompilerParams(vmem_limit_bytes=held + (margin << 20)),
        cost_estimate=SMALL,
        name=name,
    )(*arrays, *extra, *after)
    for owner, result in zip(owners, results):
        if owner is not None:
            owner.array = result
    return [r for owner, r in zip(owners, results) if owner is None]


def flat(ref):
    w = ref[...]
    return w.reshape(-1, w.shape[-1])


def half_rows(core, height):
    return (
        pl.ds(pl.multiple_of(core * height, height), height),
        pl.ds(pl.multiple_of((1 - core) * height, height), height),
    )


def attend_block(query, keys, values, head_masks, diagonal, bias):
    rows, width = query.shape
    lane = lax.broadcasted_iota(jnp.int32, (rows, 128), 1)
    column = lax.broadcasted_iota(jnp.int32, (rows, width), 1) // HEAD_DIM
    mixed = jnp.zeros((rows, width), F32)
    totals = jnp.zeros((rows, 128), F32)
    count = keys.shape[0]
    for h, mask in enumerate(head_masks):
        s = nt(query * mask, keys)
        if diagonal is not None:
            last = jnp.where(diagonal, s[:, count - rows :], NEG)
            s = last if count == rows else jnp.concatenate([s[:, : count - rows], last], axis=1)
        if bias is not None:
            s = s + bias
        top = jnp.max(s, axis=1, keepdims=True)
        e = jnp.exp(s - top)
        total = jnp.sum(e, axis=1, keepdims=True)
        p = (e * (1.0 / total)).astype(LOW)
        mixed = jnp.where(column == h, nn(p, values), mixed)
        totals = jnp.where(lane == h, top + jnp.log(total), totals)
    return mixed, totals


def masks_of(width):
    head = lax.broadcasted_iota(jnp.int32, (1, width), 1) // HEAD_DIM
    return [(head == h).astype(F32).astype(LOW) for h in range(width // HEAD_DIM)]


def triangle(size):
    row = lax.broadcasted_iota(jnp.int32, (size, size), 0)
    col = lax.broadcasted_iota(jnp.int32, (size, size), 1)
    return row >= col


def self_forward_body(
    need, put, core_ref, own_ref, wq_ref, got_ref, wk_ref, wv_ref, wo_ref,
    q_ref, k_ref, v_ref, o_ref, lse_ref, keep_ref, send_ref, tot_ref,
):
    height = own_ref.shape[0]
    frames, width = q_ref.shape
    mine, other = half_rows(core_ref[0], height)
    need(1)
    for i, w_ref, to_ref in ((2, wq_ref, q_ref), (4, wk_ref, k_ref), (5, wv_ref, v_ref)):
        need(i)
        w = flat(w_ref)
        to_ref[mine, :] = nn(own_ref[...], w).astype(LOW)
        need(3)
        to_ref[other, :] = nn(got_ref[...], w).astype(LOW)
    put(0, 1, 2)
    scale = jnp.asarray(HEAD_DIM**-0.5, LOW)
    head_masks = masks_of(width)
    diagonal = triangle(BLOCK)
    for i in range(frames // BLOCK):
        rows = slice(i * BLOCK, (i + 1) * BLOCK)
        mixed, totals = attend_block(
            q_ref[rows, :] * scale,
            k_ref[: (i + 1) * BLOCK, :],
            v_ref[: (i + 1) * BLOCK, :],
            head_masks,
            diagonal,
            None,
        )
        o_ref[rows, :] = mixed.astype(LOW)
        tot_ref[rows, :] = totals
    put(3)
    need(6)
    wo = flat(wo_ref)
    send_ref[...] = nt(o_ref[other, :], wo).astype(LOW)
    put(6)
    keep_ref[...] = nt(o_ref[mine, :], wo).astype(LOW)
    put(5)
    lse_ref[...] = jnp.transpose(tot_ref[...])[:8, :]


def cross_forward_body(
    need, put, core_ref, own_ref, wq_ref, got_ref, bias_ref, k_ref, v_ref, wo_ref,
    q_ref, o_ref, lse_ref, keep_ref, send_ref, tot_ref,
):
    height = own_ref.shape[0]
    frames, width = q_ref.shape
    mine, other = half_rows(core_ref[0], height)
    need(1, 2)
    w = flat(wq_ref)
    q_ref[mine, :] = nn(own_ref[...], w).astype(LOW)
    need(3)
    q_ref[other, :] = nn(got_ref[...], w).astype(LOW)
    put(0)
    scale = jnp.asarray(HEAD_DIM**-0.5, LOW)
    head_masks = masks_of(width)
    need(4, 5, 6)
    for i in range(frames // BLOCK):
        rows = slice(i * BLOCK, (i + 1) * BLOCK)
        mixed, totals = attend_block(
            q_ref[rows, :] * scale, k_ref[...], v_ref[...], head_masks, None, bias_ref[...]
        )
        o_ref[rows, :] = mixed.astype(LOW)
        tot_ref[rows, :] = totals
    put(1)
    need(7)
    wo = flat(wo_ref)
    send_ref[...] = nt(o_ref[other, :], wo).astype(LOW)
    put(4)
    keep_ref[...] = nt(o_ref[mine, :], wo).astype(LOW)
    put(3)
    lse_ref[...] = jnp.transpose(tot_ref[...])[:8, :]


def ffn_forward_body(
    need, put, core_ref, own_ref, got_ref, w1_ref, w2_ref,
    act_ref, slope_ref, keep_ref, send_ref,
):
    height = own_ref.shape[0]
    mine, other = half_rows(core_ref[0], height)
    need(1, 2, 3)
    w1 = flat(w1_ref)
    for j, source, rows, to_ref in (
        (3, got_ref, other, send_ref),
        (2, own_ref, mine, keep_ref),
    ):
        u = nn(source[...], w1)
        phi = 0.5 * (1.0 + lax.erf(u * (2.0**-0.5)))
        act = (u * phi).astype(LOW)
        density = jnp.exp(-0.5 * u * u) * ((2.0 * math.pi) ** -0.5)
        act_ref[rows, :] = act
        slope_ref[rows, :] = (phi + u * density).astype(LOW)
        need(4)
        to_ref[...] = nt(act, flat(w2_ref)).astype(to_ref.dtype)
        put(j)


def head_forward_body(
    need, put, core_ref, own_ref, target_ref, got_ref, *refs
):
    *w_refs, logits_ref, stats_ref, tot_ref = refs
    height = own_ref.shape[0]
    books = len(w_refs)
    vocab = w_refs[0].shape[2]
    halves = half_rows(core_ref[0], height)
    lane = lax.broadcasted_iota(jnp.int32, (height, 128), 1)
    code = lax.broadcasted_iota(jnp.int32, (height, vocab), 1)
    need(1, 2)
    totals = [jnp.zeros((height, 128), F32)] * 2
    for k, w_ref in enumerate(w_refs):
        need(4 + k)
        w = flat(w_ref)
        for j, (source, rows) in enumerate(zip((own_ref, got_ref), halves)):
            need(1 + 2 * j)
            s = nn(source[...], w)
            logits_ref[rows, k * vocab : (k + 1) * vocab] = s
            top = jnp.max(s, axis=1, keepdims=True)
            total = jnp.sum(jnp.exp(s - top), axis=1, keepdims=True)
            hit = code == target_ref[rows, k : k + 1]
            pick = jnp.sum(jnp.where(hit, s, 0.0), axis=1, keepdims=True)
            totals[j] = jnp.where(lane == k, top + jnp.log(total), totals[j])
            totals[j] = jnp.where(lane == books + k, pick, totals[j])
    put(0)
    for rows, t in zip(halves, totals):
        tot_ref[rows, :] = t
    stats_ref[...] = jnp.transpose(tot_ref[...])[: 2 * books, :]


def head_backward_body(
    need, put, core_ref, total_ref, weight_ref, target_ref, logits_ref, *refs
):
    *w_refs, valid_ref, grad_ref, keep_ref, send_ref, loss_ref, col_ref = refs
    height = keep_ref.shape[0]
    books = len(w_refs)
    vocab = w_refs[0].shape[2]
    mine, other = half_rows(core_ref[0], height)
    frames = logits_ref.shape[0]
    need(1, 2, 3)
    wide = jnp.concatenate(
        [total_ref[...], jnp.zeros((128 - total_ref.shape[0], frames), F32)], axis=0
    )
    col_ref[...] = jnp.transpose(wide)
    share = 1.0 / valid_ref[0:1, 0:1]
    gap = (col_ref[:, :books] - col_ref[:, books : 2 * books]) * (weight_ref[...] * share)
    loss_ref[...] = jnp.broadcast_to(jnp.sum(gap).reshape(1, 1), loss_ref.shape)
    code = lax.broadcasted_iota(jnp.int32, (height, vocab), 1)
    need(4)
    for j, rows, to_ref in ((2, other, send_ref), (1, mine, keep_ref)):
        weight = weight_ref[rows, :] * share
        total = col_ref[rows, :]
        acc = None
        for k, w_ref in enumerate(w_refs):
            s = logits_ref[rows, k * vocab : (k + 1) * vocab]
            p = jnp.exp(s - total[:, k : k + 1])
            hit = jnp.where(code == target_ref[rows, k : k + 1], 1.0, 0.0)
            g = ((p - hit) * weight[:, k : k + 1]).astype(LOW)
            grad_ref[rows, k * vocab : (k + 1) * vocab] = g
            need(5 + k)
            part = nt(g, flat(w_ref))
            acc = part if acc is None else acc + part
        to_ref[...] = acc.astype(to_ref.dtype)
        put(j)


def ffn_backward_body(
    need, put, core_ref, own_ref, got_ref, w2_ref, slope_ref, w1_ref,
    grad_ref, keep_ref, send_ref,
):
    height = own_ref.shape[0]
    mine, other = half_rows(core_ref[0], height)
    need(1, 2, 3, 4)
    w2 = flat(w2_ref)
    for j, source, rows, to_ref in (
        (2, got_ref, other, send_ref),
        (1, own_ref, mine, keep_ref),
    ):
        g = (nn(source[...], w2) * slope_ref[rows, :].astype(F32)).astype(LOW)
        grad_ref[rows, :] = g
        need(5)
        to_ref[...] = nt(g, flat(w1_ref)).astype(to_ref.dtype)
        put(j)


def attend_back(
    q, k, v, g, lse, head_masks, scale, diagonal, bias, dq_ref, rows, dk_ref, dv_ref, first
):
    count, width = k.shape
    step = q.shape[0]
    dq = jnp.zeros((step, width), F32)
    dk = jnp.zeros((count, width), F32)
    dv = jnp.zeros((count, width), F32)
    for h, mask in enumerate(head_masks):
        qm = q * mask
        gm = g * mask
        s = nt(k, qm)
        if diagonal is not None:
            last = jnp.where(diagonal, s[count - step :, :], NEG)
            s = last if count == step else jnp.concatenate([s[: count - step, :], last], axis=0)
        if bias is not None:
            s = s + bias
        p = jnp.exp(s - lse[h : h + 1, :])
        dp = nt(v, gm)
        inner = jnp.sum(p * dp, axis=0, keepdims=True)
        ds = (p * (dp - inner)).astype(LOW)
        dq = dq + tn(ds, k * mask)
        dk = dk + nn(ds, qm)
        dv = dv + nn(p.astype(LOW), gm)
    dq_ref[rows, :width] = (dq * scale).astype(LOW)
    dk_ref[:count, :] = dk if first else dk_ref[:count, :] + dk
    dv_ref[:count, :] = dv if first else dv_ref[:count, :] + dv


def self_backward_body(
    need, put, core_ref, own_ref, wo_ref, got_ref, q_ref, k_ref, v_ref, lse_ref,
    wq_ref, wk_ref, wv_ref, grad_ref, keep_ref, send_ref, g_ref, dk_acc, dv_acc,
):
    height = own_ref.shape[0]
    frames, width = q_ref.shape
    mine, other = half_rows(core_ref[0], height)
    need(1, 2)
    wo = flat(wo_ref)
    g_ref[mine, :] = nn(own_ref[...], wo).astype(LOW)
    need(3)
    g_ref[other, :] = nn(got_ref[...], wo).astype(LOW)
    scale = HEAD_DIM**-0.5
    head_masks = masks_of(width)
    row = lax.broadcasted_iota(jnp.int32, (BLOCK, BLOCK), 0)
    col = lax.broadcasted_iota(jnp.int32, (BLOCK, BLOCK), 1)
    diagonal = col >= row
    blocks = frames // BLOCK
    need(4, 5, 6, 7)
    for i in reversed(range(blocks)):
        rows = slice(i * BLOCK, (i + 1) * BLOCK)
        count = (i + 1) * BLOCK
        attend_back(
            q_ref[rows, :] * jnp.asarray(scale, LOW),
            k_ref[:count, :],
            v_ref[:count, :],
            g_ref[rows, :],
            lse_ref[:, rows],
            head_masks,
            scale,
            diagonal,
            None,
            grad_ref,
            rows,
            dk_acc,
            dv_acc,
            i == blocks - 1,
        )
    grad_ref[:, width : 2 * width] = dk_acc[...].astype(LOW)
    grad_ref[:, 2 * width :] = dv_acc[...].astype(LOW)
    put(0)
    need(8, 9, 10)
    for j, rows, to_ref in ((2, other, send_ref), (1, mine, keep_ref)):
        part = None
        for n, w_ref in enumerate((wq_ref, wk_ref, wv_ref)):
            term = nt(grad_ref[rows, n * width : (n + 1) * width], flat(w_ref))
            part = term if part is None else part + term
        to_ref[...] = part.astype(to_ref.dtype)
        put(j)


def cross_backward_body(
    need, put, core_ref, own_ref, wo_ref, got_ref, bias_ref, q_ref, k_ref, v_ref, lse_ref, wq_ref,
    dq_ref, dk_ref, dv_ref, keep_ref, send_ref, g_ref, dk_acc, dv_acc,
):
    height = own_ref.shape[0]
    frames, width = q_ref.shape
    mine, other = half_rows(core_ref[0], height)
    need(1, 2)
    wo = flat(wo_ref)
    g_ref[mine, :] = nn(own_ref[...], wo).astype(LOW)
    need(3)
    g_ref[other, :] = nn(got_ref[...], wo).astype(LOW)
    scale = HEAD_DIM**-0.5
    head_masks = masks_of(width)
    need(4, 5, 6, 7, 8)
    for i in range(frames // BLOCK):
        rows = slice(i * BLOCK, (i + 1) * BLOCK)
        attend_back(
            q_ref[rows, :] * jnp.asarray(scale, LOW),
            k_ref[...],
            v_ref[...],
            g_ref[rows, :],
            lse_ref[:, rows],
            head_masks,
            scale,
            None,
            bias_ref[...],
            dq_ref,
            rows,
            dk_acc,
            dv_acc,
            i == 0,
        )
    put(0)
    need(9)
    wq = flat(wq_ref)
    for j, rows, to_ref in ((4, other, send_ref), (3, mine, keep_ref)):
        to_ref[...] = nt(dq_ref[rows, :], wq).astype(to_ref.dtype)
        put(j)
    dk_ref[...] = dk_acc[...].astype(LOW)
    dv_ref[...] = dv_acc[...].astype(LOW)


def normalize(values, gain, shift):
    center = values - jnp.mean(values, axis=1, keepdims=True)
    spread = jnp.mean(center * center, axis=1, keepdims=True)
    return center * lax.rsqrt(spread + 1e-05) * gain + shift


def count_body(books, *refs):
    *packet_refs, out_ref = refs
    total = sum(p[books : books + 1, 0:128] for p in packet_refs)
    out_ref[...] = jnp.broadcast_to(total, out_ref.shape).astype(F32)


def merge_body(books, own_ref, far_ref, out_ref):
    own, far = own_ref[:books, :], far_ref[:books, :]
    high = jnp.maximum(own, far)
    out_ref[:books, :] = high + jnp.log(jnp.exp(own - high) + jnp.exp(far - high))
    out_ref[books:, :] = own_ref[books:, :] + far_ref[books:, :]


def text_in_body(need, put, place_ref, norm_ref, rows_ref, w_ref, out_ref):
    columns = out_ref.shape[1]
    at = pl.ds(pl.multiple_of(place_ref[0] * columns, columns), columns)
    need(2, 3)
    out_ref[...] = (nn(rows_ref[...], flat(w_ref)) + norm_ref[8:9, at]).astype(LOW)


def add_body(keep_ref, got_ref, out_ref):
    out_ref[...] = (keep_ref[...].astype(F32) + got_ref[...].astype(F32)).astype(LOW)


def add_parts_body(keep_ref, got_ref, *out_refs):
    start = 0
    for out_ref in out_refs:
        at = slice(start, start + out_ref.shape[0])
        start += out_ref.shape[0]
        out_ref[...] = (keep_ref[at, :].astype(F32) + got_ref[at, :].astype(F32)).astype(LOW)


def joined(refs):
    half = len(refs) // 2
    sums = [a[...].astype(F32) + b[...].astype(F32) for a, b in zip(refs[:half], refs[half:])]
    return jnp.concatenate(sums, axis=0)


def norm_body(which, hidden_ref, *refs):
    *part_refs, norm_ref, new_ref, out_ref = refs
    new = hidden_ref[...] + joined(part_refs)
    new_ref[...] = new
    out_ref[...] = normalize(
        new, norm_ref[which : which + 1, :], norm_ref[which + 4 : which + 5, :]
    ).astype(LOW)


def embed_norm_body(need, put, side_ref, place_ref, norm_ref, *refs):
    *part_refs, new_ref, out_ref = refs
    side = side_ref[0]
    rows = part_refs[0].shape[0]
    need(1, 2)
    for s, part in enumerate(part_refs):
        need(3 + s)
        at = pl.ds(pl.multiple_of((side ^ s) * rows, rows), rows)
        new = part[...].astype(F32) + place_ref[at, :]
        new_ref[at, :] = new
        out_ref[at, :] = normalize(new, norm_ref[0:1, :], norm_ref[4:5, :]).astype(LOW)
    put(1, 0)


def norm_back_body(which, parts, hidden_ref, *refs):
    *before, norm_ref, new_ref, low_ref, sums_ref = refs[parts:]
    sums = before.pop() if before and before[-1].shape[0] == sums_ref.shape[0] else None
    values = hidden_ref[...]
    grad = joined(refs[:parts])
    gain = norm_ref[which : which + 1, :]
    center = values - jnp.mean(values, axis=1, keepdims=True)
    spread = jnp.mean(center * center, axis=1, keepdims=True)
    inverse = lax.rsqrt(spread + 1e-05)
    unit = center * inverse
    scaled = grad * gain
    first = jnp.mean(scaled, axis=1, keepdims=True)
    second = jnp.mean(scaled * unit, axis=1, keepdims=True)
    new = inverse * (scaled - first - unit * second)
    if before:
        new = before[0][...] + new
    new_ref[...] = new
    low_ref[...] = new.astype(LOW)
    sums_ref[...] = jnp.zeros(sums_ref.shape, F32) if sums is None else sums[...]
    sums_ref[which : which + 1, :] += jnp.sum(grad * unit, axis=0, keepdims=True)
    sums_ref[which + 4 : which + 5, :] += jnp.sum(grad, axis=0, keepdims=True)


def weight_grad_body(clips, turn_left, need, put, core_ref, *refs):
    lefts = refs[: 2 * clips]
    rights = refs[2 * clips : 3 * clips]
    outs = refs[3 * clips : -1]
    turned = refs[-1]
    height, width = lefts[0].shape
    frames = rights[0].shape[0]
    group = outs[0].shape[2]
    core = core_ref[0]

    def place(c, at):
        return pl.ds(pl.multiple_of(c * frames + at * height, 128), height)

    if turn_left:
        step = min(group, 512)
        for m, v in [(m, v) for m in range(len(outs)) for v in range(0, group, step)]:
            total = None
            for c in range(clips):
                if m == 0 and v == 0:
                    for j, at in ((0, core), (1, 1 - core)):
                        need(1 + 2 * c + j)
                        turned[:, place(c, at)] = jnp.transpose(lefts[2 * c + j][...])
                    need(1 + 2 * clips + c)
                part = nn(
                    turned[:, c * frames : (c + 1) * frames],
                    rights[c][:, m * group + v : m * group + v + step],
                )
                total = part if total is None else total + part
            outs[m][:, :, v : v + step] = total.astype(LOW).reshape(-1, outs[m].shape[1], step)
            if v + step == group:
                put(m)
    else:
        total = None
        for c in range(clips):
            need(1 + 2 * clips + c)
            turned[:, c * frames : (c + 1) * frames] = jnp.transpose(rights[c][...])
            for j, at in ((0, core), (1, 1 - core)):
                need(1 + 2 * c + j)
                part = nn(turned[:, place(c, at)], lefts[2 * c + j][...])
                total = part if total is None else total + part
        for m, out_ref in enumerate(outs):
            member = total[m * group : (m + 1) * group, :]
            out_ref[...] = jnp.transpose(member).astype(LOW).reshape(out_ref.shape)
            put(m)


def norm_rows_kernel(body, outs, operands, norm_rows, after, name="norm"):
    height, width = operands[0].shape
    operands = list(operands) + ([] if norm_rows is None else [norm_rows])
    nbytes = sum(nbytes_of(a.shape, a.dtype) for a in operands + list(outs))
    return pl.pallas_call(
        later(body, len(after), len(operands)),
        out_shape=tuple(pltpu.VMEM(o.shape, o.dtype) for o in outs),
        in_specs=[in_vmem()] * len(operands) + [anywhere()] * len(after),
        out_specs=tuple(in_vmem() for _ in outs),
        compiler_params=pltpu.CompilerParams(vmem_limit_bytes=12 << 20),
        cost_estimate=SMALL,
        name=name,
    )(*(hold(a, pltpu.VMEM) for a in operands), *after)


def equal_to(code, local):
    local = jnp.clip(local, -1.0, 256.0).astype(LOW)
    return jnp.where(code == local, jnp.asarray(1, LOW), jnp.asarray(0, LOW))


def embed_body(count, books, base_ref, *refs):
    packets, tables, outs = refs[:count], refs[count : len(refs) - count], refs[len(refs) - count :]
    features, vocab = tables[0].shape[1:]
    rows = outs[0].shape[0]
    padded = packets[0].shape[1]
    chunk = min(256, vocab)
    code = lax.broadcasted_iota(jnp.int32, (chunk, padded), 0).astype(F32).astype(LOW)
    for packet, out_ref in zip(packets, outs):
        lines = packet[...].astype(F32)
        acc = jnp.zeros((features, padded), F32)
        for k in range(books):
            for b, table in enumerate(tables):
                local = lines[k : k + 1, :] - base_ref[b].astype(F32)
                for v in range(0, vocab, chunk):
                    acc = acc + nn(table[k, :, v : v + chunk], equal_to(code, local - float(v)))
        out_ref[...] = jnp.transpose(acc)[:rows, :].astype(LOW)


def embed(base, packets, tables, rows, after):
    books, features = tables[0].shape[:2]
    count = len(packets)
    return pl.pallas_call(
        later(partial(embed_body, count, books), len(after), 1 + count + len(tables)),
        out_shape=[sds((rows, features), LOW)] * count,
        in_specs=[scalars()]
        + [in_vmem()] * (count + len(tables))
        + [anywhere()] * len(after),
        out_specs=[in_vmem()] * count,
        compiler_params=pltpu.CompilerParams(vmem_limit_bytes=16 << 20),
        cost_estimate=SMALL,
        name="embed",
    )(base, *packets, *tables, *after)


def embed_back_body(groups, base_ref, line_ref, *refs):
    grads, (out_ref, turned, columns) = refs[:groups], refs[groups:]
    vocab = out_ref.shape[3]
    chunk = min(256, vocab)
    total = line_ref.shape[1]
    rows = total // groups

    @pl.when((pl.program_id(0) == 0) & (pl.program_id(1) == 0))
    def _():
        whole_rows = jnp.concatenate([g[:rows, :] for g in grads], axis=0)
        turned[...] = jnp.transpose(whole_rows)
        wide = jnp.concatenate(
            [line_ref[...].astype(F32), jnp.zeros((128 - line_ref.shape[0], total), F32)], axis=0
        )
        columns[...] = jnp.transpose(wide)

    base = base_ref[pl.program_id(0)].astype(F32)
    lane = lax.broadcasted_iota(jnp.int32, (total, 128), 1)
    column = jnp.sum(
        jnp.where(lane == pl.program_id(1), columns[...], 0.0), axis=1, keepdims=True
    )
    code = lax.broadcasted_iota(jnp.int32, (total, chunk), 1).astype(F32).astype(LOW)
    for v in range(0, vocab, chunk):
        hit = equal_to(code, column - (base + float(v)))
        out_ref[0, 0, :, v : v + chunk] = nn(turned[...], hit).astype(LOW)


def embed_back(base, lines, grads, books, vocab, after):
    parts = base.shape[0]
    groups = len(grads)
    features = grads[0].shape[1]
    rows = lines.shape[1] // groups
    return pl.pallas_call(
        later(partial(embed_back_body, groups), len(after), 2 + groups),
        out_shape=sds((parts, books, features, vocab), LOW),
        grid=(parts, books),
        in_specs=[scalars()] + [in_vmem()] * (1 + groups) + [anywhere()] * len(after),
        out_specs=pl.BlockSpec((1, 1, features, vocab), lambda i, k: (i, k, 0, 0)),
        scratch_shapes=[
            pltpu.VMEM((features, groups * rows), LOW),
            pltpu.VMEM((groups * rows, 128), F32),
        ],
        compiler_params=pltpu.CompilerParams(vmem_limit_bytes=32 << 20),
        cost_estimate=SMALL,
        name="embed_back",
    )(base, lines, *grads, *after)


def gather_features_body(need, put, where_ref, *refs):
    clips = sum(r.shape[1] != refs[0].shape[1] for r in refs)
    part_refs, outs = refs[:-clips], refs[-clips:]
    features = part_refs[0].shape[1]
    strip = outs[0].shape[0]
    for m, part in enumerate(part_refs):
        at = pl.ds(pl.multiple_of(where_ref[m] * features, features), features)
        for c, out_ref in enumerate(outs):
            out_ref[:, at] = part[c * strip : (c + 1) * strip, :]


def split_features_body(scale, need, put, where_ref, side_ref, place_ref, sums_ref, bias_ref, *refs):
    clips = side_ref.shape[0] - 1
    *refs, extra_ref = refs
    grads, outs = refs[:clips], refs[clips:]
    features = outs[0].shape[1]
    columns = bias_ref.shape[1]
    rows = (outs[0].shape[0] - extra_ref.shape[0]) // clips
    at_rows = pl.ds(pl.multiple_of(side_ref[0] * rows, rows), rows)
    extra_ref[...] = jnp.zeros(extra_ref.shape, F32)
    extra_ref[:8, :] = sums_ref[...] * scale
    at = pl.ds(pl.multiple_of(place_ref[0] * columns, columns), columns)
    extra_ref[8:9, at] = bias_ref[0:1, :]
    for m, out_ref in enumerate(outs):
        at = pl.ds(pl.multiple_of(where_ref[m] * features, features), features)
        for c in range(clips):
            out_ref[c * rows : (c + 1) * rows, :] = grads[c][at_rows, at]
        out_ref[clips * rows :, :] = extra_ref[:, at].astype(LOW)


def extra_body(*refs):
    *part_refs, out_ref = refs
    count = out_ref.shape[0]
    out_ref[...] = sum(p[p.shape[0] - count :, :].astype(F32) for p in part_refs)


def text_body(need, put, where_ref, *refs):
    *part_refs, wk_ref, wv_ref, tp_ref, k_ref, v_ref = refs
    columns = part_refs[0].shape[1]
    for m, part in enumerate(part_refs):
        need(1 + m)
        at = pl.ds(pl.multiple_of(where_ref[m] * columns, columns), columns)
        tp_ref[:, at] = part[...]
    put(0)
    for j, w_ref, to_ref in ((1, wk_ref, k_ref), (2, wv_ref, v_ref)):
        need(len(part_refs) + j)
        to_ref[...] = nn(tp_ref[...], flat(w_ref)).astype(LOW)
        put(j)


def text_back_body(clips, need, put, where_ref, *refs):
    dks, dvs = refs[:clips], refs[clips : 2 * clips]
    wk_ref, wv_ref, tp_ref = refs[2 * clips : 2 * clips + 3]
    *part_refs, gk_ref, gv_ref, full_ref = refs[2 * clips + 3 :]
    columns = part_refs[0].shape[1]
    length = dks[0].shape[0]
    need(*range(1, 1 + 2 * clips + 2))
    wk, wv = flat(wk_ref), flat(wv_ref)
    for c in range(clips):
        tp_rows = slice(c * length, (c + 1) * length)
        full_ref[tp_rows, :] = (nt(dks[c][...], wk) + nt(dvs[c][...], wv)).astype(LOW)
    for m, part_ref in enumerate(part_refs):
        at = pl.ds(pl.multiple_of(where_ref[m] * columns, columns), columns)
        part_ref[...] = full_ref[:, at]
    put(*range(len(part_refs)))
    need(3 + 2 * clips)
    turned = jnp.transpose(tp_ref[...])
    for j, grads, to_ref in ((0, dks, gk_ref), (1, dvs, gv_ref)):
        total = None
        for c in range(clips):
            part = nn(turned[:, c * length : (c + 1) * length], grads[c][...])
            total = part if total is None else total + part
        to_ref[...] = total.astype(LOW).reshape(to_ref.shape)
        put(len(part_refs) + j)


def text_weight_body(need, put, rows_ref, own_ref, far_ref, out_ref, bias_ref):
    need(0)
    grad = (own_ref[...].astype(F32) + far_ref[...].astype(F32)).astype(LOW)
    out_ref[...] = tn(rows_ref[...], grad).astype(LOW).reshape(out_ref.shape)
    bias_ref[...] = jnp.broadcast_to(
        jnp.sum(grad.astype(F32), axis=0, keepdims=True), bias_ref.shape
    )


def positions_rows(start, count, feature_count):
    half_width = feature_count // 2
    frequency = jnp.exp(
        jnp.arange(half_width, dtype=F32) * (-math.log(10000.0) / (half_width - 1))
    )
    angles = (start + jnp.arange(count, dtype=jnp.int32)).astype(F32)[:, None] * frequency[None, :]
    return jnp.concatenate([jnp.cos(angles), jnp.sin(angles)], axis=1)


def adam_update(weight, gradient, first_moment, second_moment, step_rate, factor):
    clipped = gradient * factor
    new_first = moment_decay * first_moment + (1.0 - moment_decay) * clipped
    new_second = moment_decay * second_moment + (1.0 - moment_decay) * clipped * clipped
    first_hat = new_first / (1.0 - moment_decay**STEP)
    second_hat = new_second / (1.0 - moment_decay**STEP)
    new_weight = weight * (1.0 - step_rate * weight_decay) - step_rate * first_hat / (
        jnp.sqrt(second_hat) + stability_offset
    )
    return (new_weight, new_first, new_second)


def swap(values, axis, mask):
    size = lax.axis_size(axis)
    return lax.ppermute(values, axis, [(i, i ^ mask) for i in range(size)])


def on_device(
    audio_codes,
    delay_mask,
    frame_mask,
    text_states,
    text_mask,
    attention,
    feedforward,
    tables,
    text_proj,
    norm_params,
    attention_first,
    attention_second,
    feedforward_first,
    feedforward_second,
    tables_first,
    tables_second,
    text_first,
    text_second,
    norm_first,
    norm_second,
):
    clips, frames, books = audio_codes.shape
    text_len, text_width = text_states.shape[1:]
    dp = lax.axis_size("dp")
    tensor = lax.axis_size("tensor")
    group = lax.axis_index("dp")
    place = lax.axis_index("tensor")
    core = place & 1
    side = place >> 1
    sides = tensor // 2
    height = frames // 2
    strip = height // sides
    share = attention.shape[1]
    columns = attention.shape[2]
    width = share * dp
    vocab = tables.shape[2]
    text_share = text_proj.shape[1]
    core_arg = Scalar(core.astype(jnp.int32).reshape(1))
    side_arg = Scalar(side.astype(jnp.int32).reshape(1))
    swap_core = partial(swap, axis="tensor", mask=1)

    def spread_tensor(values):
        held = [values]
        mask = tensor // 2
        order = [0]
        while mask:
            held = held + [swap(v, "tensor", mask) for v in held]
            order = order + [o | mask for o in order]
            mask //= 2
        return [v for _, v in sorted(zip(order, held), key=lambda t: t[0])]

    def collect_tensor(parts):
        mask = 1
        live = {m: p for m, p in enumerate(parts)}
        while mask < tensor:
            fresh = {}
            for m in live:
                if not m & mask:
                    got = swap(live[m | mask].astype(LOW), "tensor", mask)
                    fresh[m] = live[m].astype(F32) + got.astype(F32)
            live = fresh
            mask *= 2
        return live[0]

    def across(values):
        own = values
        mask = 2
        rest = None
        while mask < tensor:
            got = swap(own, "tensor", mask)
            mask *= 2
            if mask < tensor:
                own = (own.astype(F32) + got.astype(F32)).astype(LOW)
            rest = got
        if rest is None:
            rest = jnp.zeros_like(own)
        return own, rest

    def total_over(values, axes):
        for axis in axes:
            mask = 1
            while mask < lax.axis_size(axis):
                values = values + swap(values, axis, mask)
                mask *= 2
        return values

    last = []

    def run(body, outs, operands, after=(), **rest):
        *results, token = kernel(body, outs, operands, after=last + list(after), **rest)
        last[:] = [token]
        return results

    def run_block(*args, **rest):
        return run(*args, **rest)

    def run_weight(*args, **rest):
        results = run(*args, after=older[:1] or soon[:1], **rest)
        if older:
            older.clear()
        else:
            soon.clear()
        return results

    norm_pad = jnp.pad(norm_params.astype(LOW), ((0, 16 - norm_params.shape[0]), (0, columns - share)))
    attn_rows = attention.astype(LOW)
    self_flat = jnp.concatenate([attn_rows[n] for n in SELF] + [norm_pad], axis=0)
    cross_flat = jnp.concatenate([attn_rows[n] for n in CROSS] + [text_proj.astype(LOW).T], axis=0)
    self_all = lax.all_gather(self_flat, "dp", axis=0)
    cross_all = lax.all_gather(cross_flat, "dp", axis=0)
    ffn_all = lax.all_gather(feedforward.astype(LOW), "dp", axis=0)
    head_all = lax.all_gather(tables[books:].astype(LOW), "dp", axis=0)

    frame_live = (jnp.arange(frames, dtype=jnp.int32) < frames - 1).astype(jnp.int32)
    weight_int = delay_mask * frame_mask[:, :, None] * frame_live[None, :, None]
    start = core * height + side * strip
    strip_codes = lax.dynamic_slice_in_dim(audio_codes, start, strip, 1)
    count = clips * strip
    padded = -(-count // 128) * 128
    lines = jnp.transpose(strip_codes, (2, 0, 1)).reshape(books, count)
    lines = jnp.pad(lines, ((0, 0), (0, padded - count)), constant_values=-1)
    count_line = jnp.broadcast_to(jnp.sum(weight_int), (8 - books, padded))
    packet = jnp.concatenate([lines, count_line], axis=0)
    packets = [packet] + [swap(packet, "dp", m) for m in range(1, dp)]
    vocab_base = (place ^ jnp.arange(tensor, dtype=jnp.int32)) * vocab
    group_order = group ^ jnp.arange(dp, dtype=jnp.int32)
    place_order = place ^ jnp.arange(tensor, dtype=jnp.int32)

    text_bias_row = jnp.where(text_mask > 0, 0.0, NEG).astype(F32)
    bias_lines = [text_bias_row[c : c + 1] for c in range(clips)]
    bias_columns = [jnp.transpose(line) for line in bias_lines]
    targets = (jnp.roll(audio_codes, -1, axis=1) - place * vocab).astype(jnp.int32)
    targets = [targets[c] for c in range(clips)]
    loss_weight = [weight_int[c].astype(F32) for c in range(clips)]

    table_parts = spread_tensor(tables[:books].astype(LOW))
    step = max(1, dp // 4)
    arrived = [None] * dp
    for low_end in reversed(range(0, dp, step)):
        embedded = embed(
            vocab_base, packets[low_end : low_end + step], table_parts, count, list(last)
        )
        last[:] = [embedded[-1]]
        if low_end + step == dp:
            begin, _ = lax.optimization_barrier((core * height, embedded[0]))
            placed = positions_rows(begin, height, width)
        for m, piece in enumerate(embedded, low_end):
            arrived[m] = swap(piece, "dp", m) if m else piece
        last += [a for a in arrived[low_end + step : low_end + 2 * step] if a is not None]
    (counted,) = norm_rows_kernel(
        partial(count_body, books), [sds((8, 128), F32)], packets, None, last, name="count"
    )
    back_lines = jnp.concatenate([p[:, :count] for p in packets], axis=1)
    last[:] = bias_lines + bias_columns + targets + loss_weight + [placed, counted, back_lines]
    last += [a for a in arrived if a is not None]
    aligned = share % 128 == 0
    if aligned:
        strips = run(
            gather_features_body,
            [Flow(sds((strip, width), LOW))] * clips,
            [Scalar(group_order)] + arrived,
            name="gather_features",
        )
        strips = [free(a) for a in strips]
    else:
        strips = jnp.take(jnp.stack(arrived), group_order, axis=0)
        strips = jnp.transpose(strips, (1, 0, 2)).reshape(clips, strip, width)

    norm_rows = self_all[:, 4 * share :, :share]
    norm_rows = jnp.transpose(norm_rows, (1, 0, 2)).reshape(16, width).astype(F32)

    def w_attn(n):
        array, at = (self_all, SELF.index(n)) if n in SELF else (cross_all, CROSS.index(n))
        return Window(
            array, (dp, share, columns), lambda ref: ref.at[:, pl.ds(at * share, share), :]
        )

    def w_member(array, n):
        return Window(array, (dp,) + array.shape[2:], lambda ref: ref.at[:, n])

    half_sds = sds((height, width), F32)
    half_low = sds((height, width), LOW)
    flow = Flow(half_low)

    def fetch(a):
        return Window(a, a.shape, everything)


    def norm_step(which, hidden, parts):
        new, out = norm_rows_kernel(
            partial(norm_body, which),
            [half_sds, half_low],
            [hidden, *parts],
            norm_rows,
            last + soon,
        )
        soon[:] = []
        last[:] = [out]
        return new, (out, swap_core(free(out)))

    def norm_back(which, c, parts, before):
        rows = near.get((which, c, "back"), hidden[which][c])
        if before is not None:
            before = near_grad.get((which, c), before)
        operands = [rows, *parts] + ([before] if before is not None else []) + sums
        new, out, total = norm_rows_kernel(
            partial(norm_back_body, which, len(parts)),
            [half_sds, half_low, sds((8, width), F32)],
            operands,
            norm_rows,
            last + soon,
        )
        soon[:] = []
        last[:] = [out]
        sums[:] = [total]
        return new, (out, swap_core(free(out)))

    sums = []
    waiting, soon, older, newest = [], [], [], []
    moving = [None] * clips

    def flush():
        if waiting:
            c, keep, got = waiting.pop()
            parts = norm_rows_kernel(
                add_parts_body,
                [sds((height * part // sum(PIECES), width), LOW) for part in PIECES],
                [keep, got],
                None,
                last,
                name="add",
            )
            last[:] = [parts[-1]]
            fars = [across(free(part))[1] for part in parts]
            moving[c] = (*parts, *fars)
            soon[:] = fars[:-1]
            older[:] = newest
            newest[:] = fars[-1:]

    def reduce_rows(c, keep, send):
        waiting.append((c, keep, swap_core(free(send))))

    text_rows = text_states.reshape(clips * text_len, text_width)
    def text_in_step():
        (result,) = run(
            text_in_body,
            [Flow(sds((clips * text_len, columns), LOW))],
            [
                Scalar(place.astype(jnp.int32).reshape(1)),
                norm_rows,
                fetch(text_rows),
                Window(
                    cross_all,
                    (dp, text_share, columns),
                    lambda ref: ref.at[:, pl.ds(4 * share, text_share), :],
                ),
            ],
            flops=2 * clips * text_len * text_width * columns,
            name="text_in",
        )
        return spread_tensor(free(result))

    full = sds((frames, columns), LOW)
    lse_sds = sds((8, frames), F32)
    tot = [pltpu.VMEM((frames, 128), F32)]
    heads = columns // HEAD_DIM
    score_flops = 2 * heads * frames * HEAD_DIM
    units = feedforward.shape[2]
    inner = sds((frames, units), LOW)
    every = range(clips)

    near, near_grad = {}, {}

    def ahead(phase, c):
        at, clip = (phase - 1, c + 1) if c + 1 < clips else (phase, 0)
        if at < 0 or (phase == 3 and clip == 0) or (clip == c):
            return []
        return [Ahead(hidden[at][clip])]

    def took(phase, c, results):
        at, clip = (phase - 1, c + 1) if c + 1 < clips else (phase, 0)
        if ahead(phase, c):
            *results, near[at, clip] = results
        return results

    def ahead_back(phase, c):
        at, clip = (phase, c + 1) if c + 1 < clips else (phase - 1, 0)
        if clip == c:
            return []
        found = [Ahead(hidden[at][clip])]
        if at < 3:
            found.append(Ahead(grads[clip]))
        return found

    def took_back(phase, c, results):
        at, clip = (phase, c + 1) if c + 1 < clips else (phase - 1, 0)
        count = len(ahead_back(phase, c))
        if count == 2:
            near_grad[at, clip] = results[-1]
        if count:
            near[at, clip, "back"] = results[len(results) - count]
        return results[: len(results) - count]

    def embed_step(c):
        mine = strips[c]
        parts = [mine] + [swap(mine, "tensor", 2 * s) for s in range(1, sides)]
        new, out = run(
            embed_norm_body,
            [Flow(half_sds), Flow(half_low)],
            [side_arg, placed, norm_rows] + parts,
            flops=10 * height * width,
            name="embed_norm",
        )
        return new, (out, swap_core(free(out)))

    def self_step(c, pair):
        own, got = pair
        *saved, keep, send, left, right, hidden[0][c] = took(0, c, run_block(
            self_forward_body,
            [full, full, full, full, lse_sds, flow, flow, Copy(1), Copy(3)],
            [core_arg, own, w_attn(0), got, w_attn(1), w_attn(2), w_attn(6)]
            + [Carry(hidden[0][c])]
            + ahead(0, c),
            flops=8 * frames * width * columns + 4 * score_flops * frames,
            scratch=tot,
            name="self_forward",
        ))
        pairs[0][c] = (left, right)
        reduce_rows(c, keep, send)
        return saved

    text_full = sds((clips * text_len, width), LOW)
    text_cols = sds((clips * text_len, columns), LOW)

    def text_step():
        return run(
            text_body,
            [text_full, text_cols, text_cols],
            [Scalar(place_order)] + text_parts + [w_attn(4), w_attn(5)],
            flops=4 * clips * text_len * width * columns,
            name="text",
        )

    def text_rows_of(array, c):
        return Window(
            array, (text_len, columns), lambda ref: ref.at[pl.ds(c * text_len, text_len), :]
        )

    def cross_step(c, pair):
        own, got = pair
        k, v = text_rows_of(text_key, c), text_rows_of(text_value, c)
        q, o, lse, keep, send, left, right, hidden[1][c] = took(1, c, run_block(
            cross_forward_body,
            [full, full, lse_sds, flow, flow, Copy(1), Copy(3)],
            [core_arg, own, w_attn(3), got, bias_lines[c], k, v, w_attn(7)]
            + [Carry(hidden[1][c])]
            + ahead(1, c),
            flops=4 * frames * width * columns + 4 * score_flops * text_len,
            scratch=tot,
            name="cross_forward",
        ))
        pairs[1][c] = (left, right)
        reduce_rows(c, keep, send)
        return (q, k, v, o, lse)

    def ffn_step(c, pair):
        *saved, keep, send, left, right, hidden[2][c] = took(2, c, run_block(
            ffn_forward_body,
            [inner, inner, flow, flow, Copy(1), Copy(2)],
            [core_arg, *pair, w_member(ffn_all, 0), w_member(ffn_all, 1), Carry(hidden[2][c])]
            + ahead(2, c),
            flops=4 * frames * width * units,
            name="ffn_forward",
        ))
        pairs[2][c] = (left, right)
        reduce_rows(c, keep, send)
        return saved

    hidden = [[None] * clips for _ in range(4)]
    pairs = [[None] * clips for _ in range(4)]
    kept = [[None] * clips for _ in range(3)]
    for c in every:
        hidden[0][c], pairs[0][c] = embed_step(c)
        flush()
        kept[0][c] = self_step(c, pairs[0][c])
        if c == min(1, clips - 1):
            text_parts = text_in_step()
    text_hidden, text_key, text_value = text_step()
    for c in every:
        hidden[1][c], pairs[1][c] = norm_step(1, near.get((0, c), hidden[0][c]), moving[c])
        flush()
        kept[1][c] = cross_step(c, pairs[1][c])
    for c in every:
        hidden[2][c], pairs[2][c] = norm_step(2, near.get((1, c), hidden[1][c]), moving[c])
        flush()
        kept[2][c] = ffn_step(c, pairs[2][c])

    loss_part = [None] * clips

    def head_step(c, pair):
        own, got = pair
        logits, stats, left, right, hidden[3][c] = took(3, c, run_block(
            head_forward_body,
            [
                sds((frames, books * vocab), F32),
                Flow(sds((2 * books, frames), F32)),
                Copy(1),
                Copy(3),
            ],
            [core_arg, own, targets[c], got]
            + [w_member(head_all, k) for k in range(books)]
            + [Carry(hidden[3][c])]
            + ahead(3, c),
            flops=2 * frames * width * books * vocab,
            scratch=tot,
            name="head_forward",
        ))
        pairs[3][c] = (left, right)
        return logits, stats

    def merge_step(stats):
        mask = 1
        while mask < tensor:
            far = swap(free(stats), "tensor", mask)
            (stats,) = norm_rows_kernel(
                partial(merge_body, books),
                [sds((2 * books, frames), F32)],
                [stats, far],
                None,
                last,
                name="merge",
            )
            last[:] = [stats]
            mask *= 2
        return stats

    def head_back_step(c, logits, stats, pieces):
        grad, keep, send, loss = run_block(
            head_backward_body,
            [sds((frames, books * vocab), LOW), flow, flow, Flow(sds((8, 128), F32))],
            [core_arg, stats, loss_weight[c], targets[c], fetch(logits)]
            + [w_member(head_all, k) for k in range(books)]
            + [counted],
            flops=2 * frames * width * books * vocab,
            scratch=tot,
            after=pieces,
            name="head_backward",
        )
        loss_part[c] = free(loss)[0, 0]
        reduce_rows(c, keep, send)
        return grad

    self_shared = Shared((dp, 4 * share + text_share, columns), LOW)
    cross_shared = Shared((dp, 4 * share, columns), LOW)
    ffn_shared = Shared((dp,) + feedforward.shape, LOW)
    head_shared = Shared((dp, books, share, vocab), LOW)

    def attn_into(n):
        shared, at = (
            (self_shared, SELF.index(n)) if n in SELF else (cross_shared, CROSS.index(n))
        )
        return Into(
            shared, (dp, share, columns), lambda ref: ref.at[:, pl.ds(at * share, share), :]
        )

    def member_into(shared, n):
        return Into(shared, (dp,) + shared.full.shape[2:], lambda ref: ref.at[:, n])

    def halves(rights, shared, n):
        step = rights[0].shape[1] // 2
        found = []
        for at in (0, step):
            windows = [
                Window(a, (frames, step), lambda ref, at=at: ref.at[:, pl.ds(at, step)])
                for a in rights
            ]
            into = Into(
                shared, (dp, share, step), lambda ref, at=at: ref.at[:, n, :, pl.ds(at, step)]
            )
            found.append((windows, [into]))
        return found

    def weights(lefts, rights, outs, name):
        rights = [a if isinstance(a, Window) else fetch(a) for a in rights]
        total = rights[0].shape[1]
        turn_left = 2 * total > width
        run_weight(
            partial(weight_grad_body, clips, turn_left),
            outs,
            [core_arg] + [fetch(half) for pair in lefts for half in pair] + rights,
            flops=2 * clips * frames * width * total,
            scratch=[pltpu.VMEM((width if turn_left else total, clips * frames), LOW)],
            name=name,
            margin=16,
        )

    logit_grads = [None] * clips
    ready = [None] * clips
    for c in every:
        hidden[3][c], pairs[3][c] = norm_step(3, near.get((2, c), hidden[2][c]), moving[c])
        flush()
        ready[c] = head_step(c, pairs[3][c])
        if c:
            pieces = list(soon)
            flush()
            logits, stats = ready[c - 1]
            logit_grads[c - 1] = head_back_step(c - 1, logits, merge_step(stats), pieces)
    logits, stats = ready[-1]
    stats = merge_step(stats)
    pieces = list(newest)
    flush()
    logit_grads[-1] = head_back_step(clips - 1, logits, stats, pieces)

    def ffn_back_step(c, pair):
        own, got = pair
        grad, keep, send, left, right, grads[c] = took_back(3, c, run_block(
            ffn_backward_body,
            [inner, flow, flow, Copy(1), Copy(2)],
            [core_arg, own, got, w_member(ffn_all, 1), fetch(kept[2][c][1]), w_member(ffn_all, 0)]
            + [Carry(grads[c])]
            + ahead_back(3, c),
            flops=4 * frames * width * units,
            name="ffn_backward",
        ))
        back_pairs[3][c] = (left, right)
        reduce_rows(c, keep, send)
        return grad

    grads = [None] * clips
    back_pairs = [[None] * clips for _ in range(4)]
    inner_grads = [None] * clips
    for c in every:
        grads[c], back_pairs[3][c] = norm_back(3, c, moving[c], None)
        flush()
        inner_grads[c] = ffn_back_step(c, back_pairs[3][c])
        if c == 0:
            step = books // 2 * vocab
            for at in (0, 1):
                windows = [
                    Window(a, (frames, step), lambda ref, at=at: ref.at[:, pl.ds(at * step, step)])
                    for a in logit_grads
                ]
                into = [
                    member_into(head_shared, k) for k in range(at * books // 2, (at + 1) * books // 2)
                ]
                weights(pairs[3], windows, into, "head_weights")
    head_sum = lax.psum_scatter(free(head_shared.array), "dp", scatter_dimension=0, tiled=False)

    acc_text = [pltpu.VMEM((text_len, columns), F32)] * 2
    small = sds((text_len, columns), LOW)

    def cross_back_step(c, pair):
        own, got = pair
        q, k, v, o, lse = kept[1][c]
        bias = bias_columns[c]
        dq, dk, dv, keep, send, left, right, grads[c] = took_back(2, c, run_block(
            cross_backward_body,
            [full, small, small, flow, flow, Copy(1), Copy(3)],
            [core_arg, own, w_attn(7), got, bias, fetch(q), k, v, fetch(lse), w_attn(3)]
            + [Carry(grads[c])]
            + ahead_back(2, c),
            flops=4 * frames * width * columns + 10 * score_flops * text_len,
            scratch=[pltpu.VMEM((frames, columns), LOW)] + acc_text,
            name="cross_backward",
        ))
        back_pairs[2][c] = (left, right)
        reduce_rows(c, keep, send)
        return (dq, dk, dv)

    cross_grads = [None] * clips
    for c in every:
        grads[c], back_pairs[2][c] = norm_back(2, c, moving[c], grads[c])
        flush()
        cross_grads[c] = cross_back_step(c, back_pairs[2][c])
        if c == 0:
            for windows, into in halves([k[0] for k in kept[2]], ffn_shared, 1):
                weights(back_pairs[3], windows, into, "ffn_two")
        if c == min(1, clips - 1):
            for windows, into in halves(inner_grads, ffn_shared, 0):
                weights(pairs[2], windows, into, "ffn_one")
    ffn_sum = lax.psum_scatter(free(ffn_shared.array), "dp", scatter_dimension=0, tiled=False)

    def text_back_step():
        results = run_weight(
            partial(text_back_body, clips),
            [Flow(text_cols)] * tensor + [attn_into(4), attn_into(5)],
            [Scalar(place_order)]
            + [fetch(g[1]) for g in cross_grads]
            + [fetch(g[2]) for g in cross_grads]
            + [w_attn(4), w_attn(5), fetch(text_hidden)],
            flops=8 * clips * text_len * width * columns,
            scratch=[pltpu.VMEM((clips * text_len, width), LOW)],
            name="text_back",
        )
        live = dict(enumerate(results))
        mask = 1
        while mask < tensor:
            fresh = {}
            for m in live:
                if not m & mask:
                    fresh[m] = (live[m], swap(free(live[m | mask]), "tensor", mask))
            mask *= 2
            if mask < tensor:
                for m, both in fresh.items():
                    (fresh[m],) = norm_rows_kernel(
                        add_body, [text_cols], list(both), None, last, name="add"
                    )
                    last[:] = [fresh[m]]
            live = fresh
        return live[0]

    acc_self = [pltpu.VMEM((frames, columns), F32)] * 2

    def self_back_step(c, pair):
        own, got = pair
        q, k, v, o, lse = kept[0][c]
        grad, keep, send, left, right, grads[c] = took_back(1, c, run_block(
            self_backward_body,
            [sds((frames, 3 * columns), LOW), flow, flow, Copy(1), Copy(3)],
            [core_arg, own, w_attn(6), got]
            + [fetch(a) for a in (q, k, v, lse)]
            + [w_attn(0), w_attn(1), w_attn(2), Carry(grads[c])]
            + ahead_back(1, c),
            flops=8 * frames * width * columns + 10 * score_flops * frames,
            scratch=[pltpu.VMEM((frames, columns), LOW)] + acc_self,
            name="self_backward",
        ))
        back_pairs[1][c] = (left, right)
        reduce_rows(c, keep, send)
        return grad

    self_grads = [None] * clips
    last.append(head_sum)
    for c in every:
        grads[c], back_pairs[1][c] = norm_back(1, c, moving[c], grads[c])
        flush()
        self_grads[c] = self_back_step(c, back_pairs[1][c])
        if c == 0:
            text_grad = text_back_step()
            weights(back_pairs[2], [k[3] for k in kept[1]], [attn_into(7)], "cross_out")
            weights(pairs[1], [g[0] for g in cross_grads], [attn_into(3)], "cross_query")
            cross_sum = lax.psum_scatter(
                free(cross_shared.array), "dp", scatter_dimension=0, tiled=False
            )

    zero_lows = [None] * clips

    def zero_step(c):
        _, (zero_lows[c], _) = norm_back(0, c, moving[c], grads[c])

    weights(back_pairs[1], [k[3] for k in kept[0]], [attn_into(6)], "self_out")
    first = list(soon)
    flush()
    text_into = Into(
        self_shared,
        (dp, text_share, columns),
        lambda ref: ref.at[:, pl.ds(4 * share, text_share), :],
    )
    (bias_grad,) = run(
        text_weight_body,
        [text_into, Flow(sds((8, columns), F32))],
        [fetch(text_rows), *text_grad],
        after=[ffn_sum] + first,
        flops=2 * clips * text_len * text_width * columns,
        name="text_weight",
    )
    def self_in(members):
        size = len(members) * columns
        windows = [
            Window(a, (frames, size), lambda ref: ref.at[:, pl.ds(members[0] * columns, size)])
            for a in self_grads
        ]
        weights(pairs[0], windows, [attn_into(n) for n in members], "self_in")

    self_in((0, 1))
    for c in every:
        if c == clips - 1:
            older[:] = newest
            self_in((2,))
            self_sum = lax.psum_scatter(
                free(self_shared.array), "dp", scatter_dimension=0, tiled=False
            )
        zero_step(c)

    if aligned:
        pieces = run(
            partial(split_features_body, 1.0 / sides),
            [Flow(sds((clips * strip + 16, share), LOW))] * dp,
            [
                Scalar(group_order),
                Scalar(jnp.broadcast_to(side.astype(jnp.int32), (clips + 1,))),
                Scalar(place.astype(jnp.int32).reshape(1)),
                sums[0],
                bias_grad,
            ]
            + zero_lows,
            scratch=[pltpu.VMEM((16, width), F32)],
            after=[cross_sum],
            name="split_features",
        )
        pieces = [free(p) for p in pieces]
    else:
        rows = jnp.concatenate(
            [lax.dynamic_slice_in_dim(free(a), side * strip, strip, 0) for a in zero_lows], axis=0
        )
        rows = jnp.transpose(rows.reshape(clips * strip, dp, share), (1, 0, 2))
        pieces = list(jnp.take(rows, group_order, axis=0))
    rows_all = [pieces[0]] + [swap(pieces[m], "dp", m) for m in range(1, dp)]
    embed_parts = embed_back(vocab_base, back_lines, rows_all, books, vocab, list(last))
    grad_embed = collect_tensor([embed_parts[m] for m in range(tensor)])

    if aligned:
        (extra,) = norm_rows_kernel(
            extra_body, [sds((16, share), F32)], rows_all, None, last, name="extra"
        )
        grad_norm_rows = total_over(free(extra), ("tensor",))[: norm_params.shape[0]]
    else:
        norm_part = free(sums[0]) * (1.0 / sides)
        bias_row = lax.dynamic_update_slice_in_dim(
            jnp.zeros((width,), F32), free(bias_grad)[0], place * columns, 0
        )
        norm_total = total_over(
            jnp.concatenate([norm_part, bias_row[None]], axis=0), ("tensor", "dp")
        )
        grad_norm_rows = lax.dynamic_slice_in_dim(norm_total, group * share, share, 1)

    own_self = self_sum[: 4 * share].reshape(4, share, columns)
    own_cross = cross_sum.reshape(4, share, columns)
    grad_attention = jnp.concatenate(
        [own_self[:3], own_cross[:3], own_self[3:], own_cross[3:]], axis=0
    ).astype(F32)
    grad_text_proj = jnp.transpose(self_sum[4 * share :]).astype(F32)
    grad_feedforward = ffn_sum.astype(F32)
    grad_heads = head_sum.astype(F32)
    local_square = (
        jnp.sum(jnp.square(self_sum.astype(F32)))
        + jnp.sum(jnp.square(cross_sum.astype(F32)))
        + jnp.sum(grad_feedforward * grad_feedforward)
        + jnp.sum(grad_heads * grad_heads)
        + jnp.sum(grad_embed * grad_embed)
        + jnp.sum(grad_norm_rows * grad_norm_rows) / tensor
    )
    both = total_over(
        jnp.stack([local_square, sum(loss_part) / tensor]).reshape(1, 2), ("tensor", "dp")
    )[0]
    grad_norm = jnp.sqrt(both[0])
    mean_loss = both[1]
    factor = clip_limit / jnp.maximum(grad_norm, clip_limit)
    grad_tables = jnp.concatenate([grad_embed, grad_heads], 0)
    attn_new, attn_first_new, attn_second_new = adam_update(
        attention, grad_attention, attention_first, attention_second, rate_matrix, factor
    )
    ffn_new, ffn_first_new, ffn_second_new = adam_update(
        feedforward, grad_feedforward, feedforward_first, feedforward_second, rate_matrix, factor
    )
    table_new, table_first_new, table_second_new = adam_update(
        tables, grad_tables, tables_first, tables_second, rate_table, factor
    )
    text_new, text_first_new, text_second_new = adam_update(
        text_proj, grad_text_proj, text_first, text_second, rate_matrix, factor
    )
    norm_new, norm_first_new, norm_second_new = adam_update(
        norm_params, grad_norm_rows, norm_first, norm_second, rate_norm, factor
    )
    return (
        mean_loss,
        free(counted)[0, 0],
        grad_norm,
        attn_new,
        attn_new.astype(LOW),
        attn_first_new,
        attn_second_new,
        ffn_new,
        ffn_new.astype(LOW),
        ffn_first_new,
        ffn_second_new,
        table_new,
        table_new.astype(LOW),
        table_first_new,
        table_second_new,
        text_new,
        text_new.astype(LOW),
        text_first_new,
        text_second_new,
        norm_new,
        norm_first_new,
        norm_second_new,
    )


def solution(mesh):
    clip3 = P("dp", None, None)
    clip2 = P("dp", None)
    matrix = P(None, "dp", "tensor")
    text = P("tensor", "dp")
    norm = P(None, "dp")
    placed = (
        (clip3, clip3, clip2, clip3, clip2)
        + (matrix, matrix, matrix, text, norm)
        + (matrix,) * 6
        + (text, text, norm, norm)
    )
    return jax.shard_map(
        on_device,
        mesh=mesh,
        in_specs=placed,
        out_specs=(P(), P(), P()) + (matrix,) * 12 + (text,) * 4 + (norm,) * 3,
        check_vma=False,
    )
```

```python
from functools import partial
import math

import jax
import jax.numpy as jnp
from jax import lax
from jax.experimental import pallas as pl
from jax.experimental.pallas import tpu as pltpu
from jax.sharding import PartitionSpec as P

HEAD_DIM = 64
STEP = 5
BLOCK = 256
NEG = -1e30
LOW = jnp.bfloat16
F32 = jnp.float32

SELF = (0, 1, 2, 6)
CROSS = (3, 4, 5, 7)

SMALL = pl.CostEstimate(flops=1024, bytes_accessed=1024, transcendentals=0)

PIECES = (1, 1)

clip_limit = 0.004
stability_offset = 1e-08
weight_decay = 0.01
moment_decay = 0.5
rate_matrix = 0.03
rate_table = 0.05
rate_norm = 0.2


def nn(a, b):
    return lax.dot_general(a, b, (((1,), (0,)), ((), ())), preferred_element_type=F32)


def nt(a, b):
    return lax.dot_general(a, b, (((1,), (1,)), ((), ())), preferred_element_type=F32)


def tn(a, b):
    return lax.dot_general(a, b, (((0,), (0,)), ((), ())), preferred_element_type=F32)


def sds(shape, kind):
    return jax.ShapeDtypeStruct(shape, kind)


def scalars():
    return pl.BlockSpec(memory_space=pltpu.SMEM)


def anywhere():
    return pl.BlockSpec(memory_space=pl.ANY)


def in_hbm():
    return pl.BlockSpec(memory_space=pltpu.HBM)


def in_vmem():
    return pl.BlockSpec(memory_space=pltpu.VMEM)


def whole(a):
    rank = len(a.shape)
    return pl.BlockSpec(a.shape, lambda i: (0,) * rank)


def later(body, count, at):
    def ordered(*refs):
        return body(*refs[:at], *refs[at + count :])

    return ordered


class Scalar:
    def __init__(self, array):
        self.array = array


class Window:
    def __init__(self, array, shape, pick):
        self.array, self.shape, self.pick = array, tuple(shape), pick


def hold(array, space):
    return pltpu.with_memory_space_constraint(array, space)


def free(array):
    return pltpu.with_memory_space_constraint(array, pl.ANY)


class Flow:
    def __init__(self, shape):
        self.shape = shape


class Copy:
    def __init__(self, i):
        self.i = i


class Carry:
    def __init__(self, array):
        self.array = array


class Ahead:
    def __init__(self, array):
        self.array = array


class Shared:
    def __init__(self, shape, kind):
        self.full, self.array = sds(shape, kind), None


class Into:
    def __init__(self, shared, shape, pick):
        self.shared, self.shape, self.pick = shared, tuple(shape), pick


def everything(ref):
    return ref


def nbytes_of(shape, kind):
    return math.prod(shape) * jnp.dtype(kind).itemsize


def kernel(body, outs, operands, flops=0, scratch=(), name=None, exps=0, after=(), margin=12):
    arrays, specs, windows, shown, fetched = [], [], [], [], {}
    outs = list(outs)
    for i, a in enumerate(operands):
        shown.append(not isinstance(a, (Carry, Ahead)))
        if isinstance(a, Ahead):
            arrays.append(hold(a.array, pltpu.HBM))
            specs.append(in_hbm())
            windows.append(None)
            outs.append(Flow(sds(a.array.shape, a.array.dtype)))
            fetched[len(outs) - 1] = i
        elif isinstance(a, Carry):
            arrays.append(hold(a.array, pltpu.VMEM))
            specs.append(in_vmem())
            windows.append(None)
            outs.append(Copy(i))
        elif isinstance(a, Scalar):
            arrays.append(a.array)
            specs.append(scalars())
            windows.append(None)
        elif isinstance(a, Window):
            arrays.append(hold(a.array, pltpu.HBM))
            specs.append(in_hbm())
            windows.append(a)
        else:
            arrays.append(hold(a, pltpu.VMEM))
            specs.append(in_vmem())
            windows.append(None)
    aliases, out_shapes, out_specs, out_parts, owners = {}, [], [], [], []
    extra = []
    for o in outs:
        if isinstance(o, Into):
            if o.shared not in owners:
                if o.shared.array is not None:
                    aliases[len(arrays) + len(extra)] = len(out_shapes)
                    extra.append(o.shared.array)
                out_shapes.append(pltpu.HBM(o.shared.full.shape, o.shared.full.dtype))
                out_specs.append(in_hbm())
                owners.append(o.shared)
            out_parts.append(("put", o.shape, o.shared.full.dtype, o.pick, owners.index(o.shared)))
            continue
        if isinstance(o, Flow):
            out_parts.append(("flow", None, None, None, len(out_shapes)))
            out_shapes.append(pltpu.VMEM(o.shape.shape, o.shape.dtype))
            out_specs.append(in_vmem())
        elif isinstance(o, Copy):
            a = arrays[o.i]
            out_parts.append(("copy", o.i, None, None, len(out_shapes)))
            out_shapes.append(pltpu.HBM(a.shape, a.dtype))
            out_specs.append(in_hbm())
        else:
            out_parts.append(("put", o.shape, o.dtype, everything, len(out_shapes)))
            out_shapes.append(pltpu.HBM(o.shape, o.dtype))
            out_specs.append(in_hbm())
        owners.append(None)
    out_parts.append(("token", None, None, None, len(out_shapes)))
    out_shapes.append(pltpu.VMEM((8, 128), F32))
    out_specs.append(in_vmem())
    owners.append(None)
    moved = [w for w in windows if w is not None]
    made = [p for p in out_parts if p[0] == "put"]
    count_in, count_extra, count_after = len(arrays), len(extra), len(after)
    count_out, count_moved, count_arrays = len(out_parts), len(moved), len(out_shapes)

    def run_body(*refs):
        refs = list(refs)
        ins = refs[:count_in]
        at = count_in + count_extra + count_after
        out_refs = refs[at : at + count_arrays]
        at += count_arrays
        in_buffers = refs[at : at + count_moved]
        at += count_moved
        made_buffers = refs[at : at + len(made)]
        at += len(made)
        in_sems, out_sems = refs[at], refs[at + 1]
        rest = refs[at + 2 :]
        views, copies, waited = [], {}, set()
        n = 0
        for i, (ref, w) in enumerate(zip(ins, windows)):
            if not shown[i]:
                continue
            if w is None:
                views.append(ref)
            else:
                copies[i] = pltpu.make_async_copy(w.pick(ref), in_buffers[n], in_sems.at[n])
                copies[i].start()
                views.append(in_buffers[n])
                n += 1
        sent, sources = {}, {}

        def need(*which):
            for i in which:
                if i in copies and i not in waited:
                    waited.add(i)
                    copies[i].wait()

        def put(*which):
            for j in which:
                if j in sources:
                    source, target = sources[j]
                    sent[j] = pltpu.make_async_copy(source, target, out_sems.at[j])
                    sent[j].start()

        body_outs = []
        n = 0
        for j, (kind, what, _, pick, owner) in enumerate(out_parts):
            if kind == "put":
                sources[j] = (made_buffers[n], pick(out_refs[owner]))
                body_outs.append(made_buffers[n])
                n += 1
            elif kind == "copy":
                sources[j] = (ins[what], out_refs[owner])
                put(j)
            elif kind == "token":
                out_refs[owner][...] = jnp.zeros((8, 128), F32)
            elif j in fetched:
                sources[j] = (ins[fetched[j]], out_refs[owner])
                put(j)
            else:
                body_outs.append(out_refs[owner])
        body(need, put, *views, *body_outs, *rest)
        need(*copies)
        put(*(j for j in sources if j not in sent))
        for copy in sent.values():
            copy.wait()

    nbytes = sum(nbytes_of(w.shape, w.array.dtype) for w in moved)
    nbytes += sum(nbytes_of(p[1], p[2]) for p in made)
    held = nbytes + sum(nbytes_of(m.shape, m.dtype) for m in scratch)
    results = pl.pallas_call(
        run_body,
        out_shape=tuple(out_shapes),
        in_specs=specs + [anywhere()] * (count_extra + count_after),
        out_specs=tuple(out_specs),
        input_output_aliases=aliases,
        scratch_shapes=[pltpu.VMEM(w.shape, w.array.dtype) for w in moved]
        + [pltpu.VMEM(p[1], p[2]) for p in made]
        + [
            pltpu.SemaphoreType.DMA((max(1, count_moved),)),
            pltpu.SemaphoreType.DMA((max(1, count_out),)),
        ]
        + list(scratch),
        compiler_params=pltpu.CompilerParams(vmem_limit_bytes=held + (margin << 20)),
        cost_estimate=SMALL,
        name=name,
    )(*arrays, *extra, *after)
    for owner, result in zip(owners, results):
        if owner is not None:
            owner.array = result
    return [r for owner, r in zip(owners, results) if owner is None]


def flat(ref):
    w = ref[...]
    return w.reshape(-1, w.shape[-1])


def half_rows(core, height):
    return (
        pl.ds(pl.multiple_of(core * height, height), height),
        pl.ds(pl.multiple_of((1 - core) * height, height), height),
    )


def attend_block(query, keys, values, head_masks, diagonal, bias):
    rows, width = query.shape
    lane = lax.broadcasted_iota(jnp.int32, (rows, 128), 1)
    column = lax.broadcasted_iota(jnp.int32, (rows, width), 1) // HEAD_DIM
    mixed = jnp.zeros((rows, width), F32)
    totals = jnp.zeros((rows, 128), F32)
    count = keys.shape[0]
    for h, mask in enumerate(head_masks):
        s = nt(query * mask, keys)
        if diagonal is not None:
            last = jnp.where(diagonal, s[:, count - rows :], NEG)
            s = last if count == rows else jnp.concatenate([s[:, : count - rows], last], axis=1)
        if bias is not None:
            s = s + bias
        top = jnp.max(s, axis=1, keepdims=True)
        e = jnp.exp(s - top)
        total = jnp.sum(e, axis=1, keepdims=True)
        p = (e * (1.0 / total)).astype(LOW)
        mixed = jnp.where(column == h, nn(p, values), mixed)
        totals = jnp.where(lane == h, top + jnp.log(total), totals)
    return mixed, totals


def masks_of(width):
    head = lax.broadcasted_iota(jnp.int32, (1, width), 1) // HEAD_DIM
    return [(head == h).astype(F32).astype(LOW) for h in range(width // HEAD_DIM)]


def triangle(size):
    row = lax.broadcasted_iota(jnp.int32, (size, size), 0)
    col = lax.broadcasted_iota(jnp.int32, (size, size), 1)
    return row >= col


def self_forward_body(
    need, put, core_ref, own_ref, wq_ref, got_ref, wk_ref, wv_ref, wo_ref,
    q_ref, k_ref, v_ref, o_ref, lse_ref, keep_ref, send_ref, tot_ref,
):
    height = own_ref.shape[0]
    frames, width = q_ref.shape
    mine, other = half_rows(core_ref[0], height)
    need(1)
    for i, w_ref, to_ref in ((2, wq_ref, q_ref), (4, wk_ref, k_ref), (5, wv_ref, v_ref)):
        need(i)
        w = flat(w_ref)
        to_ref[mine, :] = nn(own_ref[...], w).astype(LOW)
        need(3)
        to_ref[other, :] = nn(got_ref[...], w).astype(LOW)
    put(0, 1, 2)
    scale = jnp.asarray(HEAD_DIM**-0.5, LOW)
    head_masks = masks_of(width)
    diagonal = triangle(BLOCK)
    for i in range(frames // BLOCK):
        rows = slice(i * BLOCK, (i + 1) * BLOCK)
        mixed, totals = attend_block(
            q_ref[rows, :] * scale,
            k_ref[: (i + 1) * BLOCK, :],
            v_ref[: (i + 1) * BLOCK, :],
            head_masks,
            diagonal,
            None,
        )
        o_ref[rows, :] = mixed.astype(LOW)
        tot_ref[rows, :] = totals
    put(3)
    need(6)
    wo = flat(wo_ref)
    send_ref[...] = nt(o_ref[other, :], wo).astype(LOW)
    put(6)
    keep_ref[...] = nt(o_ref[mine, :], wo).astype(LOW)
    put(5)
    lse_ref[...] = jnp.transpose(tot_ref[...])[:8, :]


def cross_forward_body(
    need, put, core_ref, own_ref, wq_ref, got_ref, bias_ref, k_ref, v_ref, wo_ref,
    q_ref, o_ref, lse_ref, keep_ref, send_ref, tot_ref,
):
    height = own_ref.shape[0]
    frames, width = q_ref.shape
    mine, other = half_rows(core_ref[0], height)
    need(1, 2)
    w = flat(wq_ref)
    q_ref[mine, :] = nn(own_ref[...], w).astype(LOW)
    need(3)
    q_ref[other, :] = nn(got_ref[...], w).astype(LOW)
    put(0)
    scale = jnp.asarray(HEAD_DIM**-0.5, LOW)
    head_masks = masks_of(width)
    need(4, 5, 6)
    for i in range(frames // BLOCK):
        rows = slice(i * BLOCK, (i + 1) * BLOCK)
        mixed, totals = attend_block(
            q_ref[rows, :] * scale, k_ref[...], v_ref[...], head_masks, None, bias_ref[...]
        )
        o_ref[rows, :] = mixed.astype(LOW)
        tot_ref[rows, :] = totals
    put(1)
    need(7)
    wo = flat(wo_ref)
    send_ref[...] = nt(o_ref[other, :], wo).astype(LOW)
    put(4)
    keep_ref[...] = nt(o_ref[mine, :], wo).astype(LOW)
    put(3)
    lse_ref[...] = jnp.transpose(tot_ref[...])[:8, :]


def ffn_forward_body(
    need, put, core_ref, own_ref, got_ref, w1_ref, w2_ref,
    act_ref, slope_ref, keep_ref, send_ref,
):
    height = own_ref.shape[0]
    mine, other = half_rows(core_ref[0], height)
    need(1, 2, 3)
    w1 = flat(w1_ref)
    for j, source, rows, to_ref in (
        (3, got_ref, other, send_ref),
        (2, own_ref, mine, keep_ref),
    ):
        u = nn(source[...], w1)
        phi = 0.5 * (1.0 + lax.erf(u * (2.0**-0.5)))
        act = (u * phi).astype(LOW)
        density = jnp.exp(-0.5 * u * u) * ((2.0 * math.pi) ** -0.5)
        act_ref[rows, :] = act
        slope_ref[rows, :] = (phi + u * density).astype(LOW)
        need(4)
        to_ref[...] = nt(act, flat(w2_ref)).astype(to_ref.dtype)
        put(j)


def head_forward_body(
    need, put, core_ref, own_ref, target_ref, got_ref, *refs
):
    *w_refs, logits_ref, stats_ref, tot_ref = refs
    height = own_ref.shape[0]
    books = len(w_refs)
    vocab = w_refs[0].shape[2]
    halves = half_rows(core_ref[0], height)
    lane = lax.broadcasted_iota(jnp.int32, (height, 128), 1)
    code = lax.broadcasted_iota(jnp.int32, (height, vocab), 1)
    need(1, 2)
    totals = [jnp.zeros((height, 128), F32)] * 2
    for k, w_ref in enumerate(w_refs):
        need(4 + k)
        w = flat(w_ref)
        for j, (source, rows) in enumerate(zip((own_ref, got_ref), halves)):
            need(1 + 2 * j)
            s = nn(source[...], w)
            logits_ref[rows, k * vocab : (k + 1) * vocab] = s
            top = jnp.max(s, axis=1, keepdims=True)
            total = jnp.sum(jnp.exp(s - top), axis=1, keepdims=True)
            hit = code == target_ref[rows, k : k + 1]
            pick = jnp.sum(jnp.where(hit, s, 0.0), axis=1, keepdims=True)
            totals[j] = jnp.where(lane == k, top + jnp.log(total), totals[j])
            totals[j] = jnp.where(lane == books + k, pick, totals[j])
    put(0)
    for rows, t in zip(halves, totals):
        tot_ref[rows, :] = t
    stats_ref[...] = jnp.transpose(tot_ref[...])[: 2 * books, :]


def head_backward_body(
    need, put, core_ref, total_ref, weight_ref, target_ref, logits_ref, *refs
):
    *w_refs, valid_ref, grad_ref, keep_ref, send_ref, loss_ref, col_ref = refs
    height = keep_ref.shape[0]
    books = len(w_refs)
    vocab = w_refs[0].shape[2]
    mine, other = half_rows(core_ref[0], height)
    frames = logits_ref.shape[0]
    need(1, 2, 3)
    wide = jnp.concatenate(
        [total_ref[...], jnp.zeros((128 - total_ref.shape[0], frames), F32)], axis=0
    )
    col_ref[...] = jnp.transpose(wide)
    share = 1.0 / valid_ref[0:1, 0:1]
    gap = (col_ref[:, :books] - col_ref[:, books : 2 * books]) * (weight_ref[...] * share)
    loss_ref[...] = jnp.broadcast_to(jnp.sum(gap).reshape(1, 1), loss_ref.shape)
    code = lax.broadcasted_iota(jnp.int32, (height, vocab), 1)
    need(4)
    for j, rows, to_ref in ((2, other, send_ref), (1, mine, keep_ref)):
        weight = weight_ref[rows, :] * share
        total = col_ref[rows, :]
        acc = None
        for k, w_ref in enumerate(w_refs):
            s = logits_ref[rows, k * vocab : (k + 1) * vocab]
            p = jnp.exp(s - total[:, k : k + 1])
            hit = jnp.where(code == target_ref[rows, k : k + 1], 1.0, 0.0)
            g = ((p - hit) * weight[:, k : k + 1]).astype(LOW)
            grad_ref[rows, k * vocab : (k + 1) * vocab] = g
            need(5 + k)
            part = nt(g, flat(w_ref))
            acc = part if acc is None else acc + part
        to_ref[...] = acc.astype(to_ref.dtype)
        put(j)


def ffn_backward_body(
    need, put, core_ref, own_ref, got_ref, w2_ref, slope_ref, w1_ref,
    grad_ref, keep_ref, send_ref,
):
    height = own_ref.shape[0]
    mine, other = half_rows(core_ref[0], height)
    need(1, 2, 3, 4)
    w2 = flat(w2_ref)
    for j, source, rows, to_ref in (
        (2, got_ref, other, send_ref),
        (1, own_ref, mine, keep_ref),
    ):
        g = (nn(source[...], w2) * slope_ref[rows, :].astype(F32)).astype(LOW)
        grad_ref[rows, :] = g
        need(5)
        to_ref[...] = nt(g, flat(w1_ref)).astype(to_ref.dtype)
        put(j)


def attend_back(
    q, k, v, g, lse, head_masks, scale, diagonal, bias, dq_ref, rows, dk_ref, dv_ref, first
):
    count, width = k.shape
    step = q.shape[0]
    dq = jnp.zeros((step, width), F32)
    dk = jnp.zeros((count, width), F32)
    dv = jnp.zeros((count, width), F32)
    for h, mask in enumerate(head_masks):
        qm = q * mask
        gm = g * mask
        s = nt(k, qm)
        if diagonal is not None:
            last = jnp.where(diagonal, s[count - step :, :], NEG)
            s = last if count == step else jnp.concatenate([s[: count - step, :], last], axis=0)
        if bias is not None:
            s = s + bias
        p = jnp.exp(s - lse[h : h + 1, :])
        dp = nt(v, gm)
        inner = jnp.sum(p * dp, axis=0, keepdims=True)
        ds = (p * (dp - inner)).astype(LOW)
        dq = dq + tn(ds, k * mask)
        dk = dk + nn(ds, qm)
        dv = dv + nn(p.astype(LOW), gm)
    dq_ref[rows, :width] = (dq * scale).astype(LOW)
    dk_ref[:count, :] = dk if first else dk_ref[:count, :] + dk
    dv_ref[:count, :] = dv if first else dv_ref[:count, :] + dv


def self_backward_body(
    need, put, core_ref, own_ref, wo_ref, got_ref, q_ref, k_ref, v_ref, lse_ref,
    wq_ref, wk_ref, wv_ref, grad_ref, keep_ref, send_ref, g_ref, dk_acc, dv_acc,
):
    height = own_ref.shape[0]
    frames, width = q_ref.shape
    mine, other = half_rows(core_ref[0], height)
    need(1, 2)
    wo = flat(wo_ref)
    g_ref[mine, :] = nn(own_ref[...], wo).astype(LOW)
    need(3)
    g_ref[other, :] = nn(got_ref[...], wo).astype(LOW)
    scale = HEAD_DIM**-0.5
    head_masks = masks_of(width)
    row = lax.broadcasted_iota(jnp.int32, (BLOCK, BLOCK), 0)
    col = lax.broadcasted_iota(jnp.int32, (BLOCK, BLOCK), 1)
    diagonal = col >= row
    blocks = frames // BLOCK
    need(4, 5, 6, 7)
    for i in reversed(range(blocks)):
        rows = slice(i * BLOCK, (i + 1) * BLOCK)
        count = (i + 1) * BLOCK
        attend_back(
            q_ref[rows, :] * jnp.asarray(scale, LOW),
            k_ref[:count, :],
            v_ref[:count, :],
            g_ref[rows, :],
            lse_ref[:, rows],
            head_masks,
            scale,
            diagonal,
            None,
            grad_ref,
            rows,
            dk_acc,
            dv_acc,
            i == blocks - 1,
        )
    grad_ref[:, width : 2 * width] = dk_acc[...].astype(LOW)
    grad_ref[:, 2 * width :] = dv_acc[...].astype(LOW)
    put(0)
    need(8, 9, 10)
    for j, rows, to_ref in ((2, other, send_ref), (1, mine, keep_ref)):
        part = None
        for n, w_ref in enumerate((wq_ref, wk_ref, wv_ref)):
            term = nt(grad_ref[rows, n * width : (n + 1) * width], flat(w_ref))
            part = term if part is None else part + term
        to_ref[...] = part.astype(to_ref.dtype)
        put(j)


def cross_backward_body(
    need, put, core_ref, own_ref, wo_ref, got_ref, bias_ref, q_ref, k_ref, v_ref, lse_ref, wq_ref,
    dq_ref, dk_ref, dv_ref, keep_ref, send_ref, g_ref, dk_acc, dv_acc,
):
    height = own_ref.shape[0]
    frames, width = q_ref.shape
    mine, other = half_rows(core_ref[0], height)
    need(1, 2)
    wo = flat(wo_ref)
    g_ref[mine, :] = nn(own_ref[...], wo).astype(LOW)
    need(3)
    g_ref[other, :] = nn(got_ref[...], wo).astype(LOW)
    scale = HEAD_DIM**-0.5
    head_masks = masks_of(width)
    need(4, 5, 6, 7, 8)
    for i in range(frames // BLOCK):
        rows = slice(i * BLOCK, (i + 1) * BLOCK)
        attend_back(
            q_ref[rows, :] * jnp.asarray(scale, LOW),
            k_ref[...],
            v_ref[...],
            g_ref[rows, :],
            lse_ref[:, rows],
            head_masks,
            scale,
            None,
            bias_ref[...],
            dq_ref,
            rows,
            dk_acc,
            dv_acc,
            i == 0,
        )
    put(0)
    need(9)
    wq = flat(wq_ref)
    for j, rows, to_ref in ((4, other, send_ref), (3, mine, keep_ref)):
        to_ref[...] = nt(dq_ref[rows, :], wq).astype(to_ref.dtype)
        put(j)
    dk_ref[...] = dk_acc[...].astype(LOW)
    dv_ref[...] = dv_acc[...].astype(LOW)


def normalize(values, gain, shift):
    center = values - jnp.mean(values, axis=1, keepdims=True)
    spread = jnp.mean(center * center, axis=1, keepdims=True)
    return center * lax.rsqrt(spread + 1e-05) * gain + shift


def count_body(books, *refs):
    *packet_refs, out_ref = refs
    total = sum(p[books : books + 1, 0:128] for p in packet_refs)
    out_ref[...] = jnp.broadcast_to(total, out_ref.shape).astype(F32)


def merge_body(books, own_ref, far_ref, out_ref):
    own, far = own_ref[:books, :], far_ref[:books, :]
    high = jnp.maximum(own, far)
    out_ref[:books, :] = high + jnp.log(jnp.exp(own - high) + jnp.exp(far - high))
    out_ref[books:, :] = own_ref[books:, :] + far_ref[books:, :]


def text_in_body(need, put, place_ref, norm_ref, rows_ref, w_ref, out_ref):
    columns = out_ref.shape[1]
    at = pl.ds(pl.multiple_of(place_ref[0] * columns, columns), columns)
    need(2, 3)
    out_ref[...] = (nn(rows_ref[...], flat(w_ref)) + norm_ref[8:9, at]).astype(LOW)


def add_body(keep_ref, got_ref, out_ref):
    out_ref[...] = (keep_ref[...].astype(F32) + got_ref[...].astype(F32)).astype(LOW)


def add_parts_body(keep_ref, got_ref, *out_refs):
    start = 0
    for out_ref in out_refs:
        at = slice(start, start + out_ref.shape[0])
        start += out_ref.shape[0]
        out_ref[...] = (keep_ref[at, :].astype(F32) + got_ref[at, :].astype(F32)).astype(LOW)


def joined(refs):
    half = len(refs) // 2
    sums = [a[...].astype(F32) + b[...].astype(F32) for a, b in zip(refs[:half], refs[half:])]
    return jnp.concatenate(sums, axis=0)


def norm_body(which, hidden_ref, *refs):
    *part_refs, norm_ref, new_ref, out_ref = refs
    new = hidden_ref[...] + joined(part_refs)
    new_ref[...] = new
    out_ref[...] = normalize(
        new, norm_ref[which : which + 1, :], norm_ref[which + 4 : which + 5, :]
    ).astype(LOW)


def embed_norm_body(need, put, side_ref, place_ref, norm_ref, *refs):
    *part_refs, new_ref, out_ref = refs
    side = side_ref[0]
    rows = part_refs[0].shape[0]
    need(1, 2)
    for s, part in enumerate(part_refs):
        need(3 + s)
        at = pl.ds(pl.multiple_of((side ^ s) * rows, rows), rows)
        new = part[...].astype(F32) + place_ref[at, :]
        new_ref[at, :] = new
        out_ref[at, :] = normalize(new, norm_ref[0:1, :], norm_ref[4:5, :]).astype(LOW)
    put(1, 0)


def norm_back_body(which, parts, hidden_ref, *refs):
    *before, norm_ref, new_ref, low_ref, sums_ref = refs[parts:]
    sums = before.pop() if before and before[-1].shape[0] == sums_ref.shape[0] else None
    values = hidden_ref[...]
    grad = joined(refs[:parts])
    gain = norm_ref[which : which + 1, :]
    center = values - jnp.mean(values, axis=1, keepdims=True)
    spread = jnp.mean(center * center, axis=1, keepdims=True)
    inverse = lax.rsqrt(spread + 1e-05)
    unit = center * inverse
    scaled = grad * gain
    first = jnp.mean(scaled, axis=1, keepdims=True)
    second = jnp.mean(scaled * unit, axis=1, keepdims=True)
    new = inverse * (scaled - first - unit * second)
    if before:
        new = before[0][...] + new
    new_ref[...] = new
    low_ref[...] = new.astype(LOW)
    sums_ref[...] = jnp.zeros(sums_ref.shape, F32) if sums is None else sums[...]
    sums_ref[which : which + 1, :] += jnp.sum(grad * unit, axis=0, keepdims=True)
    sums_ref[which + 4 : which + 5, :] += jnp.sum(grad, axis=0, keepdims=True)


def weight_grad_body(clips, turn_left, need, put, core_ref, *refs):
    lefts = refs[: 2 * clips]
    rights = refs[2 * clips : 3 * clips]
    outs = refs[3 * clips : -1]
    turned = refs[-1]
    height, width = lefts[0].shape
    frames = rights[0].shape[0]
    group = outs[0].shape[2]
    core = core_ref[0]

    def place(c, at):
        return pl.ds(pl.multiple_of(c * frames + at * height, 128), height)

    if turn_left:
        step = min(group, 512)
        for m, v in [(m, v) for m in range(len(outs)) for v in range(0, group, step)]:
            total = None
            for c in range(clips):
                if m == 0 and v == 0:
                    for j, at in ((0, core), (1, 1 - core)):
                        need(1 + 2 * c + j)
                        turned[:, place(c, at)] = jnp.transpose(lefts[2 * c + j][...])
                    need(1 + 2 * clips + c)
                part = nn(
                    turned[:, c * frames : (c + 1) * frames],
                    rights[c][:, m * group + v : m * group + v + step],
                )
                total = part if total is None else total + part
            outs[m][:, :, v : v + step] = total.astype(LOW).reshape(-1, outs[m].shape[1], step)
            if v + step == group:
                put(m)
    else:
        total = None
        for c in range(clips):
            need(1 + 2 * clips + c)
            turned[:, c * frames : (c + 1) * frames] = jnp.transpose(rights[c][...])
            for j, at in ((0, core), (1, 1 - core)):
                need(1 + 2 * c + j)
                part = nn(turned[:, place(c, at)], lefts[2 * c + j][...])
                total = part if total is None else total + part
        for m, out_ref in enumerate(outs):
            member = total[m * group : (m + 1) * group, :]
            out_ref[...] = jnp.transpose(member).astype(LOW).reshape(out_ref.shape)
            put(m)


def norm_rows_kernel(body, outs, operands, norm_rows, after, name="norm"):
    height, width = operands[0].shape
    operands = list(operands) + ([] if norm_rows is None else [norm_rows])
    nbytes = sum(nbytes_of(a.shape, a.dtype) for a in operands + list(outs))
    return pl.pallas_call(
        later(body, len(after), len(operands)),
        out_shape=tuple(pltpu.VMEM(o.shape, o.dtype) for o in outs),
        in_specs=[in_vmem()] * len(operands) + [anywhere()] * len(after),
        out_specs=tuple(in_vmem() for _ in outs),
        compiler_params=pltpu.CompilerParams(vmem_limit_bytes=12 << 20),
        cost_estimate=SMALL,
        name=name,
    )(*(hold(a, pltpu.VMEM) for a in operands), *after)


def equal_to(code, local):
    local = jnp.clip(local, -1.0, 256.0).astype(LOW)
    return jnp.where(code == local, jnp.asarray(1, LOW), jnp.asarray(0, LOW))


def embed_body(count, books, base_ref, *refs):
    packets, tables, outs = refs[:count], refs[count : len(refs) - count], refs[len(refs) - count :]
    features, vocab = tables[0].shape[1:]
    rows = outs[0].shape[0]
    padded = packets[0].shape[1]
    chunk = min(256, vocab)
    code = lax.broadcasted_iota(jnp.int32, (chunk, padded), 0).astype(F32).astype(LOW)
    for packet, out_ref in zip(packets, outs):
        lines = packet[...].astype(F32)
        acc = jnp.zeros((features, padded), F32)
        for k in range(books):
            for b, table in enumerate(tables):
                local = lines[k : k + 1, :] - base_ref[b].astype(F32)
                for v in range(0, vocab, chunk):
                    acc = acc + nn(table[k, :, v : v + chunk], equal_to(code, local - float(v)))
        out_ref[...] = jnp.transpose(acc)[:rows, :].astype(LOW)


def embed(base, packets, tables, rows, after):
    books, features = tables[0].shape[:2]
    count = len(packets)
    return pl.pallas_call(
        later(partial(embed_body, count, books), len(after), 1 + count + len(tables)),
        out_shape=[sds((rows, features), LOW)] * count,
        in_specs=[scalars()]
        + [in_vmem()] * (count + len(tables))
        + [anywhere()] * len(after),
        out_specs=[in_vmem()] * count,
        compiler_params=pltpu.CompilerParams(vmem_limit_bytes=16 << 20),
        cost_estimate=SMALL,
        name="embed",
    )(base, *packets, *tables, *after)


def embed_back_body(groups, base_ref, line_ref, *refs):
    grads, (out_ref, turned, columns) = refs[:groups], refs[groups:]
    vocab = out_ref.shape[3]
    chunk = min(256, vocab)
    total = line_ref.shape[1]
    rows = total // groups

    @pl.when((pl.program_id(0) == 0) & (pl.program_id(1) == 0))
    def _():
        whole_rows = jnp.concatenate([g[:rows, :] for g in grads], axis=0)
        turned[...] = jnp.transpose(whole_rows)
        wide = jnp.concatenate(
            [line_ref[...].astype(F32), jnp.zeros((128 - line_ref.shape[0], total), F32)], axis=0
        )
        columns[...] = jnp.transpose(wide)

    base = base_ref[pl.program_id(0)].astype(F32)
    lane = lax.broadcasted_iota(jnp.int32, (total, 128), 1)
    column = jnp.sum(
        jnp.where(lane == pl.program_id(1), columns[...], 0.0), axis=1, keepdims=True
    )
    code = lax.broadcasted_iota(jnp.int32, (total, chunk), 1).astype(F32).astype(LOW)
    for v in range(0, vocab, chunk):
        hit = equal_to(code, column - (base + float(v)))
        out_ref[0, 0, :, v : v + chunk] = nn(turned[...], hit).astype(LOW)


def embed_back(base, lines, grads, books, vocab, after):
    parts = base.shape[0]
    groups = len(grads)
    features = grads[0].shape[1]
    rows = lines.shape[1] // groups
    return pl.pallas_call(
        later(partial(embed_back_body, groups), len(after), 2 + groups),
        out_shape=sds((parts, books, features, vocab), LOW),
        grid=(parts, books),
        in_specs=[scalars()] + [in_vmem()] * (1 + groups) + [anywhere()] * len(after),
        out_specs=pl.BlockSpec((1, 1, features, vocab), lambda i, k: (i, k, 0, 0)),
        scratch_shapes=[
            pltpu.VMEM((features, groups * rows), LOW),
            pltpu.VMEM((groups * rows, 128), F32),
        ],
        compiler_params=pltpu.CompilerParams(vmem_limit_bytes=32 << 20),
        cost_estimate=SMALL,
        name="embed_back",
    )(base, lines, *grads, *after)


def gather_features_body(need, put, where_ref, *refs):
    clips = sum(r.shape[1] != refs[0].shape[1] for r in refs)
    part_refs, outs = refs[:-clips], refs[-clips:]
    features = part_refs[0].shape[1]
    strip = outs[0].shape[0]
    for m, part in enumerate(part_refs):
        at = pl.ds(pl.multiple_of(where_ref[m] * features, features), features)
        for c, out_ref in enumerate(outs):
            out_ref[:, at] = part[c * strip : (c + 1) * strip, :]


def split_features_body(scale, need, put, where_ref, side_ref, place_ref, sums_ref, bias_ref, *refs):
    clips = side_ref.shape[0] - 1
    *refs, extra_ref = refs
    grads, outs = refs[:clips], refs[clips:]
    features = outs[0].shape[1]
    columns = bias_ref.shape[1]
    rows = (outs[0].shape[0] - extra_ref.shape[0]) // clips
    at_rows = pl.ds(pl.multiple_of(side_ref[0] * rows, rows), rows)
    extra_ref[...] = jnp.zeros(extra_ref.shape, F32)
    extra_ref[:8, :] = sums_ref[...] * scale
    at = pl.ds(pl.multiple_of(place_ref[0] * columns, columns), columns)
    extra_ref[8:9, at] = bias_ref[0:1, :]
    for m, out_ref in enumerate(outs):
        at = pl.ds(pl.multiple_of(where_ref[m] * features, features), features)
        for c in range(clips):
            out_ref[c * rows : (c + 1) * rows, :] = grads[c][at_rows, at]
        out_ref[clips * rows :, :] = extra_ref[:, at].astype(LOW)


def extra_body(*refs):
    *part_refs, out_ref = refs
    count = out_ref.shape[0]
    out_ref[...] = sum(p[p.shape[0] - count :, :].astype(F32) for p in part_refs)


def text_body(need, put, where_ref, *refs):
    *part_refs, wk_ref, wv_ref, tp_ref, k_ref, v_ref = refs
    columns = part_refs[0].shape[1]
    for m, part in enumerate(part_refs):
        need(1 + m)
        at = pl.ds(pl.multiple_of(where_ref[m] * columns, columns), columns)
        tp_ref[:, at] = part[...]
    put(0)
    for j, w_ref, to_ref in ((1, wk_ref, k_ref), (2, wv_ref, v_ref)):
        need(len(part_refs) + j)
        to_ref[...] = nn(tp_ref[...], flat(w_ref)).astype(LOW)
        put(j)


def text_back_body(clips, need, put, where_ref, *refs):
    dks, dvs = refs[:clips], refs[clips : 2 * clips]
    wk_ref, wv_ref, tp_ref = refs[2 * clips : 2 * clips + 3]
    *part_refs, gk_ref, gv_ref, full_ref = refs[2 * clips + 3 :]
    columns = part_refs[0].shape[1]
    length = dks[0].shape[0]
    need(*range(1, 1 + 2 * clips + 2))
    wk, wv = flat(wk_ref), flat(wv_ref)
    for c in range(clips):
        tp_rows = slice(c * length, (c + 1) * length)
        full_ref[tp_rows, :] = (nt(dks[c][...], wk) + nt(dvs[c][...], wv)).astype(LOW)
    for m, part_ref in enumerate(part_refs):
        at = pl.ds(pl.multiple_of(where_ref[m] * columns, columns), columns)
        part_ref[...] = full_ref[:, at]
    put(*range(len(part_refs)))
    need(3 + 2 * clips)
    turned = jnp.transpose(tp_ref[...])
    for j, grads, to_ref in ((0, dks, gk_ref), (1, dvs, gv_ref)):
        total = None
        for c in range(clips):
            part = nn(turned[:, c * length : (c + 1) * length], grads[c][...])
            total = part if total is None else total + part
        to_ref[...] = total.astype(LOW).reshape(to_ref.shape)
        put(len(part_refs) + j)


def text_weight_body(need, put, rows_ref, own_ref, far_ref, out_ref, bias_ref):
    need(0)
    grad = (own_ref[...].astype(F32) + far_ref[...].astype(F32)).astype(LOW)
    out_ref[...] = tn(rows_ref[...], grad).astype(LOW).reshape(out_ref.shape)
    bias_ref[...] = jnp.broadcast_to(
        jnp.sum(grad.astype(F32), axis=0, keepdims=True), bias_ref.shape
    )


def positions_rows(start, count, feature_count):
    half_width = feature_count // 2
    frequency = jnp.exp(
        jnp.arange(half_width, dtype=F32) * (-math.log(10000.0) / (half_width - 1))
    )
    angles = (start + jnp.arange(count, dtype=jnp.int32)).astype(F32)[:, None] * frequency[None, :]
    return jnp.concatenate([jnp.cos(angles), jnp.sin(angles)], axis=1)


def adam_update(weight, gradient, first_moment, second_moment, step_rate, factor):
    clipped = gradient * factor
    new_first = moment_decay * first_moment + (1.0 - moment_decay) * clipped
    new_second = moment_decay * second_moment + (1.0 - moment_decay) * clipped * clipped
    first_hat = new_first / (1.0 - moment_decay**STEP)
    second_hat = new_second / (1.0 - moment_decay**STEP)
    new_weight = weight * (1.0 - step_rate * weight_decay) - step_rate * first_hat / (
        jnp.sqrt(second_hat) + stability_offset
    )
    return (new_weight, new_first, new_second)


def swap(values, axis, mask):
    size = lax.axis_size(axis)
    return lax.ppermute(values, axis, [(i, i ^ mask) for i in range(size)])


def on_device(
    audio_codes,
    delay_mask,
    frame_mask,
    text_states,
    text_mask,
    attention,
    feedforward,
    tables,
    text_proj,
    norm_params,
    attention_first,
    attention_second,
    feedforward_first,
    feedforward_second,
    tables_first,
    tables_second,
    text_first,
    text_second,
    norm_first,
    norm_second,
):
    clips, frames, books = audio_codes.shape
    text_len, text_width = text_states.shape[1:]
    dp = lax.axis_size("dp")
    tensor = lax.axis_size("tensor")
    group = lax.axis_index("dp")
    place = lax.axis_index("tensor")
    core = place & 1
    side = place >> 1
    sides = tensor // 2
    height = frames // 2
    strip = height // sides
    share = attention.shape[1]
    columns = attention.shape[2]
    width = share * dp
    vocab = tables.shape[2]
    text_share = text_proj.shape[1]
    core_arg = Scalar(core.astype(jnp.int32).reshape(1))
    side_arg = Scalar(side.astype(jnp.int32).reshape(1))
    swap_core = partial(swap, axis="tensor", mask=1)

    def spread_tensor(values):
        held = [values]
        mask = tensor // 2
        order = [0]
        while mask:
            held = held + [swap(v, "tensor", mask) for v in held]
            order = order + [o | mask for o in order]
            mask //= 2
        return [v for _, v in sorted(zip(order, held), key=lambda t: t[0])]

    def collect_tensor(parts):
        mask = 1
        live = {m: p for m, p in enumerate(parts)}
        while mask < tensor:
            fresh = {}
            for m in live:
                if not m & mask:
                    got = swap(live[m | mask].astype(LOW), "tensor", mask)
                    fresh[m] = live[m].astype(F32) + got.astype(F32)
            live = fresh
            mask *= 2
        return live[0]

    def across(values):
        own = values
        mask = 2
        rest = None
        while mask < tensor:
            got = swap(own, "tensor", mask)
            mask *= 2
            if mask < tensor:
                own = (own.astype(F32) + got.astype(F32)).astype(LOW)
            rest = got
        if rest is None:
            rest = jnp.zeros_like(own)
        return own, rest

    def total_over(values, axes):
        for axis in axes:
            mask = 1
            while mask < lax.axis_size(axis):
                values = values + swap(values, axis, mask)
                mask *= 2
        return values

    last = []

    def run(body, outs, operands, after=(), **rest):
        *results, token = kernel(body, outs, operands, after=last + list(after), **rest)
        last[:] = [token]
        return results

    def run_block(*args, **rest):
        return run(*args, **rest)

    def run_weight(*args, **rest):
        results = run(*args, after=older[:1] or soon[:1], **rest)
        if older:
            older.clear()
        else:
            soon.clear()
        return results

    norm_pad = jnp.pad(norm_params.astype(LOW), ((0, 16 - norm_params.shape[0]), (0, columns - share)))
    attn_rows = attention.astype(LOW)
    self_flat = jnp.concatenate([attn_rows[n] for n in SELF] + [norm_pad], axis=0)
    cross_flat = jnp.concatenate([attn_rows[n] for n in CROSS] + [text_proj.astype(LOW).T], axis=0)
    self_all = lax.all_gather(self_flat, "dp", axis=0)
    cross_all = lax.all_gather(cross_flat, "dp", axis=0)
    ffn_all = lax.all_gather(feedforward.astype(LOW), "dp", axis=0)
    head_all = lax.all_gather(tables[books:].astype(LOW), "dp", axis=0)

    frame_live = (jnp.arange(frames, dtype=jnp.int32) < frames - 1).astype(jnp.int32)
    weight_int = delay_mask * frame_mask[:, :, None] * frame_live[None, :, None]
    start = core * height + side * strip
    strip_codes = lax.dynamic_slice_in_dim(audio_codes, start, strip, 1)
    count = clips * strip
    padded = -(-count // 128) * 128
    lines = jnp.transpose(strip_codes, (2, 0, 1)).reshape(books, count)
    lines = jnp.pad(lines, ((0, 0), (0, padded - count)), constant_values=-1)
    count_line = jnp.broadcast_to(jnp.sum(weight_int), (8 - books, padded))
    packet = jnp.concatenate([lines, count_line], axis=0)
    packets = [packet] + [swap(packet, "dp", m) for m in range(1, dp)]
    vocab_base = (place ^ jnp.arange(tensor, dtype=jnp.int32)) * vocab
    group_order = group ^ jnp.arange(dp, dtype=jnp.int32)
    place_order = place ^ jnp.arange(tensor, dtype=jnp.int32)

    text_bias_row = jnp.where(text_mask > 0, 0.0, NEG).astype(F32)
    bias_lines = [text_bias_row[c : c + 1] for c in range(clips)]
    bias_columns = [jnp.transpose(line) for line in bias_lines]
    targets = (jnp.roll(audio_codes, -1, axis=1) - place * vocab).astype(jnp.int32)
    targets = [targets[c] for c in range(clips)]
    loss_weight = [weight_int[c].astype(F32) for c in range(clips)]

    table_parts = spread_tensor(tables[:books].astype(LOW))
    step = max(1, dp // 4)
    arrived = [None] * dp
    for low_end in reversed(range(0, dp, step)):
        embedded = embed(
            vocab_base, packets[low_end : low_end + step], table_parts, count, list(last)
        )
        last[:] = [embedded[-1]]
        if low_end + step == dp:
            begin, _ = lax.optimization_barrier((core * height, embedded[0]))
            placed = positions_rows(begin, height, width)
        for m, piece in enumerate(embedded, low_end):
            arrived[m] = swap(piece, "dp", m) if m else piece
        last += [a for a in arrived[low_end + step : low_end + 2 * step] if a is not None]
    (counted,) = norm_rows_kernel(
        partial(count_body, books), [sds((8, 128), F32)], packets, None, last, name="count"
    )
    back_lines = jnp.concatenate([p[:, :count] for p in packets], axis=1)
    last[:] = bias_lines + bias_columns + targets + loss_weight + [placed, counted, back_lines]
    last += [a for a in arrived if a is not None]
    aligned = share % 128 == 0
    if aligned:
        strips = run(
            gather_features_body,
            [Flow(sds((strip, width), LOW))] * clips,
            [Scalar(group_order)] + arrived,
            name="gather_features",
        )
        strips = [free(a) for a in strips]
    else:
        strips = jnp.take(jnp.stack(arrived), group_order, axis=0)
        strips = jnp.transpose(strips, (1, 0, 2)).reshape(clips, strip, width)

    norm_rows = self_all[:, 4 * share :, :share]
    norm_rows = jnp.transpose(norm_rows, (1, 0, 2)).reshape(16, width).astype(F32)

    def w_attn(n):
        array, at = (self_all, SELF.index(n)) if n in SELF else (cross_all, CROSS.index(n))
        return Window(
            array, (dp, share, columns), lambda ref: ref.at[:, pl.ds(at * share, share), :]
        )

    def w_member(array, n):
        return Window(array, (dp,) + array.shape[2:], lambda ref: ref.at[:, n])

    half_sds = sds((height, width), F32)
    half_low = sds((height, width), LOW)
    flow = Flow(half_low)

    def fetch(a):
        return Window(a, a.shape, everything)


    def norm_step(which, hidden, parts):
        new, out = norm_rows_kernel(
            partial(norm_body, which),
            [half_sds, half_low],
            [hidden, *parts],
            norm_rows,
            last + soon,
        )
        soon[:] = []
        last[:] = [out]
        return new, (out, swap_core(free(out)))

    def norm_back(which, c, parts, before):
        rows = near.get((which, c, "back"), hidden[which][c])
        if before is not None:
            before = near_grad.get((which, c), before)
        operands = [rows, *parts] + ([before] if before is not None else []) + sums
        new, out, total = norm_rows_kernel(
            partial(norm_back_body, which, len(parts)),
            [half_sds, half_low, sds((8, width), F32)],
            operands,
            norm_rows,
            last + soon,
        )
        soon[:] = []
        last[:] = [out]
        sums[:] = [total]
        return new, (out, swap_core(free(out)))

    sums = []
    waiting, soon, older, newest = [], [], [], []
    moving = [None] * clips

    def flush():
        if waiting:
            c, keep, got = waiting.pop()
            parts = norm_rows_kernel(
                add_parts_body,
                [sds((height * part // sum(PIECES), width), LOW) for part in PIECES],
                [keep, got],
                None,
                last,
                name="add",
            )
            last[:] = [parts[-1]]
            fars = [across(free(part))[1] for part in parts]
            moving[c] = (*parts, *fars)
            soon[:] = fars[:-1]
            older[:] = newest
            newest[:] = fars[-1:]

    def reduce_rows(c, keep, send):
        waiting.append((c, keep, swap_core(free(send))))

    text_rows = text_states.reshape(clips * text_len, text_width)
    def text_in_step():
        (result,) = run(
            text_in_body,
            [Flow(sds((clips * text_len, columns), LOW))],
            [
                Scalar(place.astype(jnp.int32).reshape(1)),
                norm_rows,
                fetch(text_rows),
                Window(
                    cross_all,
                    (dp, text_share, columns),
                    lambda ref: ref.at[:, pl.ds(4 * share, text_share), :],
                ),
            ],
            flops=2 * clips * text_len * text_width * columns,
            name="text_in",
        )
        return spread_tensor(free(result))

    full = sds((frames, columns), LOW)
    lse_sds = sds((8, frames), F32)
    tot = [pltpu.VMEM((frames, 128), F32)]
    heads = columns // HEAD_DIM
    score_flops = 2 * heads * frames * HEAD_DIM
    units = feedforward.shape[2]
    inner = sds((frames, units), LOW)
    every = range(clips)

    near, near_grad = {}, {}

    def ahead(phase, c):
        at, clip = (phase - 1, c + 1) if c + 1 < clips else (phase, 0)
        if at < 0 or (phase == 3 and clip == 0) or (clip == c):
            return []
        return [Ahead(hidden[at][clip])]

    def took(phase, c, results):
        at, clip = (phase - 1, c + 1) if c + 1 < clips else (phase, 0)
        if ahead(phase, c):
            *results, near[at, clip] = results
        return results

    def ahead_back(phase, c):
        at, clip = (phase, c + 1) if c + 1 < clips else (phase - 1, 0)
        if clip == c:
            return []
        found = [Ahead(hidden[at][clip])]
        if at < 3:
            found.append(Ahead(grads[clip]))
        return found

    def took_back(phase, c, results):
        at, clip = (phase, c + 1) if c + 1 < clips else (phase - 1, 0)
        count = len(ahead_back(phase, c))
        if count == 2:
            near_grad[at, clip] = results[-1]
        if count:
            near[at, clip, "back"] = results[len(results) - count]
        return results[: len(results) - count]

    def embed_step(c):
        mine = strips[c]
        parts = [mine] + [swap(mine, "tensor", 2 * s) for s in range(1, sides)]
        new, out = run(
            embed_norm_body,
            [Flow(half_sds), Flow(half_low)],
            [side_arg, placed, norm_rows] + parts,
            flops=10 * height * width,
            name="embed_norm",
        )
        return new, (out, swap_core(free(out)))

    def self_step(c, pair):
        own, got = pair
        *saved, keep, send, left, right, hidden[0][c] = took(0, c, run_block(
            self_forward_body,
            [full, full, full, full, lse_sds, flow, flow, Copy(1), Copy(3)],
            [core_arg, own, w_attn(0), got, w_attn(1), w_attn(2), w_attn(6)]
            + [Carry(hidden[0][c])]
            + ahead(0, c),
            flops=8 * frames * width * columns + 4 * score_flops * frames,
            scratch=tot,
            name="self_forward",
        ))
        pairs[0][c] = (left, right)
        reduce_rows(c, keep, send)
        return saved

    text_full = sds((clips * text_len, width), LOW)
    text_cols = sds((clips * text_len, columns), LOW)

    def text_step():
        return run(
            text_body,
            [text_full, text_cols, text_cols],
            [Scalar(place_order)] + text_parts + [w_attn(4), w_attn(5)],
            flops=4 * clips * text_len * width * columns,
            name="text",
        )

    def text_rows_of(array, c):
        return Window(
            array, (text_len, columns), lambda ref: ref.at[pl.ds(c * text_len, text_len), :]
        )

    def cross_step(c, pair):
        own, got = pair
        k, v = text_rows_of(text_key, c), text_rows_of(text_value, c)
        q, o, lse, keep, send, left, right, hidden[1][c] = took(1, c, run_block(
            cross_forward_body,
            [full, full, lse_sds, flow, flow, Copy(1), Copy(3)],
            [core_arg, own, w_attn(3), got, bias_lines[c], k, v, w_attn(7)]
            + [Carry(hidden[1][c])]
            + ahead(1, c),
            flops=4 * frames * width * columns + 4 * score_flops * text_len,
            scratch=tot,
            name="cross_forward",
        ))
        pairs[1][c] = (left, right)
        reduce_rows(c, keep, send)
        return (q, k, v, o, lse)

    def ffn_step(c, pair):
        *saved, keep, send, left, right, hidden[2][c] = took(2, c, run_block(
            ffn_forward_body,
            [inner, inner, flow, flow, Copy(1), Copy(2)],
            [core_arg, *pair, w_member(ffn_all, 0), w_member(ffn_all, 1), Carry(hidden[2][c])]
            + ahead(2, c),
            flops=4 * frames * width * units,
            name="ffn_forward",
        ))
        pairs[2][c] = (left, right)
        reduce_rows(c, keep, send)
        return saved

    hidden = [[None] * clips for _ in range(4)]
    pairs = [[None] * clips for _ in range(4)]
    kept = [[None] * clips for _ in range(3)]
    for c in every:
        hidden[0][c], pairs[0][c] = embed_step(c)
        flush()
        kept[0][c] = self_step(c, pairs[0][c])
        if c == min(1, clips - 1):
            text_parts = text_in_step()
    text_hidden, text_key, text_value = text_step()
    for c in every:
        hidden[1][c], pairs[1][c] = norm_step(1, near.get((0, c), hidden[0][c]), moving[c])
        flush()
        kept[1][c] = cross_step(c, pairs[1][c])
    for c in every:
        hidden[2][c], pairs[2][c] = norm_step(2, near.get((1, c), hidden[1][c]), moving[c])
        flush()
        kept[2][c] = ffn_step(c, pairs[2][c])

    loss_part = [None] * clips

    def head_step(c, pair):
        own, got = pair
        logits, stats, left, right, hidden[3][c] = took(3, c, run_block(
            head_forward_body,
            [
                sds((frames, books * vocab), F32),
                Flow(sds((2 * books, frames), F32)),
                Copy(1),
                Copy(3),
            ],
            [core_arg, own, targets[c], got]
            + [w_member(head_all, k) for k in range(books)]
            + [Carry(hidden[3][c])]
            + ahead(3, c),
            flops=2 * frames * width * books * vocab,
            scratch=tot,
            name="head_forward",
        ))
        pairs[3][c] = (left, right)
        return logits, stats

    def merge_step(stats):
        mask = 1
        while mask < tensor:
            far = swap(free(stats), "tensor", mask)
            (stats,) = norm_rows_kernel(
                partial(merge_body, books),
                [sds((2 * books, frames), F32)],
                [stats, far],
                None,
                last,
                name="merge",
            )
            last[:] = [stats]
            mask *= 2
        return stats

    def head_back_step(c, logits, stats, pieces):
        grad, keep, send, loss = run_block(
            head_backward_body,
            [sds((frames, books * vocab), LOW), flow, flow, Flow(sds((8, 128), F32))],
            [core_arg, stats, loss_weight[c], targets[c], fetch(logits)]
            + [w_member(head_all, k) for k in range(books)]
            + [counted],
            flops=2 * frames * width * books * vocab,
            scratch=tot,
            after=pieces,
            name="head_backward",
        )
        loss_part[c] = free(loss)[0, 0]
        reduce_rows(c, keep, send)
        return grad

    self_shared = Shared((dp, 4 * share + text_share, columns), LOW)
    cross_shared = Shared((dp, 4 * share, columns), LOW)
    ffn_shared = Shared((dp,) + feedforward.shape, LOW)
    head_shared = Shared((dp, books, share, vocab), LOW)

    def attn_into(n):
        shared, at = (
            (self_shared, SELF.index(n)) if n in SELF else (cross_shared, CROSS.index(n))
        )
        return Into(
            shared, (dp, share, columns), lambda ref: ref.at[:, pl.ds(at * share, share), :]
        )

    def member_into(shared, n):
        return Into(shared, (dp,) + shared.full.shape[2:], lambda ref: ref.at[:, n])

    def halves(rights, shared, n):
        step = rights[0].shape[1] // 2
        found = []
        for at in (0, step):
            windows = [
                Window(a, (frames, step), lambda ref, at=at: ref.at[:, pl.ds(at, step)])
                for a in rights
            ]
            into = Into(
                shared, (dp, share, step), lambda ref, at=at: ref.at[:, n, :, pl.ds(at, step)]
            )
            found.append((windows, [into]))
        return found

    def weights(lefts, rights, outs, name):
        rights = [a if isinstance(a, Window) else fetch(a) for a in rights]
        total = rights[0].shape[1]
        turn_left = 2 * total > width
        run_weight(
            partial(weight_grad_body, clips, turn_left),
            outs,
            [core_arg] + [fetch(half) for pair in lefts for half in pair] + rights,
            flops=2 * clips * frames * width * total,
            scratch=[pltpu.VMEM((width if turn_left else total, clips * frames), LOW)],
            name=name,
            margin=16,
        )

    logit_grads = [None] * clips
    ready = [None] * clips
    for c in every:
        hidden[3][c], pairs[3][c] = norm_step(3, near.get((2, c), hidden[2][c]), moving[c])
        flush()
        ready[c] = head_step(c, pairs[3][c])
        if c:
            pieces = soon + (newest if c == clips - 1 else [])
            flush()
            logits, stats = ready[c - 1]
            logit_grads[c - 1] = head_back_step(c - 1, logits, merge_step(stats), pieces)
    logits, stats = ready[-1]
    stats = merge_step(stats)
    pieces = []
    flush()
    logit_grads[-1] = head_back_step(clips - 1, logits, stats, pieces)

    def ffn_back_step(c, pair):
        own, got = pair
        grad, keep, send, left, right, grads[c] = took_back(3, c, run_block(
            ffn_backward_body,
            [inner, flow, flow, Copy(1), Copy(2)],
            [core_arg, own, got, w_member(ffn_all, 1), fetch(kept[2][c][1]), w_member(ffn_all, 0)]
            + [Carry(grads[c])]
            + ahead_back(3, c),
            flops=4 * frames * width * units,
            name="ffn_backward",
        ))
        back_pairs[3][c] = (left, right)
        reduce_rows(c, keep, send)
        return grad

    grads = [None] * clips
    back_pairs = [[None] * clips for _ in range(4)]
    inner_grads = [None] * clips
    for c in every:
        grads[c], back_pairs[3][c] = norm_back(3, c, moving[c], None)
        flush()
        inner_grads[c] = ffn_back_step(c, back_pairs[3][c])
        if c == 0:
            step = books // 2 * vocab
            for at in (0, 1):
                windows = [
                    Window(a, (frames, step), lambda ref, at=at: ref.at[:, pl.ds(at * step, step)])
                    for a in logit_grads
                ]
                into = [
                    member_into(head_shared, k) for k in range(at * books // 2, (at + 1) * books // 2)
                ]
                weights(pairs[3], windows, into, "head_weights")
    head_sum = lax.psum_scatter(free(head_shared.array), "dp", scatter_dimension=0, tiled=False)

    acc_text = [pltpu.VMEM((text_len, columns), F32)] * 2
    small = sds((text_len, columns), LOW)

    def cross_back_step(c, pair):
        own, got = pair
        q, k, v, o, lse = kept[1][c]
        bias = bias_columns[c]
        dq, dk, dv, keep, send, left, right, grads[c] = took_back(2, c, run_block(
            cross_backward_body,
            [full, small, small, flow, flow, Copy(1), Copy(3)],
            [core_arg, own, w_attn(7), got, bias, fetch(q), k, v, fetch(lse), w_attn(3)]
            + [Carry(grads[c])]
            + ahead_back(2, c),
            flops=4 * frames * width * columns + 10 * score_flops * text_len,
            scratch=[pltpu.VMEM((frames, columns), LOW)] + acc_text,
            name="cross_backward",
        ))
        back_pairs[2][c] = (left, right)
        reduce_rows(c, keep, send)
        return (dq, dk, dv)

    cross_grads = [None] * clips
    for c in every:
        grads[c], back_pairs[2][c] = norm_back(2, c, moving[c], grads[c])
        flush()
        cross_grads[c] = cross_back_step(c, back_pairs[2][c])
        if c == 0:
            for windows, into in halves([k[0] for k in kept[2]], ffn_shared, 1):
                weights(back_pairs[3], windows, into, "ffn_two")
        if c == min(1, clips - 1):
            for windows, into in halves(inner_grads, ffn_shared, 0):
                weights(pairs[2], windows, into, "ffn_one")
    ffn_sum = lax.psum_scatter(free(ffn_shared.array), "dp", scatter_dimension=0, tiled=False)

    def text_back_step():
        results = run_weight(
            partial(text_back_body, clips),
            [Flow(text_cols)] * tensor + [attn_into(4), attn_into(5)],
            [Scalar(place_order)]
            + [fetch(g[1]) for g in cross_grads]
            + [fetch(g[2]) for g in cross_grads]
            + [w_attn(4), w_attn(5), fetch(text_hidden)],
            flops=8 * clips * text_len * width * columns,
            scratch=[pltpu.VMEM((clips * text_len, width), LOW)],
            name="text_back",
        )
        live = dict(enumerate(results))
        mask = 1
        while mask < tensor:
            fresh = {}
            for m in live:
                if not m & mask:
                    fresh[m] = (live[m], swap(free(live[m | mask]), "tensor", mask))
            mask *= 2
            if mask < tensor:
                for m, both in fresh.items():
                    (fresh[m],) = norm_rows_kernel(
                        add_body, [text_cols], list(both), None, last, name="add"
                    )
                    last[:] = [fresh[m]]
            live = fresh
        return live[0]

    acc_self = [pltpu.VMEM((frames, columns), F32)] * 2

    def self_back_step(c, pair):
        own, got = pair
        q, k, v, o, lse = kept[0][c]
        grad, keep, send, left, right, grads[c] = took_back(1, c, run_block(
            self_backward_body,
            [sds((frames, 3 * columns), LOW), flow, flow, Copy(1), Copy(3)],
            [core_arg, own, w_attn(6), got]
            + [fetch(a) for a in (q, k, v, lse)]
            + [w_attn(0), w_attn(1), w_attn(2), Carry(grads[c])]
            + ahead_back(1, c),
            flops=8 * frames * width * columns + 10 * score_flops * frames,
            scratch=[pltpu.VMEM((frames, columns), LOW)] + acc_self,
            name="self_backward",
        ))
        back_pairs[1][c] = (left, right)
        reduce_rows(c, keep, send)
        return grad

    self_grads = [None] * clips
    last.append(head_sum)
    for c in every:
        grads[c], back_pairs[1][c] = norm_back(1, c, moving[c], grads[c])
        flush()
        self_grads[c] = self_back_step(c, back_pairs[1][c])
        if c == 0:
            text_grad = text_back_step()
            weights(back_pairs[2], [k[3] for k in kept[1]], [attn_into(7)], "cross_out")
            weights(pairs[1], [g[0] for g in cross_grads], [attn_into(3)], "cross_query")
            cross_sum = lax.psum_scatter(
                free(cross_shared.array), "dp", scatter_dimension=0, tiled=False
            )

    zero_lows = [None] * clips

    def zero_step(c):
        _, (zero_lows[c], _) = norm_back(0, c, moving[c], grads[c])

    weights(back_pairs[1], [k[3] for k in kept[0]], [attn_into(6)], "self_out")
    first = list(soon)
    flush()
    text_into = Into(
        self_shared,
        (dp, text_share, columns),
        lambda ref: ref.at[:, pl.ds(4 * share, text_share), :],
    )
    (bias_grad,) = run(
        text_weight_body,
        [text_into, Flow(sds((8, columns), F32))],
        [fetch(text_rows), *text_grad],
        after=[ffn_sum] + first,
        flops=2 * clips * text_len * text_width * columns,
        name="text_weight",
    )
    def self_in(members):
        size = len(members) * columns
        windows = [
            Window(a, (frames, size), lambda ref: ref.at[:, pl.ds(members[0] * columns, size)])
            for a in self_grads
        ]
        weights(pairs[0], windows, [attn_into(n) for n in members], "self_in")

    self_in((0, 1))
    for c in every:
        if c == clips - 1:
            older[:] = newest
            self_in((2,))
            self_sum = lax.psum_scatter(
                free(self_shared.array), "dp", scatter_dimension=0, tiled=False
            )
        zero_step(c)

    if aligned:
        pieces = run(
            partial(split_features_body, 1.0 / sides),
            [Flow(sds((clips * strip + 16, share), LOW))] * dp,
            [
                Scalar(group_order),
                Scalar(jnp.broadcast_to(side.astype(jnp.int32), (clips + 1,))),
                Scalar(place.astype(jnp.int32).reshape(1)),
                sums[0],
                bias_grad,
            ]
            + zero_lows,
            scratch=[pltpu.VMEM((16, width), F32)],
            after=[cross_sum],
            name="split_features",
        )
        pieces = [free(p) for p in pieces]
    else:
        rows = jnp.concatenate(
            [lax.dynamic_slice_in_dim(free(a), side * strip, strip, 0) for a in zero_lows], axis=0
        )
        rows = jnp.transpose(rows.reshape(clips * strip, dp, share), (1, 0, 2))
        pieces = list(jnp.take(rows, group_order, axis=0))
    rows_all = [pieces[0]] + [swap(pieces[m], "dp", m) for m in range(1, dp)]
    embed_parts = embed_back(vocab_base, back_lines, rows_all, books, vocab, list(last))
    grad_embed = collect_tensor([embed_parts[m] for m in range(tensor)])

    if aligned:
        (extra,) = norm_rows_kernel(
            extra_body, [sds((16, share), F32)], rows_all, None, last, name="extra"
        )
        grad_norm_rows = total_over(free(extra), ("tensor",))[: norm_params.shape[0]]
    else:
        norm_part = free(sums[0]) * (1.0 / sides)
        bias_row = lax.dynamic_update_slice_in_dim(
            jnp.zeros((width,), F32), free(bias_grad)[0], place * columns, 0
        )
        norm_total = total_over(
            jnp.concatenate([norm_part, bias_row[None]], axis=0), ("tensor", "dp")
        )
        grad_norm_rows = lax.dynamic_slice_in_dim(norm_total, group * share, share, 1)

    own_self = self_sum[: 4 * share].reshape(4, share, columns)
    own_cross = cross_sum.reshape(4, share, columns)
    grad_attention = jnp.concatenate(
        [own_self[:3], own_cross[:3], own_self[3:], own_cross[3:]], axis=0
    ).astype(F32)
    grad_text_proj = jnp.transpose(self_sum[4 * share :]).astype(F32)
    grad_feedforward = ffn_sum.astype(F32)
    grad_heads = head_sum.astype(F32)
    local_square = (
        jnp.sum(jnp.square(self_sum.astype(F32)))
        + jnp.sum(jnp.square(cross_sum.astype(F32)))
        + jnp.sum(grad_feedforward * grad_feedforward)
        + jnp.sum(grad_heads * grad_heads)
        + jnp.sum(grad_embed * grad_embed)
        + jnp.sum(grad_norm_rows * grad_norm_rows) / tensor
    )
    both = total_over(
        jnp.stack([local_square, sum(loss_part) / tensor]).reshape(1, 2), ("tensor", "dp")
    )[0]
    grad_norm = jnp.sqrt(both[0])
    mean_loss = both[1]
    factor = clip_limit / jnp.maximum(grad_norm, clip_limit)
    grad_tables = jnp.concatenate([grad_embed, grad_heads], 0)
    attn_new, attn_first_new, attn_second_new = adam_update(
        attention, grad_attention, attention_first, attention_second, rate_matrix, factor
    )
    ffn_new, ffn_first_new, ffn_second_new = adam_update(
        feedforward, grad_feedforward, feedforward_first, feedforward_second, rate_matrix, factor
    )
    table_new, table_first_new, table_second_new = adam_update(
        tables, grad_tables, tables_first, tables_second, rate_table, factor
    )
    text_new, text_first_new, text_second_new = adam_update(
        text_proj, grad_text_proj, text_first, text_second, rate_matrix, factor
    )
    norm_new, norm_first_new, norm_second_new = adam_update(
        norm_params, grad_norm_rows, norm_first, norm_second, rate_norm, factor
    )
    return (
        mean_loss,
        free(counted)[0, 0],
        grad_norm,
        attn_new,
        attn_new.astype(LOW),
        attn_first_new,
        attn_second_new,
        ffn_new,
        ffn_new.astype(LOW),
        ffn_first_new,
        ffn_second_new,
        table_new,
        table_new.astype(LOW),
        table_first_new,
        table_second_new,
        text_new,
        text_new.astype(LOW),
        text_first_new,
        text_second_new,
        norm_new,
        norm_first_new,
        norm_second_new,
    )


def solution(mesh):
    clip3 = P("dp", None, None)
    clip2 = P("dp", None)
    matrix = P(None, "dp", "tensor")
    text = P("tensor", "dp")
    norm = P(None, "dp")
    placed = (
        (clip3, clip3, clip2, clip3, clip2)
        + (matrix, matrix, matrix, text, norm)
        + (matrix,) * 6
        + (text, text, norm, norm)
    )
    return jax.shard_map(
        on_device,
        mesh=mesh,
        in_specs=placed,
        out_specs=(P(), P(), P()) + (matrix,) * 12 + (text,) * 4 + (norm,) * 3,
        check_vma=False,
    )
```
